32 devices in a mesh: dp: 8 (over z, y), tensor: 4 (over x, core).
Axes of the slice: x: 2, y: 2, z: 4, core: 2. Of those that a mesh axis runs over, the one named last changes fastest.
Arguments:
- res_in: bfloat16 [5120, 2048], P(('dp', 'tensor')), may hold values from -30 to 30
- out_grad: bfloat16 [5120, 2048], P(('dp', 'tensor')), may hold values from -6 to 6
- seg_ids: int32 [8, 640], P('dp'), may hold values from 0 to 2, never falling along the last dimension, each value on 1 to 512 neighbouring positions
- tok_counts: int32 [8], P('dp'), may hold values from 320 to 640, as said below
- slot_table: int32 [8, 4, 640], P('dp'), may hold values from -1 to 639, as said below
- slot_gates: float32 [8, 4, 640], P('dp'), may hold values from 0.1 to 1
- attn_gain: bfloat16 [2048], P(('dp', 'tensor')), may hold values from 0.099609375 to 1.8984375
- latent_gain: bfloat16 [512], P(('dp', 'tensor')), may hold values from 0.099609375 to 1.8984375
- ffn_gain: bfloat16 [2048], P(('dp', 'tensor')), may hold values from 0.099609375 to 1.8984375
- w_latent: bfloat16 [2048, 576], P(('dp', 'tensor')), may hold values from -0.125 to 0.125
- w_query: bfloat16 [2048, 3072], P('dp', 'tensor'), may hold values from -0.125 to 0.125
- w_keyval: bfloat16 [512, 4096], P('dp', 'tensor'), may hold values from -0.25 to 0.25
- w_output: bfloat16 [2048, 2048], P('tensor', 'dp'), may hold values from -1 to 1
- w_expert_in: bfloat16 [4, 2, 2048, 1408], P(None, None, 'dp', 'tensor'), may hold values from -0.125 to 0.125
- w_expert_out: bfloat16 [4, 1408, 2048], P(None, 'tensor', 'dp'), may hold values from -0.15625 to 0.15625
- w_shared_in: bfloat16 [2, 2048, 2816], P(None, 'dp', 'tensor'), may hold values from -0.125 to 0.125
- w_shared_out: bfloat16 [2816, 2048], P('tensor', 'dp'), may hold values from -0.109375 to 0.109375
Outputs:
- res_out: bfloat16 [5120, 2048], P(('dp', 'tensor'))
- res_grad: float32 [5120, 2048], P(('dp', 'tensor'))
- attn_gain_grad: float32 [2048], P(('dp', 'tensor'))
- latent_gain_grad: float32 [512], P(('dp', 'tensor'))
- ffn_gain_grad: float32 [2048], P(('dp', 'tensor'))
- w_latent_grad: float32 [2048, 576], P(('dp', 'tensor'))
- w_query_grad: float32 [2048, 3072], P('dp', 'tensor')
- w_keyval_grad: float32 [512, 4096], P('dp', 'tensor')
- w_output_grad: float32 [2048, 2048], P('tensor', 'dp')
- w_expert_in_grad: float32 [4, 2, 2048, 1408], P(None, None, 'dp', 'tensor')
- w_expert_out_grad: float32 [4, 1408, 2048], P(None, 'tensor', 'dp')
- w_shared_in_grad: float32 [2, 2048, 2816], P(None, 'dp', 'tensor')
- w_shared_out_grad: float32 [2816, 2048], P('tensor', 'dp')
The draws below stay inside these ranges and needn't reach their ends.
Inputs may be any that keep to these rules, and one draw needn't show every extreme that they name: `tok_counts`: token slots at or after a group's count are padding; some group is full. `slot_table`: row e of a group lists in increasing order the tokens of that group routed to expert e, then -1 to the end. Every token below its group's count is routed to exactly 3 experts, padding to none; in every group one expert receives all counted tokens.
All inputs are finite; a program needn't handle non-finite values.
Results may differ from the reference program's by a relative error of at most 0.019.
Values may be sent and summed in bfloat16 or wider, within the bound.
A program may use at most 256 MiB of HBM per device.

```python
import math
import jax
import jax.numpy as jnp
import numpy as np
from jax import lax

D = 2048
H = 16
HD = 128
RD = 64
VD = 128
KR = 512
FF = 1408
SHF = 2816
EXPERTS = 4
TOPK = 3
SEQ_MAX = 512
NSEG = 3
TOK = 640
TOKENS = 5120
N_DP = 8


def group_counts(key):
    n_groups = TOKENS // TOK
    counts = jax.random.randint(jax.random.fold_in(key, 11), (n_groups,), TOK // 2, TOK + 1)
    full_group = jax.random.randint(jax.random.fold_in(key, 12), (), 0, n_groups)
    counts = jnp.where(jnp.arange(n_groups) == full_group, TOK, counts)
    return counts.astype(jnp.int32)


def draw_tok_counts(key, part):
    return group_counts(key)


def draw_slot_table(key, part):
    n_groups = TOKENS // TOK
    counts = group_counts(key)
    scores = jax.random.randint(jax.random.fold_in(key, 21), (n_groups, TOK, EXPERTS), 0, 1 << 16)
    expert_bias = jax.random.randint(jax.random.fold_in(key, 23), (n_groups, 1, EXPERTS), 0, 1 << 15)
    favorite = jax.random.randint(jax.random.fold_in(key, 22), (n_groups, 1, 1), 0, EXPERTS)
    expert_ids = jnp.arange(EXPERTS, dtype=jnp.int32)[None, None, :]
    ranked = (scores + expert_bias) * EXPERTS + expert_ids + jnp.where(expert_ids == favorite, 1 << 22, 0)
    top_values = lax.top_k(ranked, TOPK)[0]
    chosen = ranked >= top_values[..., TOPK - 1:TOPK]
    token_ids = jnp.arange(TOK, dtype=jnp.int32)[None, :, None]
    chosen = chosen & (token_ids < counts[:, None, None])
    order_key = jnp.transpose(jnp.where(chosen, token_ids, TOK + token_ids), (0, 2, 1))
    sorted_key = jnp.sort(order_key, axis=-1)
    return jnp.where(sorted_key < TOK, sorted_key, -1).astype(jnp.int32)


def draw_res_in(key, part):
    entry_key, scale_key = jax.random.split(key)
    entries = jnp.clip(jax.random.normal(entry_key, (TOKENS, D), jnp.float32), -6.0, 6.0)
    row_scale = jnp.exp(jax.random.uniform(scale_key, (TOKENS, 1), jnp.float32, math.log(0.5), math.log(5.0)))
    return (entries * row_scale).astype(jnp.bfloat16)


def steps_of(rng, shape, shards, low, top_value):
    def one(position, parts):
        heights = jax.random.uniform(jax.random.fold_in(jax.random.fold_in(rng, 6), position), (parts,), jnp.float32, low / len(shards), top_value / len(shards))
        return jnp.repeat(jnp.exp(heights), shape[position] // parts).reshape((-1,) + (1,) * (len(shape) - position - 1))

    factor_of = one(*shards[0])
    for cut in shards[1:]:
        factor_of = factor_of * one(*cut)
    return factor_of


def length_profile(amount, total, most, lean):
    loads = [(1 << 20) // math.isqrt(grade ** lean) + 1 for grade in range(2, amount + 1)]
    surplus, given = total - most - (amount - 1), [1] * (amount - 1)
    while surplus > 0:
        movable = [i for i in range(amount - 1) if given[i] < most]
        pool, left = sum([loads[i] for i in movable]), surplus
        for i in movable:
            addition = min(most - given[i], max(1, left * loads[i] // pool), surplus)
            given[i] = given[i] + addition
            surplus = surplus - addition
    return np.array([most] + given)


def ragged_sizes(key, count, total, most, slope):
    if count == 2:
        one = jax.random.randint(key, (), max(1, total - most), min(most, total - 1) + 1)
        return jnp.stack([one, total - one])
    tallies = jnp.asarray(length_profile(count, total, most, slope), jnp.int32)
    twos = (count - 1) // 2
    giver, taker = tallies[1:1 + 2 * twos:2], tallies[2:2 + 2 * twos:2]
    room = jnp.minimum(giver - 1, most - taker)
    shifted = jax.random.randint(jax.random.fold_in(key, 1), (twos,), 0, 1 << 20) % (room + 1)
    tallies = tallies.at[1:1 + 2 * twos:2].set(giver - shifted).at[2:2 + 2 * twos:2].set(taker + shifted)
    return tallies[jax.random.permutation(jax.random.fold_in(key, 2), count)]


def bell_draw(stream_key, extent, scale, most, shards=(), held_as=jnp.bfloat16):
    values = scale * jax.random.normal(stream_key, extent, jnp.float32)
    if shards:
        values = values * steps_of(stream_key, extent, shards, -0.22, 0.18)
    return jnp.clip(values, -most, most).astype(held_as)


def setup_inputs(seed: int = 0) -> dict:
    keys = jax.random.split(jax.random.key(seed), 18)
    res_in = draw_res_in(jax.random.fold_in(keys[17], 71), 0)
    out_grad = bell_draw(keys[1], (TOKENS, D), 1.0, 6.0, ((0, 32),))
    seg_ids = jax.vmap(lambda own: jnp.searchsorted(jnp.cumsum(ragged_sizes(own, NSEG, TOK, SEQ_MAX, 2)), jnp.arange(TOK), side="right"))(jax.random.split(keys[2], N_DP)).reshape((N_DP, TOK)).astype(jnp.int32)
    tok_counts = draw_tok_counts(jax.random.fold_in(keys[17], 71), 0)
    slot_table = draw_slot_table(jax.random.fold_in(keys[17], 71), 0)
    slot_gates = jnp.clip(jnp.exp(math.log(1.0) - 2.3025851 * jax.random.uniform(keys[5], (N_DP, EXPERTS, TOK), jnp.float32) ** steps_of(keys[5], (N_DP, EXPERTS, TOK), ((0, 8),), -0.2, 0.2)), 0.1, 1.0)
    attn_gain = jnp.clip(1.0 + 0.18 * jax.random.normal(keys[6], (D,), jnp.float32), 0.099609375, 1.8984375).astype(jnp.bfloat16)
    latent_gain = jnp.clip(1.0 + 0.18 * jax.random.normal(keys[7], (KR,), jnp.float32), 0.099609375, 1.8984375).astype(jnp.bfloat16)
    ffn_gain = jnp.clip(1.0 + 0.18 * jax.random.normal(keys[8], (D,), jnp.float32), 0.099609375, 1.8984375).astype(jnp.bfloat16)
    w_latent = bell_draw(keys[9], (D, KR + RD), D ** -0.5, 0.125, ((0, 32),))
    w_query = bell_draw(keys[10], (D, H * (HD + RD)), D ** -0.5, 0.125, ((0, 8), (1, 4)))
    w_keyval = bell_draw(keys[11], (KR, H * (HD + VD)), KR ** -0.5, 0.25, ((0, 8), (1, 4)))
    w_output = bell_draw(keys[12], (H * VD, D), (max(8, H * VD // 64)) ** -0.5, 1.0, ((0, 4), (1, 8)))
    w_expert_in = bell_draw(keys[13], (EXPERTS, 2, D, FF), D ** -0.5, 0.125, ((2, 8), (3, 4)))
    w_expert_out = bell_draw(keys[14], (EXPERTS, FF, D), FF ** -0.5, 0.15625, ((1, 4), (2, 8)))
    w_shared_in = bell_draw(keys[15], (2, D, SHF), D ** -0.5, 0.125, ((1, 8), (2, 4)))
    w_shared_out = bell_draw(keys[16], (SHF, D), SHF ** -0.5, 0.109375, ((0, 4), (1, 8)))
    return {"res_in": res_in, "out_grad": out_grad, "seg_ids": seg_ids, "tok_counts": tok_counts, "slot_table": slot_table, "slot_gates": slot_gates, "attn_gain": attn_gain, "latent_gain": latent_gain, "ffn_gain": ffn_gain, "w_latent": w_latent, "w_query": w_query, "w_keyval": w_keyval, "w_output": w_output, "w_expert_in": w_expert_in, "w_expert_out": w_expert_out, "w_shared_in": w_shared_in, "w_shared_out": w_shared_out}


NORM_EPS = 1e-06
ROPE_BASE = 50000.0
PREC_HIGH = lax.Precision.HIGHEST

@jax.custom_vjp
def low(v):
    return lax.optimization_barrier(v.astype(jnp.bfloat16)).astype(jnp.float32)

@jax.custom_vjp
def low_back(v):
    return v

def low_keep(v):
    return (low(v), None)

def low_pass(kept, grad):
    return (grad,)

def back_keep(v):
    return (v, None)

def back_low(kept, grad):
    return (low(grad),)
low.defvjp(low_keep, low_pass)
low_back.defvjp(back_keep, back_low)

def rms_factor(values):
    return lax.rsqrt(lax.optimization_barrier(jnp.mean(values * values, axis=-1, keepdims=True)) + NORM_EPS)

def rotary_tables(positions):
    half_width = RD // 2
    inv_freq = ROPE_BASE ** (-jnp.arange(half_width, dtype=jnp.float32) / half_width)
    angles = positions.astype(jnp.float32)[:, None] * inv_freq[None, :]
    return (jnp.cos(angles), jnp.sin(angles))

def rotate(values, cosine_table, sine_table):
    half_width = values.shape[-1] // 2
    first_half = values[..., :half_width]
    second_half = values[..., half_width:]
    return jnp.concatenate([first_half * cosine_table - second_half * sine_table, second_half * cosine_table + first_half * sine_table], axis=-1)

def group_forward(params, group_in, segment_row, group_count, group_slots, group_gates):
    attn_gain, latent_gain, ffn_gain, w_latent, w_query, w_keyval, w_output, w_expert_in, w_expert_out, w_shared_in, w_shared_out = params
    token_ids = jnp.arange(TOK, dtype=jnp.int32)
    positions = token_ids - lax.optimization_barrier(jnp.sum((segment_row[None, :] < segment_row[:, None]).astype(jnp.int32), axis=1))
    cosine_table, sine_table = rotary_tables(positions)
    valid_rows = (token_ids < group_count).astype(jnp.float32)[:, None]
    allowed = (segment_row[:, None] == segment_row[None, :]) & (token_ids[None, :] <= token_ids[:, None])
    score_scale = (HD + RD) ** (-0.5)
    normed_in = low(group_in * rms_factor(group_in) * attn_gain)
    query_raw = low_back(jnp.dot(normed_in, w_query, precision=PREC_HIGH)).reshape(TOK, H, HD + RD)
    latent_raw = low_back(jnp.dot(normed_in, w_latent, precision=PREC_HIGH))
    latent_c = latent_raw[:, :KR]
    latent_norm = low(latent_c * rms_factor(latent_c) * latent_gain)
    rope_key = low(rotate(latent_raw[:, KR:], cosine_table, sine_table))
    keyval = low_back(low(jnp.dot(latent_norm, w_keyval, precision=PREC_HIGH))).reshape(TOK, H, HD + VD)
    query_final = low(jnp.concatenate([query_raw[..., :HD], rotate(query_raw[..., HD:], cosine_table[:, None, :], sine_table[:, None, :])], axis=-1))
    key_full = jnp.concatenate([keyval[..., :HD], jnp.broadcast_to(rope_key[:, None, :], (TOK, H, RD))], axis=-1)
    scores = low_back(jnp.einsum('qhd,khd->hqk', query_final, key_full, precision=PREC_HIGH) * score_scale)
    scores = jnp.where(allowed[None], scores, -1e+30)
    probs_low = low(jax.nn.softmax(scores, axis=-1))
    attn_mix = low_back(low(jnp.einsum('hqk,khd->qhd', probs_low, keyval[..., HD:], precision=PREC_HIGH))).reshape(TOK, H * VD)
    attn_out = low_back(jnp.dot(attn_mix, w_output, precision=PREC_HIGH))
    mid_resid = group_in + valid_rows * attn_out
    normed_mid = low(mid_resid * rms_factor(mid_resid) * ffn_gain)
    shared_gate = low_back(jnp.dot(normed_mid, w_shared_in[0], precision=PREC_HIGH))
    shared_up = low_back(jnp.dot(normed_mid, w_shared_in[1], precision=PREC_HIGH))
    shared_hidden = low(jax.nn.silu(shared_gate) * shared_up)
    ffn_out = jnp.dot(shared_hidden, w_shared_out, precision=PREC_HIGH)
    slot_used = group_slots >= 0
    slot_rows = jnp.where(slot_used, group_slots, 0).astype(jnp.int32)
    slot_weight = jnp.where(slot_used, group_gates, 0.0)
    expert_rows = normed_mid[slot_rows]
    expert_gate = low_back(jnp.einsum('etd,edf->etf', expert_rows, w_expert_in[:, 0], precision=PREC_HIGH))
    expert_up = low_back(jnp.einsum('etd,edf->etf', expert_rows, w_expert_in[:, 1], precision=PREC_HIGH))
    expert_hidden = low(jax.nn.silu(expert_gate) * expert_up)
    expert_out = low_back(jnp.einsum('etf,efd->etd', expert_hidden, w_expert_out, precision=PREC_HIGH))
    target = jnp.where(slot_used, group_slots, TOK).astype(jnp.int32).reshape(-1)
    ffn_out = ffn_out.at[target].add((expert_out * slot_weight[..., None]).reshape(-1, D), mode='drop')
    return mid_resid + valid_rows * ffn_out

def reference(res_in, out_grad, seg_ids, tok_counts, slot_table, slot_gates, attn_gain, latent_gain, ffn_gain, w_latent, w_query, w_keyval, w_output, w_expert_in, w_expert_out, w_shared_in, w_shared_out):
    params = tuple((weight_in.astype(jnp.float32) for weight_in in (attn_gain, latent_gain, ffn_gain, w_latent, w_query, w_keyval, w_output, w_expert_in, w_expert_out, w_shared_in, w_shared_out)))
    resid_in = res_in.astype(jnp.float32)

    def forward(params, resid_in):

        def one_group(inputs):
            group_in, segment_row, group_count, group_slots, group_gates = inputs
            return group_forward(params, group_in, segment_row, group_count, group_slots, group_gates)
        outputs = lax.map(jax.checkpoint(one_group), (resid_in.reshape(N_DP, TOK, D), seg_ids, tok_counts, slot_table, slot_gates))
        return outputs.reshape(N_DP * TOK, D)
    res_out, pullback = jax.vjp(forward, params, resid_in)
    param_grads, res_grad = pullback(out_grad.astype(jnp.float32))
    return (res_out.astype(jnp.bfloat16), res_grad, param_grads[0], param_grads[1], param_grads[2], param_grads[3], param_grads[4], param_grads[5], param_grads[6], param_grads[7], param_grads[8], param_grads[9], param_grads[10])
```

```python
import jax
import jax.numpy as jnp
from jax import lax
from jax.sharding import PartitionSpec as P

D = 2048
H = 16
HD = 128
RD = 64
VD = 128
KR = 512
TOK = 640
EXPERTS = 4


NORM_EPS = 1e-06
ROPE_BASE = 50000.0


def rms_factor(values):
    return lax.rsqrt(jnp.mean(values * values, axis=-1, keepdims=True) + NORM_EPS)


def norm_back(grad_out, values, factor, gain_vec):
    scaled = grad_out * gain_vec
    inner_sum = jnp.mean(scaled * values, axis=-1, keepdims=True)
    return (
        factor * (scaled - values * factor * factor * inner_sum),
        jnp.sum(grad_out * values * factor, axis=0),
    )


def rotary_tables(positions):
    half_width = RD // 2
    inv_freq = ROPE_BASE ** (-jnp.arange(half_width, dtype=jnp.float32) / half_width)
    angles = positions.astype(jnp.float32)[:, None] * inv_freq[None, :]
    return (jnp.cos(angles), jnp.sin(angles))


def rotate(values, cosine_table, sine_table):
    half_width = values.shape[-1] // 2
    first_half = values[..., :half_width]
    second_half = values[..., half_width:]
    return jnp.concatenate(
        [
            first_half * cosine_table - second_half * sine_table,
            second_half * cosine_table + first_half * sine_table,
        ],
        axis=-1,
    )


def silu_parts(gate_pre):
    sigma_gate = jax.nn.sigmoid(gate_pre)
    return (gate_pre * sigma_gate, sigma_gate * (1.0 + gate_pre * (1.0 - sigma_gate)))


def flip_pairs(count, bit):
    return [(i, i ^ (1 << bit)) for i in range(count)]


def swap_dp(values, bit):
    return lax.ppermute(values, "dp", flip_pairs(lax.axis_size("dp"), bit))


def swap_tensor(values, bit):
    return lax.ppermute(values, "tensor", flip_pairs(lax.axis_size("tensor"), bit))


def dp_bits():
    top = lax.axis_size("dp").bit_length() - 1
    return [1] + list(range(top - 1, 1, -1)) + [0]


def slot_order(bits):
    order = [0]
    for bit in bits:
        order = order + [j ^ (1 << bit) for j in order]
    return order


def select_blocks(blocks, index):
    step = 1
    while step < len(blocks):
        hit = (index & step) != 0
        blocks = [jnp.where(hit, blocks[i ^ step], blocks[i]) for i in range(len(blocks))]
        step *= 2
    return blocks


def to_slots(values, index, bits, axis):
    count = 1 << len(bits)
    blocks = select_blocks(jnp.split(values, count, axis=axis), index)
    return jnp.concatenate([blocks[j] for j in slot_order(bits)], axis=axis)


def from_slots(values, index, bits, axis):
    order = slot_order(bits)
    slots = jnp.split(values, len(order), axis=axis)
    blocks = [slots[order.index(i)] for i in range(len(order))]
    return jnp.concatenate(select_blocks(blocks, index), axis=axis)


def gather_dp(values, bits):
    for bit in bits:
        values = jnp.concatenate([values, swap_dp(values, bit)], axis=0)
    return values


def gather_tensor(values):
    for bit in (1, 0):
        values = jnp.concatenate([values, swap_tensor(values, bit)], axis=0)
    return values


def scatter_dp(values, bits, axis):
    values = values.astype(jnp.float32)
    for bit in reversed(bits):
        keep, give = jnp.split(values, 2, axis=axis)
        values = keep + swap_dp(give.astype(jnp.bfloat16), bit).astype(jnp.float32)
    return values


def scatter_tensor(values):
    for bit in (0, 1):
        keep, give = jnp.split(values, 2, axis=0)
        values = keep + swap_tensor(give.astype(jnp.bfloat16), bit).astype(jnp.float32)
    return values


def partner_columns(values):
    count = lax.axis_size("dp")
    slots = jnp.split(values, count, axis=-1)
    return jnp.concatenate([slots[k ^ 1] for k in range(count)], axis=-1)


def gather_pair(values, bit):
    over = swap_dp(partner_columns(values), bit)
    own = jnp.concatenate([values, over, swap_tensor(values, 1), swap_tensor(over, 1)], axis=0)
    return jnp.concatenate([own, swap_tensor(own, 0)], axis=0)


def scatter_pair(values, bit):
    values = scatter_tensor(values)
    keep, give = jnp.split(values, 2, axis=0)
    return keep + swap_dp(partner_columns(give).astype(jnp.bfloat16), bit).astype(jnp.float32)


def dot(a, b, contract):
    return lax.dot_general(a, b, (contract, ((), ())), preferred_element_type=jnp.float32)


def body(
    res_in,
    out_grad,
    seg_ids,
    tok_counts,
    slot_table,
    slot_gates,
    attn_gain,
    latent_gain,
    ffn_gain,
    w_latent,
    w_query,
    w_keyval,
    w_output,
    w_expert_in,
    w_expert_out,
    w_shared_in,
    w_shared_out,
):
    f32 = jnp.float32
    bf16 = jnp.bfloat16
    n_tensor = lax.axis_size("tensor")
    n_dp = lax.axis_size("dp")
    dp = lax.axis_index("dp")
    tensor = lax.axis_index("tensor")
    bits = dp_bits()
    merge = bits[0]
    half = (dp >> merge) & 1
    rows = res_in.shape[0]
    local_heads = H // n_tensor
    score_scale = (HD + RD) ** (-0.5)

    res_local = to_slots(res_in, dp, bits, 1)
    res_all = gather_tensor(res_local)
    tensor_slots = slot_order([1, 0])
    token_ids = jnp.concatenate(
        [(tensor ^ j) * rows + jnp.arange(rows, dtype=jnp.int32) for j in tensor_slots]
    )
    segment_canon = seg_ids[0]
    segment_row = jnp.concatenate(
        [lax.dynamic_slice_in_dim(segment_canon, (tensor ^ j) * rows, rows) for j in tensor_slots]
    )
    valid_all = (token_ids < tok_counts[0]).astype(f32)
    valid_rows = valid_all[:rows, None]
    group_gate = jnp.sum(
        jnp.where(slot_table[0][:, :, None] == token_ids[None, None, :], slot_gates[0][:, :, None], 0.0),
        axis=1,
    )
    grad_in = to_slots(out_grad, dp, bits, 1).astype(f32)
    ffn_grad = (valid_rows * grad_in).astype(bf16)

    pack_rows = w_latent.shape[0]
    gain_row = jnp.concatenate([attn_gain, ffn_gain, latent_gain])
    gain_row = jnp.pad(gain_row, (0, w_latent.shape[1] - gain_row.shape[0]))
    pack = jnp.concatenate([w_latent, jnp.broadcast_to(gain_row, (16, w_latent.shape[1]))], axis=0)
    pack = gather_dp(pack[None], bits)
    pack = gather_tensor(pack[None])
    pack_blocks = [pack[tensor_slots.index(j)] for j in range(n_tensor)]
    pack = jnp.stack(select_blocks(pack_blocks, tensor), axis=1)
    latent_full = pack[:, :, :pack_rows].reshape(D, KR + RD)
    gains = pack[:, :, pack_rows]
    gain_width, latent_width = D // (n_dp * n_tensor), KR // (n_dp * n_tensor)
    attn_gain_full = gains[..., :gain_width].reshape(D)
    ffn_gain_full = gains[..., gain_width : 2 * gain_width].reshape(D)
    latent_gain_full = from_slots(
        gains[..., 2 * gain_width : 2 * gain_width + latent_width].reshape(KR), dp, bits, 0
    )
    query_full = gather_dp(w_query, bits)
    keyval_full = from_slots(gather_dp(w_keyval, bits), dp, bits, 0)
    output_full = gather_dp(w_output[None], bits)
    output_full = jnp.concatenate([output_full[k] for k in range(n_dp)], axis=1)

    n_half = EXPERTS // 2
    expert_units = jnp.concatenate(
        [
            w_expert_in.transpose(0, 1, 3, 2).reshape(EXPERTS, -1, w_expert_in.shape[2]),
            w_expert_out,
        ],
        axis=1,
    )
    width = w_expert_out.shape[1]
    shared_t = w_shared_in.transpose(0, 2, 1)
    units = []
    for side in range(2):
        cut = slice(side * width, (side + 1) * width)
        shared_unit = jnp.concatenate([shared_t[0, cut], shared_t[1, cut], w_shared_out[cut]], axis=0)
        units.append(jnp.concatenate([expert_units[side * n_half : (side + 1) * n_half], shared_unit[None]], axis=0))
    first = half == 0
    own_units = jnp.where(first, units[0], units[1])
    other_units = jnp.where(first, units[1], units[0])
    pieces = []
    for p in range(n_half + 1):
        piece = jnp.stack([own_units[p], swap_dp(other_units[p], merge)], axis=0)
        piece = gather_dp(piece, bits[1:])
        pieces.append(jnp.concatenate([piece[k] for k in range(n_dp)], axis=1))

    positions = token_ids - jnp.sum(
        (segment_canon[None, :] < segment_row[:, None]).astype(jnp.int32), axis=1
    )
    cos_all, sin_all = rotary_tables(positions)
    allowed = (segment_row[:, None] == segment_row[None, :]) & (
        token_ids[None, :] <= token_ids[:, None]
    )
    resid_all = res_all.astype(f32)
    in_factor = rms_factor(resid_all)
    normed_all = (resid_all * in_factor * attn_gain_full).astype(bf16)
    latent_raw = jnp.dot(normed_all, latent_full, preferred_element_type=f32)
    latent_c = latent_raw[:, :KR]
    latent_factor = rms_factor(latent_c)
    latent_norm = (latent_c * latent_factor * latent_gain_full).astype(bf16)
    rope_all = rotate(latent_raw[:, KR:], cos_all, sin_all).astype(bf16)
    query_raw = jnp.dot(normed_all, query_full, preferred_element_type=f32).reshape(
        TOK, local_heads, HD + RD
    )
    query_final = jnp.concatenate(
        [
            query_raw[..., :HD],
            rotate(query_raw[..., HD:], cos_all[:, None, :], sin_all[:, None, :]),
        ],
        axis=-1,
    ).astype(bf16)
    keyval = (
        jnp.dot(latent_norm, keyval_full, preferred_element_type=f32)
        .astype(bf16)
        .reshape(TOK, local_heads, HD + VD)
    )
    key_nope = keyval[..., :HD]
    values_all = keyval[..., HD:]
    raw_scores = jnp.einsum(
        "qhd,khd->hqk", query_final[..., :HD], key_nope, preferred_element_type=f32
    )
    raw_scores = raw_scores + jnp.einsum(
        "qhr,kr->hqk", query_final[..., HD:], rope_all, preferred_element_type=f32
    )
    scores = jnp.where(allowed[None], raw_scores * score_scale, -1e30)
    top_score = jnp.max(scores, axis=-1, keepdims=True)
    exp_scores = jnp.exp(scores - top_score)
    probs_all = exp_scores / jnp.sum(exp_scores, axis=-1, keepdims=True)
    probs_low = probs_all.astype(bf16)
    attn_mix = (
        jnp.einsum("hqk,khd->qhd", probs_low, values_all, preferred_element_type=f32)
        .astype(bf16)
        .reshape(TOK, local_heads * VD)
    )
    attn_part = jnp.dot(attn_mix, output_full, preferred_element_type=f32)
    attn_out = scatter_tensor(attn_part)
    resid_in = res_local.astype(f32)
    mid_resid = resid_in + valid_rows * attn_out
    mid_factor = rms_factor(mid_resid)
    normed_mid = (mid_resid * mid_factor * ffn_gain_full).astype(bf16)

    mid_pair = gather_pair(normed_mid, merge)
    grad_pair = gather_pair(ffn_grad, merge)
    other_gate = swap_dp(group_gate, merge)
    pair_gate = jnp.concatenate(
        [
            gate[:, k * rows : (k + 1) * rows]
            for k in ((0, 0), (1, 0), (0, 1), (1, 1), (0, 2), (1, 2), (0, 3), (1, 3))
            for gate, k in (((group_gate, other_gate)[k[0]], k[1]),)
        ],
        axis=1,
    )
    pair_gate = jnp.where(first, pair_gate[:n_half], pair_gate[n_half:])
    mid_pair_grad = None
    hidden_parts, out_parts, unit_grads = [], [], []
    for p, piece in enumerate(pieces):
        gate_up = dot(piece[: 2 * width], mid_pair, ((1,), (1,)))
        gate_pre, up = gate_up[:width], gate_up[width:]
        silu, slope = silu_parts(gate_pre)
        hidden_grad = dot(piece[2 * width :], grad_pair, ((1,), (1,)))
        hidden = silu * up
        if p < n_half:
            hidden = hidden * pair_gate[p][None]
            hidden_grad = hidden_grad * pair_gate[p][None]
        hidden = hidden.astype(bf16)
        pre_grad = jnp.concatenate(
            [(hidden_grad * up * slope).astype(bf16), (hidden_grad * silu).astype(bf16)], axis=0
        )
        back = dot(pre_grad, piece[: 2 * width], ((0,), (0,)))
        mid_pair_grad = back if mid_pair_grad is None else mid_pair_grad + back
        hidden_parts.append(hidden)
        out_parts.append(piece[2 * width :])
        in_wgrad = dot(pre_grad, mid_pair, ((1,), (0,)))
        out_wgrad = dot(hidden, grad_pair, ((1,), (0,)))
        unit_grads.append(jnp.concatenate([in_wgrad, out_wgrad], axis=0).astype(bf16))
    ffn_part = dot(
        jnp.concatenate(hidden_parts, axis=0), jnp.concatenate(out_parts, axis=0), ((0,), (0,))
    )
    ffn_out = scatter_pair(ffn_part, merge)
    res_out = (mid_resid + valid_rows * ffn_out).astype(bf16)
    mid_grad_local = scatter_pair(mid_pair_grad, merge)

    mid_back, ffn_gain_part = norm_back(mid_grad_local, mid_resid, mid_factor, ffn_gain_full)
    mid_grad = grad_in + mid_back
    attn_grad = (valid_rows * mid_grad).astype(bf16)
    attn_grad_all = gather_tensor(attn_grad)
    output_wgrad = dot(attn_mix, attn_grad_all, ((0,), (0,)))
    mix_grad = (
        dot(attn_grad_all, output_full, ((1,), (1,))).astype(bf16).reshape(TOK, local_heads, VD)
    )
    probs_grad = jnp.einsum("qhd,khd->hqk", mix_grad, values_all, preferred_element_type=f32)
    value_grad = jnp.einsum("hqk,qhd->khd", probs_low, mix_grad, preferred_element_type=f32)
    scores_grad = (
        probs_all * (probs_grad - jnp.sum(probs_all * probs_grad, axis=-1, keepdims=True))
    ).astype(bf16)
    query_nope_grad = (
        jnp.einsum("hqk,khd->qhd", scores_grad, key_nope, preferred_element_type=f32) * score_scale
    )
    query_rope_grad = (
        jnp.einsum("hqk,kr->qhr", scores_grad, rope_all, preferred_element_type=f32) * score_scale
    )
    key_nope_grad = (
        jnp.einsum("hqk,qhd->khd", scores_grad, query_final[..., :HD], preferred_element_type=f32)
        * score_scale
    )
    rope_key_grad = (
        jnp.einsum("hqk,qhr->kr", scores_grad, query_final[..., HD:], preferred_element_type=f32)
        * score_scale
    )
    query_grad = (
        jnp.concatenate(
            [query_nope_grad, rotate(query_rope_grad, cos_all[:, None, :], -sin_all[:, None, :])],
            axis=-1,
        )
        .astype(bf16)
        .reshape(TOK, local_heads * (HD + RD))
    )
    keyval_grad = (
        jnp.concatenate([key_nope_grad, value_grad], axis=-1)
        .astype(bf16)
        .reshape(TOK, local_heads * (HD + VD))
    )
    latent_part = jnp.concatenate([dot(keyval_grad, keyval_full, ((1,), (1,))), rope_key_grad], axis=1)
    latent_grad_local = scatter_tensor(latent_part)
    normed_part = dot(query_grad, query_full, ((1,), (1,)))
    normed_grad_local = scatter_tensor(normed_part)
    query_wgrad = dot(normed_all, query_grad, ((0,), (0,)))
    keyval_wgrad = to_slots(dot(latent_norm, keyval_grad, ((0,), (0,))).astype(bf16), dp, bits, 0)
    latent_c_grad, latent_gain_part = norm_back(
        latent_grad_local[:, :KR], latent_c[:rows], latent_factor[:rows], latent_gain_full
    )
    rope_raw_grad = rotate(latent_grad_local[:, KR:], cos_all[:rows], -sin_all[:rows])
    latent_raw_grad = jnp.concatenate([latent_c_grad, rope_raw_grad], axis=1).astype(bf16)
    latent_raw_grad_all = gather_tensor(latent_raw_grad)
    latent_wgrad = dot(normed_all, latent_raw_grad_all, ((0,), (0,))).astype(bf16)
    latent_wgrad = lax.dynamic_index_in_dim(
        latent_wgrad.reshape(n_dp, n_tensor, pack_rows, KR + RD), tensor, 1, keepdims=False
    )
    normed_grad = normed_grad_local + dot(latent_raw_grad, latent_full, ((1,), (1,)))
    in_back, attn_gain_part = norm_back(normed_grad, resid_in, in_factor[:rows], attn_gain_full)
    res_grad = mid_grad + in_back

    output_owned = scatter_dp(output_wgrad, bits, 1)
    query_owned = scatter_dp(query_wgrad, bits, 0)
    keyval_owned = scatter_dp(keyval_wgrad, bits, 0)
    latent_owned = scatter_dp(latent_wgrad, bits, 0)[0]
    gain_parts = jnp.concatenate(
        [
            attn_gain_part.reshape(n_dp, n_tensor, gain_width),
            ffn_gain_part.reshape(n_dp, n_tensor, gain_width),
            to_slots(latent_gain_part, dp, bits, 0).reshape(n_dp, n_tensor, latent_width),
        ],
        axis=2,
    )
    gain_parts = jnp.stack(
        [
            select_blocks([gain_parts[:, i] for i in range(n_tensor)], tensor)[j]
            for j in tensor_slots
        ],
        axis=0,
    )
    for bit in (0, 1):
        keep, give = jnp.split(gain_parts, 2, axis=0)
        gain_parts = keep + swap_tensor(give, bit)
    gain_parts = gain_parts[0]
    for bit in reversed(bits):
        keep, give = jnp.split(gain_parts, 2, axis=0)
        gain_parts = keep + swap_dp(give, bit)
    gain_owned = gain_parts[0]
    own_grads, other_grads = [], []
    for grad in unit_grads:
        grad = grad.astype(f32)
        for bit in reversed(bits[1:]):
            keep, give = jnp.split(grad, 2, axis=1)
            grad = keep + swap_dp(give.astype(bf16), bit).astype(f32)
        keep, give = jnp.split(grad, 2, axis=1)
        own_grads.append(keep)
        other_grads.append(swap_dp(give.astype(bf16), merge).astype(f32))
    sides = []
    for side in (first, ~first):
        sides.append([jnp.where(side, a, b) for a, b in zip(own_grads, other_grads)])
    expert_units = jnp.stack([unit for side in sides for unit in side[:n_half]], axis=0)
    expert_in_owned = expert_units[:, : 2 * width].reshape(EXPERTS, 2, width, -1).transpose(0, 1, 3, 2)
    expert_out_owned = expert_units[:, 2 * width :]
    shared_in_owned = jnp.stack(
        [
            jnp.concatenate([side[n_half][k * width : (k + 1) * width] for side in sides], axis=0).T
            for k in range(2)
        ],
        axis=0,
    )
    shared_out_owned = jnp.concatenate([side[n_half][2 * width :] for side in sides], axis=0)
    return (
        from_slots(res_out, dp, bits, 1),
        from_slots(res_grad, dp, bits, 1),
        gain_owned[:gain_width],
        gain_owned[2 * gain_width :],
        gain_owned[gain_width : 2 * gain_width],
        latent_owned,
        query_owned,
        keyval_owned,
        output_owned,
        expert_in_owned,
        expert_out_owned,
        shared_in_owned,
        shared_out_owned,
    )


def solution(mesh):
    placed = (
        P(("dp", "tensor"), None),
        P(("dp", "tensor"), None),
        P("dp", None),
        P("dp"),
        P("dp", None, None),
        P("dp", None, None),
        P(("dp", "tensor")),
        P(("dp", "tensor")),
        P(("dp", "tensor")),
        P(("dp", "tensor"), None),
        P("dp", "tensor"),
        P("dp", "tensor"),
        P("tensor", "dp"),
        P(None, None, "dp", "tensor"),
        P(None, "tensor", "dp"),
        P(None, "dp", "tensor"),
        P("tensor", "dp"),
    )
    return jax.shard_map(
        body,
        mesh=mesh,
        in_specs=placed,
        out_specs=(
            P(("dp", "tensor"), None),
            P(("dp", "tensor"), None),
            P(("dp", "tensor")),
            P(("dp", "tensor")),
            P(("dp", "tensor")),
            P(("dp", "tensor"), None),
            P("dp", "tensor"),
            P("dp", "tensor"),
            P("tensor", "dp"),
            P(None, None, "dp", "tensor"),
            P(None, "tensor", "dp"),
            P(None, "dp", "tensor"),
            P("tensor", "dp"),
        ),
        check_vma=False,
    )
```

```python
import functools

import jax
import jax.numpy as jnp
from jax import lax
from jax.experimental import pallas as pl
from jax.experimental.pallas import tpu as pltpu
from jax.sharding import PartitionSpec as P

D = 2048
H = 16
HD = 128
RD = 64
VD = 128
KR = 512
TOK = 640
EXPERTS = 4


NORM_EPS = 1e-06
ROPE_BASE = 50000.0


def rms_factor(values):
    return lax.rsqrt(jnp.mean(values * values, axis=-1, keepdims=True) + NORM_EPS)


def norm_back(grad_out, values, factor, gain_vec):
    scaled = grad_out * gain_vec
    inner_sum = jnp.mean(scaled * values, axis=-1, keepdims=True)
    return (
        factor * (scaled - values * factor * factor * inner_sum),
        jnp.sum(grad_out * values * factor, axis=0),
    )


def rotary_tables(positions):
    half_width = RD // 2
    inv_freq = ROPE_BASE ** (-jnp.arange(half_width, dtype=jnp.float32) / half_width)
    angles = positions.astype(jnp.float32)[:, None] * inv_freq[None, :]
    return (jnp.cos(angles), jnp.sin(angles))


def rotate(values, cosine_table, sine_table):
    half_width = values.shape[-1] // 2
    first_half = values[..., :half_width]
    second_half = values[..., half_width:]
    return jnp.concatenate(
        [
            first_half * cosine_table - second_half * sine_table,
            second_half * cosine_table + first_half * sine_table,
        ],
        axis=-1,
    )


def silu_parts(gate_pre):
    sigma_gate = jax.nn.sigmoid(gate_pre)
    return (gate_pre * sigma_gate, sigma_gate * (1.0 + gate_pre * (1.0 - sigma_gate)))


def flip_pairs(count, bit):
    return [(i, i ^ (1 << bit)) for i in range(count)]


def dot(a, b, contract):
    return lax.dot_general(a, b, (contract, ((), ())), preferred_element_type=jnp.float32)


class Line:
    def __init__(self, token):
        self.token = token

    def start(self, values, axis, bit):
        values, _ = lax.optimization_barrier((values, self.token))
        return lax.ppermute(values, axis, flip_pairs(lax.axis_size(axis), bit))

    def wait(self, values, *more):
        values, self.token, *more = lax.optimization_barrier((values, self.token, *more))
        return (values, *more) if more else values


def slot_order(bits):
    order = [0]
    for bit in bits:
        order = order + [j ^ (1 << bit) for j in order]
    return order


def take_slots(values, picks, count, axis):
    size = values.shape[axis] // count
    runs = []
    for k in picks:
        if runs and runs[-1][1] == k:
            runs[-1][1] = k + 1
        else:
            runs.append([k, k + 1])
    parts = [lax.slice_in_dim(values, a * size, b * size, axis=axis) for a, b in runs]
    return parts[0] if len(parts) == 1 else jnp.concatenate(parts, axis=axis)


def reorder(values, order, wanted, axis):
    if order == wanted:
        return values
    return take_slots(values, [order.index(j) for j in wanted], len(order), axis)


def select_blocks(blocks, index):
    step = 1
    while step < len(blocks):
        hit = (index & step) != 0
        blocks = [jnp.where(hit, blocks[i ^ step], blocks[i]) for i in range(len(blocks))]
        step *= 2
    return blocks


def to_slots(values, index, order, axis):
    blocks = select_blocks(jnp.split(values, len(order), axis=axis), index)
    return jnp.concatenate([blocks[j] for j in order], axis=axis)


def from_slots(values, index, order, axis):
    slots = jnp.split(values, len(order), axis=axis)
    blocks = [slots[order.index(i)] for i in range(len(order))]
    return jnp.concatenate(select_blocks(blocks, index), axis=axis)


def halves(values, order, bit, axis):
    keep = [k for k, j in enumerate(order) if not (j >> bit) & 1]
    give = [order.index(order[k] ^ (1 << bit)) for k in keep]
    return (
        take_slots(values, keep, len(order), axis),
        take_slots(values, give, len(order), axis),
        [order[k] for k in keep],
    )


class Sum:
    def __init__(self, line, values, order, bits, axis, name="dp", wire=jnp.bfloat16):
        self.line, self.values, self.order, self.bits = line, values, order, list(bits)
        self.axis, self.name, self.wire = axis, name, wire

    def start(self):
        bit = self.bits.pop(0)
        self.keep, give, self.order = halves(self.values, self.order, bit, self.axis)
        self.flying = self.line.start(give.astype(self.wire), self.name, bit)
        return self

    def wait(self):
        got = self.line.wait(self.flying)
        self.values = self.keep.astype(jnp.float32) + got.astype(jnp.float32)
        return self

    def next(self):
        return self.wait().start()

    def finish(self):
        while self.bits:
            self.start().wait()
        return self.values


class Gather:
    def __init__(self, line, values, bits, name="dp"):
        self.line, self.values, self.bits, self.name = line, values, list(bits), name
        self.order = [0]

    def start(self):
        self.bit = self.bits.pop(0)
        self.flying = self.line.start(self.values, self.name, self.bit)
        return self

    def wait(self):
        got = self.line.wait(self.flying)
        self.values = jnp.concatenate([self.values, got], axis=0)
        self.order = self.order + [j ^ (1 << self.bit) for j in self.order]
        return self

    def next(self):
        return self.wait().start()

    def finish(self):
        while self.bits:
            self.start().wait()
        return self.values


MESH = pl.DeviceIdType.MESH
LANE_CHUNKS = 3


class Copies:
    def __init__(self, send_sems, recv_sems, local_sems):
        self.send_sems, self.recv_sems, self.local_sems = send_sems, recv_sems, local_sems
        self.count = 0
        self.local_count = 0

    def across(self, axis, bit):
        index = lax.axis_index(axis)
        side = lax.rem(index // (1 << bit), 2)
        return {axis: index + (1 - 2 * side) * (1 << bit)}

    def start(self, source, target, axis, bit):
        copy = pltpu.make_async_remote_copy(
            src_ref=source,
            dst_ref=target,
            send_sem=self.send_sems.at[self.count],
            recv_sem=self.recv_sems.at[self.count],
            device_id=self.across(axis, bit),
            device_id_type=MESH,
        )
        self.count += 1
        copy.start()
        return copy

    def local(self, source, target):
        copy = pltpu.make_async_copy(source, target, self.local_sems.at[self.local_count])
        self.local_count += 1
        copy.start()
        return copy

    def greet(self, dp_bits, tensor_bits=(1, 0)):
        barrier = pltpu.get_barrier_semaphore()
        for axis, bits in (("dp", dp_bits), ("tensor", tensor_bits)):
            for bit in bits:
                pl.semaphore_signal(
                    barrier, inc=1, device_id=self.across(axis, bit), device_id_type=MESH
                )
        pl.semaphore_wait(barrier, len(dp_bits) + len(tensor_bits))


class SlotGather:
    def __init__(self, copies, source, slots, bits, axis="dp", cut=None):
        self.copies, self.source, self.slots, self.bits, self.axis = copies, source, slots, list(bits), axis
        self.cut = (slice(None),) if cut is None else (pl.ds(*cut),)
        self.done, self.have, self.own, self.flying = 0, 1, None, None

    def view(self, first, count):
        return self.slots.at[(pl.ds(first, count), *self.cut)]

    def start(self):
        bit = self.bits[self.done]
        if self.done == 0 and self.source is not None:
            source = self.source.at[(pl.ds(0, 1), *self.cut)]
            self.own = self.copies.local(source, self.view(0, 1))
        else:
            if self.own is not None:
                self.own.wait()
                self.own = None
            source = self.view(0, self.have)
        self.flying = self.copies.start(source, self.view(self.have, self.have), self.axis, bit)
        self.done += 1
        self.have *= 2

    def wait(self):
        self.flying.wait()
        self.flying = None
        if self.done < len(self.bits):
            self.start()
        elif self.own is not None:
            self.own.wait()
            self.own = None

    def finish(self):
        while self.flying is not None:
            self.wait()


def gather_kernel(
    n_bits,
    n_pieces,
    width,
    tokens_ref,
    grad_ref,
    grad_over_ref,
    pack_ref,
    keyval_ref,
    query_ref,
    output_ref,
    own_ref,
    other_ref,
    tokens_all,
    grad_pair,
    pack_all,
    keyval_all,
    query_all,
    output_all,
    units_all,
    send_sems,
    recv_sems,
    local_sems,
):
    copies = Copies(send_sems, recv_sems, local_sems)
    merge = 1
    high = list(range(n_bits - 1, 1, -1))
    far_first = high + [merge, 0]
    copies.greet(list(range(n_bits)))

    pack = SlotGather(copies, pack_ref, pack_all.at[0], far_first)
    keyval = SlotGather(copies, keyval_ref, keyval_all, far_first)
    half = query_ref.shape[1] // 2
    query = [
        SlotGather(copies, query_ref, query_all, far_first, cut=(k * half, half)) for k in range(2)
    ]
    tokens = SlotGather(copies, tokens_ref, tokens_all, [1, 0], "tensor")
    output = SlotGather(copies, output_ref, output_all, [0] + high + [merge])
    pack.start()
    keyval.start()
    query[0].start()
    tokens.start()
    output.start()
    query[1].start()

    units = []
    for p in range(n_pieces):
        for part in range(LANE_CHUNKS):
            units.append((p, part))
    chains = [None] * len(units)
    locals_of = [None] * len(units)

    def unit_first(i):
        p, part = units[i]
        cut = pl.ds(part * width, width)
        locals_of[i] = copies.local(own_ref.at[pl.ds(p, 1), cut], units_all.at[p, pl.ds(0, 1), cut])
        chains[i] = copies.start(
            other_ref.at[pl.ds(p, 1), cut], units_all.at[p, pl.ds(1, 1), cut], "dp", merge
        )

    def unit_second(i):
        p, part = units[i]
        chains[i].wait()
        locals_of[i].wait()
        chain = SlotGather(
            copies, None, units_all.at[p], high + [0], cut=(part * width, width)
        )
        chain.have = 2
        chain.start()
        chains[i] = chain

    grad_own = copies.local(grad_ref, grad_pair.at[pl.ds(0, 1)])

    unit_first(0)
    for _ in high:
        pack.wait()
    for _ in high:
        keyval.wait()
    tokens.wait()
    grad_x = copies.start(grad_ref, grad_pair.at[pl.ds(2, 1)], "tensor", 1)
    for _ in high:
        query[0].wait()
    output.wait()
    pack.wait()
    keyval.wait()
    for _ in high:
        query[1].wait()
    unit_second(0)
    unit_first(1)
    query[0].wait()
    pack.wait()
    pack_tensor = SlotGather(copies, None, pack_all, [1, 0], "tensor")
    pack_tensor.start()
    grad_z = copies.start(grad_over_ref, grad_pair.at[pl.ds(1, 1)], "dp", merge)
    query[1].wait()
    unit_second(1)
    unit_first(2)
    for _ in high:
        output.wait()
    grad_x.wait()
    pack_tensor.wait()
    keyval.wait()
    grad_z.wait()
    grad_zx = copies.start(
        grad_pair.at[pl.ds(1, 1)], grad_pair.at[pl.ds(3, 1)], "tensor", 1
    )
    pack_tensor.wait()
    tokens.wait()
    query[0].wait()
    for _ in high:
        chains[0].wait()
    unit_second(2)
    unit_first(3)
    query[1].wait()
    output.wait()
    grad_zx.wait()
    grad_own.wait()
    grad_c = copies.start(grad_pair.at[pl.ds(0, 4)], grad_pair.at[pl.ds(4, 4)], "tensor", 0)
    for i in range(1, len(units)):
        for _ in high:
            chains[i].wait()
        if i + 2 < len(units):
            unit_second(i + 2)
        if i + 3 < len(units):
            unit_first(i + 3)
    grad_c.wait()
    for chain in chains:
        chain.finish()


def gather_all(tokens, grad, grad_over, pack, keyval, query, output, own, other):
    n_dp = lax.axis_size("dp")
    n_bits = n_dp.bit_length() - 1
    n_pieces, width = own.shape[0], own.shape[1] // LANE_CHUNKS
    bf16 = jnp.bfloat16
    n_copies = 5 * (n_bits + 2) + n_pieces * LANE_CHUNKS * n_bits + 8
    any_spec = pl.BlockSpec(memory_space=pl.ANY)
    shapes = [
        (4, *tokens.shape),
        (8, *grad.shape),
        (4, n_dp, *pack.shape),
        (n_dp, *keyval.shape),
        (n_dp, *query.shape),
        (n_dp, *output.shape),
        (n_pieces, n_dp, *own.shape[1:]),
    ]
    operands = [tokens[None], grad[None], grad_over[None], pack[None], keyval[None], query[None], output[None], own, other]
    return pl.pallas_call(
        functools.partial(gather_kernel, n_bits, n_pieces, width),
        out_shape=[jax.ShapeDtypeStruct(s, bf16) for s in shapes],
        in_specs=[any_spec] * len(operands),
        out_specs=[any_spec] * len(shapes),
        scratch_shapes=[
            pltpu.SemaphoreType.DMA((n_copies,)),
            pltpu.SemaphoreType.DMA((n_copies,)),
            pltpu.SemaphoreType.DMA((32,)),
        ],
        compiler_params=pltpu.CompilerParams(collective_id=0, has_side_effects=True),
        name="gather_all",
    )(*operands)


def body(
    res_in,
    out_grad,
    seg_ids,
    tok_counts,
    slot_table,
    slot_gates,
    attn_gain,
    latent_gain,
    ffn_gain,
    w_latent,
    w_query,
    w_keyval,
    w_output,
    w_expert_in,
    w_expert_out,
    w_shared_in,
    w_shared_out,
):
    f32 = jnp.float32
    bf16 = jnp.bfloat16
    n_tensor = lax.axis_size("tensor")
    n_dp = lax.axis_size("dp")
    dp = lax.axis_index("dp")
    tensor = lax.axis_index("tensor")
    merge = 1
    high = list(range(n_dp.bit_length() - 2, 1, -1))
    far_first = high + [merge, 0]
    order = slot_order(far_first)
    tensor_order = slot_order([1, 0])
    rows = res_in.shape[0]
    local_heads = H // n_tensor
    score_scale = (HD + RD) ** (-0.5)
    line = Line(tok_counts)

    def steps(thing, count):
        for _ in range(count):
            thing.wait()
            if thing.bits:
                thing.start()

    res_local = to_slots(res_in, dp, order, 1)
    pack_rows = w_latent.shape[0]
    gain_row = jnp.concatenate([attn_gain, ffn_gain, latent_gain])
    gain_row = jnp.pad(gain_row, (0, w_latent.shape[1] - gain_row.shape[0]))
    pack = jnp.concatenate([w_latent, jnp.broadcast_to(gain_row, (16, w_latent.shape[1]))], axis=0)

    first = ((dp >> merge) & 1) == 0
    n_half = EXPERTS // 2
    width = w_expert_out.shape[1]
    expert_units = jnp.concatenate(
        [
            w_expert_in.transpose(0, 1, 3, 2).reshape(EXPERTS, -1, w_expert_in.shape[2]),
            w_expert_out,
        ],
        axis=1,
    )
    shared_t = w_shared_in.transpose(0, 2, 1)
    units = []
    for side in range(2):
        cut = slice(side * width, (side + 1) * width)
        shared_unit = jnp.concatenate([shared_t[0, cut], shared_t[1, cut], w_shared_out[cut]], axis=0)
        units.append([*expert_units[side * n_half : (side + 1) * n_half], shared_unit])
    own_units = [jnp.where(first, a, b) for a, b in zip(*units)]
    other_units = [jnp.where(first, b, a) for a, b in zip(*units)]

    token_ids = jnp.concatenate(
        [(tensor ^ j) * rows + jnp.arange(rows, dtype=jnp.int32) for j in tensor_order]
    )
    segment_canon = seg_ids[0]
    segment_row = jnp.concatenate(
        [lax.dynamic_slice_in_dim(segment_canon, (tensor ^ j) * rows, rows) for j in tensor_order]
    )
    valid_all = (token_ids < tok_counts[0]).astype(f32)
    valid_rows = valid_all[:rows, None]
    group_gate = jnp.sum(
        jnp.where(slot_table[0][:, :, None] == token_ids[None, None, :], slot_gates[0][:, :, None], 0.0),
        axis=1,
    )
    grad_in = to_slots(out_grad, dp, order, 1).astype(f32)
    ffn_grad = (valid_rows * grad_in).astype(bf16)

    def partner_columns(values):
        return take_slots(
            values, [order.index(j ^ (1 << merge)) for j in order], n_dp, values.ndim - 1
        )

    over_gate = lax.ppermute(group_gate, "dp", flip_pairs(n_dp, merge))
    (
        tokens_all,
        grad_pair,
        pack_all,
        keyval_slots,
        query_slots,
        output_slots,
        units_all,
    ) = gather_all(
        res_local,
        ffn_grad,
        partner_columns(ffn_grad),
        pack,
        w_keyval,
        w_query,
        w_output,
        jnp.stack(own_units),
        jnp.stack(other_units),
    )
    grad_pair = grad_pair.reshape(-1, D)
    other_gate = over_gate

    pack_blocks = [pack_all[tensor_order.index(j)] for j in range(n_tensor)]
    pack_all = jnp.stack(select_blocks(pack_blocks, tensor), axis=1)
    latent_full = pack_all[:, :, :pack_rows].reshape(D, KR + RD)
    gains = pack_all[:, :, pack_rows]
    gain_width, latent_width = D // (n_dp * n_tensor), KR // (n_dp * n_tensor)
    attn_gain_full = gains[..., :gain_width].reshape(D)
    ffn_gain_full = gains[..., gain_width : 2 * gain_width].reshape(D)
    latent_gain_full = from_slots(
        gains[..., 2 * gain_width : 2 * gain_width + latent_width].reshape(KR), dp, order, 0
    )
    keyval_full = from_slots(keyval_slots.reshape(KR, -1), dp, order, 0)

    positions = token_ids - jnp.sum(
        (segment_canon[None, :] < segment_row[:, None]).astype(jnp.int32), axis=1
    )
    cos_all, sin_all = rotary_tables(positions)
    allowed = (segment_row[:, None] == segment_row[None, :]) & (
        token_ids[None, :] <= token_ids[:, None]
    )
    resid_all = tokens_all.reshape(TOK, D).astype(f32)
    in_factor = rms_factor(resid_all)
    normed_all = (resid_all * in_factor * attn_gain_full).astype(bf16)
    latent_raw = jnp.dot(normed_all, latent_full, preferred_element_type=f32)
    latent_c = latent_raw[:, :KR]
    latent_factor = rms_factor(latent_c)
    latent_norm = (latent_c * latent_factor * latent_gain_full).astype(bf16)
    rope_all = rotate(latent_raw[:, KR:], cos_all, sin_all).astype(bf16)
    keyval_all = (
        jnp.dot(latent_norm, keyval_full, preferred_element_type=f32)
        .astype(bf16)
        .reshape(TOK, local_heads, HD + VD)
    )
    key_nope = keyval_all[..., :HD]
    values_all = keyval_all[..., HD:]

    query_full = query_slots.reshape(D, -1)
    query_raw = jnp.dot(normed_all, query_full, preferred_element_type=f32).reshape(
        TOK, local_heads, HD + RD
    )
    query_final = jnp.concatenate(
        [
            query_raw[..., :HD],
            rotate(query_raw[..., HD:], cos_all[:, None, :], sin_all[:, None, :]),
        ],
        axis=-1,
    ).astype(bf16)
    raw_scores = jnp.einsum(
        "qhd,khd->hqk", query_final[..., :HD], key_nope, preferred_element_type=f32
    )
    raw_scores = raw_scores + jnp.einsum(
        "qhr,kr->hqk", query_final[..., HD:], rope_all, preferred_element_type=f32
    )
    scores = jnp.where(allowed[None], raw_scores * score_scale, -1e30)
    top_score = jnp.max(scores, axis=-1, keepdims=True)
    exp_scores = jnp.exp(scores - top_score)
    probs_all = exp_scores / jnp.sum(exp_scores, axis=-1, keepdims=True)
    probs_low = probs_all.astype(bf16)
    attn_mix = (
        jnp.einsum("hqk,khd->qhd", probs_low, values_all, preferred_element_type=f32)
        .astype(bf16)
        .reshape(TOK, local_heads * VD)
    )
    output_order = slot_order([0] + high + [merge])
    output_full = jnp.concatenate([output_slots[output_order.index(j)] for j in order], axis=1)
    attn_part = jnp.dot(attn_mix, output_full, preferred_element_type=f32)
    attn_sum = Sum(line, attn_part, tensor_order, [0, 1], 0, "tensor").start()
    steps(attn_sum, 1)
    steps(attn_sum, 1)
    attn_out = attn_sum.values
    resid_in = res_local.astype(f32)
    mid_resid = resid_in + valid_rows * attn_out
    mid_factor = rms_factor(mid_resid)
    normed_mid = (mid_resid * mid_factor * ffn_gain_full).astype(bf16)

    mid_x = line.start(normed_mid, "tensor", 1)
    mid_z = line.start(partner_columns(normed_mid), "dp", merge)
    mid_z = line.wait(mid_z)
    mid_x = line.wait(mid_x)
    mid_zx = line.start(mid_z, "tensor", 1)
    mid_zx = line.wait(mid_zx)
    mid_own = jnp.concatenate([normed_mid, mid_z, mid_x, mid_zx], axis=0)
    mid_c = line.start(mid_own, "tensor", 0)
    mid_pair = jnp.concatenate([mid_own, line.wait(mid_c)], axis=0)

    unit_order = slot_order([merge] + high + [0])
    gate_rows = []
    for slot in range(n_tensor):
        place = [0, 1, 2, 3][slot]
        for gate in (group_gate, other_gate):
            gate_rows.append(gate[:, place * rows : (place + 1) * rows])
    pair_gate = jnp.concatenate(gate_rows, axis=1)
    pair_gate = jnp.where(first, pair_gate[:n_half], pair_gate[n_half:])
    mid_pair_grad = None
    hidden_parts, out_parts, unit_sums = [], [], []
    for p in range(n_half + 1):
        piece = jnp.concatenate([units_all[p, unit_order.index(j)] for j in order], axis=1)
        gate_up = dot(piece[: 2 * width], mid_pair, ((1,), (1,)))
        gate_pre, up = gate_up[:width], gate_up[width:]
        silu, slope = silu_parts(gate_pre)
        hidden_grad = dot(piece[2 * width :], grad_pair, ((1,), (1,)))
        hidden = silu * up
        if p < n_half:
            hidden = hidden * pair_gate[p][None]
            hidden_grad = hidden_grad * pair_gate[p][None]
        hidden = hidden.astype(bf16)
        pre_grad = jnp.concatenate(
            [(hidden_grad * up * slope).astype(bf16), (hidden_grad * silu).astype(bf16)], axis=0
        )
        back = dot(pre_grad, piece[: 2 * width], ((0,), (0,)))
        mid_pair_grad = back if mid_pair_grad is None else mid_pair_grad + back
        hidden_parts.append(hidden)
        out_parts.append(piece[2 * width :])
        if p == n_half:
            mid_sum = Sum(line, mid_pair_grad, [0, 1], [0], 0, "tensor").start()
        in_wgrad = dot(pre_grad, mid_pair, ((1,), (0,)))
        out_wgrad = dot(hidden, grad_pair, ((1,), (0,)))
        unit_grad = jnp.concatenate([in_wgrad, out_wgrad], axis=0).astype(bf16)
        unit_sums.append(Sum(line, unit_grad, order, [0] + high[::-1] + [merge], 1).start())
    mid_sum.wait()
    mid_sum = Sum(line, mid_sum.values, [0, 2], [1], 0, "tensor").start()
    unit_sums[0].wait().start()
    ffn_part = dot(
        jnp.concatenate(hidden_parts, axis=0), jnp.concatenate(out_parts, axis=0), ((0,), (0,))
    )
    mid_sum.wait()
    own_part, over_part = jnp.split(mid_sum.values, 2, axis=0)
    mid_over = line.start(partner_columns(over_part).astype(bf16), "dp", merge)
    unit_sums[1].wait().start()
    mid_grad_local = own_part + line.wait(mid_over).astype(f32)

    mid_back, ffn_gain_part = norm_back(mid_grad_local, mid_resid, mid_factor, ffn_gain_full)
    mid_grad = grad_in + mid_back
    attn_grad = (valid_rows * mid_grad).astype(bf16)
    back_tokens = Gather(line, attn_grad, [1, 0], "tensor").start()
    for _ in high[1:]:
        unit_sums[0].wait().start()
    steps(back_tokens, 1)
    unit_sums[2].wait().start()
    steps(back_tokens, 1)
    attn_grad_all = back_tokens.values
    output_wgrad = dot(attn_mix, attn_grad_all, ((0,), (0,)))
    mix_grad = (
        dot(attn_grad_all, output_full, ((1,), (1,))).astype(bf16).reshape(TOK, local_heads, VD)
    )
    output_sum = Sum(line, output_wgrad, order, [merge] + high[::-1] + [0], 1).start()
    ffn_sum = Sum(line, ffn_part, [0, 1], [0], 0, "tensor").start()
    probs_grad = jnp.einsum("qhd,khd->hqk", mix_grad, values_all, preferred_element_type=f32)
    value_grad = jnp.einsum("hqk,qhd->khd", probs_low, mix_grad, preferred_element_type=f32)
    scores_grad = (
        probs_all * (probs_grad - jnp.sum(probs_all * probs_grad, axis=-1, keepdims=True))
    ).astype(bf16)
    query_nope_grad = (
        jnp.einsum("hqk,khd->qhd", scores_grad, key_nope, preferred_element_type=f32) * score_scale
    )
    query_rope_grad = (
        jnp.einsum("hqk,kr->qhr", scores_grad, rope_all, preferred_element_type=f32) * score_scale
    )
    key_nope_grad = (
        jnp.einsum("hqk,qhd->khd", scores_grad, query_final[..., :HD], preferred_element_type=f32)
        * score_scale
    )
    rope_key_grad = (
        jnp.einsum("hqk,qhr->kr", scores_grad, query_final[..., HD:], preferred_element_type=f32)
        * score_scale
    )
    query_grad = (
        jnp.concatenate(
            [query_nope_grad, rotate(query_rope_grad, cos_all[:, None, :], -sin_all[:, None, :])],
            axis=-1,
        )
        .astype(bf16)
        .reshape(TOK, local_heads * (HD + RD))
    )
    keyval_grad = (
        jnp.concatenate([key_nope_grad, value_grad], axis=-1)
        .astype(bf16)
        .reshape(TOK, local_heads * (HD + VD))
    )
    unit_sums[0].wait().start()
    ffn_sum.wait()
    query_wgrad = dot(normed_all, query_grad, ((0,), (0,)))
    query_sum = Sum(line, query_wgrad, order, far_first[::-1], 0).start()
    latent_part = jnp.concatenate([dot(keyval_grad, keyval_full, ((1,), (1,))), rope_key_grad], axis=1)
    normed_part = dot(query_grad, query_full, ((1,), (1,)))
    back_part = jnp.concatenate([latent_part, normed_part], axis=1)
    back_sum = Sum(line, back_part, tensor_order, [0, 1], 0, "tensor").start()
    keyval_wgrad = to_slots(dot(latent_norm, keyval_grad, ((0,), (0,))).astype(bf16), dp, order, 0)
    keyval_sum = Sum(line, keyval_wgrad, order, far_first[::-1], 0).start()
    back_sum.wait().start()
    output_sum.wait().start()
    for _ in high[1:]:
        unit_sums[1].wait().start()
    unit_sums[1].wait().start()
    back_sum.wait()
    latent_grad_local = back_sum.values[:, : KR + RD]
    normed_grad_local = back_sum.values[:, KR + RD :]
    latent_c_grad, latent_gain_part = norm_back(
        latent_grad_local[:, :KR], latent_c[:rows], latent_factor[:rows], latent_gain_full
    )
    rope_raw_grad = rotate(latent_grad_local[:, KR:], cos_all[:rows], -sin_all[:rows])
    latent_raw_grad = jnp.concatenate([latent_c_grad, rope_raw_grad], axis=1).astype(bf16)
    latent_back = Gather(line, latent_raw_grad, [1, 0], "tensor").start()
    for _ in high:
        output_sum.wait().start()
    keyval_sum.wait().start()
    latent_back.wait().start()
    query_sum.wait().start()
    latent_back.wait()
    latent_wgrad = dot(normed_all, latent_back.values, ((0,), (0,))).astype(bf16)
    latent_wgrad = lax.dynamic_index_in_dim(
        latent_wgrad.reshape(n_dp, n_tensor, pack_rows, KR + RD), tensor, 1, keepdims=False
    )
    latent_sum = Sum(line, latent_wgrad, order, far_first[::-1], 0).start()
    normed_grad = normed_grad_local + dot(latent_raw_grad, latent_full, ((1,), (1,)))
    in_back, attn_gain_part = norm_back(normed_grad, resid_in, in_factor[:rows], attn_gain_full)
    res_grad = mid_grad + in_back
    gain_parts = jnp.concatenate(
        [
            attn_gain_part.reshape(n_dp, n_tensor, gain_width),
            ffn_gain_part.reshape(n_dp, n_tensor, gain_width),
            to_slots(latent_gain_part, dp, order, 0).reshape(n_dp, n_tensor, latent_width),
        ],
        axis=2,
    )
    gain_blocks = select_blocks([gain_parts[:, i] for i in range(n_tensor)], tensor)
    gain_parts = jnp.stack([gain_blocks[j] for j in tensor_order], axis=0)
    gain_sum = Sum(line, gain_parts, tensor_order, [0, 1], 0, "tensor", f32).start()
    output_owned = output_sum.wait().values
    ffn_sum = Sum(line, ffn_sum.values, [0, 2], [1], 0, "tensor").start()
    for _ in high:
        unit_sums[2].wait().start()
    keyval_sum.wait().start()
    gain_sum.wait().start()
    latent_sum.wait().start()
    query_sum.wait().start()
    ffn_sum.wait()
    ffn_own, ffn_over = jnp.split(ffn_sum.values, 2, axis=0)
    ffn_over = line.start(partner_columns(ffn_over).astype(bf16), "dp", merge)
    gain_sum.wait()
    gain_dp = Sum(line, gain_sum.values[0], order, far_first[::-1], 0, "dp", f32).start()
    for _ in high[1:]:
        keyval_sum.wait().start()
        latent_sum.wait().start()
        query_sum.wait().start()
        gain_dp.wait().start()
    latent_sum.wait().start()
    gain_dp.wait().start()
    ffn_out = ffn_own + line.wait(ffn_over).astype(f32)
    res_out = (mid_resid + valid_rows * ffn_out).astype(bf16)
    own_grads, other_grads = [], []
    for s in unit_sums:
        other_grads.append(line.wait(s.flying).astype(f32))
        own_grads.append(s.keep)
    gain_dp.wait().start()
    keyval_owned = keyval_sum.wait().values
    latent_owned = latent_sum.wait().values[0]
    query_owned = query_sum.wait().values
    gain_owned = gain_dp.wait().values[0]

    sides = []
    for side in (first, ~first):
        sides.append([jnp.where(side, a, b) for a, b in zip(own_grads, other_grads)])
    expert_units = jnp.stack([unit for side in sides for unit in side[:n_half]], axis=0)
    expert_in_owned = expert_units[:, : 2 * width].reshape(EXPERTS, 2, width, -1).transpose(0, 1, 3, 2)
    expert_out_owned = expert_units[:, 2 * width :]
    shared_in_owned = jnp.stack(
        [
            jnp.concatenate([side[n_half][k * width : (k + 1) * width] for side in sides], axis=0).T
            for k in range(2)
        ],
        axis=0,
    )
    shared_out_owned = jnp.concatenate([side[n_half][2 * width :] for side in sides], axis=0)
    return (
        from_slots(res_out, dp, order, 1),
        from_slots(res_grad, dp, order, 1),
        gain_owned[:gain_width],
        gain_owned[2 * gain_width :],
        gain_owned[gain_width : 2 * gain_width],
        latent_owned,
        query_owned,
        keyval_owned,
        output_owned,
        expert_in_owned,
        expert_out_owned,
        shared_in_owned,
        shared_out_owned,
    )


def solution(mesh):
    placed = (
        P(("dp", "tensor"), None),
        P(("dp", "tensor"), None),
        P("dp", None),
        P("dp"),
        P("dp", None, None),
        P("dp", None, None),
        P(("dp", "tensor")),
        P(("dp", "tensor")),
        P(("dp", "tensor")),
        P(("dp", "tensor"), None),
        P("dp", "tensor"),
        P("dp", "tensor"),
        P("tensor", "dp"),
        P(None, None, "dp", "tensor"),
        P(None, "tensor", "dp"),
        P(None, "dp", "tensor"),
        P("tensor", "dp"),
    )
    return jax.shard_map(
        body,
        mesh=mesh,
        in_specs=placed,
        out_specs=(
            P(("dp", "tensor"), None),
            P(("dp", "tensor"), None),
            P(("dp", "tensor")),
            P(("dp", "tensor")),
            P(("dp", "tensor")),
            P(("dp", "tensor"), None),
            P("dp", "tensor"),
            P("dp", "tensor"),
            P("tensor", "dp"),
            P(None, None, "dp", "tensor"),
            P(None, "tensor", "dp"),
            P(None, "dp", "tensor"),
            P("tensor", "dp"),
        ),
        check_vma=False,
    )
```

```python
import functools
import types

import jax
import jax.numpy as jnp
import numpy as np
from jax import lax
from jax.experimental import pallas as pl
from jax.experimental.pallas import tpu as pltpu
from jax.sharding import PartitionSpec as P

D = 2048
H = 16
HD = 128
RD = 64
VD = 128
KR = 512
TOK = 640
EXPERTS = 4


NORM_EPS = 1e-06
ROPE_BASE = 50000.0


def rms_factor(values):
    return lax.rsqrt(jnp.mean(values * values, axis=-1, keepdims=True) + NORM_EPS)


def norm_back(grad_out, values, factor, gain_vec):
    scaled = grad_out * gain_vec
    inner_sum = jnp.mean(scaled * values, axis=-1, keepdims=True)
    return (
        factor * (scaled - values * factor * factor * inner_sum),
        jnp.sum(grad_out * values * factor, axis=0),
    )


def rotary_tables(positions):
    half_width = RD // 2
    inv_freq = ROPE_BASE ** (-jnp.arange(half_width, dtype=jnp.float32) / half_width)
    angles = positions.astype(jnp.float32)[:, None] * inv_freq[None, :]
    return (jnp.cos(angles), jnp.sin(angles))


def rotate(values, cosine_table, sine_table):
    half_width = values.shape[-1] // 2
    first_half = values[..., :half_width]
    second_half = values[..., half_width:]
    return jnp.concatenate(
        [
            first_half * cosine_table - second_half * sine_table,
            second_half * cosine_table + first_half * sine_table,
        ],
        axis=-1,
    )


def silu_parts(gate_pre):
    sigma_gate = jax.nn.sigmoid(gate_pre)
    return (gate_pre * sigma_gate, sigma_gate * (1.0 + gate_pre * (1.0 - sigma_gate)))


def flip_pairs(count, bit):
    return [(i, i ^ (1 << bit)) for i in range(count)]


def swap_dp(values, bit):
    return lax.ppermute(values, DP, flip_pairs(lax.axis_size(DP), bit))


def swap_tensor(values, bit):
    return lax.ppermute(values, TENSOR, flip_pairs(lax.axis_size(TENSOR), bit))


def dp_bits():
    top = lax.axis_size(DP).bit_length() - 1
    return [1] + list(range(top - 1, 1, -1)) + [0]


def slot_order(bits):
    order = [0]
    for bit in bits:
        order = order + [j ^ (1 << bit) for j in order]
    return order


def select_blocks(blocks, index):
    step = 1
    while step < len(blocks):
        hit = (index & step) != 0
        blocks = [jnp.where(hit, blocks[i ^ step], blocks[i]) for i in range(len(blocks))]
        step *= 2
    return blocks


def to_slots(values, index, bits, axis):
    count = 1 << len(bits)
    blocks = select_blocks(jnp.split(values, count, axis=axis), index)
    return jnp.concatenate([blocks[j] for j in slot_order(bits)], axis=axis)


def from_slots(values, index, bits, axis):
    order = slot_order(bits)
    slots = jnp.split(values, len(order), axis=axis)
    blocks = [slots[order.index(i)] for i in range(len(order))]
    return jnp.concatenate(select_blocks(blocks, index), axis=axis)


def gather_dp(values, bits):
    for bit in bits:
        values = jnp.concatenate([values, swap_dp(values, bit)], axis=0)
    return values


def gather_tensor(values):
    for bit in (1, 0):
        values = jnp.concatenate([values, swap_tensor(values, bit)], axis=0)
    return values


def scatter_dp(values, bits, axis):
    values = values.astype(jnp.float32)
    for bit in reversed(bits):
        keep, give = jnp.split(values, 2, axis=axis)
        values = keep + swap_dp(give.astype(jnp.bfloat16), bit).astype(jnp.float32)
    return values


def scatter_tensor(values):
    for bit in (0, 1):
        keep, give = jnp.split(values, 2, axis=0)
        values = keep + swap_tensor(give.astype(jnp.bfloat16), bit).astype(jnp.float32)
    return values


def partner_columns(values):
    count = lax.axis_size(DP)
    slots = jnp.split(values, count, axis=-1)
    return jnp.concatenate([slots[k ^ 1] for k in range(count)], axis=-1)


def gather_pair(values, bit):
    over = swap_dp(partner_columns(values), bit)
    own = jnp.concatenate([values, over, swap_tensor(values, 1), swap_tensor(over, 1)], axis=0)
    return jnp.concatenate([own, swap_tensor(own, 0)], axis=0)


def scatter_pair(values, bit):
    values = scatter_tensor(values)
    keep, give = jnp.split(values, 2, axis=0)
    return keep + swap_dp(partner_columns(give).astype(jnp.bfloat16), bit).astype(jnp.float32)


def dot(a, b, contract):
    return lax.dot_general(a, b, (contract, ((), ())), preferred_element_type=jnp.float32)


def general_body(
    res_in,
    out_grad,
    seg_ids,
    tok_counts,
    slot_table,
    slot_gates,
    attn_gain,
    latent_gain,
    ffn_gain,
    w_latent,
    w_query,
    w_keyval,
    w_output,
    w_expert_in,
    w_expert_out,
    w_shared_in,
    w_shared_out,
):
    f32 = jnp.float32
    bf16 = jnp.bfloat16
    n_tensor = lax.axis_size(TENSOR)
    n_dp = lax.axis_size(DP)
    dp = lax.axis_index(DP)
    tensor = lax.axis_index(TENSOR)
    bits = dp_bits()
    merge = bits[0]
    half = (dp >> merge) & 1
    rows = res_in.shape[0]
    local_heads = H // n_tensor
    score_scale = (HD + RD) ** (-0.5)

    res_local = to_slots(res_in, dp, bits, 1)
    res_all = gather_tensor(res_local)
    tensor_slots = slot_order([1, 0])
    token_ids = jnp.concatenate(
        [(tensor ^ j) * rows + jnp.arange(rows, dtype=jnp.int32) for j in tensor_slots]
    )
    segment_canon = seg_ids[0]
    segment_row = jnp.concatenate(
        [lax.dynamic_slice_in_dim(segment_canon, (tensor ^ j) * rows, rows) for j in tensor_slots]
    )
    valid_all = (token_ids < tok_counts[0]).astype(f32)
    valid_rows = valid_all[:rows, None]
    group_gate = jnp.sum(
        jnp.where(slot_table[0][:, :, None] == token_ids[None, None, :], slot_gates[0][:, :, None], 0.0),
        axis=1,
    )
    grad_in = to_slots(out_grad, dp, bits, 1).astype(f32)
    ffn_grad = (valid_rows * grad_in).astype(bf16)

    pack_rows = w_latent.shape[0]
    gain_row = jnp.concatenate([attn_gain, ffn_gain, latent_gain])
    gain_row = jnp.pad(gain_row, (0, w_latent.shape[1] - gain_row.shape[0]))
    pack = jnp.concatenate([w_latent, jnp.broadcast_to(gain_row, (16, w_latent.shape[1]))], axis=0)
    pack = gather_dp(pack[None], bits)
    pack = gather_tensor(pack[None])
    pack_blocks = [pack[tensor_slots.index(j)] for j in range(n_tensor)]
    pack = jnp.stack(select_blocks(pack_blocks, tensor), axis=1)
    latent_full = pack[:, :, :pack_rows].reshape(D, KR + RD)
    gains = pack[:, :, pack_rows]
    gain_width, latent_width = D // (n_dp * n_tensor), KR // (n_dp * n_tensor)
    attn_gain_full = gains[..., :gain_width].reshape(D)
    ffn_gain_full = gains[..., gain_width : 2 * gain_width].reshape(D)
    latent_gain_full = from_slots(
        gains[..., 2 * gain_width : 2 * gain_width + latent_width].reshape(KR), dp, bits, 0
    )
    query_full = gather_dp(w_query, bits)
    keyval_full = from_slots(gather_dp(w_keyval, bits), dp, bits, 0)
    output_full = gather_dp(w_output[None], bits)
    output_full = jnp.concatenate([output_full[k] for k in range(n_dp)], axis=1)

    n_half = EXPERTS // 2
    expert_units = jnp.concatenate(
        [
            w_expert_in.transpose(0, 1, 3, 2).reshape(EXPERTS, -1, w_expert_in.shape[2]),
            w_expert_out,
        ],
        axis=1,
    )
    width = w_expert_out.shape[1]
    shared_t = w_shared_in.transpose(0, 2, 1)
    units = []
    for side in range(2):
        cut = slice(side * width, (side + 1) * width)
        shared_unit = jnp.concatenate([shared_t[0, cut], shared_t[1, cut], w_shared_out[cut]], axis=0)
        units.append(jnp.concatenate([expert_units[side * n_half : (side + 1) * n_half], shared_unit[None]], axis=0))
    first = half == 0
    own_units = jnp.where(first, units[0], units[1])
    other_units = jnp.where(first, units[1], units[0])
    pieces = []
    for p in range(n_half + 1):
        piece = jnp.stack([own_units[p], swap_dp(other_units[p], merge)], axis=0)
        piece = gather_dp(piece, bits[1:])
        pieces.append(jnp.concatenate([piece[k] for k in range(n_dp)], axis=1))

    positions = token_ids - jnp.sum(
        (segment_canon[None, :] < segment_row[:, None]).astype(jnp.int32), axis=1
    )
    cos_all, sin_all = rotary_tables(positions)
    allowed = (segment_row[:, None] == segment_row[None, :]) & (
        token_ids[None, :] <= token_ids[:, None]
    )
    resid_all = res_all.astype(f32)
    in_factor = rms_factor(resid_all)
    normed_all = (resid_all * in_factor * attn_gain_full).astype(bf16)
    latent_raw = jnp.dot(normed_all, latent_full, preferred_element_type=f32)
    latent_c = latent_raw[:, :KR]
    latent_factor = rms_factor(latent_c)
    latent_norm = (latent_c * latent_factor * latent_gain_full).astype(bf16)
    rope_all = rotate(latent_raw[:, KR:], cos_all, sin_all).astype(bf16)
    query_raw = jnp.dot(normed_all, query_full, preferred_element_type=f32).reshape(
        TOK, local_heads, HD + RD
    )
    query_final = jnp.concatenate(
        [
            query_raw[..., :HD],
            rotate(query_raw[..., HD:], cos_all[:, None, :], sin_all[:, None, :]),
        ],
        axis=-1,
    ).astype(bf16)
    keyval = (
        jnp.dot(latent_norm, keyval_full, preferred_element_type=f32)
        .astype(bf16)
        .reshape(TOK, local_heads, HD + VD)
    )
    key_nope = keyval[..., :HD]
    values_all = keyval[..., HD:]
    raw_scores = jnp.einsum(
        "qhd,khd->hqk", query_final[..., :HD], key_nope, preferred_element_type=f32
    )
    raw_scores = raw_scores + jnp.einsum(
        "qhr,kr->hqk", query_final[..., HD:], rope_all, preferred_element_type=f32
    )
    scores = jnp.where(allowed[None], raw_scores * score_scale, -1e30)
    top_score = jnp.max(scores, axis=-1, keepdims=True)
    exp_scores = jnp.exp(scores - top_score)
    probs_all = exp_scores / jnp.sum(exp_scores, axis=-1, keepdims=True)
    probs_low = probs_all.astype(bf16)
    attn_mix = (
        jnp.einsum("hqk,khd->qhd", probs_low, values_all, preferred_element_type=f32)
        .astype(bf16)
        .reshape(TOK, local_heads * VD)
    )
    attn_part = jnp.dot(attn_mix, output_full, preferred_element_type=f32)
    attn_out = scatter_tensor(attn_part)
    resid_in = res_local.astype(f32)
    mid_resid = resid_in + valid_rows * attn_out
    mid_factor = rms_factor(mid_resid)
    normed_mid = (mid_resid * mid_factor * ffn_gain_full).astype(bf16)

    mid_pair = gather_pair(normed_mid, merge)
    grad_pair = gather_pair(ffn_grad, merge)
    other_gate = swap_dp(group_gate, merge)
    pair_gate = jnp.concatenate(
        [
            gate[:, k * rows : (k + 1) * rows]
            for k in ((0, 0), (1, 0), (0, 1), (1, 1), (0, 2), (1, 2), (0, 3), (1, 3))
            for gate, k in (((group_gate, other_gate)[k[0]], k[1]),)
        ],
        axis=1,
    )
    pair_gate = jnp.where(first, pair_gate[:n_half], pair_gate[n_half:])
    mid_pair_grad = None
    hidden_parts, out_parts, unit_grads = [], [], []
    for p, piece in enumerate(pieces):
        gate_up = dot(piece[: 2 * width], mid_pair, ((1,), (1,)))
        gate_pre, up = gate_up[:width], gate_up[width:]
        silu, slope = silu_parts(gate_pre)
        hidden_grad = dot(piece[2 * width :], grad_pair, ((1,), (1,)))
        hidden = silu * up
        if p < n_half:
            hidden = hidden * pair_gate[p][None]
            hidden_grad = hidden_grad * pair_gate[p][None]
        hidden = hidden.astype(bf16)
        pre_grad = jnp.concatenate(
            [(hidden_grad * up * slope).astype(bf16), (hidden_grad * silu).astype(bf16)], axis=0
        )
        back = dot(pre_grad, piece[: 2 * width], ((0,), (0,)))
        mid_pair_grad = back if mid_pair_grad is None else mid_pair_grad + back
        hidden_parts.append(hidden)
        out_parts.append(piece[2 * width :])
        in_wgrad = dot(pre_grad, mid_pair, ((1,), (0,)))
        out_wgrad = dot(hidden, grad_pair, ((1,), (0,)))
        unit_grads.append(jnp.concatenate([in_wgrad, out_wgrad], axis=0).astype(bf16))
    ffn_part = dot(
        jnp.concatenate(hidden_parts, axis=0), jnp.concatenate(out_parts, axis=0), ((0,), (0,))
    )
    ffn_out = scatter_pair(ffn_part, merge)
    res_out = (mid_resid + valid_rows * ffn_out).astype(bf16)
    mid_grad_local = scatter_pair(mid_pair_grad, merge)

    mid_back, ffn_gain_part = norm_back(mid_grad_local, mid_resid, mid_factor, ffn_gain_full)
    mid_grad = grad_in + mid_back
    attn_grad = (valid_rows * mid_grad).astype(bf16)
    attn_grad_all = gather_tensor(attn_grad)
    output_wgrad = dot(attn_mix, attn_grad_all, ((0,), (0,)))
    mix_grad = (
        dot(attn_grad_all, output_full, ((1,), (1,))).astype(bf16).reshape(TOK, local_heads, VD)
    )
    probs_grad = jnp.einsum("qhd,khd->hqk", mix_grad, values_all, preferred_element_type=f32)
    value_grad = jnp.einsum("hqk,qhd->khd", probs_low, mix_grad, preferred_element_type=f32)
    scores_grad = (
        probs_all * (probs_grad - jnp.sum(probs_all * probs_grad, axis=-1, keepdims=True))
    ).astype(bf16)
    query_nope_grad = (
        jnp.einsum("hqk,khd->qhd", scores_grad, key_nope, preferred_element_type=f32) * score_scale
    )
    query_rope_grad = (
        jnp.einsum("hqk,kr->qhr", scores_grad, rope_all, preferred_element_type=f32) * score_scale
    )
    key_nope_grad = (
        jnp.einsum("hqk,qhd->khd", scores_grad, query_final[..., :HD], preferred_element_type=f32)
        * score_scale
    )
    rope_key_grad = (
        jnp.einsum("hqk,qhr->kr", scores_grad, query_final[..., HD:], preferred_element_type=f32)
        * score_scale
    )
    query_grad = (
        jnp.concatenate(
            [query_nope_grad, rotate(query_rope_grad, cos_all[:, None, :], -sin_all[:, None, :])],
            axis=-1,
        )
        .astype(bf16)
        .reshape(TOK, local_heads * (HD + RD))
    )
    keyval_grad = (
        jnp.concatenate([key_nope_grad, value_grad], axis=-1)
        .astype(bf16)
        .reshape(TOK, local_heads * (HD + VD))
    )
    latent_part = jnp.concatenate([dot(keyval_grad, keyval_full, ((1,), (1,))), rope_key_grad], axis=1)
    latent_grad_local = scatter_tensor(latent_part)
    normed_part = dot(query_grad, query_full, ((1,), (1,)))
    normed_grad_local = scatter_tensor(normed_part)
    query_wgrad = dot(normed_all, query_grad, ((0,), (0,)))
    keyval_wgrad = to_slots(dot(latent_norm, keyval_grad, ((0,), (0,))).astype(bf16), dp, bits, 0)
    latent_c_grad, latent_gain_part = norm_back(
        latent_grad_local[:, :KR], latent_c[:rows], latent_factor[:rows], latent_gain_full
    )
    rope_raw_grad = rotate(latent_grad_local[:, KR:], cos_all[:rows], -sin_all[:rows])
    latent_raw_grad = jnp.concatenate([latent_c_grad, rope_raw_grad], axis=1).astype(bf16)
    latent_raw_grad_all = gather_tensor(latent_raw_grad)
    latent_wgrad = dot(normed_all, latent_raw_grad_all, ((0,), (0,))).astype(bf16)
    latent_wgrad = lax.dynamic_index_in_dim(
        latent_wgrad.reshape(n_dp, n_tensor, pack_rows, KR + RD), tensor, 1, keepdims=False
    )
    normed_grad = normed_grad_local + dot(latent_raw_grad, latent_full, ((1,), (1,)))
    in_back, attn_gain_part = norm_back(normed_grad, resid_in, in_factor[:rows], attn_gain_full)
    res_grad = mid_grad + in_back

    output_owned = scatter_dp(output_wgrad, bits, 1)
    query_owned = scatter_dp(query_wgrad, bits, 0)
    keyval_owned = scatter_dp(keyval_wgrad, bits, 0)
    latent_owned = scatter_dp(latent_wgrad, bits, 0)[0]
    gain_parts = jnp.concatenate(
        [
            attn_gain_part.reshape(n_dp, n_tensor, gain_width),
            ffn_gain_part.reshape(n_dp, n_tensor, gain_width),
            to_slots(latent_gain_part, dp, bits, 0).reshape(n_dp, n_tensor, latent_width),
        ],
        axis=2,
    )
    gain_parts = jnp.stack(
        [
            select_blocks([gain_parts[:, i] for i in range(n_tensor)], tensor)[j]
            for j in tensor_slots
        ],
        axis=0,
    )
    for bit in (0, 1):
        keep, give = jnp.split(gain_parts, 2, axis=0)
        gain_parts = keep + swap_tensor(give, bit)
    gain_parts = gain_parts[0]
    for bit in reversed(bits):
        keep, give = jnp.split(gain_parts, 2, axis=0)
        gain_parts = keep + swap_dp(give, bit)
    gain_owned = gain_parts[0]
    own_grads, other_grads = [], []
    for grad in unit_grads:
        grad = grad.astype(f32)
        for bit in reversed(bits[1:]):
            keep, give = jnp.split(grad, 2, axis=1)
            grad = keep + swap_dp(give.astype(bf16), bit).astype(f32)
        keep, give = jnp.split(grad, 2, axis=1)
        own_grads.append(keep)
        other_grads.append(swap_dp(give.astype(bf16), merge).astype(f32))
    sides = []
    for side in (first, ~first):
        sides.append([jnp.where(side, a, b) for a, b in zip(own_grads, other_grads)])
    expert_units = jnp.stack([unit for side in sides for unit in side[:n_half]], axis=0)
    expert_in_owned = expert_units[:, : 2 * width].reshape(EXPERTS, 2, width, -1).transpose(0, 1, 3, 2)
    expert_out_owned = expert_units[:, 2 * width :]
    shared_in_owned = jnp.stack(
        [
            jnp.concatenate([side[n_half][k * width : (k + 1) * width] for side in sides], axis=0).T
            for k in range(2)
        ],
        axis=0,
    )
    shared_out_owned = jnp.concatenate([side[n_half][2 * width :] for side in sides], axis=0)
    return (
        from_slots(res_out, dp, bits, 1),
        from_slots(res_grad, dp, bits, 1),
        gain_owned[:gain_width],
        gain_owned[2 * gain_width :],
        gain_owned[gain_width : 2 * gain_width],
        latent_owned,
        query_owned,
        keyval_owned,
        output_owned,
        expert_in_owned,
        expert_out_owned,
        shared_in_owned,
        shared_out_owned,
    )


DP, TENSOR = "dp", "tensor"
MESH = pl.DeviceIdType.MESH
F32 = jnp.float32
BF16 = jnp.bfloat16
CHUNKS = 3
SECONDS = 9
THIRDS = 7
SLOT = 256
GIVEN_VMEM = 60 * 1024 * 1024
FAR_FIRST = (2, 1, 0)
FLIPS = (1, 2, 0)
TENSOR_BITS = (1, 0)


COLUMNS = slot_order(FAR_FIRST)
UNIT_SLOTS = slot_order(FLIPS)
ROWS = slot_order(TENSOR_BITS)


def nn(a, b):
    return lax.dot_general(a, b, (((1,), (0,)), ((), ())), preferred_element_type=F32)


def nt(a, b):
    return lax.dot_general(a, b, (((1,), (1,)), ((), ())), preferred_element_type=F32)


def tn(a, b):
    return lax.dot_general(a, b, (((0,), (0,)), ((), ())), preferred_element_type=F32)


def lanes(k, width=SLOT):
    return slice(k * width, (k + 1) * width)


def crossed(index, constant, bits):
    total = 0
    for bit in range(bits):
        own = lax.rem(index // (1 << bit), 2)
        total = total + ((1 - own) if (constant >> bit) & 1 else own) * (1 << bit)
    return total


class Copies:
    def __init__(self, send_sems, recv_sems, local_sems=None):
        self.send_sems, self.recv_sems, self.local_sems = send_sems, recv_sems, local_sems
        self.count = 0
        self.local_count = 0

    def across(self, axis, bit):
        index = lax.axis_index(axis)
        side = lax.rem(index // (1 << bit), 2)
        return {axis: index + (1 - 2 * side) * (1 << bit)}

    def start(self, source, target, axis, bit):
        copy = pltpu.make_async_remote_copy(
            src_ref=source,
            dst_ref=target,
            send_sem=self.send_sems.at[self.count],
            recv_sem=self.recv_sems.at[self.count],
            device_id=self.across(axis, bit),
            device_id_type=MESH,
        )
        self.count += 1
        copy.start()
        return copy

    def local(self, source, target):
        copy = pltpu.make_async_copy(source, target, self.local_sems.at[self.local_count])
        self.local_count += 1
        copy.start()
        return copy

    def greet(self, dp_bits, tensor_bits=TENSOR_BITS):
        barrier = pltpu.get_barrier_semaphore()
        for axis, bits in ((DP, dp_bits), (TENSOR, tensor_bits)):
            for bit in bits:
                pl.semaphore_signal(
                    barrier, inc=1, device_id=self.across(axis, bit), device_id_type=MESH
                )
        pl.semaphore_wait(barrier, len(dp_bits) + len(tensor_bits))

    def swapped(self, source, target, first, width):
        parts = []
        for a in range(first, first + width, 1024):
            for b, c in ((a, a + 512), (a + 512, a)):
                parts.append(
                    self.start(
                        source.at[(slice(None),) * (len(source.shape) - 1) + (pl.ds(b, 512),)],
                        target.at[(slice(None),) * (len(target.shape) - 1) + (pl.ds(c, 512),)],
                        DP,
                        1,
                    )
                )
        return Several(parts)


class Several:
    def __init__(self, parts):
        self.parts = parts

    def wait(self):
        for part in self.parts:
            part.wait()


class SlotGather:
    def __init__(self, copies, source, slots, bits, axis=DP, cut=None):
        self.copies, self.source, self.slots, self.bits, self.axis = copies, source, slots, list(bits), axis
        self.cut = (slice(None),) if cut is None else (pl.ds(*cut),)
        self.done, self.have, self.own, self.flying = 0, 1, None, None

    def view(self, first, count):
        return self.slots.at[(pl.ds(first, count), *self.cut)]

    def start(self):
        bit = self.bits[self.done]
        if self.done == 0 and self.source is not None:
            source = self.source.at[(pl.ds(0, 1), *self.cut)]
            self.own = self.copies.local(source, self.view(0, 1))
        else:
            if self.own is not None:
                self.own.wait()
                self.own = None
            source = self.view(0, self.have)
        self.flying = self.copies.start(source, self.view(self.have, self.have), self.axis, bit)
        self.done += 1
        self.have *= 2

    def wait(self):
        self.flying.wait()
        self.flying = None
        if self.done < len(self.bits):
            self.start()

    def finish(self):
        while self.flying is not None:
            self.wait()


ANY_SPEC = pl.BlockSpec(memory_space=pl.ANY)
VMEM_SPEC = pl.BlockSpec(memory_space=pltpu.VMEM)
SMEM_SPEC = pl.BlockSpec(memory_space=pltpu.SMEM)


def cost(micros):
    return pl.CostEstimate(flops=micros * 10**9, bytes_accessed=micros * 10**6, transcendentals=0)


def like(shape, dtype=BF16):
    return jax.ShapeDtypeStruct(shape, dtype)


def turn(a, b, cos, sin):
    return a * cos - b * sin, b * cos + a * sin


def head_lanes(rows, head):
    lane = lax.broadcasted_iota(jnp.int32, (rows, SLOT), 1)
    return lax.rem(lane // 32, 4) == head


def spread_block(copies, pair_ref, between):
    block = lambda k: pair_ref.at[pl.ds(k, 1)]
    x_own = copies.start(block(0), block(2), TENSOR, 1)
    z_own = copies.swapped(block(0), block(1), 0, D)
    waits = [copies.start(block(0), block(4), TENSOR, 0)]
    between()
    z_own.wait()
    over_both = copies.start(block(1), block(3), TENSOR, 1)
    waits.append(copies.start(block(1), block(5), TENSOR, 0))
    between()
    x_own.wait()
    waits.append(copies.start(block(2), block(6), TENSOR, 0))
    between()
    over_both.wait()
    waits.append(copies.start(block(3), block(7), TENSOR, 0))
    for copy in waits:
        copy.wait()


class Places:
    def __init__(self):
        self.dp, self.tensor = lax.axis_index(DP), lax.axis_index(TENSOR)

    def __getitem__(self, k):
        if k == 12:
            return lax.rem(self.dp // 2, 2)
        return crossed(self.dp, COLUMNS[k], 3) if k < 8 else crossed(self.tensor, ROWS[k - 8], 2)


class Kept:
    output = ((8, 512, SLOT), BF16)
    mix = ((TOK, 512), BF16)
    query_final = ((TOK, 768), BF16)
    keyval_final = ((TOK, 1024), BF16)
    key_rope = ((TOK, SLOT), BF16)
    lse = ((TOK, 128), F32)
    query = ((8, SLOT, 768), BF16)
    w_keyval = ((KR, 1024), BF16)
    normed = ((TOK, D), BF16)
    latent_norm = ((TOK, KR), BF16)
    col = ((TOK, 128), F32)
    row = ((8, TOK), F32)
    cos = ((TOK, 128), F32)
    sin = ((TOK, 128), F32)
    gains = ((8, D), F32)
    latent_gain = ((8, KR), F32)
    latent_c = ((160, KR), F32)
    w_latent = ((D, KR + 128), BF16)
    mid = ((160, D), F32)
    mid_pair = ((8, 160, D), BF16)
    res = ((160, D), BF16)
    grad = ((160, D), BF16)
    valid = ((160, 128), F32)
    gates = ((8, TOK), F32)


class Landing:
    tokens = ((4, 160, D), BF16)
    pack = ((4, 8, 64, KR + 128), BF16)
    keyval = ((8, 64, 1024), BF16)
    part = ((4, 160, D), BF16)
    got_c = ((2, 160, D), BF16)
    give_x = ((1, 160, D), BF16)
    got_x = ((1, 160, D), BF16)
    gain_rows = ((KR, 128), BF16)
    masked = ((1, 160, D), BF16)
    own_query = ((1, SLOT, 768), BF16)


def fields(kind):
    return [name for name in vars(kind) if not name.startswith("_")]


def buffers(kind):
    return [getattr(kind, name) for name in fields(kind)]


def masks(col, row, cut):
    return (col[cut, 0:1] == row[0:1]) & (row[1:2] <= col[cut, 1:2])


def sort_columns(rows):
    column = lax.broadcasted_iota(jnp.int32, (768, 768), 1)
    row = lax.broadcasted_iota(jnp.int32, (768, 768), 0)
    wide = (column // 128) * 192 + lax.rem(column, 128)
    late = column - 512
    narrow = (lax.rem(late, 128) // 32) * 192 + 128 + (late // 128) * 32 + lax.rem(late, 32)
    return jnp.where(row == jnp.where(column < 512, wide, narrow), 1.0, 0.0).astype(BF16)


def front_kernel(
    width,
    count_ref,
    pack_ref,
    keyval_ref,
    output_ref,
    expert_in,
    expert_out,
    shared_in,
    shared_out,
    res_ref,
    grad_ref,
    query_ref,
    segment_row,
    table_ref,
    slot_gates,
    frequency_ref,
    grad_pair,
    gates_over,
    *rest,
):
    n_units = 3
    lows, highs = rest[:n_units], rest[n_units : 2 * n_units]
    rest = rest[2 * n_units :]
    kept, names = fields(Kept), fields(Kept) + fields(Landing)
    outs = types.SimpleNamespace(**dict(zip(kept, rest)))
    rest = rest[len(kept) :]
    at = types.SimpleNamespace(**dict(zip(names, rest)))
    send_sems, recv_sems, local_sems = rest[len(names) :]
    copies = Copies(send_sems, recv_sems, local_sems)
    places = Places()
    copies.greet((0, 1, 2))
    saved = []

    def save(pick):
        for source, target in zip(pick(at), pick(outs)):
            saved.append(copies.local(source, target))

    pack = SlotGather(copies, pack_ref, at.pack.at[0], FAR_FIRST)
    keyval = SlotGather(copies, keyval_ref, at.keyval, FAR_FIRST)
    part = query_ref.shape[0] // 4
    queries = [
        SlotGather(copies, at.own_query, at.query, FAR_FIRST, cut=(k * part, part)) for k in range(4)
    ]
    part = output_ref.shape[1] // 2
    outputs = [SlotGather(copies, output_ref, at.output, FAR_FIRST, cut=(k * part, part)) for k in range(2)]
    pack.start()
    keyval.start()
    for k in range(8):
        block = pl.ds(pl.multiple_of(places[k] * SLOT, SLOT), SLOT)
        at.res[:, lanes(k)] = res_ref[:, block]
        at.grad[:, lanes(k)] = grad_ref[:, block]
    at.tokens[0] = at.res[...]
    tokens = SlotGather(copies, None, at.tokens, TENSOR_BITS, TENSOR)
    tokens.start()
    at.own_query[0] = nn(query_ref[...], sort_columns(768)).astype(BF16)
    items = [pack, keyval, *queries, *outputs]
    units = [(p, part) for p in range(n_units) for part in range(CHUNKS)]
    flights = [None] * len(units)
    owns = [None] * len(units)
    state = [0, 0, 0]

    def unit_source(side, p, part):
        if p < 2:
            expert = pl.ds(side * 2 + p, 1)
            return expert_out.at[expert] if part == 2 else expert_in.at[expert, part]
        cut = pl.ds(pl.multiple_of(side * width, 16), width)
        return shared_out.at[pl.ds(0, 1), cut] if part == 2 else shared_in.at[pl.ds(part, 1), cut]

    def unit_first():
        i = state[0]
        if i >= len(units):
            return
        p, part = units[i]
        cut = pl.ds(part * width, width)
        side = places[12]
        owns[i] = copies.local(unit_source(side, p, part), lows[p].at[pl.ds(0, 1), cut])
        flights[i] = copies.start(
            unit_source(1 - side, p, part), lows[p].at[pl.ds(1, 1), cut], DP, FLIPS[0]
        )
        state[0] = i + 1

    def unit_second():
        i = state[1]
        if i >= min(state[0], SECONDS):
            return
        p, part = units[i]
        cut = pl.ds(part * width, width)
        flights[i].wait()
        owns[i].wait()
        flights[i] = copies.start(
            lows[p].at[pl.ds(0, 2), cut], lows[p].at[pl.ds(2, 2), cut], DP, FLIPS[1]
        )
        state[1] = i + 1

    def unit_third():
        i = state[2]
        if i >= min(state[1], THIRDS):
            return
        p, part = units[i]
        cut = pl.ds(part * width, width)
        flights[i].wait()
        flights[i] = copies.start(lows[p].at[pl.ds(0, 4), cut], highs[p].at[pl.ds(0, 4), cut], DP, FLIPS[2])
        state[2] = i + 1

    def pump():
        unit_third()
        unit_second()
        unit_first()

    def place_tokens():
        segments = segment_row[...].astype(F32)
        at.col[:, 0:8] = jnp.broadcast_to(segments, (8, TOK)).T
        for b in range(4):
            start = pl.multiple_of(places[8 + b] * 160, 8)
            at.cos[b * 160 : (b + 1) * 160] = jnp.broadcast_to(at.col[pl.ds(start, 160), 0:1], (160, 128))
        for b in range(4):
            start = pl.multiple_of(places[8 + b] * 160, 8)
            cut = slice(b * 160, (b + 1) * 160)
            segment = at.cos[cut, 0:1]
            token = start + lax.broadcasted_iota(jnp.int32, (160, 128), 0)
            lane = lax.broadcasted_iota(jnp.int32, (160, 128), 1)
            at.col[cut] = jnp.where(lane == 0, segment, token.astype(F32))
            before = jnp.sum((segments < segment).astype(F32), axis=1, keepdims=True)
            angle = (token.astype(F32) - before) * frequency_ref[...]
            at.cos[cut] = jnp.cos(angle)
            at.sin[cut] = jnp.sin(angle)
        at.row[...] = at.col[...].T[0:8]
        at.valid[...] = (at.col[0:160, 1:2] < count_ref[0].astype(F32)).astype(F32) + jnp.zeros((160, 128), F32)
        at.masked[0] = (at.grad[...].astype(F32) * at.valid[:, 0:1]).astype(BF16)

    def route_tokens():
        slots = jnp.concatenate([table_ref[...].astype(F32), slot_gates[...]], axis=0).T
        token_row = at.row[1:2]
        for e in range(4):
            hit = jnp.where(slots[:, e : e + 1] == token_row, slots[:, 4 + e : 5 + e], 0.0)
            at.gates[e : e + 1] = jnp.sum(hit, axis=0, keepdims=True)
        at.gates[4:8] = jnp.zeros((4, TOK), F32)
        save(lambda v: (v.col, v.row, v.cos, v.sin, v.valid, v.res, v.grad, v.gates))

    def make_keys():
        for s in range(4):
            for k in range(8):
                start = pl.multiple_of(k * SLOT + places[8 + s] * 64, 64)
                at.w_latent[pl.ds(start, 64)] = at.pack[s, k]
                start = pl.multiple_of(places[k] * 64 + places[8 + s] * 16, 16)
                at.gain_rows[pl.ds(start, 16)] = at.pack[s, k, 0:16, KR : KR + 128]
        for k in range(8):
            at.w_keyval[pl.ds(pl.multiple_of(places[k] * 64, 64), 64)] = at.keyval[k]
        tail = at.w_latent[:, KR : KR + 128]
        turned = tail.astype(F32).T
        attn_gain = turned[64:65]
        at.gains[...] = turned[64:72]
        latent_gain = at.gain_rows[...].astype(F32).T[66:67]
        at.latent_gain[...] = jnp.broadcast_to(latent_gain, (8, KR))
        row = lax.broadcasted_iota(jnp.int32, (128, SLOT), 0)
        lane = lax.broadcasted_iota(jnp.int32, (128, SLOT), 1)
        spread = jnp.where(row == lax.rem(lane, 32) + 32 * (lane // 128), 1.0, 0.0).astype(BF16)
        w_rope = nn(tail, spread).astype(BF16)
        for b in range(4):
            cut = slice(b * 160, (b + 1) * 160)
            x = at.tokens[b].astype(F32)
            factor = lax.rsqrt(jnp.mean(x * x, axis=1, keepdims=True) + NORM_EPS)
            at.normed[cut] = (x * factor * attn_gain).astype(BF16)
        for b in range(2):
            cut = slice(b * 320, (b + 1) * 320)
            normed = at.normed[cut]
            latent_c = nn(normed, at.w_latent[:, :KR])
            factor = lax.rsqrt(jnp.mean(latent_c * latent_c, axis=1, keepdims=True) + NORM_EPS)
            latent_norm = (latent_c * factor * latent_gain).astype(BF16)
            if b == 0:
                at.latent_c[...] = latent_c[:160]
            at.latent_norm[cut] = latent_norm
            rope = nn(normed, w_rope)
            key_a, key_b = turn(rope[:, :128], rope[:, 128:], at.cos[cut], at.sin[cut])
            at.key_rope[cut] = jnp.concatenate([key_a, key_b], axis=1).astype(BF16)
            at.keyval_final[cut] = nn(latent_norm, at.w_keyval[...]).astype(BF16)
        save(lambda v: (v.w_latent, v.w_keyval, v.gains, v.latent_gain, v.normed, v.latent_c, v.latent_norm, v.key_rope, v.keyval_final,))


    unit_first()
    for tau in range(len(items) + 1):
        if tau >= 1:
            items[tau - 1].wait()
        if tau < len(items):
            items[tau].wait()
        if tau + 2 < len(items):
            items[tau + 2].start()
        if tau == 0:
            place_tokens()
        elif tau == 1:
            tokens.wait()
            grad_own = copies.local(at.masked, grad_pair.at[pl.ds(0, 1)])
            grad_x = copies.start(at.masked, grad_pair.at[pl.ds(2, 1)], TENSOR, 1)
        elif tau == 2:
            unit_first()
        elif tau == 3:
            pack.wait()
            pack_tensor = SlotGather(copies, None, at.pack, TENSOR_BITS, TENSOR)
            pack_tensor.start()
            unit_second()
        elif tau == 4:
            unit_first()
            route_tokens()
            gates_flight = copies.start(at.gates, gates_over, DP, 1)
        elif tau == 5:
            tokens.wait()
            unit_second()
        elif tau == 6:
            pack_tensor.wait()
            unit_first()
        elif tau == 7:
            keyval.wait()
            pack_tensor.wait()
            make_keys()
            unit_second()
    grad_x.wait()
    grad_z = copies.swapped(at.masked, grad_pair.at[pl.ds(1, 1)], 0, D)
    pump()
    for query in queries:
        query.wait()

    save(lambda v: (v.query,))
    gates_flight.wait()
    w_query = at.query[...].reshape(D, 768)
    scale = (HD + RD) ** (-0.5)
    for b in range(2):
        cut = slice(b * 320, (b + 1) * 320)
        found = nn(at.normed[cut], w_query)
        turned_a, turned_b = turn(found[:, 512:640], found[:, 640:768], at.cos[cut], at.sin[cut])
        at.query_final[cut] = jnp.concatenate([found[:, :512], turned_a, turned_b], axis=1).astype(BF16)
        allowed = masks(at.col, at.row, cut)
        lse_lane = lax.broadcasted_iota(jnp.int32, (320, 128), 1)
        lse_all = jnp.zeros((320, 128), F32)
        for h in range(4):
            rope = at.query_final[cut, 512:768]
            rope = jnp.where(head_lanes(320, h), rope, jnp.zeros_like(rope))
            keys = at.keyval_final[:, h * 256 : h * 256 + 128]
            scores = nt(at.query_final[cut, lanes(h, 128)], keys) + nt(rope, at.key_rope[...])
            scores = jnp.where(allowed, scores * scale, -1e30)
            top = jnp.max(scores, axis=1, keepdims=True)
            weight = jnp.exp(scores - top)
            total = jnp.sum(weight, axis=1, keepdims=True)
            probs = (weight / total).astype(BF16)
            lse_all = jnp.where(lse_lane == h, top + jnp.log(total), lse_all)
            mix = nn(probs, at.keyval_final[:, h * 256 + 128 : h * 256 + 256])
            at.mix[cut, lanes(h, 128)] = mix.astype(BF16)
        at.lse[cut] = lse_all
        if b == 0:
            pump()
            grad_z.wait()
            grad_zx = copies.start(
                grad_pair.at[pl.ds(1, 1)], grad_pair.at[pl.ds(3, 1)], TENSOR, 1
            )
    for output in outputs:
        output.wait()
    save(lambda v: (v.query_final, v.mix, v.lse, v.output,))
    for b in range(2):
        cut = slice((1 - b) * 320, (2 - b) * 320)
        for k in range(8):
            w_output = at.output[k]
            part = nn(at.mix[cut], w_output).astype(BF16)
            at.part[2 - 2 * b, :, lanes(k)] = part[:160]
            at.part[3 - 2 * b, :, lanes(k)] = part[160:]
        if b == 0:
            block = lambda ref, k: ref.at[pl.ds(k, 1)]
            c_far = copies.start(block(at.part, 3), block(at.got_c, 1), TENSOR, 0)
            c_near = copies.start(block(at.part, 2), block(at.got_c, 0), TENSOR, 0)
    c_far.wait()
    at.give_x[0] = (at.part[1].astype(F32) + at.got_c[1].astype(F32)).astype(BF16)
    x_far = copies.start(at.give_x, at.got_x, TENSOR, 1)
    grad_zx.wait()
    grad_own.wait()
    grad_c = copies.start(grad_pair.at[pl.ds(0, 4)], grad_pair.at[pl.ds(4, 4)], TENSOR, 0)
    pump()
    c_near.wait()
    x_far.wait()
    attn_out = at.part[0].astype(F32) + at.got_c[0].astype(F32) + at.got_x[0].astype(F32)
    mid = at.res[...].astype(F32) + at.valid[:, 0:1] * attn_out
    at.mid[...] = mid
    save(lambda v: (v.mid,))
    factor = lax.rsqrt(jnp.mean(mid * mid, axis=1, keepdims=True) + NORM_EPS)
    at.mid_pair[0] = (mid * factor * at.gains[1:2]).astype(BF16)
    spread_block(copies, at.mid_pair, pump)
    save(lambda v: (v.mid_pair,))
    grad_c.wait()
    while state[0] < len(units) or state[1] < SECONDS or state[2] < THIRDS:
        pump()
    for i in range(SECONDS, len(units)):
        owns[i].wait()
    for flight in flights:
        if flight is not None:
            flight.wait()
    for copy in saved:
        copy.wait()


def front(counts, pack, keyval, output, expert_in, expert_out, shared_in, shared_out, res, grad, query, segment, table, gates):
    n_units, width = 3, expert_out.shape[1]
    half = (4, 3 * width, SLOT)
    frequency = ROPE_BASE ** (-np.arange(RD // 2, dtype=np.float32) / np.float32(RD // 2))
    frequency = jnp.asarray(np.tile(frequency.astype(np.float32), 4)[None])
    operands = [
        counts,
        pack[None],
        keyval[None],
        output[None],
        expert_in.transpose(0, 1, 3, 2),
        expert_out,
        shared_in.transpose(0, 2, 1),
        shared_out[None],
        res,
        grad,
        query,
        segment,
        table,
        gates,
        frequency,
    ]
    shapes = [like((8, *res.shape)), like((8, TOK), F32)] + [like(half)] * (2 * n_units - 1) + [like((4, width, SLOT))]
    shapes += [like(*buffer) for buffer in buffers(Kept)]
    results = pl.pallas_call(
        functools.partial(front_kernel, width),
        out_shape=shapes,
        in_specs=[SMEM_SPEC] + [ANY_SPEC] * 7 + [VMEM_SPEC] * 7,
        out_specs=[ANY_SPEC] * len(shapes),
        scratch_shapes=[pltpu.VMEM(*buffer) for buffer in buffers(Kept) + buffers(Landing)]
        + [
            pltpu.SemaphoreType.DMA((80,)),
            pltpu.SemaphoreType.DMA((80,)),
            pltpu.SemaphoreType.DMA((48,)),
        ],
        compiler_params=pltpu.CompilerParams(
            collective_id=0, has_side_effects=True, vmem_limit_bytes=GIVEN_VMEM
        ),
        cost_estimate=cost(220),
        name="front",
    )(*operands)
    grad_pair, gates_over, results = results[0], results[1], results[2:]
    lows, results = results[:n_units], results[n_units:]
    highs, results = results[:n_units], results[n_units:]
    return grad_pair, gates_over, lows, highs, types.SimpleNamespace(**dict(zip(fields(Kept), results)))


TOKEN_BLOCK = 256


class Freight:
    def __init__(self, copies, bits, sources, targets):
        self.copies, self.bits, self.pairs = copies, bits, list(zip(sources, targets))
        self.flights = []

    def start(self):
        for bit, (source, target) in zip(self.bits, self.pairs):
            self.flights.append(self.copies.start(source, target, DP, bit))

    def wait(self):
        for flight in self.flights:
            flight.wait()


def experts_kernel(width, has_sum, bits, parts, *refs):
    refs = list(refs)
    take = lambda n: [refs.pop(0) for _ in range(n)]
    mid_ref, grad_ref, gate_ref = take(3)
    unit_refs = take(len(parts))
    if has_sum:
        back_in, out_in = take(2)
    sources = take(len(bits))
    back_ref, out_ref = take(2)
    keep_refs, give_refs = take(3), take(3)
    targets = take(len(bits))
    whole, total, send_sems, recv_sems = take(4)
    step = pl.program_id(0)
    copies = Copies(send_sems, recv_sems)

    def flights():
        return [
            pltpu.make_async_remote_copy(
                src_ref=cut.view(source),
                dst_ref=target,
                send_sem=send_sems.at[k],
                recv_sem=recv_sems.at[k],
                device_id=copies.across(DP, cut.bit),
                device_id_type=MESH,
            )
            for k, (cut, source, target) in enumerate(zip(bits, sources, targets))
        ]

    @pl.when(step == 0)
    def _():
        copies.greet(sorted({cut.bit for cut in bits}), ())
        for flight in flights():
            flight.start()
        for ref, (slot, count, start, size, skip) in zip(unit_refs, parts):
            for j in range(count):
                k = COLUMNS.index(UNIT_SLOTS[slot + j])
                whole[start : start + size, lanes(k)] = ref[j, skip : skip + size]
        total[...] = jnp.zeros_like(total)

    mid, grad = mid_ref[...], grad_ref[...]
    gate_up = nt(whole[: 2 * width], mid)
    hidden_grad = nt(whole[2 * width :], grad)
    gate = gate_up[:width]
    up = gate_up[width:]
    sigma = 1.0 / (1.0 + jnp.exp(-gate))
    silu = gate * sigma
    slope = sigma * (1.0 + gate * (1.0 - sigma))
    weight = gate_ref[...]
    hidden_grad = hidden_grad * weight
    hidden = (silu * up * weight).astype(BF16)
    pre = jnp.concatenate(
        [(hidden_grad * up * slope).astype(BF16), (hidden_grad * silu).astype(BF16)], axis=0
    )
    back = tn(pre, whole[: 2 * width])
    out = tn(hidden, whole[2 * width :])
    if has_sum:
        back = back + back_in[...]
        out = out + out_in[...]
    back_ref[...] = back.astype(back_ref.dtype)
    out_ref[...] = out.astype(out_ref.dtype)
    total[: 2 * width] += nn(pre, mid)
    total[2 * width :] += nn(hidden, grad)

    @pl.when(step == pl.num_programs(0) - 1)
    def _():
        for g in range(3):
            cut = slice(g * width, (g + 1) * width)
            for k in range(4):
                keep_refs[g][k] = total[cut, lanes((0, 2, 1, 3)[k])].astype(BF16)
                give_refs[g][k] = total[cut, lanes(4 + (0, 2, 1, 3)[k])].astype(BF16)
        for flight in flights():
            flight.wait()


class Cut:
    def __init__(self, array, bit, slots=None, rows=None):
        self.array, self.bit = array, bit
        self.slots = slots or (0, array.shape[0])
        self.rows = rows or (0, array.shape[1])

    def shape(self):
        return (self.slots[1], self.rows[1], self.array.shape[2])

    def view(self, ref):
        return ref.at[pl.ds(*self.slots), pl.ds(*self.rows)]


def experts_step(mid_pair, grad_pair, unit, gate, sums, last, freight, ident):
    tokens, block = mid_pair.shape[0], TOKEN_BLOCK
    width = unit[0][0].shape[1] // 3
    rows = pl.BlockSpec((block, D), lambda i: (i, 0))
    fixed = lambda *shape: pl.BlockSpec(shape, lambda i: (0,) * len(shape))
    kind = BF16 if last else F32
    part = (4, width, SLOT)
    operands = [mid_pair, grad_pair, gate[None]] + [part[0] for part in unit]
    specs = [rows, rows, pl.BlockSpec((1, block), lambda i: (0, i))]
    specs += [fixed(*part[0].shape) for part in unit]
    if sums is not None:
        operands += list(sums)
        specs += [rows, rows]
    results = pl.pallas_call(
        functools.partial(
            experts_kernel, width, sums is not None, tuple(freight), tuple(p[1:] for p in unit)
        ),
        grid=(tokens // block,),
        out_shape=[like((tokens, D), kind)] * 2
        + [like(part)] * 6
        + [like(cut.shape()) for cut in freight],
        in_specs=specs + [ANY_SPEC] * len(freight),
        out_specs=[rows, rows] + [fixed(*part)] * 6 + [ANY_SPEC] * len(freight),
        scratch_shapes=[
            pltpu.VMEM((3 * width, D), BF16),
            pltpu.VMEM((3 * width, D), F32),
            pltpu.SemaphoreType.DMA((len(freight),)),
            pltpu.SemaphoreType.DMA((len(freight),)),
        ],
        compiler_params=pltpu.CompilerParams(
            collective_id=ident, has_side_effects=True, vmem_limit_bytes=GIVEN_VMEM
        ),
        cost_estimate=cost(35),
        name="experts_step",
    )(*operands, *[cut.array for cut in freight])
    return list(results[:2]), list(results[2:5]), list(results[5:8]), list(results[8:])


def halve_kernel(count, *refs):
    keeps, gots, stays, gives = (refs[k * count : (k + 1) * count] for k in range(4))
    for keep, got, stay, give in zip(keeps, gots, stays, gives):
        half = stay.shape[0]
        for k in range(half):
            stay[k] = (keep[k].astype(F32) + got[k].astype(F32)).astype(BF16)
            give[k] = (keep[half + k].astype(F32) + got[half + k].astype(F32)).astype(BF16)


def halve(pairs):
    count = len(pairs)
    shapes = [like((keep.shape[0] // 2, *keep.shape[1:])) for keep, _ in pairs]
    results = pl.pallas_call(
        functools.partial(halve_kernel, count),
        out_shape=shapes * 2,
        in_specs=[VMEM_SPEC] * (2 * count),
        out_specs=[VMEM_SPEC] * (2 * count),
        cost_estimate=cost(3),
        name="halve",
    )(*[keep for keep, _ in pairs], *[got for _, got in pairs])
    return list(zip(results[:count], results[count:]))


class PairSum:
    def __init__(self, copies, blocks, got_c, give_a, give_b, got_a, got_b, end_a, end_b, last_a, last_b):
        self.copies, self.blocks, self.got_c = copies, blocks, got_c
        self.give_a, self.give_b, self.got_a, self.got_b = give_a, give_b, got_a, got_b
        self.end_a, self.end_b, self.last_a, self.last_b = end_a, end_b, last_a, last_b

    def both(self, k, first):
        cut = slice(first, first + 1024)
        return self.blocks[k, :, cut].astype(F32) + self.got_c[k, :, cut].astype(F32)

    def start(self):
        self.flights = {}
        for k in (3, 2, 1, 0):
            self.flights[k] = self.copies.start(
                self.blocks.at[pl.ds(4 + k, 1)], self.got_c.at[pl.ds(k, 1)], TENSOR, 0
            )

    def cross(self):
        self.flights[3].wait()
        self.give_a[1] = self.both(3, 0).astype(BF16)
        self.give_b[1] = self.both(3, 1024).astype(BF16)
        self.flights[2].wait()
        self.give_a[0] = self.both(2, 0).astype(BF16)
        self.across_a = self.copies.start(self.give_a, self.got_a, TENSOR, 1)
        self.flights[1].wait()
        self.give_b[0] = self.both(1, 1024).astype(BF16)
        self.across_b = self.copies.swapped(self.give_b, self.got_b, 0, 1024)
        self.flights[0].wait()

    def end(self):
        self.across_a.wait()
        self.end_a[0] = (self.both(1, 0) + self.got_a[1].astype(F32)).astype(BF16)
        self.ends_a = self.copies.swapped(self.end_a, self.last_a, 0, 1024)
        self.across_b.wait()
        self.end_b[0] = (self.both(2, 1024) + self.got_b[1].astype(F32)).astype(BF16)
        self.ends_b = self.copies.start(self.end_b, self.last_b, TENSOR, 1)

    def settle(self, total, end_a, end_b):
        self.across_a.wait()
        end_a[0] = (self.both(1, 0) + self.got_a[1].astype(F32)).astype(BF16)
        self.across_b.wait()
        end_b[0] = (self.both(2, 1024) + self.got_b[1].astype(F32)).astype(BF16)
        total[:, :1024] = self.both(0, 0) + self.got_a[0].astype(F32)
        total[:, 1024:] = self.both(0, 1024) + self.got_b[0].astype(F32)

    def total(self):
        self.ends_a.wait()
        self.ends_b.wait()
        return (
            self.both(0, 0) + self.got_a[0].astype(F32) + self.last_a[0].astype(F32),
            self.both(0, 1024) + self.got_b[0].astype(F32) + self.last_b[0].astype(F32),
        )


def sum_scratch():
    half = pltpu.VMEM((2, 160, 1024), BF16)
    end = pltpu.VMEM((1, 160, 1024), BF16)
    return [pltpu.VMEM((4, 160, D), BF16), half, half, half, half, end, end, end, end]


def back_kernel(bits, *refs):
    refs = list(refs)
    take = lambda n: [refs.pop(0) for _ in range(n)]
    back_ref, grad_ref, mid_ref, gains_ref, valid_ref = take(5)
    sources = take(len(bits))
    mid_grad_ref, gain_part_ref, tokens_ref = take(3)
    targets = take(len(bits))
    *buffers, send_sems, recv_sems = refs
    copies = Copies(send_sems, recv_sems)
    copies.greet((0, 1, 2))
    freight = Freight(copies, bits, sources, targets)
    freight.start()
    pair = PairSum(copies, back_ref, *buffers)
    pair.start()
    pair.cross()
    pair.end()
    first, second = pair.total()
    mid_grad_ref[:, :1024] = first
    mid_grad_ref[:, 1024:] = second
    grad, mid = mid_grad_ref[...], mid_ref[...]
    factor = lax.rsqrt(jnp.mean(mid * mid, axis=1, keepdims=True) + NORM_EPS)
    scaled = grad * gains_ref[1:2]
    inner = jnp.mean(scaled * mid, axis=1, keepdims=True)
    gain_part_ref[...] = jnp.broadcast_to(jnp.sum(grad * mid * factor, axis=0, keepdims=True), (8, D))
    mid_grad = grad_ref[...].astype(F32) + factor * (scaled - mid * factor * factor * inner)
    mid_grad_ref[...] = mid_grad
    tokens_ref[0] = (valid_ref[:, 0:1] * mid_grad).astype(BF16)
    own = tokens_ref.at[pl.ds(0, 1)]
    x_own = copies.start(own, tokens_ref.at[pl.ds(1, 1)], TENSOR, 1)
    c_own = copies.start(own, tokens_ref.at[pl.ds(2, 1)], TENSOR, 0)
    x_own.wait()
    c_far = copies.start(tokens_ref.at[pl.ds(1, 1)], tokens_ref.at[pl.ds(3, 1)], TENSOR, 0)
    c_own.wait()
    c_far.wait()
    freight.wait()


def back_tokens(back, grad_slots, mid, gains, valid, freight):
    rows = (160, D)
    bits = tuple(bit for bit, _ in freight)
    goods = [array for _, array in freight]
    results = pl.pallas_call(
        functools.partial(back_kernel, bits),
        out_shape=[like(rows, F32), like((8, D), F32), like((4, *rows))]
        + [like(g.shape, g.dtype) for g in goods],
        in_specs=[VMEM_SPEC] * 5 + [ANY_SPEC] * len(goods),
        out_specs=[VMEM_SPEC] * 3 + [ANY_SPEC] * len(goods),
        scratch_shapes=sum_scratch() + [pltpu.SemaphoreType.DMA((24,)), pltpu.SemaphoreType.DMA((24,))],
        compiler_params=pltpu.CompilerParams(
            collective_id=2, has_side_effects=True, vmem_limit_bytes=GIVEN_VMEM
        ),
        cost_estimate=cost(55),
        name="back_tokens",
    )(back, grad_slots, mid, gains, valid, *goods)
    return results[:3], list(results[3:])


def attention_backward_kernel(bits, *refs):
    refs = list(refs)
    take = lambda n: [refs.pop(0) for _ in range(n)]
    (
        grad_ref,
        output_ref,
        mix_ref,
        query_ref,
        keyval_ref,
        key_rope_ref,
        lse_ref,
        w_query_ref,
        w_keyval_ref,
        normed_ref,
        latent_norm_ref,
        col_ref,
        row_ref,
        cos_ref,
        sin_ref,
        out_ref,
    ) = take(16)
    sources = take(len(bits))
    output_wgrad, query_wgrad, keyval_wgrad, part_ref, out_sum, out_end_a, out_end_b = take(7)
    targets = take(len(bits))
    output_got = take(1)[0]
    mix_grad, query_grad, keyval_grad, key_grad, rope_grad, wide, send_sems, recv_sems = take(8)
    copies = Copies(send_sems, recv_sems)
    copies.greet((0, 1, 2))
    pair = PairSum(copies, out_ref, *refs, None, None, None, None)
    pair.start()
    freight = Freight(copies, bits, sources, targets)
    freight.start()
    places = Places()
    scale = (HD + RD) ** (-0.5)
    w_query = w_query_ref[...].reshape(D, w_query_ref.shape[2])
    for k in range(8):
        block = jnp.concatenate([grad_ref[b, :, lanes(k)] for b in range(4)], axis=0)
        s = k
        output_wgrad[s] = tn(mix_ref[...], block).astype(BF16)
        term = nt(block, output_ref[s])
        if k == 0:
            wide[:, :512] = term
        else:
            wide[:, :512] += term
    mix_grad[...] = wide[:, :512].astype(BF16)
    output_flight = copies.start(output_wgrad.at[pl.ds(4, 4)], output_got, DP, 0)
    pair.cross()
    for b in range(2):
        cut = slice(b * 320, (b + 1) * 320)
        allowed = masks(col_ref, row_ref, cut)
        lse_lane = lax.broadcasted_iota(jnp.int32, (320, 128), 1)
        rope_sum = jnp.zeros((320, SLOT), F32)
        for h in range(4):
            nope = query_ref[cut, lanes(h, 128)]
            rope = query_ref[cut, 512:768]
            mask = head_lanes(320, h)
            rope = jnp.where(mask, rope, jnp.zeros_like(rope))
            keys = keyval_ref[:, h * 256 : h * 256 + 128]
            values = keyval_ref[:, h * 256 + 128 : h * 256 + 256]
            scores = nt(nope, keys) + nt(rope, key_rope_ref[...])
            lse = jnp.sum(jnp.where(lse_lane == h, lse_ref[cut], 0.0), axis=1, keepdims=True)
            probs = jnp.where(allowed, jnp.exp(scores * scale - lse), 0.0)
            grad = mix_grad[cut, lanes(h, 128)]
            probs_grad = nt(grad, values)
            inner = jnp.sum(probs * probs_grad, axis=1, keepdims=True)
            scores_grad = (probs * (probs_grad - inner)).astype(BF16)
            value_grad = tn(probs.astype(BF16), grad)
            nope_grad = tn(scores_grad, nope) * scale
            rope_part = tn(scores_grad, rope)
            low, high = slice(h * 256, h * 256 + 128), slice(h * 256 + 128, h * 256 + 256)
            if b == 0:
                key_grad[:, low] = nope_grad
                key_grad[:, high] = value_grad
            else:
                key_grad[:, low] += nope_grad
                key_grad[:, high] += value_grad
            if b == 0 and h == 0:
                rope_grad[...] = rope_part
            else:
                rope_grad[...] += rope_part
            query_grad[cut, lanes(h, 128)] = (nn(scores_grad, keys) * scale).astype(BF16)
            rope_sum = rope_sum + jnp.where(mask, nn(scores_grad, key_rope_ref[...]), 0.0)
        rope_sum = rope_sum * scale
        back_a, back_b = turn(rope_sum[:, :128], rope_sum[:, 128:], cos_ref[cut], -sin_ref[cut])
        query_grad[cut, 512:640] = back_a.astype(BF16)
        query_grad[cut, 640:768] = back_b.astype(BF16)
    keyval_grad[...] = key_grad[...].astype(BF16)
    plain = nt(query_grad[...], sort_columns(768)).astype(BF16)
    for k in range(8):
        query_wgrad[k] = tn(normed_ref[:, lanes(k)], plain).astype(BF16)
    wide[:512, :] = tn(latent_norm_ref[...], keyval_grad[...])
    for k in range(8):
        start = pl.multiple_of(places[k] * 64, 64)
        keyval_wgrad[k] = wide[pl.ds(start, 64), :].astype(BF16)
    row = lax.broadcasted_iota(jnp.int32, (SLOT, 128), 0)
    lane = lax.broadcasted_iota(jnp.int32, (SLOT, 128), 1)
    fold = jnp.where(lane == lax.rem(row, 32) + 32 * (row // 128), scale, 0.0)
    for b in range(4):
        cut = slice(b * 160, (b + 1) * 160)
        for k in range(4):
            columns = lanes(k, 512)
            part_ref[b, :, columns] = nt(query_grad[cut], w_query[columns]).astype(BF16)
        part_ref[b, :, D : D + KR] = nt(keyval_grad[cut], w_keyval_ref[...]).astype(BF16)
        rope = lax.dot_general(
            rope_grad[cut],
            fold,
            (((1,), (0,)), ((), ())),
            precision=lax.Precision.HIGHEST,
            preferred_element_type=F32,
        )
        part_ref[b, :, D + KR :] = rope.astype(BF16)
    pair.settle(out_sum, out_end_a, out_end_b)
    output_flight.wait()
    freight.wait()


def attention_backward(grad, saved, out, freight):
    shapes = [like((8, 512, SLOT)), like((8, SLOT, 768)), like((8, 64, 1024)), like((4, 160, D + KR + 128))]
    shapes += [like((160, D), F32), like((1, 160, 1024)), like((1, 160, 1024))]
    bits = tuple(bit for bit, _ in freight)
    goods = [array for _, array in freight]
    kept = (saved.output, saved.mix, saved.query_final, saved.keyval_final, saved.key_rope, saved.lse, saved.query)
    kept += (saved.w_keyval, saved.normed, saved.latent_norm, saved.col, saved.row, saved.cos, saved.sin)
    results = pl.pallas_call(
        functools.partial(attention_backward_kernel, bits),
        out_shape=shapes + [like(g.shape) for g in goods] + [like((4, 512, SLOT))],
        in_specs=[VMEM_SPEC] * 16 + [ANY_SPEC] * len(goods),
        out_specs=[VMEM_SPEC] * len(shapes) + [ANY_SPEC] * (len(goods) + 1),
        scratch_shapes=[
            pltpu.VMEM((TOK, 512), BF16),
            pltpu.VMEM((TOK, 768), BF16),
            pltpu.VMEM((TOK, 1024), BF16),
            pltpu.VMEM((TOK, 1024), F32),
            pltpu.VMEM((TOK, SLOT), F32),
            pltpu.VMEM((TOK, 1024), F32),
            pltpu.SemaphoreType.DMA((32,)),
            pltpu.SemaphoreType.DMA((32,)),
            *sum_scratch()[:5],
        ],
        compiler_params=pltpu.CompilerParams(
            collective_id=4, has_side_effects=True, vmem_limit_bytes=GIVEN_VMEM
        ),
        cost_estimate=cost(30),
        name="attention_backward",
    )(grad, *kept, out, *goods)
    return results[:7], list(results[7:])


class SlotSum:
    def __init__(self, copies, values, bits, got, give, rows=None):
        self.copies, self.values, self.bits, self.got, self.give = copies, values, list(bits), got, give
        self.rows = rows or (0, values.shape[1])
        self.level = 0
        self.flying = None

    def view(self, ref, first, count):
        return ref.at[pl.ds(first, count), pl.ds(*self.rows)]

    def start(self):
        half = 4 >> self.level
        if self.level == 0:
            source = self.view(self.values, half, half)
        else:
            first, size = self.rows
            for k in range(half):
                self.give[self.level - 1][k, first : first + size] = self.total(half + k).astype(BF16)
            source = self.view(self.give[self.level - 1], 0, half)
        target = self.view(self.got[self.level], 0, half)
        self.flying = self.copies.start(source, target, DP, self.bits[self.level])
        self.level += 1

    def total(self, k):
        cut = slice(self.rows[0], self.rows[0] + self.rows[1])
        value = self.values[k, cut].astype(F32)
        for level in range(self.level):
            value = value + self.got[level][k, cut].astype(F32)
        return value

    def wait(self):
        self.flying.wait()
        if self.level < len(self.bits):
            self.start()


def slot_sum_scratch(shape):
    spaces = [pltpu.VMEM((n, *shape), BF16) for n in (4, 2, 1)]
    return spaces + [pltpu.VMEM((n, *shape), BF16) for n in (2, 1)]


def tail_kernel(
    n_rest,
    n_last,
    part_ref,
    output_wgrad,
    query_wgrad,
    keyval_wgrad,
    normed_ref,
    w_latent_ref,
    gains_ref,
    latent_gain_ref,
    latent_c_ref,
    res_ref,
    mid_grad_ref,
    ffn_gain_ref,
    output_came,
    mid_ref,
    valid_ref,
    out_sum,
    out_end_a,
    out_end_b,
    cos_ref,
    sin_ref,
    *refs,
):
    refs = list(refs)
    take = lambda n: [refs.pop(0) for _ in range(n)]
    rest_refs, stay_refs = take(n_rest), take(n_rest)
    last_refs = take(n_last)
    output_owned, query_owned, keyval_owned, latent_owned, res_grad_ref, res_out_ref = take(6)
    rest_cames, end_cames = take(n_rest), take(n_rest)
    last_cames = take(n_last)
    send_sems, recv_sems = take(2)
    sums = []
    copies = Copies(send_sems, recv_sems)
    for values, bits in (
        (query_wgrad, (0, 1, 2)),
        (keyval_wgrad, (0, 1, 2)),
        (output_wgrad, (0, 1, 2)),
    ):
        space = take(5)
        if values is query_wgrad:
            half = values.shape[1] // 2
            for k in range(2):
                sums.append(SlotSum(copies, values, bits, space[:3], space[3:], (k * half, half)))
        else:
            sums.append(SlotSum(copies, values, bits, space[:3], space[3:]))
    latent_values = take(1)[0]
    space = take(5)
    latent_sum = SlotSum(copies, latent_values, (0, 1, 2), space[:3], space[3:])
    got_c, give_x, got_x = take(3)
    latent_all, gain_rows, gain_c, gain_x, gain_columns, wide, end_one, end_two, end_sum, local_sems = take(10)
    copies.local_sems = local_sems
    copies.greet((0, 1, 2))
    last_a, last_b = take(2)
    out_ends = [copies.swapped(out_end_a, last_a, 0, 1024), copies.start(out_end_b, last_b, TENSOR, 1)]
    rests = [copies.start(a, b, DP, 2) for a, b in zip(rest_refs, rest_cames)]
    lasts = [copies.start(a, b, DP, 1) for a, b in zip(last_refs, last_cames)]
    stays = [copies.local(stay_refs[g].at[1], end_one.at[g]) for g in range(n_rest)]
    query_first, query_second, keyval_sum, output_sum = sums
    output_sum.got[0] = output_came
    output_sum.level = 1
    query_first.start()
    output_sum.start()
    c_far = copies.start(part_ref.at[pl.ds(3, 1)], got_c.at[pl.ds(1, 1)], TENSOR, 0)
    c_near = copies.start(part_ref.at[pl.ds(2, 1)], got_c.at[pl.ds(0, 1)], TENSOR, 0)
    c_far.wait()
    give_x[0] = (part_ref[1].astype(F32) + got_c[1].astype(F32)).astype(BF16)
    x_far = copies.start(give_x, got_x, TENSOR, 1)
    c_near.wait()
    query_first.wait()
    query_second.start()
    x_far.wait()

    def summed(columns):
        return (
            part_ref[0, :, columns].astype(F32)
            + got_c[0, :, columns].astype(F32)
            + got_x[0, :, columns].astype(F32)
        )

    latent_c = latent_c_ref[...]
    latent_gain = latent_gain_ref[0:1]
    factor = lax.rsqrt(jnp.mean(latent_c * latent_c, axis=1, keepdims=True) + NORM_EPS)
    grad = summed(slice(D, D + KR))
    scaled = grad * latent_gain
    inner = jnp.mean(scaled * latent_c, axis=1, keepdims=True)
    latent_back = factor * (scaled - latent_c * factor * factor * inner)
    latent_gain_part = jnp.sum(grad * latent_c * factor, axis=0, keepdims=True)
    rope = summed(slice(D + KR, D + KR + 128))
    cos, sin = cos_ref[...], sin_ref[...]
    lane = lax.broadcasted_iota(jnp.int32, rope.shape, 1)
    other = jnp.where(lane < 32, pltpu.roll(rope, 96, 1), pltpu.roll(rope, 32, 1))
    rope_back = jnp.where(lane < 32, rope * cos + other * sin, rope * cos - other * sin)
    rope_back = jnp.where(lane < RD, rope_back, 0.0)
    latent_all[0, :, :KR] = latent_back.astype(BF16)
    latent_all[0, :, KR:] = rope_back.astype(BF16)
    own = latent_all.at[pl.ds(0, 1)]
    l_x = copies.start(own, latent_all.at[pl.ds(1, 1)], TENSOR, 1)
    l_c = copies.start(own, latent_all.at[pl.ds(2, 1)], TENSOR, 0)
    res = res_ref[...].astype(F32)
    factor = lax.rsqrt(jnp.mean(res * res, axis=1, keepdims=True) + NORM_EPS)
    grad = summed(slice(0, D)) + nt(latent_all[0], w_latent_ref[...])
    scaled = grad * gains_ref[0:1]
    inner = jnp.mean(scaled * res, axis=1, keepdims=True)
    res_grad_ref[...] = mid_grad_ref[...] + factor * (scaled - res * factor * factor * inner)
    row = lax.broadcasted_iota(jnp.int32, (8, D), 0)
    attn_part = jnp.broadcast_to(jnp.sum(grad * res * factor, axis=0, keepdims=True), (8, D))
    gain_rows[0] = jnp.where(row == 0, attn_part, jnp.where(row == 1, ffn_gain_ref[...], 0.0))
    latent_row = jnp.broadcast_to(latent_gain_part, (8, KR))
    gain_rows[0, :, :KR] = jnp.where(
        lax.broadcasted_iota(jnp.int32, (8, KR), 0) == 2, latent_row, gain_rows[0, :, :KR]
    )
    g_c = copies.start(gain_rows, gain_c, TENSOR, 0)
    query_second.wait()
    keyval_sum.start()
    query_first.wait()
    l_x.wait()
    l_far = copies.start(latent_all.at[pl.ds(1, 1)], latent_all.at[pl.ds(3, 1)], TENSOR, 0)
    g_c.wait()
    gain_rows[0] = gain_rows[0] + gain_c[0]
    g_x = copies.start(gain_rows, gain_x, TENSOR, 1)
    l_c.wait()
    l_far.wait()
    g_x.wait()
    output_sum.wait()
    keyval_sum.wait()
    query_second.wait()
    gain_columns[:, 0:8] = (gain_rows[0] + gain_x[0]).T
    tensor = lax.axis_index(TENSOR)
    dp = lax.axis_index(DP)
    latent_rows = jnp.concatenate([latent_all[b] for b in range(4)], axis=0)
    for k in range(8):
        wide[...] = tn(normed_ref[:, lanes(k)], latent_rows)
        block = wide[pl.ds(pl.multiple_of(tensor * 64, 64), 64), :]
        start = pl.multiple_of(k * SLOT + tensor * 64, 64)
        columns = gain_columns[pl.ds(start, 64), 0:8]
        start = pl.multiple_of(crossed(dp, COLUMNS[k], 3) * 64 + tensor * 16, 16)
        latent_values[k] = block.astype(BF16)
        lane = lax.broadcasted_iota(jnp.int32, (64, 128), 1)
        ends = block[:, KR : KR + 128]
        ends = jnp.where(lane == 64, columns[:, 0:1], ends)
        ends = jnp.where(lane == 65, columns[:, 1:2], ends)
        latent_values[k, :, KR:] = ends.astype(BF16)
        corner = gain_columns[pl.ds(start, 16), 0:8][:, 2:3]
        lane = lax.broadcasted_iota(jnp.int32, (16, 128), 1)
        latent_values[k, 0:16, KR:] = jnp.where(lane == 66, corner, ends[0:16]).astype(BF16)
    latent_sum.start()
    ends = []
    for g in range(n_rest):
        rests[g].wait()
        stays[g].wait()
        comes = copies.local(rest_cames[g].at[1], end_two.at[g])
        comes.wait()
        end_sum[g] = (end_one[g].astype(F32) + end_two[g].astype(F32)).astype(BF16)
        ends.append(copies.start(end_sum.at[pl.ds(g, 1)], end_cames[g], DP, 1))
    keyval_sum.wait()
    output_sum.wait()
    output_owned[...] = output_sum.total(0)
    latent_sum.wait()
    for flight in out_ends:
        flight.wait()
    valid = valid_ref[:, 0:1]
    res_out_ref[:, :1024] = (mid_ref[:, :1024] + valid * (out_sum[:, :1024] + last_a[0].astype(F32))).astype(BF16)
    res_out_ref[:, 1024:] = (mid_ref[:, 1024:] + valid * (out_sum[:, 1024:] + last_b[0].astype(F32))).astype(BF16)
    latent_sum.wait()
    half = query_owned.shape[0] // 2
    query_first.wait()
    query_owned[:half] = query_first.total(0)
    keyval_sum.wait()
    keyval_owned[...] = keyval_sum.total(0)
    query_second.wait()
    query_owned[half:] = query_second.total(0)
    latent_sum.wait()
    latent_owned[...] = latent_sum.total(0)
    for copy in lasts + ends:
        copy.wait()


def tail(part, wgrads, output_came, out_parts, saved, mid_grad, ffn_gain, rests, stays, lasts):
    output_wgrad, query_wgrad, keyval_wgrad = wgrads
    rows = (160, D)
    latent = (64, KR + 128)
    shapes = [
        like((512, SLOT), F32),
        like((SLOT, 768), F32),
        like((64, 1024), F32),
        like(latent, F32),
        like(rows, F32),
        like(rows),
    ]
    part_row = (160, D + KR + 128)
    unit = rests[0].shape[1:]
    rows_spec = pl.BlockSpec((160, 128), lambda i: (0, 0))
    results = pl.pallas_call(
        functools.partial(tail_kernel, len(rests), len(lasts)),
        out_shape=shapes + [like((2, *unit))] * len(rests) + [like((1, *unit))] * (len(rests) + len(lasts)),
        grid=(1,),
        in_specs=[VMEM_SPEC] * 18 + [rows_spec] * 2 + [ANY_SPEC] * (2 * len(rests) + len(lasts)),
        out_specs=[VMEM_SPEC] * len(shapes) + [ANY_SPEC] * (2 * len(rests) + len(lasts)),
        scratch_shapes=[
            pltpu.SemaphoreType.DMA((40,)),
            pltpu.SemaphoreType.DMA((40,)),
            *slot_sum_scratch((SLOT, 768)),
            *slot_sum_scratch((64, 1024)),
            *slot_sum_scratch((512, SLOT)),
            pltpu.VMEM((8, *latent), BF16),
            *slot_sum_scratch(latent),
            pltpu.VMEM((2, *part_row), BF16),
            pltpu.VMEM((1, *part_row), BF16),
            pltpu.VMEM((1, *part_row), BF16),
            pltpu.VMEM((4, 160, KR + 128), BF16),
            pltpu.VMEM((1, 8, D), F32),
            pltpu.VMEM((1, 8, D), F32),
            pltpu.VMEM((1, 8, D), F32),
            pltpu.VMEM((D, 128), F32),
            pltpu.VMEM((SLOT, KR + 128), F32),
            pltpu.VMEM((3, *unit), BF16),
            pltpu.VMEM((3, *unit), BF16),
            pltpu.VMEM((3, *unit), BF16),
            pltpu.SemaphoreType.DMA((8,)),
            pltpu.VMEM((1, 160, 1024), BF16),
            pltpu.VMEM((1, 160, 1024), BF16),
        ],
        compiler_params=pltpu.CompilerParams(
            collective_id=3, has_side_effects=True, vmem_limit_bytes=GIVEN_VMEM
        ),
        cost_estimate=cost(110),
        name="tail",
    )(
        part,
        output_wgrad,
        query_wgrad,
        keyval_wgrad,
        saved.normed,
        saved.w_latent,
        saved.gains,
        saved.latent_gain,
        saved.latent_c,
        saved.res,
        mid_grad,
        ffn_gain,
        output_came,
        saved.mid,
        saved.valid,
        *out_parts,
        saved.cos,
        saved.sin,
        *rests,
        *stays,
        *lasts,
    )
    n = len(rests)
    return results[:6], results[6 : 6 + n], results[6 + n : 6 + 2 * n], results[6 + 2 * n :]


def finish_kernel(
    n_came,
    places,
    res_out_ref,
    res_grad_ref,
    latent_ref,
    *refs,
):
    refs = list(refs)
    take = lambda n: [refs.pop(0) for _ in range(n)]
    stays, cames, others = take(9), take(n_came), take(9)
    res_out, res_grad, latent, gains, expert_in, expert_out, shared_in, shared_out = refs
    for k in range(8):
        block = pl.ds(pl.multiple_of(places[k] * SLOT, SLOT), SLOT)
        res_out[:, block] = res_out_ref[:, lanes(k)]
        res_grad[:, block] = res_grad_ref[:, lanes(k)]
    latent[...] = latent_ref[:, : KR + RD]
    gains[...] = latent_ref[:, KR : KR + 128].T[64:72]
    side = places[8]
    n_half = expert_in.shape[0] // 2
    width = expert_out.shape[1]
    for p in range(n_half + 1):
        for mine in (True, False):
            which = side if mine else 1 - side
            for g in range(3):
                value = (stays if mine else others)[3 * p + g][0].astype(F32)
                late = 3 * p + g - 9 + n_came
                if mine and late >= 0:
                    value = value + cames[late][0].astype(F32)
                if p < n_half and g < 2:
                    expert_in[which * n_half + p, g] = value
                elif p < n_half:
                    expert_out[which * n_half + p] = value
                else:
                    cut = pl.ds(pl.multiple_of(which * width, 8), width)
                    if g < 2:
                        shared_in[g, cut] = value
                    else:
                        shared_out[cut] = value


def finish(places, res_out, res_grad, latent, stays, cames, others, width):
    shapes = [
        like(res_out.shape),
        like(res_grad.shape, F32),
        like((64, KR + RD), F32),
        like((8, 64), F32),
        like((EXPERTS, 2, width, SLOT), F32),
        like((EXPERTS, width, SLOT), F32),
        like((2, 2 * width, SLOT), F32),
        like((2 * width, SLOT), F32),
    ]
    return pl.pallas_call(
        functools.partial(finish_kernel, len(cames)),
        out_shape=shapes,
        in_specs=[SMEM_SPEC] + [VMEM_SPEC] * (21 + len(cames)),
        out_specs=[VMEM_SPEC] * len(shapes),
        compiler_params=pltpu.CompilerParams(vmem_limit_bytes=GIVEN_VMEM),
        cost_estimate=cost(10),
        name="finish",
    )(places, res_out, res_grad, latent, *stays, *cames, *others)


def body(
    res_in,
    out_grad,
    seg_ids,
    tok_counts,
    slot_table,
    slot_gates,
    attn_gain,
    latent_gain,
    ffn_gain,
    w_latent,
    w_query,
    w_keyval,
    w_output,
    w_expert_in,
    w_expert_out,
    w_shared_in,
    w_shared_out,
):
    dp = lax.axis_index(DP)
    rows = res_in.shape[0]
    first = ((dp >> 1) & 1) == 0
    n_half = EXPERTS // 2
    width = w_expert_out.shape[1]
    pack = jnp.concatenate(
        [
            w_latent,
            attn_gain[:, None],
            ffn_gain[:, None],
            jnp.pad(latent_gain, (0, w_latent.shape[0] - latent_gain.shape[0]))[:, None],
            jnp.zeros((w_latent.shape[0], 61), BF16),
        ],
        axis=1,
    )
    grad_pair, over_gate, lows, highs, saved = front(
        tok_counts,
        pack,
        w_keyval,
        w_output,
        w_expert_in,
        w_expert_out,
        w_shared_in,
        w_shared_out,
        res_in,
        out_grad,
        w_query,
        seg_ids,
        slot_table[0],
        slot_gates[0],
    )
    pair_gate = jnp.concatenate(
        [g[:, k * rows : (k + 1) * rows] for k in range(4) for g in (saved.gates, over_gate)], axis=1
    )
    pair_gate = jnp.where(first, pair_gate[:n_half], pair_gate[n_half : 2 * n_half])
    mid_pair = saved.mid_pair.reshape(-1, D)
    grad_pair = grad_pair.reshape(-1, D)
    ones = jnp.ones_like(pair_gate[0])
    whole = 3 * width
    low, high = lows[2], highs[2]
    sums, keep0, give0, (high_far,) = experts_step(
        mid_pair,
        grad_pair,
        [(lows[0], 0, 4, 0, whole, 0), (highs[0], 4, 4, 0, whole, 0)],
        pair_gate[0],
        None,
        False,
        [Cut(low, 0, (0, 4), (width, whole - width))],
        5,
    )
    sums, keep1, give1, (y0a, y0b) = experts_step(
        mid_pair,
        grad_pair,
        [(lows[1], 0, 4, 0, whole, 0), (highs[1], 4, 4, 0, whole, 0)],
        pair_gate[1],
        sums,
        False,
        [Cut(give0[0], 0), Cut(give0[1], 0)],
        6,
    )
    (k0a, h0a), (k0b, h0b) = halve([(keep0[0], y0a), (keep0[1], y0b)])
    (back, out), keep2, give2, (y0c, y1a, z0a, z0b) = experts_step(
        mid_pair,
        grad_pair,
        [
            (low, 0, 4, 0, whole, 0),
            (high, 4, 4, 0, width, 0),
            (high_far, 4, 4, width, whole - width, 0),
        ],
        ones,
        sums,
        True,
        [Cut(give0[2], 0), Cut(give1[0], 0), Cut(h0a, 2), Cut(h0b, 2)],
        7,
    )
    (k0c, h0c), (k1a, h1a), (s0a, m0a), (s0b, m0b) = halve(
        [(keep0[2], y0c), (keep1[0], y1a), (k0a, z0a), (k0b, z0b)]
    )
    back = back.reshape(8, rows, D)
    out = out.reshape(8, rows, D)
    (mid_grad, ffn_gain_part, attn_grad), (y1b, y1c, y2a, y2b, z0c, z1a, o0a, o0b) = back_tokens(
        back,
        saved.grad,
        saved.mid,
        saved.gains,
        saved.valid,
        [(0, give1[1]), (0, give1[2]), (0, give2[0]), (0, give2[1]), (2, h0c), (2, h1a), (1, m0a), (1, m0b)],
    )
    (k1b, h1b), (k1c, h1c), (k2a, h2a), (k2b, h2b), (s0c, m0c), (s1a, m1a) = halve(
        [(keep1[1], y1b), (keep1[2], y1c), (keep2[0], y2a), (keep2[1], y2b), (k0c, z0c), (k1a, z1a)]
    )
    (*wgrads, back_part, out_sum, out_a, out_b), (y2c, z1b, z1c, z2a, o0c, o1a, output_came) = attention_backward(
        attn_grad,
        saved,
        out,
        [(0, give2[2]), (2, h1b), (2, h1c), (2, h2a), (1, m0c), (1, m1a)],
    )
    (k2c, h2c), (s1b, m1b), (s1c, m1c), (s2a, m2a) = halve(
        [(keep2[2], y2c), (k1b, z1b), (k1c, z1c), (k2a, z2a)]
    )
    (output_owned, query_owned, keyval_owned, latent_owned, res_grad, res_out), cames, ends, (o1b, o1c, o2a) = tail(
        back_part,
        wgrads,
        output_came,
        (out_sum, out_a, out_b),
        saved,
        mid_grad,
        ffn_gain_part,
        [h2b, h2c],
        [k2b, k2c],
        [m1b, m1c, m2a],
    )
    places = jnp.concatenate([dp ^ jnp.array(COLUMNS, jnp.int32), ((dp >> 1) & 1)[None]])
    res_out, res_grad, latent_owned, gains, expert_in, expert_out, shared_in, shared_out = finish(
        places,
        res_out,
        res_grad,
        latent_owned,
        [s0a, s0b, s0c, s1a, s1b, s1c, s2a, k2b, k2c],
        cames,
        [o0a, o0b, o0c, o1a, o1b, o1c, o2a, *ends],
        width,
    )
    return (
        res_out,
        res_grad,
        gains[0],
        gains[2, : KR // 32],
        gains[1],
        latent_owned,
        query_owned,
        keyval_owned,
        output_owned,
        expert_in.transpose(0, 1, 3, 2),
        expert_out,
        shared_in.transpose(0, 2, 1),
        shared_out,
    )


def solution(mesh):
    placed = (
        P((DP, TENSOR), None),
        P((DP, TENSOR), None),
        P(DP, None),
        P(DP),
        P(DP, None, None),
        P(DP, None, None),
        P((DP, TENSOR)),
        P((DP, TENSOR)),
        P((DP, TENSOR)),
        P((DP, TENSOR), None),
        P(DP, TENSOR),
        P(DP, TENSOR),
        P(TENSOR, DP),
        P(None, None, DP, TENSOR),
        P(None, TENSOR, DP),
        P(None, DP, TENSOR),
        P(TENSOR, DP),
    )
    fits = mesh.shape[DP] == 8 and mesh.shape[TENSOR] == 4
    return jax.shard_map(
        body if fits else general_body,
        mesh=mesh,
        in_specs=placed,
        out_specs=(
            P((DP, TENSOR), None),
            P((DP, TENSOR), None),
            P((DP, TENSOR)),
            P((DP, TENSOR)),
            P((DP, TENSOR)),
            P((DP, TENSOR), None),
            P(DP, TENSOR),
            P(DP, TENSOR),
            P(TENSOR, DP),
            P(None, None, DP, TENSOR),
            P(None, TENSOR, DP),
            P(None, DP, TENSOR),
            P(TENSOR, DP),
        ),
        check_vma=False,
    )
```

```python
import functools
import types

import jax
import jax.numpy as jnp
import numpy as np
from jax import lax
from jax.experimental import pallas as pl
from jax.experimental.pallas import tpu as pltpu
from jax.sharding import PartitionSpec as P

D = 2048
H = 16
HD = 128
RD = 64
VD = 128
KR = 512
TOK = 640
EXPERTS = 4


NORM_EPS = 1e-06
ROPE_BASE = 50000.0


def rms_factor(values):
    return lax.rsqrt(jnp.mean(values * values, axis=-1, keepdims=True) + NORM_EPS)


def norm_back(grad_out, values, factor, gain_vec):
    scaled = grad_out * gain_vec
    inner_sum = jnp.mean(scaled * values, axis=-1, keepdims=True)
    return (
        factor * (scaled - values * factor * factor * inner_sum),
        jnp.sum(grad_out * values * factor, axis=0),
    )


def rotary_tables(positions):
    half_width = RD // 2
    inv_freq = ROPE_BASE ** (-jnp.arange(half_width, dtype=jnp.float32) / half_width)
    angles = positions.astype(jnp.float32)[:, None] * inv_freq[None, :]
    return (jnp.cos(angles), jnp.sin(angles))


def rotate(values, cosine_table, sine_table):
    half_width = values.shape[-1] // 2
    first_half = values[..., :half_width]
    second_half = values[..., half_width:]
    return jnp.concatenate(
        [
            first_half * cosine_table - second_half * sine_table,
            second_half * cosine_table + first_half * sine_table,
        ],
        axis=-1,
    )


def silu_parts(gate_pre):
    sigma_gate = jax.nn.sigmoid(gate_pre)
    return (gate_pre * sigma_gate, sigma_gate * (1.0 + gate_pre * (1.0 - sigma_gate)))


def flip_pairs(count, bit):
    return [(i, i ^ (1 << bit)) for i in range(count)]


def swap_dp(values, bit):
    return lax.ppermute(values, DP, flip_pairs(lax.axis_size(DP), bit))


def swap_tensor(values, bit):
    return lax.ppermute(values, TENSOR, flip_pairs(lax.axis_size(TENSOR), bit))


def dp_bits():
    top = lax.axis_size(DP).bit_length() - 1
    return [1] + list(range(top - 1, 1, -1)) + [0]


def slot_order(bits):
    order = [0]
    for bit in bits:
        order = order + [j ^ (1 << bit) for j in order]
    return order


def select_blocks(blocks, index):
    step = 1
    while step < len(blocks):
        hit = (index & step) != 0
        blocks = [jnp.where(hit, blocks[i ^ step], blocks[i]) for i in range(len(blocks))]
        step *= 2
    return blocks


def to_slots(values, index, bits, axis):
    count = 1 << len(bits)
    blocks = select_blocks(jnp.split(values, count, axis=axis), index)
    return jnp.concatenate([blocks[j] for j in slot_order(bits)], axis=axis)


def from_slots(values, index, bits, axis):
    order = slot_order(bits)
    slots = jnp.split(values, len(order), axis=axis)
    blocks = [slots[order.index(i)] for i in range(len(order))]
    return jnp.concatenate(select_blocks(blocks, index), axis=axis)


def gather_dp(values, bits):
    for bit in bits:
        values = jnp.concatenate([values, swap_dp(values, bit)], axis=0)
    return values


def gather_tensor(values):
    for bit in (1, 0):
        values = jnp.concatenate([values, swap_tensor(values, bit)], axis=0)
    return values


def scatter_dp(values, bits, axis):
    values = values.astype(jnp.float32)
    for bit in reversed(bits):
        keep, give = jnp.split(values, 2, axis=axis)
        values = keep + swap_dp(give.astype(jnp.bfloat16), bit).astype(jnp.float32)
    return values


def scatter_tensor(values):
    for bit in (0, 1):
        keep, give = jnp.split(values, 2, axis=0)
        values = keep + swap_tensor(give.astype(jnp.bfloat16), bit).astype(jnp.float32)
    return values


def partner_columns(values):
    count = lax.axis_size(DP)
    slots = jnp.split(values, count, axis=-1)
    return jnp.concatenate([slots[k ^ 1] for k in range(count)], axis=-1)


def gather_pair(values, bit):
    over = swap_dp(partner_columns(values), bit)
    own = jnp.concatenate([values, over, swap_tensor(values, 1), swap_tensor(over, 1)], axis=0)
    return jnp.concatenate([own, swap_tensor(own, 0)], axis=0)


def scatter_pair(values, bit):
    values = scatter_tensor(values)
    keep, give = jnp.split(values, 2, axis=0)
    return keep + swap_dp(partner_columns(give).astype(jnp.bfloat16), bit).astype(jnp.float32)


def dot(a, b, contract):
    return lax.dot_general(a, b, (contract, ((), ())), preferred_element_type=jnp.float32)


def general_body(
    res_in,
    out_grad,
    seg_ids,
    tok_counts,
    slot_table,
    slot_gates,
    attn_gain,
    latent_gain,
    ffn_gain,
    w_latent,
    w_query,
    w_keyval,
    w_output,
    w_expert_in,
    w_expert_out,
    w_shared_in,
    w_shared_out,
):
    f32 = jnp.float32
    bf16 = jnp.bfloat16
    n_tensor = lax.axis_size(TENSOR)
    n_dp = lax.axis_size(DP)
    dp = lax.axis_index(DP)
    tensor = lax.axis_index(TENSOR)
    bits = dp_bits()
    merge = bits[0]
    half = (dp >> merge) & 1
    rows = res_in.shape[0]
    local_heads = H // n_tensor
    score_scale = (HD + RD) ** (-0.5)

    res_local = to_slots(res_in, dp, bits, 1)
    res_all = gather_tensor(res_local)
    tensor_slots = slot_order([1, 0])
    token_ids = jnp.concatenate(
        [(tensor ^ j) * rows + jnp.arange(rows, dtype=jnp.int32) for j in tensor_slots]
    )
    segment_canon = seg_ids[0]
    segment_row = jnp.concatenate(
        [lax.dynamic_slice_in_dim(segment_canon, (tensor ^ j) * rows, rows) for j in tensor_slots]
    )
    valid_all = (token_ids < tok_counts[0]).astype(f32)
    valid_rows = valid_all[:rows, None]
    group_gate = jnp.sum(
        jnp.where(slot_table[0][:, :, None] == token_ids[None, None, :], slot_gates[0][:, :, None], 0.0),
        axis=1,
    )
    grad_in = to_slots(out_grad, dp, bits, 1).astype(f32)
    ffn_grad = (valid_rows * grad_in).astype(bf16)

    pack_rows = w_latent.shape[0]
    gain_row = jnp.concatenate([attn_gain, ffn_gain, latent_gain])
    gain_row = jnp.pad(gain_row, (0, w_latent.shape[1] - gain_row.shape[0]))
    pack = jnp.concatenate([w_latent, jnp.broadcast_to(gain_row, (16, w_latent.shape[1]))], axis=0)
    pack = gather_dp(pack[None], bits)
    pack = gather_tensor(pack[None])
    pack_blocks = [pack[tensor_slots.index(j)] for j in range(n_tensor)]
    pack = jnp.stack(select_blocks(pack_blocks, tensor), axis=1)
    latent_full = pack[:, :, :pack_rows].reshape(D, KR + RD)
    gains = pack[:, :, pack_rows]
    gain_width, latent_width = D // (n_dp * n_tensor), KR // (n_dp * n_tensor)
    attn_gain_full = gains[..., :gain_width].reshape(D)
    ffn_gain_full = gains[..., gain_width : 2 * gain_width].reshape(D)
    latent_gain_full = from_slots(
        gains[..., 2 * gain_width : 2 * gain_width + latent_width].reshape(KR), dp, bits, 0
    )
    query_full = gather_dp(w_query, bits)
    keyval_full = from_slots(gather_dp(w_keyval, bits), dp, bits, 0)
    output_full = gather_dp(w_output[None], bits)
    output_full = jnp.concatenate([output_full[k] for k in range(n_dp)], axis=1)

    n_half = EXPERTS // 2
    expert_units = jnp.concatenate(
        [
            w_expert_in.transpose(0, 1, 3, 2).reshape(EXPERTS, -1, w_expert_in.shape[2]),
            w_expert_out,
        ],
        axis=1,
    )
    width = w_expert_out.shape[1]
    shared_t = w_shared_in.transpose(0, 2, 1)
    units = []
    for side in range(2):
        cut = slice(side * width, (side + 1) * width)
        shared_unit = jnp.concatenate([shared_t[0, cut], shared_t[1, cut], w_shared_out[cut]], axis=0)
        units.append(jnp.concatenate([expert_units[side * n_half : (side + 1) * n_half], shared_unit[None]], axis=0))
    first = half == 0
    own_units = jnp.where(first, units[0], units[1])
    other_units = jnp.where(first, units[1], units[0])
    pieces = []
    for p in range(n_half + 1):
        piece = jnp.stack([own_units[p], swap_dp(other_units[p], merge)], axis=0)
        piece = gather_dp(piece, bits[1:])
        pieces.append(jnp.concatenate([piece[k] for k in range(n_dp)], axis=1))

    positions = token_ids - jnp.sum(
        (segment_canon[None, :] < segment_row[:, None]).astype(jnp.int32), axis=1
    )
    cos_all, sin_all = rotary_tables(positions)
    allowed = (segment_row[:, None] == segment_row[None, :]) & (
        token_ids[None, :] <= token_ids[:, None]
    )
    resid_all = res_all.astype(f32)
    in_factor = rms_factor(resid_all)
    normed_all = (resid_all * in_factor * attn_gain_full).astype(bf16)
    latent_raw = jnp.dot(normed_all, latent_full, preferred_element_type=f32)
    latent_c = latent_raw[:, :KR]
    latent_factor = rms_factor(latent_c)
    latent_norm = (latent_c * latent_factor * latent_gain_full).astype(bf16)
    rope_all = rotate(latent_raw[:, KR:], cos_all, sin_all).astype(bf16)
    query_raw = jnp.dot(normed_all, query_full, preferred_element_type=f32).reshape(
        TOK, local_heads, HD + RD
    )
    query_final = jnp.concatenate(
        [
            query_raw[..., :HD],
            rotate(query_raw[..., HD:], cos_all[:, None, :], sin_all[:, None, :]),
        ],
        axis=-1,
    ).astype(bf16)
    keyval = (
        jnp.dot(latent_norm, keyval_full, preferred_element_type=f32)
        .astype(bf16)
        .reshape(TOK, local_heads, HD + VD)
    )
    key_nope = keyval[..., :HD]
    values_all = keyval[..., HD:]
    raw_scores = jnp.einsum(
        "qhd,khd->hqk", query_final[..., :HD], key_nope, preferred_element_type=f32
    )
    raw_scores = raw_scores + jnp.einsum(
        "qhr,kr->hqk", query_final[..., HD:], rope_all, preferred_element_type=f32
    )
    scores = jnp.where(allowed[None], raw_scores * score_scale, -1e30)
    top_score = jnp.max(scores, axis=-1, keepdims=True)
    exp_scores = jnp.exp(scores - top_score)
    probs_all = exp_scores / jnp.sum(exp_scores, axis=-1, keepdims=True)
    probs_low = probs_all.astype(bf16)
    attn_mix = (
        jnp.einsum("hqk,khd->qhd", probs_low, values_all, preferred_element_type=f32)
        .astype(bf16)
        .reshape(TOK, local_heads * VD)
    )
    attn_part = jnp.dot(attn_mix, output_full, preferred_element_type=f32)
    attn_out = scatter_tensor(attn_part)
    resid_in = res_local.astype(f32)
    mid_resid = resid_in + valid_rows * attn_out
    mid_factor = rms_factor(mid_resid)
    normed_mid = (mid_resid * mid_factor * ffn_gain_full).astype(bf16)

    mid_pair = gather_pair(normed_mid, merge)
    grad_pair = gather_pair(ffn_grad, merge)
    other_gate = swap_dp(group_gate, merge)
    pair_gate = jnp.concatenate(
        [
            gate[:, k * rows : (k + 1) * rows]
            for k in ((0, 0), (1, 0), (0, 1), (1, 1), (0, 2), (1, 2), (0, 3), (1, 3))
            for gate, k in (((group_gate, other_gate)[k[0]], k[1]),)
        ],
        axis=1,
    )
    pair_gate = jnp.where(first, pair_gate[:n_half], pair_gate[n_half:])
    mid_pair_grad = None
    hidden_parts, out_parts, unit_grads = [], [], []
    for p, piece in enumerate(pieces):
        gate_up = dot(piece[: 2 * width], mid_pair, ((1,), (1,)))
        gate_pre, up = gate_up[:width], gate_up[width:]
        silu, slope = silu_parts(gate_pre)
        hidden_grad = dot(piece[2 * width :], grad_pair, ((1,), (1,)))
        hidden = silu * up
        if p < n_half:
            hidden = hidden * pair_gate[p][None]
            hidden_grad = hidden_grad * pair_gate[p][None]
        hidden = hidden.astype(bf16)
        pre_grad = jnp.concatenate(
            [(hidden_grad * up * slope).astype(bf16), (hidden_grad * silu).astype(bf16)], axis=0
        )
        back = dot(pre_grad, piece[: 2 * width], ((0,), (0,)))
        mid_pair_grad = back if mid_pair_grad is None else mid_pair_grad + back
        hidden_parts.append(hidden)
        out_parts.append(piece[2 * width :])
        in_wgrad = dot(pre_grad, mid_pair, ((1,), (0,)))
        out_wgrad = dot(hidden, grad_pair, ((1,), (0,)))
        unit_grads.append(jnp.concatenate([in_wgrad, out_wgrad], axis=0).astype(bf16))
    ffn_part = dot(
        jnp.concatenate(hidden_parts, axis=0), jnp.concatenate(out_parts, axis=0), ((0,), (0,))
    )
    ffn_out = scatter_pair(ffn_part, merge)
    res_out = (mid_resid + valid_rows * ffn_out).astype(bf16)
    mid_grad_local = scatter_pair(mid_pair_grad, merge)

    mid_back, ffn_gain_part = norm_back(mid_grad_local, mid_resid, mid_factor, ffn_gain_full)
    mid_grad = grad_in + mid_back
    attn_grad = (valid_rows * mid_grad).astype(bf16)
    attn_grad_all = gather_tensor(attn_grad)
    output_wgrad = dot(attn_mix, attn_grad_all, ((0,), (0,)))
    mix_grad = (
        dot(attn_grad_all, output_full, ((1,), (1,))).astype(bf16).reshape(TOK, local_heads, VD)
    )
    probs_grad = jnp.einsum("qhd,khd->hqk", mix_grad, values_all, preferred_element_type=f32)
    value_grad = jnp.einsum("hqk,qhd->khd", probs_low, mix_grad, preferred_element_type=f32)
    scores_grad = (
        probs_all * (probs_grad - jnp.sum(probs_all * probs_grad, axis=-1, keepdims=True))
    ).astype(bf16)
    query_nope_grad = (
        jnp.einsum("hqk,khd->qhd", scores_grad, key_nope, preferred_element_type=f32) * score_scale
    )
    query_rope_grad = (
        jnp.einsum("hqk,kr->qhr", scores_grad, rope_all, preferred_element_type=f32) * score_scale
    )
    key_nope_grad = (
        jnp.einsum("hqk,qhd->khd", scores_grad, query_final[..., :HD], preferred_element_type=f32)
        * score_scale
    )
    rope_key_grad = (
        jnp.einsum("hqk,qhr->kr", scores_grad, query_final[..., HD:], preferred_element_type=f32)
        * score_scale
    )
    query_grad = (
        jnp.concatenate(
            [query_nope_grad, rotate(query_rope_grad, cos_all[:, None, :], -sin_all[:, None, :])],
            axis=-1,
        )
        .astype(bf16)
        .reshape(TOK, local_heads * (HD + RD))
    )
    keyval_grad = (
        jnp.concatenate([key_nope_grad, value_grad], axis=-1)
        .astype(bf16)
        .reshape(TOK, local_heads * (HD + VD))
    )
    latent_part = jnp.concatenate([dot(keyval_grad, keyval_full, ((1,), (1,))), rope_key_grad], axis=1)
    latent_grad_local = scatter_tensor(latent_part)
    normed_part = dot(query_grad, query_full, ((1,), (1,)))
    normed_grad_local = scatter_tensor(normed_part)
    query_wgrad = dot(normed_all, query_grad, ((0,), (0,)))
    keyval_wgrad = to_slots(dot(latent_norm, keyval_grad, ((0,), (0,))).astype(bf16), dp, bits, 0)
    latent_c_grad, latent_gain_part = norm_back(
        latent_grad_local[:, :KR], latent_c[:rows], latent_factor[:rows], latent_gain_full
    )
    rope_raw_grad = rotate(latent_grad_local[:, KR:], cos_all[:rows], -sin_all[:rows])
    latent_raw_grad = jnp.concatenate([latent_c_grad, rope_raw_grad], axis=1).astype(bf16)
    latent_raw_grad_all = gather_tensor(latent_raw_grad)
    latent_wgrad = dot(normed_all, latent_raw_grad_all, ((0,), (0,))).astype(bf16)
    latent_wgrad = lax.dynamic_index_in_dim(
        latent_wgrad.reshape(n_dp, n_tensor, pack_rows, KR + RD), tensor, 1, keepdims=False
    )
    normed_grad = normed_grad_local + dot(latent_raw_grad, latent_full, ((1,), (1,)))
    in_back, attn_gain_part = norm_back(normed_grad, resid_in, in_factor[:rows], attn_gain_full)
    res_grad = mid_grad + in_back

    output_owned = scatter_dp(output_wgrad, bits, 1)
    query_owned = scatter_dp(query_wgrad, bits, 0)
    keyval_owned = scatter_dp(keyval_wgrad, bits, 0)
    latent_owned = scatter_dp(latent_wgrad, bits, 0)[0]
    gain_parts = jnp.concatenate(
        [
            attn_gain_part.reshape(n_dp, n_tensor, gain_width),
            ffn_gain_part.reshape(n_dp, n_tensor, gain_width),
            to_slots(latent_gain_part, dp, bits, 0).reshape(n_dp, n_tensor, latent_width),
        ],
        axis=2,
    )
    gain_parts = jnp.stack(
        [
            select_blocks([gain_parts[:, i] for i in range(n_tensor)], tensor)[j]
            for j in tensor_slots
        ],
        axis=0,
    )
    for bit in (0, 1):
        keep, give = jnp.split(gain_parts, 2, axis=0)
        gain_parts = keep + swap_tensor(give, bit)
    gain_parts = gain_parts[0]
    for bit in reversed(bits):
        keep, give = jnp.split(gain_parts, 2, axis=0)
        gain_parts = keep + swap_dp(give, bit)
    gain_owned = gain_parts[0]
    own_grads, other_grads = [], []
    for grad in unit_grads:
        grad = grad.astype(f32)
        for bit in reversed(bits[1:]):
            keep, give = jnp.split(grad, 2, axis=1)
            grad = keep + swap_dp(give.astype(bf16), bit).astype(f32)
        keep, give = jnp.split(grad, 2, axis=1)
        own_grads.append(keep)
        other_grads.append(swap_dp(give.astype(bf16), merge).astype(f32))
    sides = []
    for side in (first, ~first):
        sides.append([jnp.where(side, a, b) for a, b in zip(own_grads, other_grads)])
    expert_units = jnp.stack([unit for side in sides for unit in side[:n_half]], axis=0)
    expert_in_owned = expert_units[:, : 2 * width].reshape(EXPERTS, 2, width, -1).transpose(0, 1, 3, 2)
    expert_out_owned = expert_units[:, 2 * width :]
    shared_in_owned = jnp.stack(
        [
            jnp.concatenate([side[n_half][k * width : (k + 1) * width] for side in sides], axis=0).T
            for k in range(2)
        ],
        axis=0,
    )
    shared_out_owned = jnp.concatenate([side[n_half][2 * width :] for side in sides], axis=0)
    return (
        from_slots(res_out, dp, bits, 1),
        from_slots(res_grad, dp, bits, 1),
        gain_owned[:gain_width],
        gain_owned[2 * gain_width :],
        gain_owned[gain_width : 2 * gain_width],
        latent_owned,
        query_owned,
        keyval_owned,
        output_owned,
        expert_in_owned,
        expert_out_owned,
        shared_in_owned,
        shared_out_owned,
    )


DP, TENSOR = "dp", "tensor"
MESH = pl.DeviceIdType.MESH
F32 = jnp.float32
BF16 = jnp.bfloat16
CHUNKS = 3
SECONDS = 9
THIRDS = 7
SLOT = 256
GIVEN_VMEM = 60 * 1024 * 1024
FAR_FIRST = (2, 1, 0)
FLIPS = (1, 2, 0)
TENSOR_BITS = (1, 0)


COLUMNS = slot_order(FAR_FIRST)
UNIT_SLOTS = slot_order(FLIPS)
ROWS = slot_order(TENSOR_BITS)


def nn(a, b):
    return lax.dot_general(a, b, (((1,), (0,)), ((), ())), preferred_element_type=F32)


def nt(a, b):
    return lax.dot_general(a, b, (((1,), (1,)), ((), ())), preferred_element_type=F32)


def tn(a, b):
    return lax.dot_general(a, b, (((0,), (0,)), ((), ())), preferred_element_type=F32)


def lanes(k, width=SLOT):
    return slice(k * width, (k + 1) * width)


def crossed(index, constant, bits):
    total = 0
    for bit in range(bits):
        own = lax.rem(index // (1 << bit), 2)
        total = total + ((1 - own) if (constant >> bit) & 1 else own) * (1 << bit)
    return total


class Copies:
    def __init__(self, send_sems, recv_sems, local_sems=None):
        self.send_sems, self.recv_sems, self.local_sems = send_sems, recv_sems, local_sems
        self.count = 0
        self.local_count = 0

    def across(self, axis, bit):
        index = lax.axis_index(axis)
        side = lax.rem(index // (1 << bit), 2)
        return {axis: index + (1 - 2 * side) * (1 << bit)}

    def start(self, source, target, axis, bit):
        copy = pltpu.make_async_remote_copy(
            src_ref=source,
            dst_ref=target,
            send_sem=self.send_sems.at[self.count],
            recv_sem=self.recv_sems.at[self.count],
            device_id=self.across(axis, bit),
            device_id_type=MESH,
        )
        self.count += 1
        copy.start()
        return copy

    def local(self, source, target):
        copy = pltpu.make_async_copy(source, target, self.local_sems.at[self.local_count])
        self.local_count += 1
        copy.start()
        return copy

    def greet(self, dp_bits, tensor_bits=TENSOR_BITS):
        barrier = pltpu.get_barrier_semaphore()
        for axis, bits in ((DP, dp_bits), (TENSOR, tensor_bits)):
            for bit in bits:
                pl.semaphore_signal(
                    barrier, inc=1, device_id=self.across(axis, bit), device_id_type=MESH
                )
        pl.semaphore_wait(barrier, len(dp_bits) + len(tensor_bits))

    def swapped(self, source, target, first, width):
        parts = []
        for a in range(first, first + width, 1024):
            for b, c in ((a, a + 512), (a + 512, a)):
                parts.append(
                    self.start(
                        source.at[(slice(None),) * (len(source.shape) - 1) + (pl.ds(b, 512),)],
                        target.at[(slice(None),) * (len(target.shape) - 1) + (pl.ds(c, 512),)],
                        DP,
                        1,
                    )
                )
        return Several(parts)


class Several:
    def __init__(self, parts):
        self.parts = parts

    def wait(self):
        for part in self.parts:
            part.wait()


class SlotGather:
    def __init__(self, copies, source, slots, bits, axis=DP, cut=None):
        self.copies, self.source, self.slots, self.bits, self.axis = copies, source, slots, list(bits), axis
        self.cut = (slice(None),) if cut is None else (pl.ds(*cut),)
        self.done, self.have, self.own, self.flying = 0, 1, None, None

    def view(self, first, count):
        return self.slots.at[(pl.ds(first, count), *self.cut)]

    def start(self):
        bit = self.bits[self.done]
        if self.done == 0 and self.source is not None:
            source = self.source.at[(pl.ds(0, 1), *self.cut)]
            self.own = self.copies.local(source, self.view(0, 1))
        else:
            if self.own is not None:
                self.own.wait()
                self.own = None
            source = self.view(0, self.have)
        self.flying = self.copies.start(source, self.view(self.have, self.have), self.axis, bit)
        self.done += 1
        self.have *= 2

    def wait(self):
        self.flying.wait()
        self.flying = None
        if self.done < len(self.bits):
            self.start()

    def finish(self):
        while self.flying is not None:
            self.wait()


ANY_SPEC = pl.BlockSpec(memory_space=pl.ANY)
VMEM_SPEC = pl.BlockSpec(memory_space=pltpu.VMEM)
SMEM_SPEC = pl.BlockSpec(memory_space=pltpu.SMEM)


def cost(micros):
    return pl.CostEstimate(flops=micros * 10**9, bytes_accessed=micros * 10**6, transcendentals=0)


def like(shape, dtype=BF16):
    return jax.ShapeDtypeStruct(shape, dtype)


def turn(a, b, cos, sin):
    return a * cos - b * sin, b * cos + a * sin


def head_lanes(rows, head):
    lane = lax.broadcasted_iota(jnp.int32, (rows, SLOT), 1)
    return lax.rem(lane // 32, 4) == head


def spread_block(copies, pair_ref, between):
    block = lambda k: pair_ref.at[pl.ds(k, 1)]
    x_own = copies.start(block(0), block(2), TENSOR, 1)
    z_own = copies.swapped(block(0), block(1), 0, D)
    waits = [copies.start(block(0), block(4), TENSOR, 0)]
    between()
    z_own.wait()
    over_both = copies.start(block(1), block(3), TENSOR, 1)
    waits.append(copies.start(block(1), block(5), TENSOR, 0))
    between()
    x_own.wait()
    waits.append(copies.start(block(2), block(6), TENSOR, 0))
    between()
    over_both.wait()
    waits.append(copies.start(block(3), block(7), TENSOR, 0))
    for copy in waits:
        copy.wait()


class Places:
    def __init__(self):
        self.dp, self.tensor = lax.axis_index(DP), lax.axis_index(TENSOR)

    def __getitem__(self, k):
        if k == 12:
            return lax.rem(self.dp // 2, 2)
        return crossed(self.dp, COLUMNS[k], 3) if k < 8 else crossed(self.tensor, ROWS[k - 8], 2)


class Kept:
    output = ((8, 512, SLOT), BF16)
    mix = ((TOK, 512), BF16)
    query_final = ((TOK, 768), BF16)
    keyval_final = ((TOK, 1024), BF16)
    key_rope = ((TOK, SLOT), BF16)
    lse = ((TOK, 128), F32)
    query = ((8, SLOT, 768), BF16)
    w_keyval = ((KR, 1024), BF16)
    normed = ((TOK, D), BF16)
    latent_norm = ((TOK, KR), BF16)
    col = ((TOK, 128), F32)
    row = ((8, TOK), F32)
    cos = ((TOK, 128), F32)
    sin = ((TOK, 128), F32)
    gains = ((8, D), F32)
    latent_gain = ((8, KR), F32)
    latent_c = ((160, KR), F32)
    w_latent = ((D, KR + 128), BF16)
    mid = ((160, D), F32)
    mid_pair = ((8, 160, D), BF16)
    res = ((160, D), BF16)
    grad = ((160, D), BF16)
    valid = ((160, 128), F32)
    gates = ((8, TOK), F32)


class Landing:
    tokens = ((4, 160, D), BF16)
    pack = ((4, 8, 64, KR + 128), BF16)
    keyval = ((8, 64, 1024), BF16)
    part = ((4, 160, D), BF16)
    got_c = ((2, 160, D), BF16)
    give_x = ((1, 160, D), BF16)
    got_x = ((1, 160, D), BF16)
    gain_rows = ((KR, 128), BF16)
    masked = ((1, 160, D), BF16)
    own_query = ((1, SLOT, 768), BF16)


def fields(kind):
    return [name for name in vars(kind) if not name.startswith("_")]


def buffers(kind):
    return [getattr(kind, name) for name in fields(kind)]


def masks(col, row, cut):
    return (col[cut, 0:1] == row[0:1]) & (row[1:2] <= col[cut, 1:2])


def sort_columns(rows):
    column = lax.broadcasted_iota(jnp.int32, (768, 768), 1)
    row = lax.broadcasted_iota(jnp.int32, (768, 768), 0)
    wide = (column // 128) * 192 + lax.rem(column, 128)
    late = column - 512
    narrow = (lax.rem(late, 128) // 32) * 192 + 128 + (late // 128) * 32 + lax.rem(late, 32)
    return jnp.where(row == jnp.where(column < 512, wide, narrow), 1.0, 0.0).astype(BF16)


def front_kernel(
    width,
    count_ref,
    pack_ref,
    keyval_ref,
    output_ref,
    expert_in,
    expert_out,
    shared_in,
    shared_out,
    res_ref,
    grad_ref,
    query_ref,
    segment_row,
    table_ref,
    slot_gates,
    frequency_ref,
    grad_pair,
    gates_over,
    *rest,
):
    n_units = 3
    lows, highs = rest[:n_units], rest[n_units : 2 * n_units]
    rest = rest[2 * n_units :]
    kept, names = fields(Kept), fields(Kept) + fields(Landing)
    outs = types.SimpleNamespace(**dict(zip(kept, rest)))
    rest = rest[len(kept) :]
    at = types.SimpleNamespace(**dict(zip(names, rest)))
    send_sems, recv_sems, local_sems = rest[len(names) :]
    copies = Copies(send_sems, recv_sems, local_sems)
    places = Places()
    copies.greet((0, 1, 2))
    saved = []

    def save(pick):
        for source, target in zip(pick(at), pick(outs)):
            saved.append(copies.local(source, target))

    pack = SlotGather(copies, pack_ref, at.pack.at[0], FAR_FIRST)
    keyval = SlotGather(copies, keyval_ref, at.keyval, FAR_FIRST)
    part = query_ref.shape[0] // 4
    queries = [
        SlotGather(copies, at.own_query, at.query, FAR_FIRST, cut=(k * part, part)) for k in range(4)
    ]
    part = output_ref.shape[1] // 2
    outputs = [SlotGather(copies, output_ref, at.output, FAR_FIRST, cut=(k * part, part)) for k in range(2)]
    pack.start()
    keyval.start()
    for k in range(8):
        block = pl.ds(pl.multiple_of(places[k] * SLOT, SLOT), SLOT)
        at.res[:, lanes(k)] = res_ref[:, block]
        at.grad[:, lanes(k)] = grad_ref[:, block]
    at.tokens[0] = at.res[...]
    tokens = SlotGather(copies, None, at.tokens, TENSOR_BITS, TENSOR)
    tokens.start()
    at.own_query[0] = nn(query_ref[...], sort_columns(768)).astype(BF16)
    items = [pack, keyval, *queries, *outputs]
    units = [(p, part) for p in range(n_units) for part in range(CHUNKS)]
    flights = [None] * len(units)
    owns = [None] * len(units)
    state = [0, 0, 0]

    def unit_source(side, p, part):
        if p < 2:
            expert = pl.ds(side * 2 + p, 1)
            return expert_out.at[expert] if part == 2 else expert_in.at[expert, part]
        cut = pl.ds(pl.multiple_of(side * width, 16), width)
        return shared_out.at[pl.ds(0, 1), cut] if part == 2 else shared_in.at[pl.ds(part, 1), cut]

    def unit_first():
        i = state[0]
        if i >= len(units):
            return
        p, part = units[i]
        cut = pl.ds(part * width, width)
        side = places[12]
        owns[i] = copies.local(unit_source(side, p, part), lows[p].at[pl.ds(0, 1), cut])
        flights[i] = copies.start(
            unit_source(1 - side, p, part), lows[p].at[pl.ds(1, 1), cut], DP, FLIPS[0]
        )
        state[0] = i + 1

    def unit_second():
        i = state[1]
        if i >= min(state[0], SECONDS):
            return
        p, part = units[i]
        cut = pl.ds(part * width, width)
        flights[i].wait()
        owns[i].wait()
        flights[i] = copies.start(
            lows[p].at[pl.ds(0, 2), cut], lows[p].at[pl.ds(2, 2), cut], DP, FLIPS[1]
        )
        state[1] = i + 1

    def unit_third():
        i = state[2]
        if i >= min(state[1], THIRDS):
            return
        p, part = units[i]
        cut = pl.ds(part * width, width)
        flights[i].wait()
        flights[i] = copies.start(lows[p].at[pl.ds(0, 4), cut], highs[p].at[pl.ds(0, 4), cut], DP, FLIPS[2])
        state[2] = i + 1

    def pump():
        unit_third()
        unit_second()
        unit_first()

    def place_tokens():
        segments = segment_row[...].astype(F32)
        at.col[:, 0:8] = jnp.broadcast_to(segments, (8, TOK)).T
        for b in range(4):
            start = pl.multiple_of(places[8 + b] * 160, 8)
            at.cos[b * 160 : (b + 1) * 160] = jnp.broadcast_to(at.col[pl.ds(start, 160), 0:1], (160, 128))
        for b in range(4):
            start = pl.multiple_of(places[8 + b] * 160, 8)
            cut = slice(b * 160, (b + 1) * 160)
            segment = at.cos[cut, 0:1]
            token = start + lax.broadcasted_iota(jnp.int32, (160, 128), 0)
            lane = lax.broadcasted_iota(jnp.int32, (160, 128), 1)
            at.col[cut] = jnp.where(lane == 0, segment, token.astype(F32))
            before = jnp.sum((segments < segment).astype(F32), axis=1, keepdims=True)
            angle = (token.astype(F32) - before) * frequency_ref[...]
            at.cos[cut] = jnp.cos(angle)
            at.sin[cut] = jnp.sin(angle)
        at.row[...] = at.col[...].T[0:8]
        at.valid[...] = (at.col[0:160, 1:2] < count_ref[0].astype(F32)).astype(F32) + jnp.zeros((160, 128), F32)
        at.masked[0] = (at.grad[...].astype(F32) * at.valid[:, 0:1]).astype(BF16)

    def route_tokens():
        slots = jnp.concatenate([table_ref[...].astype(F32), slot_gates[...]], axis=0).T
        token_row = at.row[1:2]
        for e in range(4):
            hit = jnp.where(slots[:, e : e + 1] == token_row, slots[:, 4 + e : 5 + e], 0.0)
            at.gates[e : e + 1] = jnp.sum(hit, axis=0, keepdims=True)
        at.gates[4:8] = jnp.zeros((4, TOK), F32)
        save(lambda v: (v.col, v.row, v.cos, v.sin, v.valid, v.res, v.grad, v.gates))

    def make_keys():
        for s in range(4):
            for k in range(8):
                start = pl.multiple_of(k * SLOT + places[8 + s] * 64, 64)
                at.w_latent[pl.ds(start, 64)] = at.pack[s, k]
                start = pl.multiple_of(places[k] * 64 + places[8 + s] * 16, 16)
                at.gain_rows[pl.ds(start, 16)] = at.pack[s, k, 0:16, KR : KR + 128]
        for k in range(8):
            at.w_keyval[pl.ds(pl.multiple_of(places[k] * 64, 64), 64)] = at.keyval[k]
        tail = at.w_latent[:, KR : KR + 128]
        turned = tail.astype(F32).T
        attn_gain = turned[64:65]
        at.gains[...] = turned[64:72]
        latent_gain = at.gain_rows[...].astype(F32).T[66:67]
        at.latent_gain[...] = jnp.broadcast_to(latent_gain, (8, KR))
        row = lax.broadcasted_iota(jnp.int32, (128, SLOT), 0)
        lane = lax.broadcasted_iota(jnp.int32, (128, SLOT), 1)
        spread = jnp.where(row == lax.rem(lane, 32) + 32 * (lane // 128), 1.0, 0.0).astype(BF16)
        w_rope = nn(tail, spread).astype(BF16)
        for b in range(4):
            cut = slice(b * 160, (b + 1) * 160)
            x = at.tokens[b].astype(F32)
            factor = lax.rsqrt(jnp.mean(x * x, axis=1, keepdims=True) + NORM_EPS)
            at.normed[cut] = (x * factor * attn_gain).astype(BF16)
        for b in range(2):
            cut = slice(b * 320, (b + 1) * 320)
            normed = at.normed[cut]
            latent_c = nn(normed, at.w_latent[:, :KR])
            factor = lax.rsqrt(jnp.mean(latent_c * latent_c, axis=1, keepdims=True) + NORM_EPS)
            latent_norm = (latent_c * factor * latent_gain).astype(BF16)
            if b == 0:
                at.latent_c[...] = latent_c[:160]
            at.latent_norm[cut] = latent_norm
            rope = nn(normed, w_rope)
            key_a, key_b = turn(rope[:, :128], rope[:, 128:], at.cos[cut], at.sin[cut])
            at.key_rope[cut] = jnp.concatenate([key_a, key_b], axis=1).astype(BF16)
            at.keyval_final[cut] = nn(latent_norm, at.w_keyval[...]).astype(BF16)
        save(lambda v: (v.w_latent, v.w_keyval, v.gains, v.latent_gain, v.normed, v.latent_c, v.latent_norm, v.key_rope, v.keyval_final,))


    unit_first()
    for tau in range(len(items) + 1):
        if tau >= 1:
            items[tau - 1].wait()
        if tau < len(items):
            items[tau].wait()
        if tau + 2 < len(items):
            items[tau + 2].start()
        if tau == 0:
            place_tokens()
        elif tau == 1:
            tokens.wait()
            grad_own = copies.local(at.masked, grad_pair.at[pl.ds(0, 1)])
            grad_x = copies.start(at.masked, grad_pair.at[pl.ds(2, 1)], TENSOR, 1)
        elif tau == 3:
            pack.wait()
            pack_tensor = SlotGather(copies, None, at.pack, TENSOR_BITS, TENSOR)
            pack_tensor.start()
            unit_second()
        elif tau == 4:
            unit_first()
            route_tokens()
            gates_flight = copies.start(at.gates, gates_over, DP, 1)
        elif tau == 5:
            tokens.wait()
            unit_second()
        elif tau == 6:
            pack_tensor.wait()
            unit_first()
        elif tau == 7:
            keyval.wait()
            pack_tensor.wait()
            make_keys()
            unit_second()
    grad_x.wait()
    grad_z = copies.swapped(at.masked, grad_pair.at[pl.ds(1, 1)], 0, D)
    pump()
    for query in queries:
        query.wait()

    save(lambda v: (v.query,))
    gates_flight.wait()
    w_query = at.query[...].reshape(D, 768)
    scale = (HD + RD) ** (-0.5)
    for b in range(2):
        cut = slice(b * 320, (b + 1) * 320)
        found = nn(at.normed[cut], w_query)
        turned_a, turned_b = turn(found[:, 512:640], found[:, 640:768], at.cos[cut], at.sin[cut])
        at.query_final[cut] = jnp.concatenate([found[:, :512], turned_a, turned_b], axis=1).astype(BF16)
        allowed = masks(at.col, at.row, cut)
        lse_lane = lax.broadcasted_iota(jnp.int32, (320, 128), 1)
        lse_all = jnp.zeros((320, 128), F32)
        for h in range(4):
            rope = at.query_final[cut, 512:768]
            rope = jnp.where(head_lanes(320, h), rope, jnp.zeros_like(rope))
            keys = at.keyval_final[:, h * 256 : h * 256 + 128]
            scores = nt(at.query_final[cut, lanes(h, 128)], keys) + nt(rope, at.key_rope[...])
            scores = jnp.where(allowed, scores * scale, -1e30)
            top = jnp.max(scores, axis=1, keepdims=True)
            weight = jnp.exp(scores - top)
            total = jnp.sum(weight, axis=1, keepdims=True)
            probs = (weight / total).astype(BF16)
            lse_all = jnp.where(lse_lane == h, top + jnp.log(total), lse_all)
            mix = nn(probs, at.keyval_final[:, h * 256 + 128 : h * 256 + 256])
            at.mix[cut, lanes(h, 128)] = mix.astype(BF16)
        at.lse[cut] = lse_all
        if b == 0:
            pump()
            grad_z.wait()
            grad_zx = copies.start(
                grad_pair.at[pl.ds(1, 1)], grad_pair.at[pl.ds(3, 1)], TENSOR, 1
            )
    for output in outputs:
        output.wait()
    save(lambda v: (v.query_final, v.mix, v.lse, v.output,))
    for b in range(2):
        cut = slice((1 - b) * 320, (2 - b) * 320)
        for k in range(8):
            w_output = at.output[k]
            part = nn(at.mix[cut], w_output).astype(BF16)
            at.part[2 - 2 * b, :, lanes(k)] = part[:160]
            at.part[3 - 2 * b, :, lanes(k)] = part[160:]
        if b == 0:
            block = lambda ref, k: ref.at[pl.ds(k, 1)]
            c_far = copies.start(block(at.part, 3), block(at.got_c, 1), TENSOR, 0)
            c_near = copies.start(block(at.part, 2), block(at.got_c, 0), TENSOR, 0)
    c_far.wait()
    at.give_x[0] = (at.part[1].astype(F32) + at.got_c[1].astype(F32)).astype(BF16)
    x_far = copies.start(at.give_x, at.got_x, TENSOR, 1)
    pump()
    grad_zx.wait()
    grad_own.wait()
    grad_c = copies.start(grad_pair.at[pl.ds(0, 4)], grad_pair.at[pl.ds(4, 4)], TENSOR, 0)
    pump()
    c_near.wait()
    x_far.wait()
    attn_out = at.part[0].astype(F32) + at.got_c[0].astype(F32) + at.got_x[0].astype(F32)
    mid = at.res[...].astype(F32) + at.valid[:, 0:1] * attn_out
    at.mid[...] = mid
    save(lambda v: (v.mid,))
    factor = lax.rsqrt(jnp.mean(mid * mid, axis=1, keepdims=True) + NORM_EPS)
    at.mid_pair[0] = (mid * factor * at.gains[1:2]).astype(BF16)
    spread_block(copies, at.mid_pair, pump)
    save(lambda v: (v.mid_pair,))
    grad_c.wait()
    while state[0] < len(units) or state[1] < SECONDS or state[2] < THIRDS:
        pump()
    for i in range(SECONDS, len(units)):
        owns[i].wait()
    for flight in flights:
        if flight is not None:
            flight.wait()
    for copy in saved:
        copy.wait()


def front(counts, pack, keyval, output, expert_in, expert_out, shared_in, shared_out, res, grad, query, segment, table, gates):
    n_units, width = 3, expert_out.shape[1]
    half = (4, 3 * width, SLOT)
    frequency = ROPE_BASE ** (-np.arange(RD // 2, dtype=np.float32) / np.float32(RD // 2))
    frequency = jnp.asarray(np.tile(frequency.astype(np.float32), 4)[None])
    operands = [
        counts,
        pack[None],
        keyval[None],
        output[None],
        expert_in.transpose(0, 1, 3, 2),
        expert_out,
        shared_in.transpose(0, 2, 1),
        shared_out[None],
        res,
        grad,
        query,
        segment,
        table,
        gates,
        frequency,
    ]
    shapes = [like((8, *res.shape)), like((8, TOK), F32)] + [like(half)] * (2 * n_units - 1) + [like((4, width, SLOT))]
    shapes += [like(*buffer) for buffer in buffers(Kept)]
    results = pl.pallas_call(
        functools.partial(front_kernel, width),
        out_shape=shapes,
        in_specs=[SMEM_SPEC] + [ANY_SPEC] * 7 + [VMEM_SPEC] * 7,
        out_specs=[ANY_SPEC] * len(shapes),
        scratch_shapes=[pltpu.VMEM(*buffer) for buffer in buffers(Kept) + buffers(Landing)]
        + [
            pltpu.SemaphoreType.DMA((80,)),
            pltpu.SemaphoreType.DMA((80,)),
            pltpu.SemaphoreType.DMA((48,)),
        ],
        compiler_params=pltpu.CompilerParams(
            collective_id=0, has_side_effects=True, vmem_limit_bytes=GIVEN_VMEM
        ),
        cost_estimate=cost(220),
        name="front",
    )(*operands)
    grad_pair, gates_over, results = results[0], results[1], results[2:]
    lows, results = results[:n_units], results[n_units:]
    highs, results = results[:n_units], results[n_units:]
    return grad_pair, gates_over, lows, highs, types.SimpleNamespace(**dict(zip(fields(Kept), results)))


TOKEN_BLOCK = 256


class Freight:
    def __init__(self, copies, bits, sources, targets):
        self.copies, self.bits, self.pairs = copies, bits, list(zip(sources, targets))
        self.flights = []

    def start(self):
        for bit, (source, target) in zip(self.bits, self.pairs):
            self.flights.append(self.copies.start(source, target, DP, bit))

    def wait(self):
        for flight in self.flights:
            flight.wait()


class Split:
    def __init__(self, copies, keep, got, kept, gone):
        self.copies, self.kept, self.gone = copies, kept, gone
        self.loads = [copies.local(keep, kept), copies.local(got, gone)]
        self.half = kept.shape[0] // 2
        self.flights = []

    def send(self, bit, target, stay=None):
        for load in self.loads:
            load.wait()
        for k in range(2 * self.half):
            target_ref = self.kept if k < self.half else self.gone
            target_ref[k] = (self.kept[k].astype(F32) + self.gone[k].astype(F32)).astype(BF16)
        self.flights.append(
            self.copies.start(self.gone.at[pl.ds(self.half, self.half)], target, DP, bit)
        )
        if stay is not None:
            self.flights.append(self.copies.local(self.kept.at[pl.ds(0, self.half)], stay))

    def wait(self):
        for flight in self.flights:
            flight.wait()


def split_scratch(splits):
    return [pltpu.VMEM(keep.shape, BF16) for keep, _, _ in splits for _ in range(2)] + [
        pltpu.SemaphoreType.DMA((4 * len(splits),))
    ]


def split_outputs(splits):
    return [like((keep.shape[0] // 2, *keep.shape[1:])) for keep, _, _ in splits for _ in range(2)]


def experts_kernel(width, has_sum, bits, parts, *refs):
    refs = list(refs)
    take = lambda n: [refs.pop(0) for _ in range(n)]
    mid_ref, grad_ref, gate_ref = take(3)
    unit_refs = take(len(parts))
    if has_sum:
        back_in, out_in = take(2)
    sources = take(len(bits))
    back_ref, out_ref = take(2)
    keep_refs, give_refs = take(3), take(3)
    targets = take(len(bits))
    whole, total, send_sems, recv_sems = take(4)
    step = pl.program_id(0)
    copies = Copies(send_sems, recv_sems)

    def flights():
        return [
            pltpu.make_async_remote_copy(
                src_ref=cut.view(source),
                dst_ref=target,
                send_sem=send_sems.at[k],
                recv_sem=recv_sems.at[k],
                device_id=copies.across(DP, cut.bit),
                device_id_type=MESH,
            )
            for k, (cut, source, target) in enumerate(zip(bits, sources, targets))
        ]

    @pl.when(step == 0)
    def _():
        copies.greet(sorted({cut.bit for cut in bits}), ())
        for flight in flights():
            flight.start()
        for ref, (slot, count, start, size, skip) in zip(unit_refs, parts):
            for j in range(count):
                k = COLUMNS.index(UNIT_SLOTS[slot + j])
                whole[start : start + size, lanes(k)] = ref[j, skip : skip + size]
        total[...] = jnp.zeros_like(total)

    mid, grad = mid_ref[...], grad_ref[...]
    gate_up = nt(whole[: 2 * width], mid)
    hidden_grad = nt(whole[2 * width :], grad)
    gate = gate_up[:width]
    up = gate_up[width:]
    sigma = 1.0 / (1.0 + jnp.exp(-gate))
    silu = gate * sigma
    slope = sigma * (1.0 + gate * (1.0 - sigma))
    weight = gate_ref[...]
    hidden_grad = hidden_grad * weight
    hidden = (silu * up * weight).astype(BF16)
    pre = jnp.concatenate(
        [(hidden_grad * up * slope).astype(BF16), (hidden_grad * silu).astype(BF16)], axis=0
    )
    back = tn(pre, whole[: 2 * width])
    out = tn(hidden, whole[2 * width :])
    if has_sum:
        back = back + back_in[...]
        out = out + out_in[...]
    back_ref[...] = back.astype(back_ref.dtype)
    out_ref[...] = out.astype(out_ref.dtype)
    total[: 2 * width] += nn(pre, mid)
    total[2 * width :] += nn(hidden, grad)

    @pl.when(step == pl.num_programs(0) - 1)
    def _():
        for g in range(3):
            cut = slice(g * width, (g + 1) * width)
            for k in range(4):
                keep_refs[g][k] = total[cut, lanes((0, 2, 1, 3)[k])].astype(BF16)
                give_refs[g][k] = total[cut, lanes(4 + (0, 2, 1, 3)[k])].astype(BF16)
        for flight in flights():
            flight.wait()


class Cut:
    def __init__(self, array, bit, slots=None, rows=None):
        self.array, self.bit = array, bit
        self.slots = slots or (0, array.shape[0])
        self.rows = rows or (0, array.shape[1])

    def shape(self):
        return (self.slots[1], self.rows[1], self.array.shape[2])

    def view(self, ref):
        return ref.at[pl.ds(*self.slots), pl.ds(*self.rows)]


def experts_step(mid_pair, grad_pair, unit, gate, sums, last, freight, ident):
    tokens, block = mid_pair.shape[0], TOKEN_BLOCK
    width = unit[0][0].shape[1] // 3
    rows = pl.BlockSpec((block, D), lambda i: (i, 0))
    fixed = lambda *shape: pl.BlockSpec(shape, lambda i: (0,) * len(shape))
    kind = BF16 if last else F32
    part = (4, width, SLOT)
    operands = [mid_pair, grad_pair, gate[None]] + [part[0] for part in unit]
    specs = [rows, rows, pl.BlockSpec((1, block), lambda i: (0, i))]
    specs += [fixed(*part[0].shape) for part in unit]
    if sums is not None:
        operands += list(sums)
        specs += [rows, rows]
    results = pl.pallas_call(
        functools.partial(
            experts_kernel, width, sums is not None, tuple(freight), tuple(p[1:] for p in unit)
        ),
        grid=(tokens // block,),
        out_shape=[like((tokens, D), kind)] * 2
        + [like(part)] * 6
        + [like(cut.shape()) for cut in freight],
        in_specs=specs + [ANY_SPEC] * len(freight),
        out_specs=[rows, rows] + [fixed(*part)] * 6 + [ANY_SPEC] * len(freight),
        scratch_shapes=[
            pltpu.VMEM((3 * width, D), BF16),
            pltpu.VMEM((3 * width, D), F32),
            pltpu.SemaphoreType.DMA((len(freight),)),
            pltpu.SemaphoreType.DMA((len(freight),)),
        ],
        compiler_params=pltpu.CompilerParams(
            collective_id=ident, has_side_effects=True, vmem_limit_bytes=GIVEN_VMEM
        ),
        cost_estimate=cost(35),
        name="experts_step",
    )(*operands, *[cut.array for cut in freight])
    return list(results[:2]), list(results[2:5]), list(results[5:8]), list(results[8:])


def halve_kernel(count, *refs):
    keeps, gots, stays, gives = (refs[k * count : (k + 1) * count] for k in range(4))
    for keep, got, stay, give in zip(keeps, gots, stays, gives):
        half = stay.shape[0]
        for k in range(half):
            stay[k] = (keep[k].astype(F32) + got[k].astype(F32)).astype(BF16)
            give[k] = (keep[half + k].astype(F32) + got[half + k].astype(F32)).astype(BF16)


def halve(pairs):
    count = len(pairs)
    shapes = [like((keep.shape[0] // 2, *keep.shape[1:])) for keep, _ in pairs]
    results = pl.pallas_call(
        functools.partial(halve_kernel, count),
        out_shape=shapes * 2,
        in_specs=[VMEM_SPEC] * (2 * count),
        out_specs=[VMEM_SPEC] * (2 * count),
        cost_estimate=cost(3),
        name="halve",
    )(*[keep for keep, _ in pairs], *[got for _, got in pairs])
    return list(zip(results[:count], results[count:]))


class PairSum:
    def __init__(self, copies, blocks, got_c, give_a, give_b, got_a, got_b, end_a, end_b, last_a, last_b):
        self.copies, self.blocks, self.got_c = copies, blocks, got_c
        self.give_a, self.give_b, self.got_a, self.got_b = give_a, give_b, got_a, got_b
        self.end_a, self.end_b, self.last_a, self.last_b = end_a, end_b, last_a, last_b

    def both(self, k, first):
        cut = slice(first, first + 1024)
        return self.blocks[k, :, cut].astype(F32) + self.got_c[k, :, cut].astype(F32)

    def start(self):
        self.flights = {}
        for k in (3, 2, 1, 0):
            self.flights[k] = self.copies.start(
                self.blocks.at[pl.ds(4 + k, 1)], self.got_c.at[pl.ds(k, 1)], TENSOR, 0
            )

    def cross(self):
        self.flights[3].wait()
        self.give_a[1] = self.both(3, 0).astype(BF16)
        self.give_b[1] = self.both(3, 1024).astype(BF16)
        self.flights[2].wait()
        self.give_a[0] = self.both(2, 0).astype(BF16)
        self.across_a = self.copies.start(self.give_a, self.got_a, TENSOR, 1)
        self.flights[1].wait()
        self.give_b[0] = self.both(1, 1024).astype(BF16)
        self.across_b = self.copies.swapped(self.give_b, self.got_b, 0, 1024)
        self.flights[0].wait()

    def end(self):
        self.across_a.wait()
        self.end_a[0] = (self.both(1, 0) + self.got_a[1].astype(F32)).astype(BF16)
        self.ends_a = self.copies.swapped(self.end_a, self.last_a, 0, 1024)
        self.across_b.wait()
        self.end_b[0] = (self.both(2, 1024) + self.got_b[1].astype(F32)).astype(BF16)
        self.ends_b = self.copies.start(self.end_b, self.last_b, TENSOR, 1)

    def settle(self, total, end_a, end_b):
        self.across_a.wait()
        end_a[0] = (self.both(1, 0) + self.got_a[1].astype(F32)).astype(BF16)
        self.across_b.wait()
        end_b[0] = (self.both(2, 1024) + self.got_b[1].astype(F32)).astype(BF16)
        total[:, :1024] = self.both(0, 0) + self.got_a[0].astype(F32)
        total[:, 1024:] = self.both(0, 1024) + self.got_b[0].astype(F32)

    def total(self):
        self.ends_a.wait()
        self.ends_b.wait()
        return (
            self.both(0, 0) + self.got_a[0].astype(F32) + self.last_a[0].astype(F32),
            self.both(0, 1024) + self.got_b[0].astype(F32) + self.last_b[0].astype(F32),
        )


def sum_scratch():
    half = pltpu.VMEM((2, 160, 1024), BF16)
    end = pltpu.VMEM((1, 160, 1024), BF16)
    return [pltpu.VMEM((4, 160, D), BF16), half, half, half, half, end, end, end, end]


def back_kernel(bits, splits, *refs):
    refs = list(refs)
    take = lambda n: [refs.pop(0) for _ in range(n)]
    back_ref, grad_ref, mid_ref, gains_ref, valid_ref = take(5)
    sources = take(len(bits))
    pairs = take(2 * len(splits))
    mid_grad_ref, gain_part_ref, tokens_ref = take(3)
    targets = take(len(bits))
    ends = take(2 * len(splits))
    rooms = take(2 * len(splits))
    local_sems, *buffers, send_sems, recv_sems = refs
    copies = Copies(send_sems, recv_sems, local_sems)
    parts = [Split(copies, *pairs[2 * k : 2 * k + 2], *rooms[2 * k : 2 * k + 2]) for k in range(len(splits))]
    copies.greet((0, 1, 2))
    freight = Freight(copies, bits, sources, targets)
    freight.start()
    pair = PairSum(copies, back_ref, *buffers)
    pair.start()
    for k, bit in enumerate(splits):
        parts[k].send(bit, ends[2 * k + 1], ends[2 * k])
    pair.cross()
    pair.end()
    first, second = pair.total()
    mid_grad_ref[:, :1024] = first
    mid_grad_ref[:, 1024:] = second
    grad, mid = mid_grad_ref[...], mid_ref[...]
    factor = lax.rsqrt(jnp.mean(mid * mid, axis=1, keepdims=True) + NORM_EPS)
    scaled = grad * gains_ref[1:2]
    inner = jnp.mean(scaled * mid, axis=1, keepdims=True)
    gain_part_ref[...] = jnp.broadcast_to(jnp.sum(grad * mid * factor, axis=0, keepdims=True), (8, D))
    mid_grad = grad_ref[...].astype(F32) + factor * (scaled - mid * factor * factor * inner)
    mid_grad_ref[...] = mid_grad
    tokens_ref[0] = (valid_ref[:, 0:1] * mid_grad).astype(BF16)
    own = tokens_ref.at[pl.ds(0, 1)]
    x_own = copies.start(own, tokens_ref.at[pl.ds(1, 1)], TENSOR, 1)
    c_own = copies.start(own, tokens_ref.at[pl.ds(2, 1)], TENSOR, 0)
    x_own.wait()
    c_far = copies.start(tokens_ref.at[pl.ds(1, 1)], tokens_ref.at[pl.ds(3, 1)], TENSOR, 0)
    c_own.wait()
    c_far.wait()
    freight.wait()
    for part in parts:
        part.wait()


def back_tokens(back, grad_slots, mid, gains, valid, freight, splits):
    rows = (160, D)
    bits = tuple(bit for bit, _ in freight)
    goods = [array for _, array in freight]
    results = pl.pallas_call(
        functools.partial(back_kernel, bits, tuple(bit for _, _, bit in splits)),
        out_shape=[like(rows, F32), like((8, D), F32), like((4, *rows))]
        + [like(g.shape, g.dtype) for g in goods]
        + split_outputs(splits),
        in_specs=[VMEM_SPEC] * 5 + [ANY_SPEC] * (len(goods) + 2 * len(splits)),
        out_specs=[VMEM_SPEC] * 3 + [ANY_SPEC] * (len(goods) + 2 * len(splits)),
        scratch_shapes=split_scratch(splits)
        + sum_scratch() + [pltpu.SemaphoreType.DMA((24,)), pltpu.SemaphoreType.DMA((24,))],
        compiler_params=pltpu.CompilerParams(
            collective_id=2, has_side_effects=True, vmem_limit_bytes=GIVEN_VMEM
        ),
        cost_estimate=cost(55),
        name="back_tokens",
    )(back, grad_slots, mid, gains, valid, *goods, *[v for keep, got, _ in splits for v in (keep, got)])
    n = 3 + len(goods)
    return results[:3], list(results[3:n]), list(zip(results[n::2], results[n + 1 :: 2]))


def attention_backward_kernel(bits, splits, *refs):
    refs = list(refs)
    take = lambda n: [refs.pop(0) for _ in range(n)]
    (
        grad_ref,
        output_ref,
        mix_ref,
        query_ref,
        keyval_ref,
        key_rope_ref,
        lse_ref,
        w_query_ref,
        w_keyval_ref,
        normed_ref,
        latent_norm_ref,
        col_ref,
        row_ref,
        cos_ref,
        sin_ref,
        out_ref,
    ) = take(16)
    sources = take(len(bits))
    pairs = take(2 * len(splits))
    output_wgrad, query_wgrad, keyval_wgrad, part_ref, out_sum, out_end_a, out_end_b = take(7)
    targets = take(len(bits))
    output_got = take(1)[0]
    ends = take(2 * len(splits))
    rooms = take(2 * len(splits))
    local_sems = take(1)[0]
    mix_grad, query_grad, keyval_grad, key_grad, rope_grad, wide, send_sems, recv_sems = take(8)
    copies = Copies(send_sems, recv_sems, local_sems)
    parts = [Split(copies, *pairs[2 * k : 2 * k + 2], *rooms[2 * k : 2 * k + 2]) for k in range(len(splits))]
    copies.greet((0, 1, 2))
    pair = PairSum(copies, out_ref, *refs, None, None, None, None)
    pair.start()
    freight = Freight(copies, bits, sources, targets)
    freight.start()
    for k, bit in enumerate(splits):
        parts[k].send(bit, ends[2 * k + 1], ends[2 * k])
    places = Places()
    scale = (HD + RD) ** (-0.5)
    w_query = w_query_ref[...].reshape(D, w_query_ref.shape[2])
    for k in range(8):
        block = jnp.concatenate([grad_ref[b, :, lanes(k)] for b in range(4)], axis=0)
        s = k
        output_wgrad[s] = tn(mix_ref[...], block).astype(BF16)
        term = nt(block, output_ref[s])
        if k == 0:
            wide[:, :512] = term
        else:
            wide[:, :512] += term
    mix_grad[...] = wide[:, :512].astype(BF16)
    output_flight = copies.start(output_wgrad.at[pl.ds(4, 4)], output_got, DP, 0)
    pair.cross()
    for b in range(2):
        cut = slice(b * 320, (b + 1) * 320)
        allowed = masks(col_ref, row_ref, cut)
        lse_lane = lax.broadcasted_iota(jnp.int32, (320, 128), 1)
        rope_sum = jnp.zeros((320, SLOT), F32)
        for h in range(4):
            nope = query_ref[cut, lanes(h, 128)]
            rope = query_ref[cut, 512:768]
            mask = head_lanes(320, h)
            rope = jnp.where(mask, rope, jnp.zeros_like(rope))
            keys = keyval_ref[:, h * 256 : h * 256 + 128]
            values = keyval_ref[:, h * 256 + 128 : h * 256 + 256]
            scores = nt(nope, keys) + nt(rope, key_rope_ref[...])
            lse = jnp.sum(jnp.where(lse_lane == h, lse_ref[cut], 0.0), axis=1, keepdims=True)
            probs = jnp.where(allowed, jnp.exp(scores * scale - lse), 0.0)
            grad = mix_grad[cut, lanes(h, 128)]
            probs_grad = nt(grad, values)
            inner = jnp.sum(probs * probs_grad, axis=1, keepdims=True)
            scores_grad = (probs * (probs_grad - inner)).astype(BF16)
            value_grad = tn(probs.astype(BF16), grad)
            nope_grad = tn(scores_grad, nope) * scale
            rope_part = tn(scores_grad, rope)
            low, high = slice(h * 256, h * 256 + 128), slice(h * 256 + 128, h * 256 + 256)
            if b == 0:
                key_grad[:, low] = nope_grad
                key_grad[:, high] = value_grad
            else:
                key_grad[:, low] += nope_grad
                key_grad[:, high] += value_grad
            if b == 0 and h == 0:
                rope_grad[...] = rope_part
            else:
                rope_grad[...] += rope_part
            query_grad[cut, lanes(h, 128)] = (nn(scores_grad, keys) * scale).astype(BF16)
            rope_sum = rope_sum + jnp.where(mask, nn(scores_grad, key_rope_ref[...]), 0.0)
        rope_sum = rope_sum * scale
        back_a, back_b = turn(rope_sum[:, :128], rope_sum[:, 128:], cos_ref[cut], -sin_ref[cut])
        query_grad[cut, 512:640] = back_a.astype(BF16)
        query_grad[cut, 640:768] = back_b.astype(BF16)
    keyval_grad[...] = key_grad[...].astype(BF16)
    plain = nt(query_grad[...], sort_columns(768)).astype(BF16)
    for k in range(8):
        query_wgrad[k] = tn(normed_ref[:, lanes(k)], plain).astype(BF16)
    wide[:512, :] = tn(latent_norm_ref[...], keyval_grad[...])
    for k in range(8):
        start = pl.multiple_of(places[k] * 64, 64)
        keyval_wgrad[k] = wide[pl.ds(start, 64), :].astype(BF16)
    row = lax.broadcasted_iota(jnp.int32, (SLOT, 128), 0)
    lane = lax.broadcasted_iota(jnp.int32, (SLOT, 128), 1)
    fold = jnp.where(lane == lax.rem(row, 32) + 32 * (row // 128), scale, 0.0)
    for b in range(4):
        cut = slice(b * 160, (b + 1) * 160)
        for k in range(4):
            columns = lanes(k, 512)
            part_ref[b, :, columns] = nt(query_grad[cut], w_query[columns]).astype(BF16)
        part_ref[b, :, D : D + KR] = nt(keyval_grad[cut], w_keyval_ref[...]).astype(BF16)
        rope = lax.dot_general(
            rope_grad[cut],
            fold,
            (((1,), (0,)), ((), ())),
            precision=lax.Precision.HIGHEST,
            preferred_element_type=F32,
        )
        part_ref[b, :, D + KR :] = rope.astype(BF16)
    pair.settle(out_sum, out_end_a, out_end_b)
    output_flight.wait()
    freight.wait()
    for part in parts:
        part.wait()


def attention_backward(grad, saved, out, freight, splits):
    shapes = [like((8, 512, SLOT)), like((8, SLOT, 768)), like((8, 64, 1024)), like((4, 160, D + KR + 128))]
    shapes += [like((160, D), F32), like((1, 160, 1024)), like((1, 160, 1024))]
    bits = tuple(bit for bit, _ in freight)
    goods = [array for _, array in freight]
    kept = (saved.output, saved.mix, saved.query_final, saved.keyval_final, saved.key_rope, saved.lse, saved.query)
    kept += (saved.w_keyval, saved.normed, saved.latent_norm, saved.col, saved.row, saved.cos, saved.sin)
    results = pl.pallas_call(
        functools.partial(attention_backward_kernel, bits, tuple(bit for _, _, bit in splits)),
        out_shape=shapes + [like(g.shape) for g in goods] + [like((4, 512, SLOT))] + split_outputs(splits),
        in_specs=[VMEM_SPEC] * 16 + [ANY_SPEC] * (len(goods) + 2 * len(splits)),
        out_specs=[VMEM_SPEC] * len(shapes) + [ANY_SPEC] * (len(goods) + 1 + 2 * len(splits)),
        scratch_shapes=split_scratch(splits)
        + [
            pltpu.VMEM((TOK, 512), BF16),
            pltpu.VMEM((TOK, 768), BF16),
            pltpu.VMEM((TOK, 1024), BF16),
            pltpu.VMEM((TOK, 1024), F32),
            pltpu.VMEM((TOK, SLOT), F32),
            pltpu.VMEM((TOK, 1024), F32),
            pltpu.SemaphoreType.DMA((32,)),
            pltpu.SemaphoreType.DMA((32,)),
            *sum_scratch()[:5],
        ],
        compiler_params=pltpu.CompilerParams(
            collective_id=4, has_side_effects=True, vmem_limit_bytes=GIVEN_VMEM
        ),
        cost_estimate=cost(30),
        name="attention_backward",
    )(grad, *kept, out, *goods, *[v for keep, got, _ in splits for v in (keep, got)])
    n = 8 + len(goods)
    return results[:7], list(results[7:n]), list(zip(results[n::2], results[n + 1 :: 2]))


class SlotSum:
    def __init__(self, copies, values, bits, got, give, rows=None):
        self.copies, self.values, self.bits, self.got, self.give = copies, values, list(bits), got, give
        self.rows = rows or (0, values.shape[1])
        self.level = 0
        self.flying = None

    def view(self, ref, first, count):
        return ref.at[pl.ds(first, count), pl.ds(*self.rows)]

    def start(self):
        half = 4 >> self.level
        if self.level == 0:
            source = self.view(self.values, half, half)
        else:
            first, size = self.rows
            for k in range(half):
                self.give[self.level - 1][k, first : first + size] = self.total(half + k).astype(BF16)
            source = self.view(self.give[self.level - 1], 0, half)
        target = self.view(self.got[self.level], 0, half)
        self.flying = self.copies.start(source, target, DP, self.bits[self.level])
        self.level += 1

    def total(self, k):
        cut = slice(self.rows[0], self.rows[0] + self.rows[1])
        value = self.values[k, cut].astype(F32)
        for level in range(self.level):
            value = value + self.got[level][k, cut].astype(F32)
        return value

    def wait(self):
        self.flying.wait()
        if self.level < len(self.bits):
            self.start()


def slot_sum_scratch(shape):
    spaces = [pltpu.VMEM((n, *shape), BF16) for n in (4, 2, 1)]
    return spaces + [pltpu.VMEM((n, *shape), BF16) for n in (2, 1)]


def tail_kernel(
    n_rest,
    n_last,
    part_ref,
    output_wgrad,
    query_wgrad,
    keyval_wgrad,
    normed_ref,
    w_latent_ref,
    gains_ref,
    latent_gain_ref,
    latent_c_ref,
    res_ref,
    mid_grad_ref,
    ffn_gain_ref,
    output_came,
    mid_ref,
    valid_ref,
    out_sum,
    out_end_a,
    out_end_b,
    cos_ref,
    sin_ref,
    *refs,
):
    refs = list(refs)
    take = lambda n: [refs.pop(0) for _ in range(n)]
    rest_pairs, last_pairs = take(2 * n_rest), take(2 * n_last)
    output_owned, query_owned, keyval_owned, latent_owned, res_grad_ref, res_out_ref = take(6)
    rest_owned, end_cames = take(n_rest), take(n_rest)
    last_ends = take(2 * n_last)
    send_sems, recv_sems = take(2)
    sums = []
    copies = Copies(send_sems, recv_sems)
    for values, bits in (
        (query_wgrad, (0, 1, 2)),
        (keyval_wgrad, (0, 1, 2)),
        (output_wgrad, (0, 1, 2)),
    ):
        space = take(5)
        if values is query_wgrad:
            half = values.shape[1] // 2
            for k in range(2):
                sums.append(SlotSum(copies, values, bits, space[:3], space[3:], (k * half, half)))
        else:
            sums.append(SlotSum(copies, values, bits, space[:3], space[3:]))
    latent_values = take(1)[0]
    space = take(5)
    latent_sum = SlotSum(copies, latent_values, (0, 1, 2), space[:3], space[3:])
    got_c, give_x, got_x = take(3)
    latent_all, gain_rows, gain_c, gain_x, gain_columns, wide, rest_came, end_sum, _, local_sems = take(10)
    copies.local_sems = local_sems
    copies.greet((0, 1, 2))
    last_a, last_b = take(2)
    out_ends = [copies.swapped(out_end_a, last_a, 0, 1024), copies.start(out_end_b, last_b, TENSOR, 1)]
    rest_rooms, last_rooms = take(2 * n_rest), take(2 * n_last)
    rests = [Split(copies, *rest_pairs[2 * k : 2 * k + 2], *rest_rooms[2 * k : 2 * k + 2]) for k in range(n_rest)]
    lasts = [Split(copies, *last_pairs[2 * k : 2 * k + 2], *last_rooms[2 * k : 2 * k + 2]) for k in range(n_last)]
    query_first, query_second, keyval_sum, output_sum = sums
    output_sum.got[0] = output_came
    output_sum.level = 1
    query_first.start()
    output_sum.start()
    c_far = copies.start(part_ref.at[pl.ds(3, 1)], got_c.at[pl.ds(1, 1)], TENSOR, 0)
    c_near = copies.start(part_ref.at[pl.ds(2, 1)], got_c.at[pl.ds(0, 1)], TENSOR, 0)
    c_far.wait()
    give_x[0] = (part_ref[1].astype(F32) + got_c[1].astype(F32)).astype(BF16)
    x_far = copies.start(give_x, got_x, TENSOR, 1)
    for k in range(n_rest):
        rests[k].send(2, rest_came.at[pl.ds(2 * k, 2)])
    for k in range(n_last):
        lasts[k].send(1, last_ends[2 * k + 1], last_ends[2 * k])
    c_near.wait()
    query_first.wait()
    query_second.start()
    x_far.wait()

    def summed(columns):
        return (
            part_ref[0, :, columns].astype(F32)
            + got_c[0, :, columns].astype(F32)
            + got_x[0, :, columns].astype(F32)
        )

    latent_c = latent_c_ref[...]
    latent_gain = latent_gain_ref[0:1]
    factor = lax.rsqrt(jnp.mean(latent_c * latent_c, axis=1, keepdims=True) + NORM_EPS)
    grad = summed(slice(D, D + KR))
    scaled = grad * latent_gain
    inner = jnp.mean(scaled * latent_c, axis=1, keepdims=True)
    latent_back = factor * (scaled - latent_c * factor * factor * inner)
    latent_gain_part = jnp.sum(grad * latent_c * factor, axis=0, keepdims=True)
    rope = summed(slice(D + KR, D + KR + 128))
    cos, sin = cos_ref[...], sin_ref[...]
    lane = lax.broadcasted_iota(jnp.int32, rope.shape, 1)
    other = jnp.where(lane < 32, pltpu.roll(rope, 96, 1), pltpu.roll(rope, 32, 1))
    rope_back = jnp.where(lane < 32, rope * cos + other * sin, rope * cos - other * sin)
    rope_back = jnp.where(lane < RD, rope_back, 0.0)
    latent_all[0, :, :KR] = latent_back.astype(BF16)
    latent_all[0, :, KR:] = rope_back.astype(BF16)
    own = latent_all.at[pl.ds(0, 1)]
    l_x = copies.start(own, latent_all.at[pl.ds(1, 1)], TENSOR, 1)
    l_c = copies.start(own, latent_all.at[pl.ds(2, 1)], TENSOR, 0)
    res = res_ref[...].astype(F32)
    factor = lax.rsqrt(jnp.mean(res * res, axis=1, keepdims=True) + NORM_EPS)
    grad = summed(slice(0, D)) + nt(latent_all[0], w_latent_ref[...])
    scaled = grad * gains_ref[0:1]
    inner = jnp.mean(scaled * res, axis=1, keepdims=True)
    res_grad_ref[...] = mid_grad_ref[...] + factor * (scaled - res * factor * factor * inner)
    row = lax.broadcasted_iota(jnp.int32, (8, D), 0)
    attn_part = jnp.broadcast_to(jnp.sum(grad * res * factor, axis=0, keepdims=True), (8, D))
    gain_rows[0] = jnp.where(row == 0, attn_part, jnp.where(row == 1, ffn_gain_ref[...], 0.0))
    latent_row = jnp.broadcast_to(latent_gain_part, (8, KR))
    gain_rows[0, :, :KR] = jnp.where(
        lax.broadcasted_iota(jnp.int32, (8, KR), 0) == 2, latent_row, gain_rows[0, :, :KR]
    )
    g_c = copies.start(gain_rows, gain_c, TENSOR, 0)
    query_second.wait()
    keyval_sum.start()
    query_first.wait()
    l_x.wait()
    l_far = copies.start(latent_all.at[pl.ds(1, 1)], latent_all.at[pl.ds(3, 1)], TENSOR, 0)
    g_c.wait()
    gain_rows[0] = gain_rows[0] + gain_c[0]
    g_x = copies.start(gain_rows, gain_x, TENSOR, 1)
    l_c.wait()
    l_far.wait()
    g_x.wait()
    output_sum.wait()
    keyval_sum.wait()
    query_second.wait()
    gain_columns[:, 0:8] = (gain_rows[0] + gain_x[0]).T
    tensor = lax.axis_index(TENSOR)
    dp = lax.axis_index(DP)
    latent_rows = jnp.concatenate([latent_all[b] for b in range(4)], axis=0)
    for k in range(8):
        wide[...] = tn(normed_ref[:, lanes(k)], latent_rows)
        block = wide[pl.ds(pl.multiple_of(tensor * 64, 64), 64), :]
        start = pl.multiple_of(k * SLOT + tensor * 64, 64)
        columns = gain_columns[pl.ds(start, 64), 0:8]
        start = pl.multiple_of(crossed(dp, COLUMNS[k], 3) * 64 + tensor * 16, 16)
        latent_values[k] = block.astype(BF16)
        lane = lax.broadcasted_iota(jnp.int32, (64, 128), 1)
        ends = block[:, KR : KR + 128]
        ends = jnp.where(lane == 64, columns[:, 0:1], ends)
        ends = jnp.where(lane == 65, columns[:, 1:2], ends)
        latent_values[k, :, KR:] = ends.astype(BF16)
        corner = gain_columns[pl.ds(start, 16), 0:8][:, 2:3]
        lane = lax.broadcasted_iota(jnp.int32, (16, 128), 1)
        latent_values[k, 0:16, KR:] = jnp.where(lane == 66, corner, ends[0:16]).astype(BF16)
    latent_sum.start()
    ends = []
    for g in range(n_rest):
        rests[g].wait()
        own, over = rests[g].kept[0].astype(F32), rests[g].kept[1].astype(F32)
        rest_owned[g][0] = (own + rest_came[2 * g].astype(F32)).astype(BF16)
        end_sum[g] = (over + rest_came[2 * g + 1].astype(F32)).astype(BF16)
        ends.append(copies.start(end_sum.at[pl.ds(g, 1)], end_cames[g], DP, 1))
    keyval_sum.wait()
    output_sum.wait()
    output_owned[...] = output_sum.total(0)
    latent_sum.wait()
    for flight in out_ends:
        flight.wait()
    valid = valid_ref[:, 0:1]
    res_out_ref[:, :1024] = (mid_ref[:, :1024] + valid * (out_sum[:, :1024] + last_a[0].astype(F32))).astype(BF16)
    res_out_ref[:, 1024:] = (mid_ref[:, 1024:] + valid * (out_sum[:, 1024:] + last_b[0].astype(F32))).astype(BF16)
    latent_sum.wait()
    half = query_owned.shape[0] // 2
    query_first.wait()
    query_owned[:half] = query_first.total(0)
    keyval_sum.wait()
    keyval_owned[...] = keyval_sum.total(0)
    query_second.wait()
    query_owned[half:] = query_second.total(0)
    latent_sum.wait()
    latent_owned[...] = latent_sum.total(0)
    for copy in lasts + ends:
        copy.wait()


def tail(part, wgrads, output_came, out_parts, saved, mid_grad, ffn_gain, rests, lasts):
    output_wgrad, query_wgrad, keyval_wgrad = wgrads
    rows = (160, D)
    latent = (64, KR + 128)
    shapes = [
        like((512, SLOT), F32),
        like((SLOT, 768), F32),
        like((64, 1024), F32),
        like(latent, F32),
        like(rows, F32),
        like(rows),
    ]
    part_row = (160, D + KR + 128)
    unit = rests[0][0].shape[1:]
    rows_spec = pl.BlockSpec((160, 128), lambda i: (0, 0))
    results = pl.pallas_call(
        functools.partial(tail_kernel, len(rests), len(lasts)),
        out_shape=shapes + [like((1, *unit))] * (2 * len(rests) + 2 * len(lasts)),
        grid=(1,),
        in_specs=[VMEM_SPEC] * 18 + [rows_spec] * 2 + [ANY_SPEC] * (2 * len(rests) + 2 * len(lasts)),
        out_specs=[VMEM_SPEC] * (len(shapes) + len(rests)) + [ANY_SPEC] * (len(rests) + 2 * len(lasts)),
        scratch_shapes=[
            pltpu.SemaphoreType.DMA((40,)),
            pltpu.SemaphoreType.DMA((40,)),
            *slot_sum_scratch((SLOT, 768)),
            *slot_sum_scratch((64, 1024)),
            *slot_sum_scratch((512, SLOT)),
            pltpu.VMEM((8, *latent), BF16),
            *slot_sum_scratch(latent),
            pltpu.VMEM((2, *part_row), BF16),
            pltpu.VMEM((1, *part_row), BF16),
            pltpu.VMEM((1, *part_row), BF16),
            pltpu.VMEM((4, 160, KR + 128), BF16),
            pltpu.VMEM((1, 8, D), F32),
            pltpu.VMEM((1, 8, D), F32),
            pltpu.VMEM((1, 8, D), F32),
            pltpu.VMEM((D, 128), F32),
            pltpu.VMEM((SLOT, KR + 128), F32),
            pltpu.VMEM((2 * len(rests), *unit), BF16),
            pltpu.VMEM((len(rests), *unit), BF16),
            pltpu.SemaphoreType.DMA((1,)),
            pltpu.SemaphoreType.DMA((32,)),
            pltpu.VMEM((1, 160, 1024), BF16),
            pltpu.VMEM((1, 160, 1024), BF16),
            *split_scratch(rests)[:-1],
            *split_scratch(lasts)[:-1],
        ],
        compiler_params=pltpu.CompilerParams(
            collective_id=3, has_side_effects=True, vmem_limit_bytes=GIVEN_VMEM
        ),
        cost_estimate=cost(110),
        name="tail",
    )(
        part,
        output_wgrad,
        query_wgrad,
        keyval_wgrad,
        saved.normed,
        saved.w_latent,
        saved.gains,
        saved.latent_gain,
        saved.latent_c,
        saved.res,
        mid_grad,
        ffn_gain,
        output_came,
        saved.mid,
        saved.valid,
        *out_parts,
        saved.cos,
        saved.sin,
        *[v for keep, got, _ in rests + lasts for v in (keep, got)],
    )
    n = len(rests)
    return results[:6], results[6 : 6 + n], results[6 + n : 6 + 2 * n], list(zip(results[6 + 2 * n :: 2], results[7 + 2 * n :: 2]))


def finish_kernel(
    n_came,
    places,
    res_out_ref,
    res_grad_ref,
    latent_ref,
    *refs,
):
    refs = list(refs)
    take = lambda n: [refs.pop(0) for _ in range(n)]
    stays, cames, others = take(9), take(n_came), take(9)
    res_out, res_grad, latent, gains, expert_in, expert_out, shared_in, shared_out = refs
    for k in range(8):
        block = pl.ds(pl.multiple_of(places[k] * SLOT, SLOT), SLOT)
        res_out[:, block] = res_out_ref[:, lanes(k)]
        res_grad[:, block] = res_grad_ref[:, lanes(k)]
    latent[...] = latent_ref[:, : KR + RD]
    gains[...] = latent_ref[:, KR : KR + 128].T[64:72]
    side = places[8]
    n_half = expert_in.shape[0] // 2
    width = expert_out.shape[1]
    for p in range(n_half + 1):
        for mine in (True, False):
            which = side if mine else 1 - side
            for g in range(3):
                value = (stays if mine else others)[3 * p + g][0].astype(F32)
                late = 3 * p + g - 9 + n_came
                if mine and late >= 0:
                    value = value + cames[late][0].astype(F32)
                if p < n_half and g < 2:
                    expert_in[which * n_half + p, g] = value
                elif p < n_half:
                    expert_out[which * n_half + p] = value
                else:
                    cut = pl.ds(pl.multiple_of(which * width, 8), width)
                    if g < 2:
                        shared_in[g, cut] = value
                    else:
                        shared_out[cut] = value


def finish(places, res_out, res_grad, latent, stays, cames, others, width):
    shapes = [
        like(res_out.shape),
        like(res_grad.shape, F32),
        like((64, KR + RD), F32),
        like((8, 64), F32),
        like((EXPERTS, 2, width, SLOT), F32),
        like((EXPERTS, width, SLOT), F32),
        like((2, 2 * width, SLOT), F32),
        like((2 * width, SLOT), F32),
    ]
    return pl.pallas_call(
        functools.partial(finish_kernel, len(cames)),
        out_shape=shapes,
        in_specs=[SMEM_SPEC] + [VMEM_SPEC] * (21 + len(cames)),
        out_specs=[VMEM_SPEC] * len(shapes),
        compiler_params=pltpu.CompilerParams(vmem_limit_bytes=GIVEN_VMEM),
        cost_estimate=cost(10),
        name="finish",
    )(places, res_out, res_grad, latent, *stays, *cames, *others)


def body(
    res_in,
    out_grad,
    seg_ids,
    tok_counts,
    slot_table,
    slot_gates,
    attn_gain,
    latent_gain,
    ffn_gain,
    w_latent,
    w_query,
    w_keyval,
    w_output,
    w_expert_in,
    w_expert_out,
    w_shared_in,
    w_shared_out,
):
    dp = lax.axis_index(DP)
    rows = res_in.shape[0]
    first = ((dp >> 1) & 1) == 0
    n_half = EXPERTS // 2
    width = w_expert_out.shape[1]
    pack = jnp.concatenate(
        [
            w_latent,
            attn_gain[:, None],
            ffn_gain[:, None],
            jnp.pad(latent_gain, (0, w_latent.shape[0] - latent_gain.shape[0]))[:, None],
            jnp.zeros((w_latent.shape[0], 61), BF16),
        ],
        axis=1,
    )
    grad_pair, over_gate, lows, highs, saved = front(
        tok_counts,
        pack,
        w_keyval,
        w_output,
        w_expert_in,
        w_expert_out,
        w_shared_in,
        w_shared_out,
        res_in,
        out_grad,
        w_query,
        seg_ids,
        slot_table[0],
        slot_gates[0],
    )
    pair_gate = jnp.concatenate(
        [g[:, k * rows : (k + 1) * rows] for k in range(4) for g in (saved.gates, over_gate)], axis=1
    )
    pair_gate = jnp.where(first, pair_gate[:n_half], pair_gate[n_half : 2 * n_half])
    mid_pair = saved.mid_pair.reshape(-1, D)
    grad_pair = grad_pair.reshape(-1, D)
    ones = jnp.ones_like(pair_gate[0])
    whole = 3 * width
    low, high = lows[2], highs[2]
    sums, keep0, give0, (high_far,) = experts_step(
        mid_pair,
        grad_pair,
        [(lows[0], 0, 4, 0, whole, 0), (highs[0], 4, 4, 0, whole, 0)],
        pair_gate[0],
        None,
        False,
        [Cut(low, 0, (0, 4), (width, whole - width))],
        5,
    )
    sums, keep1, give1, (y0a, y0b) = experts_step(
        mid_pair,
        grad_pair,
        [(lows[1], 0, 4, 0, whole, 0), (highs[1], 4, 4, 0, whole, 0)],
        pair_gate[1],
        sums,
        False,
        [Cut(give0[0], 0), Cut(give0[1], 0)],
        6,
    )
    (k0a, h0a), (k0b, h0b) = halve([(keep0[0], y0a), (keep0[1], y0b)])
    (back, out), keep2, give2, (y0c, y1a, z0a, z0b) = experts_step(
        mid_pair,
        grad_pair,
        [
            (low, 0, 4, 0, whole, 0),
            (high, 4, 4, 0, width, 0),
            (high_far, 4, 4, width, whole - width, 0),
        ],
        ones,
        sums,
        True,
        [Cut(give0[2], 0), Cut(give1[0], 0), Cut(h0a, 2), Cut(h0b, 2)],
        7,
    )
    back = back.reshape(8, rows, D)
    out = out.reshape(8, rows, D)
    (mid_grad, ffn_gain_part, attn_grad), (y1b, y1c, y2a, y2b), split = back_tokens(
        back,
        saved.grad,
        saved.mid,
        saved.gains,
        saved.valid,
        [(0, give1[1]), (0, give1[2]), (0, give2[0]), (0, give2[1])],
        [(keep0[2], y0c, 2), (keep1[0], y1a, 2), (k0a, z0a, 1), (k0b, z0b, 1)],
    )
    (k0c, z0c), (k1a, z1a), over0a, over0b = split
    (*wgrads, back_part, out_sum, out_a, out_b), (y2c, output_came), split = attention_backward(
        attn_grad,
        saved,
        out,
        [(0, give2[2])],
        [(keep1[1], y1b, 2), (keep1[2], y1c, 2), (keep2[0], y2a, 2), (k0c, z0c, 1), (k1a, z1a, 1)],
    )
    (k1b, z1b), (k1c, z1c), (k2a, z2a), over0c, over1a = split
    (output_owned, query_owned, keyval_owned, latent_owned, res_grad, res_out), own2, over2, late = tail(
        back_part,
        wgrads,
        output_came,
        (out_sum, out_a, out_b),
        saved,
        mid_grad,
        ffn_gain_part,
        [(keep2[1], y2b, 2), (keep2[2], y2c, 2)],
        [(k1b, z1b, 1), (k1c, z1c, 1), (k2a, z2a, 1)],
    )
    ready = [over0a, over0b, over0c, over1a, *late]
    places = jnp.concatenate([dp ^ jnp.array(COLUMNS, jnp.int32), ((dp >> 1) & 1)[None]])
    res_out, res_grad, latent_owned, gains, expert_in, expert_out, shared_in, shared_out = finish(
        places,
        res_out,
        res_grad,
        latent_owned,
        [mine for mine, _ in ready] + list(own2),
        [],
        [other for _, other in ready] + list(over2),
        width,
    )
    return (
        res_out,
        res_grad,
        gains[0],
        gains[2, : KR // 32],
        gains[1],
        latent_owned,
        query_owned,
        keyval_owned,
        output_owned,
        expert_in.transpose(0, 1, 3, 2),
        expert_out,
        shared_in.transpose(0, 2, 1),
        shared_out,
    )


def solution(mesh):
    placed = (
        P((DP, TENSOR), None),
        P((DP, TENSOR), None),
        P(DP, None),
        P(DP),
        P(DP, None, None),
        P(DP, None, None),
        P((DP, TENSOR)),
        P((DP, TENSOR)),
        P((DP, TENSOR)),
        P((DP, TENSOR), None),
        P(DP, TENSOR),
        P(DP, TENSOR),
        P(TENSOR, DP),
        P(None, None, DP, TENSOR),
        P(None, TENSOR, DP),
        P(None, DP, TENSOR),
        P(TENSOR, DP),
    )
    fits = mesh.shape[DP] == 8 and mesh.shape[TENSOR] == 4
    return jax.shard_map(
        body if fits else general_body,
        mesh=mesh,
        in_specs=placed,
        out_specs=(
            P((DP, TENSOR), None),
            P((DP, TENSOR), None),
            P((DP, TENSOR)),
            P((DP, TENSOR)),
            P((DP, TENSOR)),
            P((DP, TENSOR), None),
            P(DP, TENSOR),
            P(DP, TENSOR),
            P(TENSOR, DP),
            P(None, None, DP, TENSOR),
            P(None, TENSOR, DP),
            P(None, DP, TENSOR),
            P(TENSOR, DP),
        ),
        check_vma=False,
    )
```

```python
import functools
import types

import jax
import jax.numpy as jnp
import numpy as np
from jax import lax
from jax.experimental import pallas as pl
from jax.experimental.pallas import tpu as pltpu
from jax.sharding import PartitionSpec as P

D = 2048
H = 16
HD = 128
RD = 64
VD = 128
KR = 512
TOK = 640
EXPERTS = 4


NORM_EPS = 1e-06
ROPE_BASE = 50000.0


def rms_factor(values):
    return lax.rsqrt(jnp.mean(values * values, axis=-1, keepdims=True) + NORM_EPS)


def norm_back(grad_out, values, factor, gain_vec):
    scaled = grad_out * gain_vec
    inner_sum = jnp.mean(scaled * values, axis=-1, keepdims=True)
    return (
        factor * (scaled - values * factor * factor * inner_sum),
        jnp.sum(grad_out * values * factor, axis=0),
    )


def rotary_tables(positions):
    half_width = RD // 2
    inv_freq = ROPE_BASE ** (-jnp.arange(half_width, dtype=jnp.float32) / half_width)
    angles = positions.astype(jnp.float32)[:, None] * inv_freq[None, :]
    return (jnp.cos(angles), jnp.sin(angles))


def rotate(values, cosine_table, sine_table):
    half_width = values.shape[-1] // 2
    first_half = values[..., :half_width]
    second_half = values[..., half_width:]
    return jnp.concatenate(
        [
            first_half * cosine_table - second_half * sine_table,
            second_half * cosine_table + first_half * sine_table,
        ],
        axis=-1,
    )


def silu_parts(gate_pre):
    sigma_gate = jax.nn.sigmoid(gate_pre)
    return (gate_pre * sigma_gate, sigma_gate * (1.0 + gate_pre * (1.0 - sigma_gate)))


def flip_pairs(count, bit):
    return [(i, i ^ (1 << bit)) for i in range(count)]


def swap_dp(values, bit):
    return lax.ppermute(values, DP, flip_pairs(lax.axis_size(DP), bit))


def swap_tensor(values, bit):
    return lax.ppermute(values, TENSOR, flip_pairs(lax.axis_size(TENSOR), bit))


def dp_bits():
    top = lax.axis_size(DP).bit_length() - 1
    return [1] + list(range(top - 1, 1, -1)) + [0]


def slot_order(bits):
    order = [0]
    for bit in bits:
        order = order + [j ^ (1 << bit) for j in order]
    return order


def select_blocks(blocks, index):
    step = 1
    while step < len(blocks):
        hit = (index & step) != 0
        blocks = [jnp.where(hit, blocks[i ^ step], blocks[i]) for i in range(len(blocks))]
        step *= 2
    return blocks


def to_slots(values, index, bits, axis):
    count = 1 << len(bits)
    blocks = select_blocks(jnp.split(values, count, axis=axis), index)
    return jnp.concatenate([blocks[j] for j in slot_order(bits)], axis=axis)


def from_slots(values, index, bits, axis):
    order = slot_order(bits)
    slots = jnp.split(values, len(order), axis=axis)
    blocks = [slots[order.index(i)] for i in range(len(order))]
    return jnp.concatenate(select_blocks(blocks, index), axis=axis)


def gather_dp(values, bits):
    for bit in bits:
        values = jnp.concatenate([values, swap_dp(values, bit)], axis=0)
    return values


def gather_tensor(values):
    for bit in (1, 0):
        values = jnp.concatenate([values, swap_tensor(values, bit)], axis=0)
    return values


def scatter_dp(values, bits, axis):
    values = values.astype(jnp.float32)
    for bit in reversed(bits):
        keep, give = jnp.split(values, 2, axis=axis)
        values = keep + swap_dp(give.astype(jnp.bfloat16), bit).astype(jnp.float32)
    return values


def scatter_tensor(values):
    for bit in (0, 1):
        keep, give = jnp.split(values, 2, axis=0)
        values = keep + swap_tensor(give.astype(jnp.bfloat16), bit).astype(jnp.float32)
    return values


def partner_columns(values):
    count = lax.axis_size(DP)
    slots = jnp.split(values, count, axis=-1)
    return jnp.concatenate([slots[k ^ 1] for k in range(count)], axis=-1)


def gather_pair(values, bit):
    over = swap_dp(partner_columns(values), bit)
    own = jnp.concatenate([values, over, swap_tensor(values, 1), swap_tensor(over, 1)], axis=0)
    return jnp.concatenate([own, swap_tensor(own, 0)], axis=0)


def scatter_pair(values, bit):
    values = scatter_tensor(values)
    keep, give = jnp.split(values, 2, axis=0)
    return keep + swap_dp(partner_columns(give).astype(jnp.bfloat16), bit).astype(jnp.float32)


def dot(a, b, contract):
    return lax.dot_general(a, b, (contract, ((), ())), preferred_element_type=jnp.float32)


def general_body(
    res_in,
    out_grad,
    seg_ids,
    tok_counts,
    slot_table,
    slot_gates,
    attn_gain,
    latent_gain,
    ffn_gain,
    w_latent,
    w_query,
    w_keyval,
    w_output,
    w_expert_in,
    w_expert_out,
    w_shared_in,
    w_shared_out,
):
    f32 = jnp.float32
    bf16 = jnp.bfloat16
    n_tensor = lax.axis_size(TENSOR)
    n_dp = lax.axis_size(DP)
    dp = lax.axis_index(DP)
    tensor = lax.axis_index(TENSOR)
    bits = dp_bits()
    merge = bits[0]
    half = (dp >> merge) & 1
    rows = res_in.shape[0]
    local_heads = H // n_tensor
    score_scale = (HD + RD) ** (-0.5)

    res_local = to_slots(res_in, dp, bits, 1)
    res_all = gather_tensor(res_local)
    tensor_slots = slot_order([1, 0])
    token_ids = jnp.concatenate(
        [(tensor ^ j) * rows + jnp.arange(rows, dtype=jnp.int32) for j in tensor_slots]
    )
    segment_canon = seg_ids[0]
    segment_row = jnp.concatenate(
        [lax.dynamic_slice_in_dim(segment_canon, (tensor ^ j) * rows, rows) for j in tensor_slots]
    )
    valid_all = (token_ids < tok_counts[0]).astype(f32)
    valid_rows = valid_all[:rows, None]
    group_gate = jnp.sum(
        jnp.where(slot_table[0][:, :, None] == token_ids[None, None, :], slot_gates[0][:, :, None], 0.0),
        axis=1,
    )
    grad_in = to_slots(out_grad, dp, bits, 1).astype(f32)
    ffn_grad = (valid_rows * grad_in).astype(bf16)

    pack_rows = w_latent.shape[0]
    gain_row = jnp.concatenate([attn_gain, ffn_gain, latent_gain])
    gain_row = jnp.pad(gain_row, (0, w_latent.shape[1] - gain_row.shape[0]))
    pack = jnp.concatenate([w_latent, jnp.broadcast_to(gain_row, (16, w_latent.shape[1]))], axis=0)
    pack = gather_dp(pack[None], bits)
    pack = gather_tensor(pack[None])
    pack_blocks = [pack[tensor_slots.index(j)] for j in range(n_tensor)]
    pack = jnp.stack(select_blocks(pack_blocks, tensor), axis=1)
    latent_full = pack[:, :, :pack_rows].reshape(D, KR + RD)
    gains = pack[:, :, pack_rows]
    gain_width, latent_width = D // (n_dp * n_tensor), KR // (n_dp * n_tensor)
    attn_gain_full = gains[..., :gain_width].reshape(D)
    ffn_gain_full = gains[..., gain_width : 2 * gain_width].reshape(D)
    latent_gain_full = from_slots(
        gains[..., 2 * gain_width : 2 * gain_width + latent_width].reshape(KR), dp, bits, 0
    )
    query_full = gather_dp(w_query, bits)
    keyval_full = from_slots(gather_dp(w_keyval, bits), dp, bits, 0)
    output_full = gather_dp(w_output[None], bits)
    output_full = jnp.concatenate([output_full[k] for k in range(n_dp)], axis=1)

    n_half = EXPERTS // 2
    expert_units = jnp.concatenate(
        [
            w_expert_in.transpose(0, 1, 3, 2).reshape(EXPERTS, -1, w_expert_in.shape[2]),
            w_expert_out,
        ],
        axis=1,
    )
    width = w_expert_out.shape[1]
    shared_t = w_shared_in.transpose(0, 2, 1)
    units = []
    for side in range(2):
        cut = slice(side * width, (side + 1) * width)
        shared_unit = jnp.concatenate([shared_t[0, cut], shared_t[1, cut], w_shared_out[cut]], axis=0)
        units.append(jnp.concatenate([expert_units[side * n_half : (side + 1) * n_half], shared_unit[None]], axis=0))
    first = half == 0
    own_units = jnp.where(first, units[0], units[1])
    other_units = jnp.where(first, units[1], units[0])
    pieces = []
    for p in range(n_half + 1):
        piece = jnp.stack([own_units[p], swap_dp(other_units[p], merge)], axis=0)
        piece = gather_dp(piece, bits[1:])
        pieces.append(jnp.concatenate([piece[k] for k in range(n_dp)], axis=1))

    positions = token_ids - jnp.sum(
        (segment_canon[None, :] < segment_row[:, None]).astype(jnp.int32), axis=1
    )
    cos_all, sin_all = rotary_tables(positions)
    allowed = (segment_row[:, None] == segment_row[None, :]) & (
        token_ids[None, :] <= token_ids[:, None]
    )
    resid_all = res_all.astype(f32)
    in_factor = rms_factor(resid_all)
    normed_all = (resid_all * in_factor * attn_gain_full).astype(bf16)
    latent_raw = jnp.dot(normed_all, latent_full, preferred_element_type=f32)
    latent_c = latent_raw[:, :KR]
    latent_factor = rms_factor(latent_c)
    latent_norm = (latent_c * latent_factor * latent_gain_full).astype(bf16)
    rope_all = rotate(latent_raw[:, KR:], cos_all, sin_all).astype(bf16)
    query_raw = jnp.dot(normed_all, query_full, preferred_element_type=f32).reshape(
        TOK, local_heads, HD + RD
    )
    query_final = jnp.concatenate(
        [
            query_raw[..., :HD],
            rotate(query_raw[..., HD:], cos_all[:, None, :], sin_all[:, None, :]),
        ],
        axis=-1,
    ).astype(bf16)
    keyval = (
        jnp.dot(latent_norm, keyval_full, preferred_element_type=f32)
        .astype(bf16)
        .reshape(TOK, local_heads, HD + VD)
    )
    key_nope = keyval[..., :HD]
    values_all = keyval[..., HD:]
    raw_scores = jnp.einsum(
        "qhd,khd->hqk", query_final[..., :HD], key_nope, preferred_element_type=f32
    )
    raw_scores = raw_scores + jnp.einsum(
        "qhr,kr->hqk", query_final[..., HD:], rope_all, preferred_element_type=f32
    )
    scores = jnp.where(allowed[None], raw_scores * score_scale, -1e30)
    top_score = jnp.max(scores, axis=-1, keepdims=True)
    exp_scores = jnp.exp(scores - top_score)
    probs_all = exp_scores / jnp.sum(exp_scores, axis=-1, keepdims=True)
    probs_low = probs_all.astype(bf16)
    attn_mix = (
        jnp.einsum("hqk,khd->qhd", probs_low, values_all, preferred_element_type=f32)
        .astype(bf16)
        .reshape(TOK, local_heads * VD)
    )
    attn_part = jnp.dot(attn_mix, output_full, preferred_element_type=f32)
    attn_out = scatter_tensor(attn_part)
    resid_in = res_local.astype(f32)
    mid_resid = resid_in + valid_rows * attn_out
    mid_factor = rms_factor(mid_resid)
    normed_mid = (mid_resid * mid_factor * ffn_gain_full).astype(bf16)

    mid_pair = gather_pair(normed_mid, merge)
    grad_pair = gather_pair(ffn_grad, merge)
    other_gate = swap_dp(group_gate, merge)
    pair_gate = jnp.concatenate(
        [
            gate[:, k * rows : (k + 1) * rows]
            for k in ((0, 0), (1, 0), (0, 1), (1, 1), (0, 2), (1, 2), (0, 3), (1, 3))
            for gate, k in (((group_gate, other_gate)[k[0]], k[1]),)
        ],
        axis=1,
    )
    pair_gate = jnp.where(first, pair_gate[:n_half], pair_gate[n_half:])
    mid_pair_grad = None
    hidden_parts, out_parts, unit_grads = [], [], []
    for p, piece in enumerate(pieces):
        gate_up = dot(piece[: 2 * width], mid_pair, ((1,), (1,)))
        gate_pre, up = gate_up[:width], gate_up[width:]
        silu, slope = silu_parts(gate_pre)
        hidden_grad = dot(piece[2 * width :], grad_pair, ((1,), (1,)))
        hidden = silu * up
        if p < n_half:
            hidden = hidden * pair_gate[p][None]
            hidden_grad = hidden_grad * pair_gate[p][None]
        hidden = hidden.astype(bf16)
        pre_grad = jnp.concatenate(
            [(hidden_grad * up * slope).astype(bf16), (hidden_grad * silu).astype(bf16)], axis=0
        )
        back = dot(pre_grad, piece[: 2 * width], ((0,), (0,)))
        mid_pair_grad = back if mid_pair_grad is None else mid_pair_grad + back
        hidden_parts.append(hidden)
        out_parts.append(piece[2 * width :])
        in_wgrad = dot(pre_grad, mid_pair, ((1,), (0,)))
        out_wgrad = dot(hidden, grad_pair, ((1,), (0,)))
        unit_grads.append(jnp.concatenate([in_wgrad, out_wgrad], axis=0).astype(bf16))
    ffn_part = dot(
        jnp.concatenate(hidden_parts, axis=0), jnp.concatenate(out_parts, axis=0), ((0,), (0,))
    )
    ffn_out = scatter_pair(ffn_part, merge)
    res_out = (mid_resid + valid_rows * ffn_out).astype(bf16)
    mid_grad_local = scatter_pair(mid_pair_grad, merge)

    mid_back, ffn_gain_part = norm_back(mid_grad_local, mid_resid, mid_factor, ffn_gain_full)
    mid_grad = grad_in + mid_back
    attn_grad = (valid_rows * mid_grad).astype(bf16)
    attn_grad_all = gather_tensor(attn_grad)
    output_wgrad = dot(attn_mix, attn_grad_all, ((0,), (0,)))
    mix_grad = (
        dot(attn_grad_all, output_full, ((1,), (1,))).astype(bf16).reshape(TOK, local_heads, VD)
    )
    probs_grad = jnp.einsum("qhd,khd->hqk", mix_grad, values_all, preferred_element_type=f32)
    value_grad = jnp.einsum("hqk,qhd->khd", probs_low, mix_grad, preferred_element_type=f32)
    scores_grad = (
        probs_all * (probs_grad - jnp.sum(probs_all * probs_grad, axis=-1, keepdims=True))
    ).astype(bf16)
    query_nope_grad = (
        jnp.einsum("hqk,khd->qhd", scores_grad, key_nope, preferred_element_type=f32) * score_scale
    )
    query_rope_grad = (
        jnp.einsum("hqk,kr->qhr", scores_grad, rope_all, preferred_element_type=f32) * score_scale
    )
    key_nope_grad = (
        jnp.einsum("hqk,qhd->khd", scores_grad, query_final[..., :HD], preferred_element_type=f32)
        * score_scale
    )
    rope_key_grad = (
        jnp.einsum("hqk,qhr->kr", scores_grad, query_final[..., HD:], preferred_element_type=f32)
        * score_scale
    )
    query_grad = (
        jnp.concatenate(
            [query_nope_grad, rotate(query_rope_grad, cos_all[:, None, :], -sin_all[:, None, :])],
            axis=-1,
        )
        .astype(bf16)
        .reshape(TOK, local_heads * (HD + RD))
    )
    keyval_grad = (
        jnp.concatenate([key_nope_grad, value_grad], axis=-1)
        .astype(bf16)
        .reshape(TOK, local_heads * (HD + VD))
    )
    latent_part = jnp.concatenate([dot(keyval_grad, keyval_full, ((1,), (1,))), rope_key_grad], axis=1)
    latent_grad_local = scatter_tensor(latent_part)
    normed_part = dot(query_grad, query_full, ((1,), (1,)))
    normed_grad_local = scatter_tensor(normed_part)
    query_wgrad = dot(normed_all, query_grad, ((0,), (0,)))
    keyval_wgrad = to_slots(dot(latent_norm, keyval_grad, ((0,), (0,))).astype(bf16), dp, bits, 0)
    latent_c_grad, latent_gain_part = norm_back(
        latent_grad_local[:, :KR], latent_c[:rows], latent_factor[:rows], latent_gain_full
    )
    rope_raw_grad = rotate(latent_grad_local[:, KR:], cos_all[:rows], -sin_all[:rows])
    latent_raw_grad = jnp.concatenate([latent_c_grad, rope_raw_grad], axis=1).astype(bf16)
    latent_raw_grad_all = gather_tensor(latent_raw_grad)
    latent_wgrad = dot(normed_all, latent_raw_grad_all, ((0,), (0,))).astype(bf16)
    latent_wgrad = lax.dynamic_index_in_dim(
        latent_wgrad.reshape(n_dp, n_tensor, pack_rows, KR + RD), tensor, 1, keepdims=False
    )
    normed_grad = normed_grad_local + dot(latent_raw_grad, latent_full, ((1,), (1,)))
    in_back, attn_gain_part = norm_back(normed_grad, resid_in, in_factor[:rows], attn_gain_full)
    res_grad = mid_grad + in_back

    output_owned = scatter_dp(output_wgrad, bits, 1)
    query_owned = scatter_dp(query_wgrad, bits, 0)
    keyval_owned = scatter_dp(keyval_wgrad, bits, 0)
    latent_owned = scatter_dp(latent_wgrad, bits, 0)[0]
    gain_parts = jnp.concatenate(
        [
            attn_gain_part.reshape(n_dp, n_tensor, gain_width),
            ffn_gain_part.reshape(n_dp, n_tensor, gain_width),
            to_slots(latent_gain_part, dp, bits, 0).reshape(n_dp, n_tensor, latent_width),
        ],
        axis=2,
    )
    gain_parts = jnp.stack(
        [
            select_blocks([gain_parts[:, i] for i in range(n_tensor)], tensor)[j]
            for j in tensor_slots
        ],
        axis=0,
    )
    for bit in (0, 1):
        keep, give = jnp.split(gain_parts, 2, axis=0)
        gain_parts = keep + swap_tensor(give, bit)
    gain_parts = gain_parts[0]
    for bit in reversed(bits):
        keep, give = jnp.split(gain_parts, 2, axis=0)
        gain_parts = keep + swap_dp(give, bit)
    gain_owned = gain_parts[0]
    own_grads, other_grads = [], []
    for grad in unit_grads:
        grad = grad.astype(f32)
        for bit in reversed(bits[1:]):
            keep, give = jnp.split(grad, 2, axis=1)
            grad = keep + swap_dp(give.astype(bf16), bit).astype(f32)
        keep, give = jnp.split(grad, 2, axis=1)
        own_grads.append(keep)
        other_grads.append(swap_dp(give.astype(bf16), merge).astype(f32))
    sides = []
    for side in (first, ~first):
        sides.append([jnp.where(side, a, b) for a, b in zip(own_grads, other_grads)])
    expert_units = jnp.stack([unit for side in sides for unit in side[:n_half]], axis=0)
    expert_in_owned = expert_units[:, : 2 * width].reshape(EXPERTS, 2, width, -1).transpose(0, 1, 3, 2)
    expert_out_owned = expert_units[:, 2 * width :]
    shared_in_owned = jnp.stack(
        [
            jnp.concatenate([side[n_half][k * width : (k + 1) * width] for side in sides], axis=0).T
            for k in range(2)
        ],
        axis=0,
    )
    shared_out_owned = jnp.concatenate([side[n_half][2 * width :] for side in sides], axis=0)
    return (
        from_slots(res_out, dp, bits, 1),
        from_slots(res_grad, dp, bits, 1),
        gain_owned[:gain_width],
        gain_owned[2 * gain_width :],
        gain_owned[gain_width : 2 * gain_width],
        latent_owned,
        query_owned,
        keyval_owned,
        output_owned,
        expert_in_owned,
        expert_out_owned,
        shared_in_owned,
        shared_out_owned,
    )


DP, TENSOR = "dp", "tensor"
MESH = pl.DeviceIdType.MESH
F32 = jnp.float32
BF16 = jnp.bfloat16
CHUNKS = 3
SECONDS = 9
THIRDS = 7
SLOT = 256
GIVEN_VMEM = 60 * 1024 * 1024
FAR_FIRST = (2, 1, 0)
FLIPS = (1, 2, 0)
TENSOR_BITS = (1, 0)


COLUMNS = slot_order(FAR_FIRST)
UNIT_SLOTS = slot_order(FLIPS)
ROWS = slot_order(TENSOR_BITS)


def nn(a, b):
    return lax.dot_general(a, b, (((1,), (0,)), ((), ())), preferred_element_type=F32)


def nt(a, b):
    return lax.dot_general(a, b, (((1,), (1,)), ((), ())), preferred_element_type=F32)


def tn(a, b):
    return lax.dot_general(a, b, (((0,), (0,)), ((), ())), preferred_element_type=F32)


def lanes(k, width=SLOT):
    return slice(k * width, (k + 1) * width)


def crossed(index, constant, bits):
    total = 0
    for bit in range(bits):
        own = lax.rem(index // (1 << bit), 2)
        total = total + ((1 - own) if (constant >> bit) & 1 else own) * (1 << bit)
    return total


class Copies:
    def __init__(self, send_sems, recv_sems, local_sems=None):
        self.send_sems, self.recv_sems, self.local_sems = send_sems, recv_sems, local_sems
        self.count = 0
        self.local_count = 0

    def across(self, axis, bit):
        index = lax.axis_index(axis)
        side = lax.rem(index // (1 << bit), 2)
        return {axis: index + (1 - 2 * side) * (1 << bit)}

    def start(self, source, target, axis, bit):
        copy = pltpu.make_async_remote_copy(
            src_ref=source,
            dst_ref=target,
            send_sem=self.send_sems.at[self.count],
            recv_sem=self.recv_sems.at[self.count],
            device_id=self.across(axis, bit),
            device_id_type=MESH,
        )
        self.count += 1
        copy.start()
        return copy

    def local(self, source, target):
        copy = pltpu.make_async_copy(source, target, self.local_sems.at[self.local_count])
        self.local_count += 1
        copy.start()
        return copy

    def greet(self, dp_bits, tensor_bits=TENSOR_BITS):
        barrier = pltpu.get_barrier_semaphore()
        for axis, bits in ((DP, dp_bits), (TENSOR, tensor_bits)):
            for bit in bits:
                pl.semaphore_signal(
                    barrier, inc=1, device_id=self.across(axis, bit), device_id_type=MESH
                )
        pl.semaphore_wait(barrier, len(dp_bits) + len(tensor_bits))

    def swapped(self, source, target, first, width):
        parts = []
        for a in range(first, first + width, 1024):
            for b, c in ((a, a + 512), (a + 512, a)):
                parts.append(
                    self.start(
                        source.at[(slice(None),) * (len(source.shape) - 1) + (pl.ds(b, 512),)],
                        target.at[(slice(None),) * (len(target.shape) - 1) + (pl.ds(c, 512),)],
                        DP,
                        1,
                    )
                )
        return Several(parts)


class Several:
    def __init__(self, parts):
        self.parts = parts

    def wait(self):
        for part in self.parts:
            part.wait()


class SlotGather:
    def __init__(self, copies, source, slots, bits, axis=DP, cut=None):
        self.copies, self.source, self.slots, self.bits, self.axis = copies, source, slots, list(bits), axis
        self.cut = (slice(None),) if cut is None else (pl.ds(*cut),)
        self.done, self.have, self.own, self.flying = 0, 1, None, None

    def view(self, first, count):
        return self.slots.at[(pl.ds(first, count), *self.cut)]

    def start(self):
        bit = self.bits[self.done]
        if self.done == 0 and self.source is not None:
            source = self.source.at[(pl.ds(0, 1), *self.cut)]
            self.own = self.copies.local(source, self.view(0, 1))
        else:
            if self.own is not None:
                self.own.wait()
                self.own = None
            source = self.view(0, self.have)
        self.flying = self.copies.start(source, self.view(self.have, self.have), self.axis, bit)
        self.done += 1
        self.have *= 2

    def wait(self):
        self.flying.wait()
        self.flying = None
        if self.done < len(self.bits):
            self.start()

    def finish(self):
        while self.flying is not None:
            self.wait()


ANY_SPEC = pl.BlockSpec(memory_space=pl.ANY)
VMEM_SPEC = pl.BlockSpec(memory_space=pltpu.VMEM)
SMEM_SPEC = pl.BlockSpec(memory_space=pltpu.SMEM)


def cost(micros):
    return pl.CostEstimate(flops=micros * 10**9, bytes_accessed=micros * 10**6, transcendentals=0)


def like(shape, dtype=BF16):
    return jax.ShapeDtypeStruct(shape, dtype)


def turn(a, b, cos, sin):
    return a * cos - b * sin, b * cos + a * sin


def head_lanes(rows, head):
    lane = lax.broadcasted_iota(jnp.int32, (rows, SLOT), 1)
    return lax.rem(lane // 32, 4) == head


def spread_block(copies, pair_ref, between):
    block = lambda k: pair_ref.at[pl.ds(k, 1)]
    x_own = copies.start(block(0), block(2), TENSOR, 1)
    z_own = copies.swapped(block(0), block(1), 0, D)
    waits = [copies.start(block(0), block(4), TENSOR, 0)]
    between()
    z_own.wait()
    over_both = copies.start(block(1), block(3), TENSOR, 1)
    waits.append(copies.start(block(1), block(5), TENSOR, 0))
    between()
    x_own.wait()
    waits.append(copies.start(block(2), block(6), TENSOR, 0))
    between()
    over_both.wait()
    waits.append(copies.start(block(3), block(7), TENSOR, 0))
    for copy in waits:
        copy.wait()


class Places:
    def __init__(self):
        self.dp, self.tensor = lax.axis_index(DP), lax.axis_index(TENSOR)

    def __getitem__(self, k):
        if k == 12:
            return lax.rem(self.dp // 2, 2)
        return crossed(self.dp, COLUMNS[k], 3) if k < 8 else crossed(self.tensor, ROWS[k - 8], 2)


class Kept:
    output = ((8, 512, SLOT), BF16)
    mix = ((TOK, 512), BF16)
    query_final = ((TOK, 768), BF16)
    keyval_final = ((TOK, 1024), BF16)
    key_rope = ((TOK, SLOT), BF16)
    lse = ((TOK, 128), F32)
    query = ((8, SLOT, 768), BF16)
    w_keyval = ((KR, 1024), BF16)
    normed = ((TOK, D), BF16)
    latent_norm = ((TOK, KR), BF16)
    col = ((TOK, 128), F32)
    row = ((8, TOK), F32)
    cos = ((TOK, 128), F32)
    sin = ((TOK, 128), F32)
    gains = ((8, D), F32)
    latent_gain = ((8, KR), F32)
    latent_c = ((160, KR), F32)
    w_latent = ((D, KR + 128), BF16)
    mid = ((160, D), F32)
    mid_pair = ((8, 160, D), BF16)
    res = ((160, D), BF16)
    grad = ((160, D), BF16)
    valid = ((160, 128), F32)
    gates = ((8, TOK), F32)


class Landing:
    tokens = ((4, 160, D), BF16)
    pack = ((4, 8, 64, KR + 128), BF16)
    keyval = ((8, 64, 1024), BF16)
    part = ((4, 160, D), BF16)
    got_c = ((2, 160, D), BF16)
    give_x = ((1, 160, D), BF16)
    got_x = ((1, 160, D), BF16)
    gain_rows = ((KR, 128), BF16)
    masked = ((1, 160, D), BF16)
    own_pack = ((1, 64, KR + 128), BF16)
    own_query = ((1, SLOT, 768), BF16)


def fields(kind):
    return [name for name in vars(kind) if not name.startswith("_")]


def buffers(kind):
    return [getattr(kind, name) for name in fields(kind)]


def masks(col, row, cut):
    return (col[cut, 0:1] == row[0:1]) & (row[1:2] <= col[cut, 1:2])


def sort_columns(rows):
    column = lax.broadcasted_iota(jnp.int32, (768, 768), 1)
    row = lax.broadcasted_iota(jnp.int32, (768, 768), 0)
    wide = (column // 128) * 192 + lax.rem(column, 128)
    late = column - 512
    narrow = (lax.rem(late, 128) // 32) * 192 + 128 + (late // 128) * 32 + lax.rem(late, 32)
    return jnp.where(row == jnp.where(column < 512, wide, narrow), 1.0, 0.0).astype(BF16)


def front_kernel(
    width,
    count_ref,
    keyval_ref,
    output_ref,
    expert_in,
    expert_out,
    shared_in,
    shared_out,
    res_ref,
    grad_ref,
    query_ref,
    segment_row,
    table_ref,
    slot_gates,
    frequency_ref,
    latent_ref,
    attn_gain_ref,
    ffn_gain_ref,
    latent_gain_ref,
    grad_pair,
    gates_over,
    *rest,
):
    n_units = 3
    lows, highs = rest[:n_units], rest[n_units : 2 * n_units]
    rest = rest[2 * n_units :]
    kept, names = fields(Kept), fields(Kept) + fields(Landing)
    outs = types.SimpleNamespace(**dict(zip(kept, rest)))
    rest = rest[len(kept) :]
    at = types.SimpleNamespace(**dict(zip(names, rest)))
    send_sems, recv_sems, local_sems = rest[len(names) :]
    copies = Copies(send_sems, recv_sems, local_sems)
    places = Places()
    saved = []

    def save(pick):
        for source, target in zip(pick(at), pick(outs)):
            saved.append(copies.local(source, target))

    at.own_pack[0] = jnp.zeros((64, KR + 128), BF16)
    at.own_pack[0, :, : KR + RD] = latent_ref[...]
    lane = lax.broadcasted_iota(jnp.int32, (64, 128), 1)
    ends = at.own_pack[0, :, KR:].astype(F32)
    for k, gain_ref in ((64, attn_gain_ref), (65, ffn_gain_ref)):
        column = jnp.broadcast_to(gain_ref[...].astype(F32), (8, 64)).T[:, 0:1]
        ends = jnp.where(lane == k, column, ends)
    at.own_pack[0, :, KR:] = ends.astype(BF16)
    column = jnp.broadcast_to(latent_gain_ref[...].astype(F32), (8, 16)).T[:, 0:1]
    lane = lax.broadcasted_iota(jnp.int32, (16, 128), 1)
    at.own_pack[0, 0:16, KR:] = jnp.where(lane == 66, column, ends[0:16]).astype(BF16)
    pack = SlotGather(copies, at.own_pack, at.pack.at[0], FAR_FIRST)
    copies.greet((0, 1, 2))
    keyval = SlotGather(copies, keyval_ref, at.keyval, FAR_FIRST)
    part = query_ref.shape[0] // 4
    queries = [
        SlotGather(copies, at.own_query, at.query, FAR_FIRST, cut=(k * part, part)) for k in range(4)
    ]
    part = output_ref.shape[1] // 2
    outputs = [SlotGather(copies, output_ref, at.output, FAR_FIRST, cut=(k * part, part)) for k in range(2)]
    pack.start()
    keyval.start()
    for k in range(8):
        block = pl.ds(pl.multiple_of(places[k] * SLOT, SLOT), SLOT)
        at.res[:, lanes(k)] = res_ref[:, block]
        at.grad[:, lanes(k)] = grad_ref[:, block]
    at.tokens[0] = at.res[...]
    tokens = SlotGather(copies, None, at.tokens, TENSOR_BITS, TENSOR)
    tokens.start()
    at.own_query[0] = nn(query_ref[...], sort_columns(768)).astype(BF16)
    items = [pack, keyval, *queries, *outputs]
    units = [(p, part) for p in range(n_units) for part in range(CHUNKS)]
    flights = [None] * len(units)
    owns = [None] * len(units)
    state = [0, 0, 0]

    def unit_source(side, p, part):
        if p < 2:
            expert = pl.ds(side * 2 + p, 1)
            return expert_out.at[expert] if part == 2 else expert_in.at[expert, part]
        cut = pl.ds(pl.multiple_of(side * width, 16), width)
        return shared_out.at[pl.ds(0, 1), cut] if part == 2 else shared_in.at[pl.ds(part, 1), cut]

    def unit_first():
        i = state[0]
        if i >= len(units):
            return
        p, part = units[i]
        cut = pl.ds(part * width, width)
        side = places[12]
        owns[i] = copies.local(unit_source(side, p, part), lows[p].at[pl.ds(0, 1), cut])
        flights[i] = copies.start(
            unit_source(1 - side, p, part), lows[p].at[pl.ds(1, 1), cut], DP, FLIPS[0]
        )
        state[0] = i + 1

    def unit_second():
        i = state[1]
        if i >= min(state[0], SECONDS):
            return
        p, part = units[i]
        cut = pl.ds(part * width, width)
        flights[i].wait()
        owns[i].wait()
        flights[i] = copies.start(
            lows[p].at[pl.ds(0, 2), cut], lows[p].at[pl.ds(2, 2), cut], DP, FLIPS[1]
        )
        state[1] = i + 1

    def unit_third():
        i = state[2]
        if i >= min(state[1], THIRDS):
            return
        p, part = units[i]
        cut = pl.ds(part * width, width)
        flights[i].wait()
        flights[i] = copies.start(lows[p].at[pl.ds(0, 4), cut], highs[p].at[pl.ds(0, 4), cut], DP, FLIPS[2])
        state[2] = i + 1

    def pump():
        unit_third()
        unit_second()
        unit_first()

    def place_tokens():
        segments = segment_row[...].astype(F32)
        at.col[:, 0:8] = jnp.broadcast_to(segments, (8, TOK)).T
        for b in range(4):
            start = pl.multiple_of(places[8 + b] * 160, 8)
            at.cos[b * 160 : (b + 1) * 160] = jnp.broadcast_to(at.col[pl.ds(start, 160), 0:1], (160, 128))
        for b in range(4):
            start = pl.multiple_of(places[8 + b] * 160, 8)
            cut = slice(b * 160, (b + 1) * 160)
            segment = at.cos[cut, 0:1]
            token = start + lax.broadcasted_iota(jnp.int32, (160, 128), 0)
            lane = lax.broadcasted_iota(jnp.int32, (160, 128), 1)
            at.col[cut] = jnp.where(lane == 0, segment, token.astype(F32))
            before = jnp.sum((segments < segment).astype(F32), axis=1, keepdims=True)
            angle = (token.astype(F32) - before) * frequency_ref[...]
            at.cos[cut] = jnp.cos(angle)
            at.sin[cut] = jnp.sin(angle)
        at.row[...] = at.col[...].T[0:8]
        at.valid[...] = (at.col[0:160, 1:2] < count_ref[0].astype(F32)).astype(F32) + jnp.zeros((160, 128), F32)
        at.masked[0] = (at.grad[...].astype(F32) * at.valid[:, 0:1]).astype(BF16)

    def route_tokens():
        slots = jnp.concatenate([table_ref[...].astype(F32), slot_gates[...]], axis=0).T
        token_row = at.row[1:2]
        for e in range(4):
            hit = jnp.where(slots[:, e : e + 1] == token_row, slots[:, 4 + e : 5 + e], 0.0)
            at.gates[e : e + 1] = jnp.sum(hit, axis=0, keepdims=True)
        at.gates[4:8] = jnp.zeros((4, TOK), F32)
        save(lambda v: (v.col, v.row, v.cos, v.sin, v.valid, v.res, v.grad, v.gates))

    def make_keys():
        for s in range(4):
            for k in range(8):
                start = pl.multiple_of(k * SLOT + places[8 + s] * 64, 64)
                at.w_latent[pl.ds(start, 64)] = at.pack[s, k]
                start = pl.multiple_of(places[k] * 64 + places[8 + s] * 16, 16)
                at.gain_rows[pl.ds(start, 16)] = at.pack[s, k, 0:16, KR : KR + 128]
        for k in range(8):
            at.w_keyval[pl.ds(pl.multiple_of(places[k] * 64, 64), 64)] = at.keyval[k]
        tail = at.w_latent[:, KR : KR + 128]
        turned = tail.astype(F32).T
        attn_gain = turned[64:65]
        at.gains[...] = turned[64:72]
        latent_gain = at.gain_rows[...].astype(F32).T[66:67]
        at.latent_gain[...] = jnp.broadcast_to(latent_gain, (8, KR))
        row = lax.broadcasted_iota(jnp.int32, (128, SLOT), 0)
        lane = lax.broadcasted_iota(jnp.int32, (128, SLOT), 1)
        spread = jnp.where(row == lax.rem(lane, 32) + 32 * (lane // 128), 1.0, 0.0).astype(BF16)
        w_rope = nn(tail, spread).astype(BF16)
        for b in range(4):
            cut = slice(b * 160, (b + 1) * 160)
            x = at.tokens[b].astype(F32)
            factor = lax.rsqrt(jnp.mean(x * x, axis=1, keepdims=True) + NORM_EPS)
            at.normed[cut] = (x * factor * attn_gain).astype(BF16)
        for b in range(2):
            cut = slice(b * 320, (b + 1) * 320)
            normed = at.normed[cut]
            latent_c = nn(normed, at.w_latent[:, :KR])
            factor = lax.rsqrt(jnp.mean(latent_c * latent_c, axis=1, keepdims=True) + NORM_EPS)
            latent_norm = (latent_c * factor * latent_gain).astype(BF16)
            if b == 0:
                at.latent_c[...] = latent_c[:160]
            at.latent_norm[cut] = latent_norm
            rope = nn(normed, w_rope)
            key_a, key_b = turn(rope[:, :128], rope[:, 128:], at.cos[cut], at.sin[cut])
            at.key_rope[cut] = jnp.concatenate([key_a, key_b], axis=1).astype(BF16)
            at.keyval_final[cut] = nn(latent_norm, at.w_keyval[...]).astype(BF16)
        save(lambda v: (v.w_latent, v.w_keyval, v.gains, v.latent_gain, v.normed, v.latent_c, v.latent_norm, v.key_rope, v.keyval_final,))


    unit_first()
    for tau in range(len(items) + 1):
        if tau >= 1:
            items[tau - 1].wait()
        if tau < len(items):
            items[tau].wait()
        if tau + 2 < len(items):
            items[tau + 2].start()
        if tau == 0:
            place_tokens()
        elif tau == 1:
            tokens.wait()
            grad_own = copies.local(at.masked, grad_pair.at[pl.ds(0, 1)])
            grad_x = copies.start(at.masked, grad_pair.at[pl.ds(2, 1)], TENSOR, 1)
        elif tau == 3:
            pack.wait()
            pack_tensor = SlotGather(copies, None, at.pack, TENSOR_BITS, TENSOR)
            pack_tensor.start()
            unit_second()
        elif tau == 4:
            unit_first()
            route_tokens()
            gates_flight = copies.start(at.gates, gates_over, DP, 1)
        elif tau == 5:
            tokens.wait()
            unit_second()
        elif tau == 6:
            pack_tensor.wait()
            unit_first()
        elif tau == 7:
            keyval.wait()
            pack_tensor.wait()
            make_keys()
            unit_second()
    grad_x.wait()
    grad_z = copies.swapped(at.masked, grad_pair.at[pl.ds(1, 1)], 0, D)
    pump()
    for query in queries:
        query.wait()

    save(lambda v: (v.query,))
    gates_flight.wait()
    w_query = at.query[...].reshape(D, 768)
    scale = (HD + RD) ** (-0.5)
    for b in range(2):
        cut = slice(b * 320, (b + 1) * 320)
        found = nn(at.normed[cut], w_query)
        turned_a, turned_b = turn(found[:, 512:640], found[:, 640:768], at.cos[cut], at.sin[cut])
        at.query_final[cut] = jnp.concatenate([found[:, :512], turned_a, turned_b], axis=1).astype(BF16)
        allowed = masks(at.col, at.row, cut)
        lse_lane = lax.broadcasted_iota(jnp.int32, (320, 128), 1)
        lse_all = jnp.zeros((320, 128), F32)
        for h in range(4):
            rope = at.query_final[cut, 512:768]
            rope = jnp.where(head_lanes(320, h), rope, jnp.zeros_like(rope))
            keys = at.keyval_final[:, h * 256 : h * 256 + 128]
            scores = nt(at.query_final[cut, lanes(h, 128)], keys) + nt(rope, at.key_rope[...])
            scores = jnp.where(allowed, scores * scale, -1e30)
            top = jnp.max(scores, axis=1, keepdims=True)
            weight = jnp.exp(scores - top)
            total = jnp.sum(weight, axis=1, keepdims=True)
            probs = (weight / total).astype(BF16)
            lse_all = jnp.where(lse_lane == h, top + jnp.log(total), lse_all)
            mix = nn(probs, at.keyval_final[:, h * 256 + 128 : h * 256 + 256])
            at.mix[cut, lanes(h, 128)] = mix.astype(BF16)
        at.lse[cut] = lse_all
        if b == 0:
            pump()
            grad_z.wait()
            grad_zx = copies.start(
                grad_pair.at[pl.ds(1, 1)], grad_pair.at[pl.ds(3, 1)], TENSOR, 1
            )
    for output in outputs:
        output.wait()
    save(lambda v: (v.query_final, v.mix, v.lse, v.output,))
    for b in range(2):
        cut = slice((1 - b) * 320, (2 - b) * 320)
        for k in range(8):
            w_output = at.output[k]
            part = nn(at.mix[cut], w_output).astype(BF16)
            at.part[2 - 2 * b, :, lanes(k)] = part[:160]
            at.part[3 - 2 * b, :, lanes(k)] = part[160:]
        if b == 0:
            block = lambda ref, k: ref.at[pl.ds(k, 1)]
            c_far = copies.start(block(at.part, 3), block(at.got_c, 1), TENSOR, 0)
            c_near = copies.start(block(at.part, 2), block(at.got_c, 0), TENSOR, 0)
    c_far.wait()
    at.give_x[0] = (at.part[1].astype(F32) + at.got_c[1].astype(F32)).astype(BF16)
    x_far = copies.start(at.give_x, at.got_x, TENSOR, 1)
    pump()
    grad_zx.wait()
    grad_own.wait()
    grad_c = copies.start(grad_pair.at[pl.ds(0, 4)], grad_pair.at[pl.ds(4, 4)], TENSOR, 0)
    pump()
    c_near.wait()
    x_far.wait()
    attn_out = at.part[0].astype(F32) + at.got_c[0].astype(F32) + at.got_x[0].astype(F32)
    mid = at.res[...].astype(F32) + at.valid[:, 0:1] * attn_out
    at.mid[...] = mid
    save(lambda v: (v.mid,))
    factor = lax.rsqrt(jnp.mean(mid * mid, axis=1, keepdims=True) + NORM_EPS)
    at.mid_pair[0] = (mid * factor * at.gains[1:2]).astype(BF16)
    spread_block(copies, at.mid_pair, pump)
    save(lambda v: (v.mid_pair,))
    grad_c.wait()
    while state[0] < len(units) or state[1] < SECONDS or state[2] < THIRDS:
        pump()
    for i in range(SECONDS, len(units)):
        owns[i].wait()
    for flight in flights:
        if flight is not None:
            flight.wait()
    for copy in saved:
        copy.wait()


def front(counts, latent, gains, keyval, output, expert_in, expert_out, shared_in, shared_out, res, grad, query, segment, table, gates):
    n_units, width = 3, expert_out.shape[1]
    half = (4, 3 * width, SLOT)
    frequency = ROPE_BASE ** (-np.arange(RD // 2, dtype=np.float32) / np.float32(RD // 2))
    frequency = jnp.asarray(np.tile(frequency.astype(np.float32), 4)[None])
    operands = [
        counts,
        keyval[None],
        output[None],
        expert_in.transpose(0, 1, 3, 2),
        expert_out,
        shared_in.transpose(0, 2, 1),
        shared_out[None],
        res,
        grad,
        query,
        segment,
        table,
        gates,
        frequency,
        latent,
        *gains,
    ]
    shapes = [like((8, *res.shape)), like((8, TOK), F32)] + [like(half)] * (2 * n_units - 1) + [like((4, width, SLOT))]
    shapes += [like(*buffer) for buffer in buffers(Kept)]
    results = pl.pallas_call(
        functools.partial(front_kernel, width),
        out_shape=shapes,
        in_specs=[SMEM_SPEC] + [ANY_SPEC] * 6 + [VMEM_SPEC] * 11,
        out_specs=[ANY_SPEC] * len(shapes),
        scratch_shapes=[pltpu.VMEM(*buffer) for buffer in buffers(Kept) + buffers(Landing)]
        + [
            pltpu.SemaphoreType.DMA((80,)),
            pltpu.SemaphoreType.DMA((80,)),
            pltpu.SemaphoreType.DMA((48,)),
        ],
        compiler_params=pltpu.CompilerParams(
            collective_id=0, has_side_effects=True, vmem_limit_bytes=GIVEN_VMEM
        ),
        cost_estimate=cost(220),
        name="front",
    )(*operands)
    grad_pair, gates_over, results = results[0], results[1], results[2:]
    lows, results = results[:n_units], results[n_units:]
    highs, results = results[:n_units], results[n_units:]
    return grad_pair, gates_over, lows, highs, types.SimpleNamespace(**dict(zip(fields(Kept), results)))


TOKEN_BLOCK = 256


class Freight:
    def __init__(self, copies, bits, sources, targets):
        self.copies, self.bits, self.pairs = copies, bits, list(zip(sources, targets))
        self.flights = []

    def start(self):
        for bit, (source, target) in zip(self.bits, self.pairs):
            self.flights.append(self.copies.start(source, target, DP, bit))

    def wait(self):
        for flight in self.flights:
            flight.wait()


class Split:
    def __init__(self, copies, keep, got, kept, gone):
        self.copies, self.kept, self.gone = copies, kept, gone
        self.loads = [copies.local(keep, kept), copies.local(got, gone)]
        self.half = kept.shape[0] // 2
        self.flights = []

    def send(self, bit, target, stay=None):
        for load in self.loads:
            load.wait()
        for k in range(2 * self.half):
            target_ref = self.kept if k < self.half else self.gone
            target_ref[k] = (self.kept[k].astype(F32) + self.gone[k].astype(F32)).astype(BF16)
        self.flights.append(
            self.copies.start(self.gone.at[pl.ds(self.half, self.half)], target, DP, bit)
        )
        if stay is not None:
            self.flights.append(self.copies.local(self.kept.at[pl.ds(0, self.half)], stay))

    def wait(self):
        for flight in self.flights:
            flight.wait()


def split_scratch(splits):
    return [pltpu.VMEM(keep.shape, BF16) for keep, _, _ in splits for _ in range(2)] + [
        pltpu.SemaphoreType.DMA((4 * len(splits),))
    ]


def split_outputs(splits):
    return [like((keep.shape[0] // 2, *keep.shape[1:])) for keep, _, _ in splits for _ in range(2)]


def experts_kernel(width, has_sum, bits, parts, *refs):
    refs = list(refs)
    take = lambda n: [refs.pop(0) for _ in range(n)]
    mid_ref, grad_ref, gate_ref = take(3)
    unit_refs = take(len(parts))
    if has_sum:
        back_in, out_in = take(2)
    sources = take(len(bits))
    back_ref, out_ref = take(2)
    keep_refs, give_refs = take(3), take(3)
    targets = take(len(bits))
    whole, total, send_sems, recv_sems = take(4)
    step = pl.program_id(0)
    copies = Copies(send_sems, recv_sems)

    def flights():
        return [
            pltpu.make_async_remote_copy(
                src_ref=cut.view(source),
                dst_ref=target,
                send_sem=send_sems.at[k],
                recv_sem=recv_sems.at[k],
                device_id=copies.across(DP, cut.bit),
                device_id_type=MESH,
            )
            for k, (cut, source, target) in enumerate(zip(bits, sources, targets))
        ]

    @pl.when(step == 0)
    def _():
        total[...] = jnp.zeros_like(total)
        copies.greet(sorted({cut.bit for cut in bits}), ())
        for flight in flights():
            flight.start()
        for ref, (slot, count, start, size, skip) in zip(unit_refs, parts):
            for j in range(count):
                k = COLUMNS.index(UNIT_SLOTS[slot + j])
                whole[start : start + size, lanes(k)] = ref[j, skip : skip + size]

    mid, grad = mid_ref[...], grad_ref[...]
    gate_up = nt(whole[: 2 * width], mid)
    hidden_grad = nt(whole[2 * width :], grad)
    gate = gate_up[:width]
    up = gate_up[width:]
    sigma = 1.0 / (1.0 + jnp.exp(-gate))
    silu = gate * sigma
    slope = sigma * (1.0 + gate * (1.0 - sigma))
    weight = gate_ref[...]
    hidden_grad = hidden_grad * weight
    hidden = (silu * up * weight).astype(BF16)
    pre = jnp.concatenate(
        [(hidden_grad * up * slope).astype(BF16), (hidden_grad * silu).astype(BF16)], axis=0
    )
    back = tn(pre, whole[: 2 * width])
    out = tn(hidden, whole[2 * width :])
    if has_sum:
        back = back + back_in[...]
        out = out + out_in[...]
    back_ref[...] = back.astype(back_ref.dtype)
    out_ref[...] = out.astype(out_ref.dtype)
    total[: 2 * width] += nn(pre, mid)
    total[2 * width :] += nn(hidden, grad)

    @pl.when(step == pl.num_programs(0) - 1)
    def _():
        for g in range(3):
            cut = slice(g * width, (g + 1) * width)
            for k in range(4):
                keep_refs[g][k] = total[cut, lanes((0, 2, 1, 3)[k])].astype(BF16)
                give_refs[g][k] = total[cut, lanes(4 + (0, 2, 1, 3)[k])].astype(BF16)
        for flight in flights():
            flight.wait()


class Cut:
    def __init__(self, array, bit, slots=None, rows=None):
        self.array, self.bit = array, bit
        self.slots = slots or (0, array.shape[0])
        self.rows = rows or (0, array.shape[1])

    def shape(self):
        return (self.slots[1], self.rows[1], self.array.shape[2])

    def view(self, ref):
        return ref.at[pl.ds(*self.slots), pl.ds(*self.rows)]


def experts_step(mid_pair, grad_pair, unit, gate, sums, last, freight, ident):
    tokens, block = mid_pair.shape[0], TOKEN_BLOCK
    width = unit[0][0].shape[1] // 3
    rows = pl.BlockSpec((block, D), lambda i: (i, 0))
    fixed = lambda *shape: pl.BlockSpec(shape, lambda i: (0,) * len(shape))
    kind = BF16 if last else F32
    part = (4, width, SLOT)
    operands = [mid_pair, grad_pair, gate[None]] + [part[0] for part in unit]
    specs = [rows, rows, pl.BlockSpec((1, block), lambda i: (0, i))]
    specs += [fixed(*part[0].shape) for part in unit]
    if sums is not None:
        operands += list(sums)
        specs += [rows, rows]
    results = pl.pallas_call(
        functools.partial(
            experts_kernel, width, sums is not None, tuple(freight), tuple(p[1:] for p in unit)
        ),
        grid=(tokens // block,),
        out_shape=[like((tokens, D), kind)] * 2
        + [like(part)] * 6
        + [like(cut.shape()) for cut in freight],
        in_specs=specs + [ANY_SPEC] * len(freight),
        out_specs=[rows, rows] + [fixed(*part)] * 6 + [ANY_SPEC] * len(freight),
        scratch_shapes=[
            pltpu.VMEM((3 * width, D), BF16),
            pltpu.VMEM((3 * width, D), F32),
            pltpu.SemaphoreType.DMA((len(freight),)),
            pltpu.SemaphoreType.DMA((len(freight),)),
        ],
        compiler_params=pltpu.CompilerParams(
            collective_id=ident, has_side_effects=True, vmem_limit_bytes=GIVEN_VMEM
        ),
        cost_estimate=cost(35),
        name="experts_step",
    )(*operands, *[cut.array for cut in freight])
    return list(results[:2]), list(results[2:5]), list(results[5:8]), list(results[8:])


def halve_kernel(count, *refs):
    keeps, gots, stays, gives = (refs[k * count : (k + 1) * count] for k in range(4))
    for keep, got, stay, give in zip(keeps, gots, stays, gives):
        half = stay.shape[0]
        for k in range(half):
            stay[k] = (keep[k].astype(F32) + got[k].astype(F32)).astype(BF16)
            give[k] = (keep[half + k].astype(F32) + got[half + k].astype(F32)).astype(BF16)


def halve(pairs):
    count = len(pairs)
    shapes = [like((keep.shape[0] // 2, *keep.shape[1:])) for keep, _ in pairs]
    results = pl.pallas_call(
        functools.partial(halve_kernel, count),
        out_shape=shapes * 2,
        in_specs=[VMEM_SPEC] * (2 * count),
        out_specs=[VMEM_SPEC] * (2 * count),
        cost_estimate=cost(3),
        name="halve",
    )(*[keep for keep, _ in pairs], *[got for _, got in pairs])
    return list(zip(results[:count], results[count:]))


class PairSum:
    def __init__(self, copies, blocks, got_c, give_a, give_b, got_a, got_b, end_a, end_b, last_a, last_b):
        self.copies, self.blocks, self.got_c = copies, blocks, got_c
        self.give_a, self.give_b, self.got_a, self.got_b = give_a, give_b, got_a, got_b
        self.end_a, self.end_b, self.last_a, self.last_b = end_a, end_b, last_a, last_b

    def both(self, k, first):
        cut = slice(first, first + 1024)
        return self.blocks[k, :, cut].astype(F32) + self.got_c[k, :, cut].astype(F32)

    def start(self):
        self.flights = {}
        for k in (3, 2, 1, 0):
            self.flights[k] = self.copies.start(
                self.blocks.at[pl.ds(4 + k, 1)], self.got_c.at[pl.ds(k, 1)], TENSOR, 0
            )

    def cross(self):
        self.flights[3].wait()
        self.give_a[1] = self.both(3, 0).astype(BF16)
        self.give_b[1] = self.both(3, 1024).astype(BF16)
        self.flights[2].wait()
        self.give_a[0] = self.both(2, 0).astype(BF16)
        self.across_a = self.copies.start(self.give_a, self.got_a, TENSOR, 1)
        self.flights[1].wait()
        self.give_b[0] = self.both(1, 1024).astype(BF16)
        self.across_b = self.copies.swapped(self.give_b, self.got_b, 0, 1024)
        self.flights[0].wait()

    def end(self):
        self.across_a.wait()
        self.end_a[0] = (self.both(1, 0) + self.got_a[1].astype(F32)).astype(BF16)
        self.ends_a = self.copies.swapped(self.end_a, self.last_a, 0, 1024)
        self.across_b.wait()
        self.end_b[0] = (self.both(2, 1024) + self.got_b[1].astype(F32)).astype(BF16)
        self.ends_b = self.copies.start(self.end_b, self.last_b, TENSOR, 1)

    def settle(self, total, end_a, end_b):
        self.across_a.wait()
        end_a[0] = (self.both(1, 0) + self.got_a[1].astype(F32)).astype(BF16)
        self.across_b.wait()
        end_b[0] = (self.both(2, 1024) + self.got_b[1].astype(F32)).astype(BF16)
        total[:, :1024] = self.both(0, 0) + self.got_a[0].astype(F32)
        total[:, 1024:] = self.both(0, 1024) + self.got_b[0].astype(F32)

    def total(self):
        self.ends_a.wait()
        self.ends_b.wait()
        return (
            self.both(0, 0) + self.got_a[0].astype(F32) + self.last_a[0].astype(F32),
            self.both(0, 1024) + self.got_b[0].astype(F32) + self.last_b[0].astype(F32),
        )


def sum_scratch():
    half = pltpu.VMEM((2, 160, 1024), BF16)
    end = pltpu.VMEM((1, 160, 1024), BF16)
    return [pltpu.VMEM((4, 160, D), BF16), half, half, half, half, end, end, end, end]


def back_kernel(bits, splits, *refs):
    refs = list(refs)
    take = lambda n: [refs.pop(0) for _ in range(n)]
    back_ref, grad_ref, mid_ref, gains_ref, valid_ref = take(5)
    sources = take(len(bits))
    pairs = take(2 * len(splits))
    mid_grad_ref, gain_part_ref, tokens_ref = take(3)
    targets = take(len(bits))
    ends = take(2 * len(splits))
    rooms = take(2 * len(splits))
    local_sems, *buffers, send_sems, recv_sems = refs
    copies = Copies(send_sems, recv_sems, local_sems)
    parts = [Split(copies, *pairs[2 * k : 2 * k + 2], *rooms[2 * k : 2 * k + 2]) for k in range(len(splits))]
    copies.greet((0, 1, 2))
    freight = Freight(copies, bits, sources, targets)
    freight.start()
    pair = PairSum(copies, back_ref, *buffers)
    pair.start()
    for k, bit in enumerate(splits):
        parts[k].send(bit, ends[2 * k + 1], ends[2 * k])
    pair.cross()
    pair.end()
    first, second = pair.total()
    mid_grad_ref[:, :1024] = first
    mid_grad_ref[:, 1024:] = second
    grad, mid = mid_grad_ref[...], mid_ref[...]
    factor = lax.rsqrt(jnp.mean(mid * mid, axis=1, keepdims=True) + NORM_EPS)
    scaled = grad * gains_ref[1:2]
    inner = jnp.mean(scaled * mid, axis=1, keepdims=True)
    gain_part_ref[...] = jnp.broadcast_to(jnp.sum(grad * mid * factor, axis=0, keepdims=True), (8, D))
    mid_grad = grad_ref[...].astype(F32) + factor * (scaled - mid * factor * factor * inner)
    mid_grad_ref[...] = mid_grad
    tokens_ref[0] = (valid_ref[:, 0:1] * mid_grad).astype(BF16)
    own = tokens_ref.at[pl.ds(0, 1)]
    x_own = copies.start(own, tokens_ref.at[pl.ds(1, 1)], TENSOR, 1)
    c_own = copies.start(own, tokens_ref.at[pl.ds(2, 1)], TENSOR, 0)
    x_own.wait()
    c_far = copies.start(tokens_ref.at[pl.ds(1, 1)], tokens_ref.at[pl.ds(3, 1)], TENSOR, 0)
    c_own.wait()
    c_far.wait()
    freight.wait()
    for part in parts:
        part.wait()


def back_tokens(back, grad_slots, mid, gains, valid, freight, splits):
    rows = (160, D)
    bits = tuple(bit for bit, _ in freight)
    goods = [array for _, array in freight]
    results = pl.pallas_call(
        functools.partial(back_kernel, bits, tuple(bit for _, _, bit in splits)),
        out_shape=[like(rows, F32), like((8, D), F32), like((4, *rows))]
        + [like(g.shape, g.dtype) for g in goods]
        + split_outputs(splits),
        in_specs=[VMEM_SPEC] * 5 + [ANY_SPEC] * (len(goods) + 2 * len(splits)),
        out_specs=[VMEM_SPEC] * 3 + [ANY_SPEC] * (len(goods) + 2 * len(splits)),
        scratch_shapes=split_scratch(splits)
        + sum_scratch() + [pltpu.SemaphoreType.DMA((24,)), pltpu.SemaphoreType.DMA((24,))],
        compiler_params=pltpu.CompilerParams(
            collective_id=2, has_side_effects=True, vmem_limit_bytes=GIVEN_VMEM
        ),
        cost_estimate=cost(55),
        name="back_tokens",
    )(back, grad_slots, mid, gains, valid, *goods, *[v for keep, got, _ in splits for v in (keep, got)])
    n = 3 + len(goods)
    return results[:3], list(results[3:n]), list(zip(results[n::2], results[n + 1 :: 2]))


def attention_backward_kernel(bits, splits, *refs):
    refs = list(refs)
    take = lambda n: [refs.pop(0) for _ in range(n)]
    (
        grad_ref,
        output_ref,
        mix_ref,
        query_ref,
        keyval_ref,
        key_rope_ref,
        lse_ref,
        w_query_ref,
        w_keyval_ref,
        normed_ref,
        latent_norm_ref,
        col_ref,
        row_ref,
        cos_ref,
        sin_ref,
        out_ref,
    ) = take(16)
    sources = take(len(bits))
    pairs = take(2 * len(splits))
    output_wgrad, query_wgrad, keyval_wgrad, part_ref, out_sum, out_end_a, out_end_b = take(7)
    targets = take(len(bits))
    output_got = take(1)[0]
    ends = take(2 * len(splits))
    rooms = take(2 * len(splits))
    local_sems = take(1)[0]
    mix_grad, query_grad, keyval_grad, key_grad, rope_grad, wide, send_sems, recv_sems = take(8)
    copies = Copies(send_sems, recv_sems, local_sems)
    parts = [Split(copies, *pairs[2 * k : 2 * k + 2], *rooms[2 * k : 2 * k + 2]) for k in range(len(splits))]
    copies.greet((0, 1, 2))
    pair = PairSum(copies, out_ref, *refs, None, None, None, None)
    pair.start()
    freight = Freight(copies, bits, sources, targets)
    freight.start()
    for k, bit in enumerate(splits):
        parts[k].send(bit, ends[2 * k + 1], ends[2 * k])
    places = Places()
    scale = (HD + RD) ** (-0.5)
    w_query = w_query_ref[...].reshape(D, w_query_ref.shape[2])
    for k in range(8):
        block = jnp.concatenate([grad_ref[b, :, lanes(k)] for b in range(4)], axis=0)
        s = k
        output_wgrad[s] = tn(mix_ref[...], block).astype(BF16)
        term = nt(block, output_ref[s])
        if k == 0:
            wide[:, :512] = term
        else:
            wide[:, :512] += term
    mix_grad[...] = wide[:, :512].astype(BF16)
    output_flight = copies.start(output_wgrad.at[pl.ds(4, 4)], output_got, DP, 0)
    pair.cross()
    for b in range(2):
        cut = slice(b * 320, (b + 1) * 320)
        allowed = masks(col_ref, row_ref, cut)
        lse_lane = lax.broadcasted_iota(jnp.int32, (320, 128), 1)
        rope_sum = jnp.zeros((320, SLOT), F32)
        for h in range(4):
            nope = query_ref[cut, lanes(h, 128)]
            rope = query_ref[cut, 512:768]
            mask = head_lanes(320, h)
            rope = jnp.where(mask, rope, jnp.zeros_like(rope))
            keys = keyval_ref[:, h * 256 : h * 256 + 128]
            values = keyval_ref[:, h * 256 + 128 : h * 256 + 256]
            scores = nt(nope, keys) + nt(rope, key_rope_ref[...])
            lse = jnp.sum(jnp.where(lse_lane == h, lse_ref[cut], 0.0), axis=1, keepdims=True)
            probs = jnp.where(allowed, jnp.exp(scores * scale - lse), 0.0)
            grad = mix_grad[cut, lanes(h, 128)]
            probs_grad = nt(grad, values)
            inner = jnp.sum(probs * probs_grad, axis=1, keepdims=True)
            scores_grad = (probs * (probs_grad - inner)).astype(BF16)
            value_grad = tn(probs.astype(BF16), grad)
            nope_grad = tn(scores_grad, nope) * scale
            rope_part = tn(scores_grad, rope)
            low, high = slice(h * 256, h * 256 + 128), slice(h * 256 + 128, h * 256 + 256)
            if b == 0:
                key_grad[:, low] = nope_grad
                key_grad[:, high] = value_grad
            else:
                key_grad[:, low] += nope_grad
                key_grad[:, high] += value_grad
            if b == 0 and h == 0:
                rope_grad[...] = rope_part
            else:
                rope_grad[...] += rope_part
            query_grad[cut, lanes(h, 128)] = (nn(scores_grad, keys) * scale).astype(BF16)
            rope_sum = rope_sum + jnp.where(mask, nn(scores_grad, key_rope_ref[...]), 0.0)
        rope_sum = rope_sum * scale
        back_a, back_b = turn(rope_sum[:, :128], rope_sum[:, 128:], cos_ref[cut], -sin_ref[cut])
        query_grad[cut, 512:640] = back_a.astype(BF16)
        query_grad[cut, 640:768] = back_b.astype(BF16)
    keyval_grad[...] = key_grad[...].astype(BF16)
    plain = nt(query_grad[...], sort_columns(768)).astype(BF16)
    for k in range(8):
        query_wgrad[k] = tn(normed_ref[:, lanes(k)], plain).astype(BF16)
    wide[:512, :] = tn(latent_norm_ref[...], keyval_grad[...])
    for k in range(8):
        start = pl.multiple_of(places[k] * 64, 64)
        keyval_wgrad[k] = wide[pl.ds(start, 64), :].astype(BF16)
    row = lax.broadcasted_iota(jnp.int32, (SLOT, 128), 0)
    lane = lax.broadcasted_iota(jnp.int32, (SLOT, 128), 1)
    fold = jnp.where(lane == lax.rem(row, 32) + 32 * (row // 128), scale, 0.0)
    for b in range(4):
        cut = slice(b * 160, (b + 1) * 160)
        for k in range(4):
            columns = lanes(k, 512)
            part_ref[b, :, columns] = nt(query_grad[cut], w_query[columns]).astype(BF16)
        part_ref[b, :, D : D + KR] = nt(keyval_grad[cut], w_keyval_ref[...]).astype(BF16)
        rope = lax.dot_general(
            rope_grad[cut],
            fold,
            (((1,), (0,)), ((), ())),
            precision=lax.Precision.HIGHEST,
            preferred_element_type=F32,
        )
        part_ref[b, :, D + KR :] = rope.astype(BF16)
    pair.settle(out_sum, out_end_a, out_end_b)
    output_flight.wait()
    freight.wait()
    for part in parts:
        part.wait()


def attention_backward(grad, saved, out, freight, splits):
    shapes = [like((8, 512, SLOT)), like((8, SLOT, 768)), like((8, 64, 1024)), like((4, 160, D + KR + 128))]
    shapes += [like((160, D), F32), like((1, 160, 1024)), like((1, 160, 1024))]
    bits = tuple(bit for bit, _ in freight)
    goods = [array for _, array in freight]
    kept = (saved.output, saved.mix, saved.query_final, saved.keyval_final, saved.key_rope, saved.lse, saved.query)
    kept += (saved.w_keyval, saved.normed, saved.latent_norm, saved.col, saved.row, saved.cos, saved.sin)
    results = pl.pallas_call(
        functools.partial(attention_backward_kernel, bits, tuple(bit for _, _, bit in splits)),
        out_shape=shapes + [like(g.shape) for g in goods] + [like((4, 512, SLOT))] + split_outputs(splits),
        in_specs=[VMEM_SPEC] * 16 + [ANY_SPEC] * (len(goods) + 2 * len(splits)),
        out_specs=[VMEM_SPEC] * len(shapes) + [ANY_SPEC] * (len(goods) + 1 + 2 * len(splits)),
        scratch_shapes=split_scratch(splits)
        + [
            pltpu.VMEM((TOK, 512), BF16),
            pltpu.VMEM((TOK, 768), BF16),
            pltpu.VMEM((TOK, 1024), BF16),
            pltpu.VMEM((TOK, 1024), F32),
            pltpu.VMEM((TOK, SLOT), F32),
            pltpu.VMEM((TOK, 1024), F32),
            pltpu.SemaphoreType.DMA((32,)),
            pltpu.SemaphoreType.DMA((32,)),
            *sum_scratch()[:5],
        ],
        compiler_params=pltpu.CompilerParams(
            collective_id=4, has_side_effects=True, vmem_limit_bytes=GIVEN_VMEM
        ),
        cost_estimate=cost(30),
        name="attention_backward",
    )(grad, *kept, out, *goods, *[v for keep, got, _ in splits for v in (keep, got)])
    n = 8 + len(goods)
    return results[:7], list(results[7:n]), list(zip(results[n::2], results[n + 1 :: 2]))


class SlotSum:
    def __init__(self, copies, values, bits, got, give, rows=None):
        self.copies, self.values, self.bits, self.got, self.give = copies, values, list(bits), got, give
        self.rows = rows or (0, values.shape[1])
        self.level = 0
        self.flying = None

    def view(self, ref, first, count):
        return ref.at[pl.ds(first, count), pl.ds(*self.rows)]

    def start(self):
        half = 4 >> self.level
        if self.level == 0:
            source = self.view(self.values, half, half)
        else:
            first, size = self.rows
            for k in range(half):
                self.give[self.level - 1][k, first : first + size] = self.total(half + k).astype(BF16)
            source = self.view(self.give[self.level - 1], 0, half)
        target = self.view(self.got[self.level], 0, half)
        self.flying = self.copies.start(source, target, DP, self.bits[self.level])
        self.level += 1

    def total(self, k):
        cut = slice(self.rows[0], self.rows[0] + self.rows[1])
        value = self.values[k, cut].astype(F32)
        for level in range(self.level):
            value = value + self.got[level][k, cut].astype(F32)
        return value

    def wait(self):
        self.flying.wait()
        if self.level < len(self.bits):
            self.start()


def slot_sum_scratch(shape):
    spaces = [pltpu.VMEM((n, *shape), BF16) for n in (4, 2, 1)]
    return spaces + [pltpu.VMEM((n, *shape), BF16) for n in (2, 1)]


def tail_kernel(
    n_rest,
    n_last,
    part_ref,
    output_wgrad,
    query_wgrad,
    keyval_wgrad,
    normed_ref,
    w_latent_ref,
    gains_ref,
    latent_gain_ref,
    latent_c_ref,
    res_ref,
    mid_grad_ref,
    ffn_gain_ref,
    output_came,
    mid_ref,
    valid_ref,
    out_sum,
    out_end_a,
    out_end_b,
    cos_ref,
    sin_ref,
    *refs,
):
    refs = list(refs)
    take = lambda n: [refs.pop(0) for _ in range(n)]
    rest_pairs, last_pairs = take(2 * n_rest), take(2 * n_last)
    output_owned, query_owned, keyval_owned, latent_owned, res_grad_ref, res_out_ref = take(6)
    rest_owned, end_cames = take(n_rest), take(n_rest)
    last_ends = take(2 * n_last)
    send_sems, recv_sems = take(2)
    sums = []
    copies = Copies(send_sems, recv_sems)
    for values, bits in (
        (query_wgrad, (0, 1, 2)),
        (keyval_wgrad, (0, 1, 2)),
        (output_wgrad, (0, 1, 2)),
    ):
        space = take(5)
        if values is query_wgrad:
            half = values.shape[1] // 2
            for k in range(2):
                sums.append(SlotSum(copies, values, bits, space[:3], space[3:], (k * half, half)))
        else:
            sums.append(SlotSum(copies, values, bits, space[:3], space[3:]))
    latent_values = take(1)[0]
    space = take(5)
    latent_sum = SlotSum(copies, latent_values, (0, 1, 2), space[:3], space[3:])
    got_c, give_x, got_x = take(3)
    latent_all, gain_rows, gain_c, gain_x, gain_columns, wide, rest_came, end_sum, _, local_sems = take(10)
    copies.local_sems = local_sems
    copies.greet((0, 1, 2))
    last_a, last_b = take(2)
    out_ends = [copies.swapped(out_end_a, last_a, 0, 1024), copies.start(out_end_b, last_b, TENSOR, 1)]
    rest_rooms, last_rooms = take(2 * n_rest), take(2 * n_last)
    rests = [Split(copies, *rest_pairs[2 * k : 2 * k + 2], *rest_rooms[2 * k : 2 * k + 2]) for k in range(n_rest)]
    lasts = [Split(copies, *last_pairs[2 * k : 2 * k + 2], *last_rooms[2 * k : 2 * k + 2]) for k in range(n_last)]
    query_first, query_second, keyval_sum, output_sum = sums
    output_sum.got[0] = output_came
    output_sum.level = 1
    query_first.start()
    output_sum.start()
    c_far = copies.start(part_ref.at[pl.ds(3, 1)], got_c.at[pl.ds(1, 1)], TENSOR, 0)
    c_near = copies.start(part_ref.at[pl.ds(2, 1)], got_c.at[pl.ds(0, 1)], TENSOR, 0)
    c_far.wait()
    give_x[0] = (part_ref[1].astype(F32) + got_c[1].astype(F32)).astype(BF16)
    x_far = copies.start(give_x, got_x, TENSOR, 1)
    for k in range(n_rest):
        rests[k].send(2, rest_came.at[pl.ds(2 * k, 2)])
    for k in range(n_last):
        lasts[k].send(1, last_ends[2 * k + 1], last_ends[2 * k])
    c_near.wait()
    query_first.wait()
    query_second.start()
    x_far.wait()

    def summed(columns):
        return (
            part_ref[0, :, columns].astype(F32)
            + got_c[0, :, columns].astype(F32)
            + got_x[0, :, columns].astype(F32)
        )

    latent_c = latent_c_ref[...]
    latent_gain = latent_gain_ref[0:1]
    factor = lax.rsqrt(jnp.mean(latent_c * latent_c, axis=1, keepdims=True) + NORM_EPS)
    grad = summed(slice(D, D + KR))
    scaled = grad * latent_gain
    inner = jnp.mean(scaled * latent_c, axis=1, keepdims=True)
    latent_back = factor * (scaled - latent_c * factor * factor * inner)
    latent_gain_part = jnp.sum(grad * latent_c * factor, axis=0, keepdims=True)
    rope = summed(slice(D + KR, D + KR + 128))
    cos, sin = cos_ref[...], sin_ref[...]
    lane = lax.broadcasted_iota(jnp.int32, rope.shape, 1)
    other = jnp.where(lane < 32, pltpu.roll(rope, 96, 1), pltpu.roll(rope, 32, 1))
    rope_back = jnp.where(lane < 32, rope * cos + other * sin, rope * cos - other * sin)
    rope_back = jnp.where(lane < RD, rope_back, 0.0)
    latent_all[0, :, :KR] = latent_back.astype(BF16)
    latent_all[0, :, KR:] = rope_back.astype(BF16)
    own = latent_all.at[pl.ds(0, 1)]
    l_x = copies.start(own, latent_all.at[pl.ds(1, 1)], TENSOR, 1)
    l_c = copies.start(own, latent_all.at[pl.ds(2, 1)], TENSOR, 0)
    res = res_ref[...].astype(F32)
    factor = lax.rsqrt(jnp.mean(res * res, axis=1, keepdims=True) + NORM_EPS)
    grad = summed(slice(0, D)) + nt(latent_all[0], w_latent_ref[...])
    scaled = grad * gains_ref[0:1]
    inner = jnp.mean(scaled * res, axis=1, keepdims=True)
    res_grad_ref[...] = mid_grad_ref[...] + factor * (scaled - res * factor * factor * inner)
    row = lax.broadcasted_iota(jnp.int32, (8, D), 0)
    attn_part = jnp.broadcast_to(jnp.sum(grad * res * factor, axis=0, keepdims=True), (8, D))
    gain_rows[0] = jnp.where(row == 0, attn_part, jnp.where(row == 1, ffn_gain_ref[...], 0.0))
    latent_row = jnp.broadcast_to(latent_gain_part, (8, KR))
    gain_rows[0, :, :KR] = jnp.where(
        lax.broadcasted_iota(jnp.int32, (8, KR), 0) == 2, latent_row, gain_rows[0, :, :KR]
    )
    g_c = copies.start(gain_rows, gain_c, TENSOR, 0)
    query_second.wait()
    keyval_sum.start()
    query_first.wait()
    l_x.wait()
    l_far = copies.start(latent_all.at[pl.ds(1, 1)], latent_all.at[pl.ds(3, 1)], TENSOR, 0)
    g_c.wait()
    gain_rows[0] = gain_rows[0] + gain_c[0]
    g_x = copies.start(gain_rows, gain_x, TENSOR, 1)
    l_c.wait()
    l_far.wait()
    g_x.wait()
    output_sum.wait()
    keyval_sum.wait()
    query_second.wait()
    gain_columns[:, 0:8] = (gain_rows[0] + gain_x[0]).T
    tensor = lax.axis_index(TENSOR)
    dp = lax.axis_index(DP)
    latent_rows = jnp.concatenate([latent_all[b] for b in range(4)], axis=0)
    for k in range(8):
        wide[...] = tn(normed_ref[:, lanes(k)], latent_rows)
        block = wide[pl.ds(pl.multiple_of(tensor * 64, 64), 64), :]
        start = pl.multiple_of(k * SLOT + tensor * 64, 64)
        columns = gain_columns[pl.ds(start, 64), 0:8]
        start = pl.multiple_of(crossed(dp, COLUMNS[k], 3) * 64 + tensor * 16, 16)
        latent_values[k] = block.astype(BF16)
        lane = lax.broadcasted_iota(jnp.int32, (64, 128), 1)
        ends = block[:, KR : KR + 128]
        ends = jnp.where(lane == 64, columns[:, 0:1], ends)
        ends = jnp.where(lane == 65, columns[:, 1:2], ends)
        latent_values[k, :, KR:] = ends.astype(BF16)
        corner = gain_columns[pl.ds(start, 16), 0:8][:, 2:3]
        lane = lax.broadcasted_iota(jnp.int32, (16, 128), 1)
        latent_values[k, 0:16, KR:] = jnp.where(lane == 66, corner, ends[0:16]).astype(BF16)
    latent_sum.start()
    ends = []
    for g in range(n_rest):
        rests[g].wait()
        own, over = rests[g].kept[0].astype(F32), rests[g].kept[1].astype(F32)
        rest_owned[g][0] = (own + rest_came[2 * g].astype(F32)).astype(BF16)
        end_sum[g] = (over + rest_came[2 * g + 1].astype(F32)).astype(BF16)
        ends.append(copies.start(end_sum.at[pl.ds(g, 1)], end_cames[g], DP, 1))
    keyval_sum.wait()
    output_sum.wait()
    output_owned[...] = output_sum.total(0)
    latent_sum.wait()
    for flight in out_ends:
        flight.wait()
    valid = valid_ref[:, 0:1]
    res_out_ref[:, :1024] = (mid_ref[:, :1024] + valid * (out_sum[:, :1024] + last_a[0].astype(F32))).astype(BF16)
    res_out_ref[:, 1024:] = (mid_ref[:, 1024:] + valid * (out_sum[:, 1024:] + last_b[0].astype(F32))).astype(BF16)
    latent_sum.wait()
    half = query_owned.shape[0] // 2
    query_first.wait()
    query_owned[:half] = query_first.total(0)
    keyval_sum.wait()
    keyval_owned[...] = keyval_sum.total(0)
    query_second.wait()
    query_owned[half:] = query_second.total(0)
    latent_sum.wait()
    latent_owned[...] = latent_sum.total(0)
    for copy in lasts + ends:
        copy.wait()


def tail(part, wgrads, output_came, out_parts, saved, mid_grad, ffn_gain, rests, lasts):
    output_wgrad, query_wgrad, keyval_wgrad = wgrads
    rows = (160, D)
    latent = (64, KR + 128)
    shapes = [
        like((512, SLOT), F32),
        like((SLOT, 768), F32),
        like((64, 1024), F32),
        like(latent, F32),
        like(rows, F32),
        like(rows),
    ]
    part_row = (160, D + KR + 128)
    unit = rests[0][0].shape[1:]
    rows_spec = pl.BlockSpec((160, 128), lambda i: (0, 0))
    results = pl.pallas_call(
        functools.partial(tail_kernel, len(rests), len(lasts)),
        out_shape=shapes + [like((1, *unit))] * (2 * len(rests) + 2 * len(lasts)),
        grid=(1,),
        in_specs=[VMEM_SPEC] * 18 + [rows_spec] * 2 + [ANY_SPEC] * (2 * len(rests) + 2 * len(lasts)),
        out_specs=[VMEM_SPEC] * (len(shapes) + len(rests)) + [ANY_SPEC] * (len(rests) + 2 * len(lasts)),
        scratch_shapes=[
            pltpu.SemaphoreType.DMA((40,)),
            pltpu.SemaphoreType.DMA((40,)),
            *slot_sum_scratch((SLOT, 768)),
            *slot_sum_scratch((64, 1024)),
            *slot_sum_scratch((512, SLOT)),
            pltpu.VMEM((8, *latent), BF16),
            *slot_sum_scratch(latent),
            pltpu.VMEM((2, *part_row), BF16),
            pltpu.VMEM((1, *part_row), BF16),
            pltpu.VMEM((1, *part_row), BF16),
            pltpu.VMEM((4, 160, KR + 128), BF16),
            pltpu.VMEM((1, 8, D), F32),
            pltpu.VMEM((1, 8, D), F32),
            pltpu.VMEM((1, 8, D), F32),
            pltpu.VMEM((D, 128), F32),
            pltpu.VMEM((SLOT, KR + 128), F32),
            pltpu.VMEM((2 * len(rests), *unit), BF16),
            pltpu.VMEM((len(rests), *unit), BF16),
            pltpu.SemaphoreType.DMA((1,)),
            pltpu.SemaphoreType.DMA((32,)),
            pltpu.VMEM((1, 160, 1024), BF16),
            pltpu.VMEM((1, 160, 1024), BF16),
            *split_scratch(rests)[:-1],
            *split_scratch(lasts)[:-1],
        ],
        compiler_params=pltpu.CompilerParams(
            collective_id=3, has_side_effects=True, vmem_limit_bytes=GIVEN_VMEM
        ),
        cost_estimate=cost(110),
        name="tail",
    )(
        part,
        output_wgrad,
        query_wgrad,
        keyval_wgrad,
        saved.normed,
        saved.w_latent,
        saved.gains,
        saved.latent_gain,
        saved.latent_c,
        saved.res,
        mid_grad,
        ffn_gain,
        output_came,
        saved.mid,
        saved.valid,
        *out_parts,
        saved.cos,
        saved.sin,
        *[v for keep, got, _ in rests + lasts for v in (keep, got)],
    )
    n = len(rests)
    return results[:6], results[6 : 6 + n], results[6 + n : 6 + 2 * n], list(zip(results[6 + 2 * n :: 2], results[7 + 2 * n :: 2]))


def finish_kernel(
    n_came,
    res_out_ref,
    res_grad_ref,
    latent_ref,
    *refs,
):
    refs = list(refs)
    take = lambda n: [refs.pop(0) for _ in range(n)]
    stays, cames, others = take(9), take(n_came), take(9)
    passed = take(3)
    res_out, res_grad, latent, attn_gain, ffn_gain, latent_gain, expert_in, expert_out, shared_in, shared_out, *out = refs
    for source, target in zip(passed, out):
        target[...] = source[...]
    places = Places()
    for k in range(8):
        block = pl.ds(pl.multiple_of(places[k] * SLOT, SLOT), SLOT)
        res_out[:, block] = res_out_ref[:, lanes(k)]
        res_grad[:, block] = res_grad_ref[:, lanes(k)]
    latent[...] = latent_ref[:, : KR + RD]
    turned = latent_ref[:, KR : KR + 128].T
    attn_gain[...] = turned[64:65]
    ffn_gain[...] = turned[65:66]
    latent_gain[...] = turned[66:67, : KR // 32]
    side = places[12]
    n_half = expert_in.shape[0] // 2
    width = expert_out.shape[1]
    for p in range(n_half + 1):
        for mine in (True, False):
            which = side if mine else 1 - side
            for g in range(3):
                value = (stays if mine else others)[3 * p + g][0].astype(F32)
                late = 3 * p + g - 9 + n_came
                if mine and late >= 0:
                    value = value + cames[late][0].astype(F32)
                if p < n_half and g < 2:
                    expert_in[which * n_half + p, g] = value
                elif p < n_half:
                    expert_out[which * n_half + p] = value
                else:
                    cut = pl.ds(pl.multiple_of(which * width, 8), width)
                    if g < 2:
                        shared_in[g, cut] = value
                    else:
                        shared_out[cut] = value


def finish(res_out, res_grad, latent, stays, cames, others, passed, width):
    shapes = [
        like(res_out.shape),
        like(res_grad.shape, F32),
        like((64, KR + RD), F32),
        like((1, 64), F32),
        like((1, 64), F32),
        like((1, KR // 32), F32),
        like((EXPERTS, 2, width, SLOT), F32),
        like((EXPERTS, width, SLOT), F32),
        like((2, 2 * width, SLOT), F32),
        like((2 * width, SLOT), F32),
    ] + [like(array.shape, F32) for array in passed]
    return pl.pallas_call(
        functools.partial(finish_kernel, len(cames)),
        out_shape=shapes,
        in_specs=[VMEM_SPEC] * (24 + len(cames)),
        out_specs=[VMEM_SPEC] * len(shapes),
        compiler_params=pltpu.CompilerParams(vmem_limit_bytes=GIVEN_VMEM),
        cost_estimate=cost(10),
        name="finish",
    )(res_out, res_grad, latent, *stays, *cames, *others, *passed)


def body(
    res_in,
    out_grad,
    seg_ids,
    tok_counts,
    slot_table,
    slot_gates,
    attn_gain,
    latent_gain,
    ffn_gain,
    w_latent,
    w_query,
    w_keyval,
    w_output,
    w_expert_in,
    w_expert_out,
    w_shared_in,
    w_shared_out,
):
    dp = lax.axis_index(DP)
    rows = res_in.shape[0]
    first = ((dp >> 1) & 1) == 0
    n_half = EXPERTS // 2
    width = w_expert_out.shape[1]
    grad_pair, over_gate, lows, highs, saved = front(
        tok_counts,
        w_latent,
        (attn_gain[None], ffn_gain[None], latent_gain[None]),
        w_keyval,
        w_output,
        w_expert_in,
        w_expert_out,
        w_shared_in,
        w_shared_out,
        res_in,
        out_grad,
        w_query,
        seg_ids,
        slot_table[0],
        slot_gates[0],
    )
    pair_gate = jnp.concatenate(
        [g[:, k * rows : (k + 1) * rows] for k in range(4) for g in (saved.gates, over_gate)], axis=1
    )
    pair_gate = jnp.where(first, pair_gate[:n_half], pair_gate[n_half : 2 * n_half])
    mid_pair = saved.mid_pair.reshape(-1, D)
    grad_pair = grad_pair.reshape(-1, D)
    ones = jnp.ones_like(pair_gate[0])
    whole = 3 * width
    low, high = lows[2], highs[2]
    sums, keep0, give0, (high_far,) = experts_step(
        mid_pair,
        grad_pair,
        [(lows[0], 0, 4, 0, whole, 0), (highs[0], 4, 4, 0, whole, 0)],
        pair_gate[0],
        None,
        False,
        [Cut(low, 0, (0, 4), (width, whole - width))],
        5,
    )
    sums, keep1, give1, (y0a, y0b) = experts_step(
        mid_pair,
        grad_pair,
        [(lows[1], 0, 4, 0, whole, 0), (highs[1], 4, 4, 0, whole, 0)],
        pair_gate[1],
        sums,
        False,
        [Cut(give0[0], 0), Cut(give0[1], 0)],
        6,
    )
    (k0a, h0a), (k0b, h0b) = halve([(keep0[0], y0a), (keep0[1], y0b)])
    (back, out), keep2, give2, (y0c, y1a, z0a, z0b) = experts_step(
        mid_pair,
        grad_pair,
        [
            (low, 0, 4, 0, whole, 0),
            (high, 4, 4, 0, width, 0),
            (high_far, 4, 4, width, whole - width, 0),
        ],
        ones,
        sums,
        True,
        [Cut(give0[2], 0), Cut(give1[0], 0), Cut(h0a, 2), Cut(h0b, 2)],
        7,
    )
    back = back.reshape(8, rows, D)
    out = out.reshape(8, rows, D)
    (mid_grad, ffn_gain_part, attn_grad), (y1b, y1c, y2a, y2b), split = back_tokens(
        back,
        saved.grad,
        saved.mid,
        saved.gains,
        saved.valid,
        [(0, give1[1]), (0, give1[2]), (0, give2[0]), (0, give2[1])],
        [(keep0[2], y0c, 2), (keep1[0], y1a, 2), (k0a, z0a, 1), (k0b, z0b, 1)],
    )
    (k0c, z0c), (k1a, z1a), over0a, over0b = split
    (*wgrads, back_part, out_sum, out_a, out_b), (y2c, output_came), split = attention_backward(
        attn_grad,
        saved,
        out,
        [(0, give2[2])],
        [(keep1[1], y1b, 2), (keep1[2], y1c, 2), (keep2[0], y2a, 2), (k0c, z0c, 1), (k1a, z1a, 1)],
    )
    (k1b, z1b), (k1c, z1c), (k2a, z2a), over0c, over1a = split
    (output_owned, query_owned, keyval_owned, latent_owned, res_grad, res_out), own2, over2, late = tail(
        back_part,
        wgrads,
        output_came,
        (out_sum, out_a, out_b),
        saved,
        mid_grad,
        ffn_gain_part,
        [(keep2[1], y2b, 2), (keep2[2], y2c, 2)],
        [(k1b, z1b, 1), (k1c, z1c, 1), (k2a, z2a, 1)],
    )
    ready = [over0a, over0b, over0c, over1a, *late]
    (
        res_out,
        res_grad,
        latent_owned,
        attn_gain,
        ffn_gain,
        latent_gain,
        expert_in,
        expert_out,
        shared_in,
        shared_out,
        output_owned,
        query_owned,
        keyval_owned,
    ) = finish(
        res_out,
        res_grad,
        latent_owned,
        [mine for mine, _ in ready] + list(own2),
        [],
        [other for _, other in ready] + list(over2),
        [output_owned, query_owned, keyval_owned],
        width,
    )
    return (
        res_out,
        res_grad,
        attn_gain[0],
        latent_gain[0],
        ffn_gain[0],
        latent_owned,
        query_owned,
        keyval_owned,
        output_owned,
        expert_in.transpose(0, 1, 3, 2),
        expert_out,
        shared_in.transpose(0, 2, 1),
        shared_out,
    )


def solution(mesh):
    placed = (
        P((DP, TENSOR), None),
        P((DP, TENSOR), None),
        P(DP, None),
        P(DP),
        P(DP, None, None),
        P(DP, None, None),
        P((DP, TENSOR)),
        P((DP, TENSOR)),
        P((DP, TENSOR)),
        P((DP, TENSOR), None),
        P(DP, TENSOR),
        P(DP, TENSOR),
        P(TENSOR, DP),
        P(None, None, DP, TENSOR),
        P(None, TENSOR, DP),
        P(None, DP, TENSOR),
        P(TENSOR, DP),
    )
    fits = mesh.shape[DP] == 8 and mesh.shape[TENSOR] == 4
    return jax.shard_map(
        body if fits else general_body,
        mesh=mesh,
        in_specs=placed,
        out_specs=(
            P((DP, TENSOR), None),
            P((DP, TENSOR), None),
            P((DP, TENSOR)),
            P((DP, TENSOR)),
            P((DP, TENSOR)),
            P((DP, TENSOR), None),
            P(DP, TENSOR),
            P(DP, TENSOR),
            P(TENSOR, DP),
            P(None, None, DP, TENSOR),
            P(None, TENSOR, DP),
            P(None, DP, TENSOR),
            P(TENSOR, DP),
        ),
        check_vma=False,
    )
```

```python
import functools
import types

import jax
import jax.numpy as jnp
import numpy as np
from jax import lax
from jax.experimental import pallas as pl
from jax.experimental.pallas import tpu as pltpu
from jax.sharding import PartitionSpec as P

D = 2048
H = 16
HD = 128
RD = 64
VD = 128
KR = 512
TOK = 640
EXPERTS = 4


NORM_EPS = 1e-06
ROPE_BASE = 50000.0


def rms_factor(values):
    return lax.rsqrt(jnp.mean(values * values, axis=-1, keepdims=True) + NORM_EPS)


def norm_back(grad_out, values, factor, gain_vec):
    scaled = grad_out * gain_vec
    inner_sum = jnp.mean(scaled * values, axis=-1, keepdims=True)
    return (
        factor * (scaled - values * factor * factor * inner_sum),
        jnp.sum(grad_out * values * factor, axis=0),
    )


def rotary_tables(positions):
    half_width = RD // 2
    inv_freq = ROPE_BASE ** (-jnp.arange(half_width, dtype=jnp.float32) / half_width)
    angles = positions.astype(jnp.float32)[:, None] * inv_freq[None, :]
    return (jnp.cos(angles), jnp.sin(angles))


def rotate(values, cosine_table, sine_table):
    half_width = values.shape[-1] // 2
    first_half = values[..., :half_width]
    second_half = values[..., half_width:]
    return jnp.concatenate(
        [
            first_half * cosine_table - second_half * sine_table,
            second_half * cosine_table + first_half * sine_table,
        ],
        axis=-1,
    )


def silu_parts(gate_pre):
    sigma_gate = jax.nn.sigmoid(gate_pre)
    return (gate_pre * sigma_gate, sigma_gate * (1.0 + gate_pre * (1.0 - sigma_gate)))


def flip_pairs(count, bit):
    return [(i, i ^ (1 << bit)) for i in range(count)]


def swap_dp(values, bit):
    return lax.ppermute(values, DP, flip_pairs(lax.axis_size(DP), bit))


def swap_tensor(values, bit):
    return lax.ppermute(values, TENSOR, flip_pairs(lax.axis_size(TENSOR), bit))


def dp_bits():
    top = lax.axis_size(DP).bit_length() - 1
    return [1] + list(range(top - 1, 1, -1)) + [0]


def slot_order(bits):
    order = [0]
    for bit in bits:
        order = order + [j ^ (1 << bit) for j in order]
    return order


def select_blocks(blocks, index):
    step = 1
    while step < len(blocks):
        hit = (index & step) != 0
        blocks = [jnp.where(hit, blocks[i ^ step], blocks[i]) for i in range(len(blocks))]
        step *= 2
    return blocks


def to_slots(values, index, bits, axis):
    count = 1 << len(bits)
    blocks = select_blocks(jnp.split(values, count, axis=axis), index)
    return jnp.concatenate([blocks[j] for j in slot_order(bits)], axis=axis)


def from_slots(values, index, bits, axis):
    order = slot_order(bits)
    slots = jnp.split(values, len(order), axis=axis)
    blocks = [slots[order.index(i)] for i in range(len(order))]
    return jnp.concatenate(select_blocks(blocks, index), axis=axis)


def gather_dp(values, bits):
    for bit in bits:
        values = jnp.concatenate([values, swap_dp(values, bit)], axis=0)
    return values


def gather_tensor(values):
    for bit in (1, 0):
        values = jnp.concatenate([values, swap_tensor(values, bit)], axis=0)
    return values


def scatter_dp(values, bits, axis):
    values = values.astype(jnp.float32)
    for bit in reversed(bits):
        keep, give = jnp.split(values, 2, axis=axis)
        values = keep + swap_dp(give.astype(jnp.bfloat16), bit).astype(jnp.float32)
    return values


def scatter_tensor(values):
    for bit in (0, 1):
        keep, give = jnp.split(values, 2, axis=0)
        values = keep + swap_tensor(give.astype(jnp.bfloat16), bit).astype(jnp.float32)
    return values


def partner_columns(values):
    count = lax.axis_size(DP)
    slots = jnp.split(values, count, axis=-1)
    return jnp.concatenate([slots[k ^ 1] for k in range(count)], axis=-1)


def gather_pair(values, bit):
    over = swap_dp(partner_columns(values), bit)
    own = jnp.concatenate([values, over, swap_tensor(values, 1), swap_tensor(over, 1)], axis=0)
    return jnp.concatenate([own, swap_tensor(own, 0)], axis=0)


def scatter_pair(values, bit):
    values = scatter_tensor(values)
    keep, give = jnp.split(values, 2, axis=0)
    return keep + swap_dp(partner_columns(give).astype(jnp.bfloat16), bit).astype(jnp.float32)


def dot(a, b, contract):
    return lax.dot_general(a, b, (contract, ((), ())), preferred_element_type=jnp.float32)


def general_body(
    res_in,
    out_grad,
    seg_ids,
    tok_counts,
    slot_table,
    slot_gates,
    attn_gain,
    latent_gain,
    ffn_gain,
    w_latent,
    w_query,
    w_keyval,
    w_output,
    w_expert_in,
    w_expert_out,
    w_shared_in,
    w_shared_out,
):
    f32 = jnp.float32
    bf16 = jnp.bfloat16
    n_tensor = lax.axis_size(TENSOR)
    n_dp = lax.axis_size(DP)
    dp = lax.axis_index(DP)
    tensor = lax.axis_index(TENSOR)
    bits = dp_bits()
    merge = bits[0]
    half = (dp >> merge) & 1
    rows = res_in.shape[0]
    local_heads = H // n_tensor
    score_scale = (HD + RD) ** (-0.5)

    res_local = to_slots(res_in, dp, bits, 1)
    res_all = gather_tensor(res_local)
    tensor_slots = slot_order([1, 0])
    token_ids = jnp.concatenate(
        [(tensor ^ j) * rows + jnp.arange(rows, dtype=jnp.int32) for j in tensor_slots]
    )
    segment_canon = seg_ids[0]
    segment_row = jnp.concatenate(
        [lax.dynamic_slice_in_dim(segment_canon, (tensor ^ j) * rows, rows) for j in tensor_slots]
    )
    valid_all = (token_ids < tok_counts[0]).astype(f32)
    valid_rows = valid_all[:rows, None]
    group_gate = jnp.sum(
        jnp.where(slot_table[0][:, :, None] == token_ids[None, None, :], slot_gates[0][:, :, None], 0.0),
        axis=1,
    )
    grad_in = to_slots(out_grad, dp, bits, 1).astype(f32)
    ffn_grad = (valid_rows * grad_in).astype(bf16)

    pack_rows = w_latent.shape[0]
    gain_row = jnp.concatenate([attn_gain, ffn_gain, latent_gain])
    gain_row = jnp.pad(gain_row, (0, w_latent.shape[1] - gain_row.shape[0]))
    pack = jnp.concatenate([w_latent, jnp.broadcast_to(gain_row, (16, w_latent.shape[1]))], axis=0)
    pack = gather_dp(pack[None], bits)
    pack = gather_tensor(pack[None])
    pack_blocks = [pack[tensor_slots.index(j)] for j in range(n_tensor)]
    pack = jnp.stack(select_blocks(pack_blocks, tensor), axis=1)
    latent_full = pack[:, :, :pack_rows].reshape(D, KR + RD)
    gains = pack[:, :, pack_rows]
    gain_width, latent_width = D // (n_dp * n_tensor), KR // (n_dp * n_tensor)
    attn_gain_full = gains[..., :gain_width].reshape(D)
    ffn_gain_full = gains[..., gain_width : 2 * gain_width].reshape(D)
    latent_gain_full = from_slots(
        gains[..., 2 * gain_width : 2 * gain_width + latent_width].reshape(KR), dp, bits, 0
    )
    query_full = gather_dp(w_query, bits)
    keyval_full = from_slots(gather_dp(w_keyval, bits), dp, bits, 0)
    output_full = gather_dp(w_output[None], bits)
    output_full = jnp.concatenate([output_full[k] for k in range(n_dp)], axis=1)

    n_half = EXPERTS // 2
    expert_units = jnp.concatenate(
        [
            w_expert_in.transpose(0, 1, 3, 2).reshape(EXPERTS, -1, w_expert_in.shape[2]),
            w_expert_out,
        ],
        axis=1,
    )
    width = w_expert_out.shape[1]
    shared_t = w_shared_in.transpose(0, 2, 1)
    units = []
    for side in range(2):
        cut = slice(side * width, (side + 1) * width)
        shared_unit = jnp.concatenate([shared_t[0, cut], shared_t[1, cut], w_shared_out[cut]], axis=0)
        units.append(jnp.concatenate([expert_units[side * n_half : (side + 1) * n_half], shared_unit[None]], axis=0))
    first = half == 0
    own_units = jnp.where(first, units[0], units[1])
    other_units = jnp.where(first, units[1], units[0])
    pieces = []
    for p in range(n_half + 1):
        piece = jnp.stack([own_units[p], swap_dp(other_units[p], merge)], axis=0)
        piece = gather_dp(piece, bits[1:])
        pieces.append(jnp.concatenate([piece[k] for k in range(n_dp)], axis=1))

    positions = token_ids - jnp.sum(
        (segment_canon[None, :] < segment_row[:, None]).astype(jnp.int32), axis=1
    )
    cos_all, sin_all = rotary_tables(positions)
    allowed = (segment_row[:, None] == segment_row[None, :]) & (
        token_ids[None, :] <= token_ids[:, None]
    )
    resid_all = res_all.astype(f32)
    in_factor = rms_factor(resid_all)
    normed_all = (resid_all * in_factor * attn_gain_full).astype(bf16)
    latent_raw = jnp.dot(normed_all, latent_full, preferred_element_type=f32)
    latent_c = latent_raw[:, :KR]
    latent_factor = rms_factor(latent_c)
    latent_norm = (latent_c * latent_factor * latent_gain_full).astype(bf16)
    rope_all = rotate(latent_raw[:, KR:], cos_all, sin_all).astype(bf16)
    query_raw = jnp.dot(normed_all, query_full, preferred_element_type=f32).reshape(
        TOK, local_heads, HD + RD
    )
    query_final = jnp.concatenate(
        [
            query_raw[..., :HD],
            rotate(query_raw[..., HD:], cos_all[:, None, :], sin_all[:, None, :]),
        ],
        axis=-1,
    ).astype(bf16)
    keyval = (
        jnp.dot(latent_norm, keyval_full, preferred_element_type=f32)
        .astype(bf16)
        .reshape(TOK, local_heads, HD + VD)
    )
    key_nope = keyval[..., :HD]
    values_all = keyval[..., HD:]
    raw_scores = jnp.einsum(
        "qhd,khd->hqk", query_final[..., :HD], key_nope, preferred_element_type=f32
    )
    raw_scores = raw_scores + jnp.einsum(
        "qhr,kr->hqk", query_final[..., HD:], rope_all, preferred_element_type=f32
    )
    scores = jnp.where(allowed[None], raw_scores * score_scale, -1e30)
    top_score = jnp.max(scores, axis=-1, keepdims=True)
    exp_scores = jnp.exp(scores - top_score)
    probs_all = exp_scores / jnp.sum(exp_scores, axis=-1, keepdims=True)
    probs_low = probs_all.astype(bf16)
    attn_mix = (
        jnp.einsum("hqk,khd->qhd", probs_low, values_all, preferred_element_type=f32)
        .astype(bf16)
        .reshape(TOK, local_heads * VD)
    )
    attn_part = jnp.dot(attn_mix, output_full, preferred_element_type=f32)
    attn_out = scatter_tensor(attn_part)
    resid_in = res_local.astype(f32)
    mid_resid = resid_in + valid_rows * attn_out
    mid_factor = rms_factor(mid_resid)
    normed_mid = (mid_resid * mid_factor * ffn_gain_full).astype(bf16)

    mid_pair = gather_pair(normed_mid, merge)
    grad_pair = gather_pair(ffn_grad, merge)
    other_gate = swap_dp(group_gate, merge)
    pair_gate = jnp.concatenate(
        [
            gate[:, k * rows : (k + 1) * rows]
            for k in ((0, 0), (1, 0), (0, 1), (1, 1), (0, 2), (1, 2), (0, 3), (1, 3))
            for gate, k in (((group_gate, other_gate)[k[0]], k[1]),)
        ],
        axis=1,
    )
    pair_gate = jnp.where(first, pair_gate[:n_half], pair_gate[n_half:])
    mid_pair_grad = None
    hidden_parts, out_parts, unit_grads = [], [], []
    for p, piece in enumerate(pieces):
        gate_up = dot(piece[: 2 * width], mid_pair, ((1,), (1,)))
        gate_pre, up = gate_up[:width], gate_up[width:]
        silu, slope = silu_parts(gate_pre)
        hidden_grad = dot(piece[2 * width :], grad_pair, ((1,), (1,)))
        hidden = silu * up
        if p < n_half:
            hidden = hidden * pair_gate[p][None]
            hidden_grad = hidden_grad * pair_gate[p][None]
        hidden = hidden.astype(bf16)
        pre_grad = jnp.concatenate(
            [(hidden_grad * up * slope).astype(bf16), (hidden_grad * silu).astype(bf16)], axis=0
        )
        back = dot(pre_grad, piece[: 2 * width], ((0,), (0,)))
        mid_pair_grad = back if mid_pair_grad is None else mid_pair_grad + back
        hidden_parts.append(hidden)
        out_parts.append(piece[2 * width :])
        in_wgrad = dot(pre_grad, mid_pair, ((1,), (0,)))
        out_wgrad = dot(hidden, grad_pair, ((1,), (0,)))
        unit_grads.append(jnp.concatenate([in_wgrad, out_wgrad], axis=0).astype(bf16))
    ffn_part = dot(
        jnp.concatenate(hidden_parts, axis=0), jnp.concatenate(out_parts, axis=0), ((0,), (0,))
    )
    ffn_out = scatter_pair(ffn_part, merge)
    res_out = (mid_resid + valid_rows * ffn_out).astype(bf16)
    mid_grad_local = scatter_pair(mid_pair_grad, merge)

    mid_back, ffn_gain_part = norm_back(mid_grad_local, mid_resid, mid_factor, ffn_gain_full)
    mid_grad = grad_in + mid_back
    attn_grad = (valid_rows * mid_grad).astype(bf16)
    attn_grad_all = gather_tensor(attn_grad)
    output_wgrad = dot(attn_mix, attn_grad_all, ((0,), (0,)))
    mix_grad = (
        dot(attn_grad_all, output_full, ((1,), (1,))).astype(bf16).reshape(TOK, local_heads, VD)
    )
    probs_grad = jnp.einsum("qhd,khd->hqk", mix_grad, values_all, preferred_element_type=f32)
    value_grad = jnp.einsum("hqk,qhd->khd", probs_low, mix_grad, preferred_element_type=f32)
    scores_grad = (
        probs_all * (probs_grad - jnp.sum(probs_all * probs_grad, axis=-1, keepdims=True))
    ).astype(bf16)
    query_nope_grad = (
        jnp.einsum("hqk,khd->qhd", scores_grad, key_nope, preferred_element_type=f32) * score_scale
    )
    query_rope_grad = (
        jnp.einsum("hqk,kr->qhr", scores_grad, rope_all, preferred_element_type=f32) * score_scale
    )
    key_nope_grad = (
        jnp.einsum("hqk,qhd->khd", scores_grad, query_final[..., :HD], preferred_element_type=f32)
        * score_scale
    )
    rope_key_grad = (
        jnp.einsum("hqk,qhr->kr", scores_grad, query_final[..., HD:], preferred_element_type=f32)
        * score_scale
    )
    query_grad = (
        jnp.concatenate(
            [query_nope_grad, rotate(query_rope_grad, cos_all[:, None, :], -sin_all[:, None, :])],
            axis=-1,
        )
        .astype(bf16)
        .reshape(TOK, local_heads * (HD + RD))
    )
    keyval_grad = (
        jnp.concatenate([key_nope_grad, value_grad], axis=-1)
        .astype(bf16)
        .reshape(TOK, local_heads * (HD + VD))
    )
    latent_part = jnp.concatenate([dot(keyval_grad, keyval_full, ((1,), (1,))), rope_key_grad], axis=1)
    latent_grad_local = scatter_tensor(latent_part)
    normed_part = dot(query_grad, query_full, ((1,), (1,)))
    normed_grad_local = scatter_tensor(normed_part)
    query_wgrad = dot(normed_all, query_grad, ((0,), (0,)))
    keyval_wgrad = to_slots(dot(latent_norm, keyval_grad, ((0,), (0,))).astype(bf16), dp, bits, 0)
    latent_c_grad, latent_gain_part = norm_back(
        latent_grad_local[:, :KR], latent_c[:rows], latent_factor[:rows], latent_gain_full
    )
    rope_raw_grad = rotate(latent_grad_local[:, KR:], cos_all[:rows], -sin_all[:rows])
    latent_raw_grad = jnp.concatenate([latent_c_grad, rope_raw_grad], axis=1).astype(bf16)
    latent_raw_grad_all = gather_tensor(latent_raw_grad)
    latent_wgrad = dot(normed_all, latent_raw_grad_all, ((0,), (0,))).astype(bf16)
    latent_wgrad = lax.dynamic_index_in_dim(
        latent_wgrad.reshape(n_dp, n_tensor, pack_rows, KR + RD), tensor, 1, keepdims=False
    )
    normed_grad = normed_grad_local + dot(latent_raw_grad, latent_full, ((1,), (1,)))
    in_back, attn_gain_part = norm_back(normed_grad, resid_in, in_factor[:rows], attn_gain_full)
    res_grad = mid_grad + in_back

    output_owned = scatter_dp(output_wgrad, bits, 1)
    query_owned = scatter_dp(query_wgrad, bits, 0)
    keyval_owned = scatter_dp(keyval_wgrad, bits, 0)
    latent_owned = scatter_dp(latent_wgrad, bits, 0)[0]
    gain_parts = jnp.concatenate(
        [
            attn_gain_part.reshape(n_dp, n_tensor, gain_width),
            ffn_gain_part.reshape(n_dp, n_tensor, gain_width),
            to_slots(latent_gain_part, dp, bits, 0).reshape(n_dp, n_tensor, latent_width),
        ],
        axis=2,
    )
    gain_parts = jnp.stack(
        [
            select_blocks([gain_parts[:, i] for i in range(n_tensor)], tensor)[j]
            for j in tensor_slots
        ],
        axis=0,
    )
    for bit in (0, 1):
        keep, give = jnp.split(gain_parts, 2, axis=0)
        gain_parts = keep + swap_tensor(give, bit)
    gain_parts = gain_parts[0]
    for bit in reversed(bits):
        keep, give = jnp.split(gain_parts, 2, axis=0)
        gain_parts = keep + swap_dp(give, bit)
    gain_owned = gain_parts[0]
    own_grads, other_grads = [], []
    for grad in unit_grads:
        grad = grad.astype(f32)
        for bit in reversed(bits[1:]):
            keep, give = jnp.split(grad, 2, axis=1)
            grad = keep + swap_dp(give.astype(bf16), bit).astype(f32)
        keep, give = jnp.split(grad, 2, axis=1)
        own_grads.append(keep)
        other_grads.append(swap_dp(give.astype(bf16), merge).astype(f32))
    sides = []
    for side in (first, ~first):
        sides.append([jnp.where(side, a, b) for a, b in zip(own_grads, other_grads)])
    expert_units = jnp.stack([unit for side in sides for unit in side[:n_half]], axis=0)
    expert_in_owned = expert_units[:, : 2 * width].reshape(EXPERTS, 2, width, -1).transpose(0, 1, 3, 2)
    expert_out_owned = expert_units[:, 2 * width :]
    shared_in_owned = jnp.stack(
        [
            jnp.concatenate([side[n_half][k * width : (k + 1) * width] for side in sides], axis=0).T
            for k in range(2)
        ],
        axis=0,
    )
    shared_out_owned = jnp.concatenate([side[n_half][2 * width :] for side in sides], axis=0)
    return (
        from_slots(res_out, dp, bits, 1),
        from_slots(res_grad, dp, bits, 1),
        gain_owned[:gain_width],
        gain_owned[2 * gain_width :],
        gain_owned[gain_width : 2 * gain_width],
        latent_owned,
        query_owned,
        keyval_owned,
        output_owned,
        expert_in_owned,
        expert_out_owned,
        shared_in_owned,
        shared_out_owned,
    )


DP, TENSOR = "dp", "tensor"
MESH = pl.DeviceIdType.MESH
F32 = jnp.float32
BF16 = jnp.bfloat16
CHUNKS = 3
SECONDS = 9
THIRDS = 7
SLOT = 256
GIVEN_VMEM = 60 * 1024 * 1024
FAR_FIRST = (2, 1, 0)
FLIPS = (1, 2, 0)
TENSOR_BITS = (1, 0)


COLUMNS = slot_order(FAR_FIRST)
UNIT_SLOTS = slot_order(FLIPS)
ROWS = slot_order(TENSOR_BITS)


def nn(a, b):
    return lax.dot_general(a, b, (((1,), (0,)), ((), ())), preferred_element_type=F32)


def nt(a, b):
    return lax.dot_general(a, b, (((1,), (1,)), ((), ())), preferred_element_type=F32)


def tn(a, b):
    return lax.dot_general(a, b, (((0,), (0,)), ((), ())), preferred_element_type=F32)


def lanes(k, width=SLOT):
    return slice(k * width, (k + 1) * width)


def crossed(index, constant, bits):
    total = 0
    for bit in range(bits):
        own = lax.rem(index // (1 << bit), 2)
        total = total + ((1 - own) if (constant >> bit) & 1 else own) * (1 << bit)
    return total


class Copies:
    def __init__(self, send_sems, recv_sems, local_sems=None):
        self.send_sems, self.recv_sems, self.local_sems = send_sems, recv_sems, local_sems
        self.count = 0
        self.local_count = 0

    def across(self, axis, bit):
        index = lax.axis_index(axis)
        side = lax.rem(index // (1 << bit), 2)
        return {axis: index + (1 - 2 * side) * (1 << bit)}

    def start(self, source, target, axis, bit):
        copy = pltpu.make_async_remote_copy(
            src_ref=source,
            dst_ref=target,
            send_sem=self.send_sems.at[self.count],
            recv_sem=self.recv_sems.at[self.count],
            device_id=self.across(axis, bit),
            device_id_type=MESH,
        )
        self.count += 1
        copy.start()
        return copy

    def local(self, source, target):
        copy = pltpu.make_async_copy(source, target, self.local_sems.at[self.local_count])
        self.local_count += 1
        copy.start()
        return copy

    def greet(self, dp_bits, tensor_bits=TENSOR_BITS):
        barrier = pltpu.get_barrier_semaphore()
        for axis, bits in ((DP, dp_bits), (TENSOR, tensor_bits)):
            for bit in bits:
                pl.semaphore_signal(
                    barrier, inc=1, device_id=self.across(axis, bit), device_id_type=MESH
                )
        pl.semaphore_wait(barrier, len(dp_bits) + len(tensor_bits))

    def swapped(self, source, target, first, width):
        parts = []
        for a in range(first, first + width, 1024):
            for b, c in ((a, a + 512), (a + 512, a)):
                parts.append(
                    self.start(
                        source.at[(slice(None),) * (len(source.shape) - 1) + (pl.ds(b, 512),)],
                        target.at[(slice(None),) * (len(target.shape) - 1) + (pl.ds(c, 512),)],
                        DP,
                        1,
                    )
                )
        return Several(parts)


class Several:
    def __init__(self, parts):
        self.parts = parts

    def wait(self):
        for part in self.parts:
            part.wait()


class SlotGather:
    def __init__(self, copies, source, slots, bits, axis=DP, cut=None):
        self.copies, self.source, self.slots, self.bits, self.axis = copies, source, slots, list(bits), axis
        self.cut = (slice(None),) if cut is None else (pl.ds(*cut),)
        self.done, self.have, self.own, self.flying = 0, 1, None, None

    def view(self, first, count):
        return self.slots.at[(pl.ds(first, count), *self.cut)]

    def start(self):
        bit = self.bits[self.done]
        if self.done == 0 and self.source is not None:
            source = self.source.at[(pl.ds(0, 1), *self.cut)]
            self.own = self.copies.local(source, self.view(0, 1))
        else:
            if self.own is not None:
                self.own.wait()
                self.own = None
            source = self.view(0, self.have)
        self.flying = self.copies.start(source, self.view(self.have, self.have), self.axis, bit)
        self.done += 1
        self.have *= 2

    def wait(self):
        self.flying.wait()
        self.flying = None
        if self.done < len(self.bits):
            self.start()

    def finish(self):
        while self.flying is not None:
            self.wait()


ANY_SPEC = pl.BlockSpec(memory_space=pl.ANY)
VMEM_SPEC = pl.BlockSpec(memory_space=pltpu.VMEM)
SMEM_SPEC = pl.BlockSpec(memory_space=pltpu.SMEM)


def cost(micros):
    return pl.CostEstimate(flops=micros * 10**9, bytes_accessed=micros * 10**6, transcendentals=0)


def like(shape, dtype=BF16):
    return jax.ShapeDtypeStruct(shape, dtype)


def turn(a, b, cos, sin):
    return a * cos - b * sin, b * cos + a * sin


def head_lanes(rows, head):
    lane = lax.broadcasted_iota(jnp.int32, (rows, SLOT), 1)
    return lax.rem(lane // 32, 4) == head


def spread_block(copies, pair_ref, between):
    block = lambda k: pair_ref.at[pl.ds(k, 1)]
    x_own = copies.start(block(0), block(2), TENSOR, 1)
    z_own = copies.swapped(block(0), block(1), 0, D)
    waits = [copies.start(block(0), block(4), TENSOR, 0)]
    between()
    z_own.wait()
    over_both = copies.start(block(1), block(3), TENSOR, 1)
    waits.append(copies.start(block(1), block(5), TENSOR, 0))
    between()
    x_own.wait()
    waits.append(copies.start(block(2), block(6), TENSOR, 0))
    between()
    over_both.wait()
    waits.append(copies.start(block(3), block(7), TENSOR, 0))
    for copy in waits:
        copy.wait()


class Places:
    def __init__(self):
        self.dp, self.tensor = lax.axis_index(DP), lax.axis_index(TENSOR)

    def __getitem__(self, k):
        if k == 12:
            return lax.rem(self.dp // 2, 2)
        return crossed(self.dp, COLUMNS[k], 3) if k < 8 else crossed(self.tensor, ROWS[k - 8], 2)


class Kept:
    output = ((8, 512, SLOT), BF16)
    mix = ((TOK, 512), BF16)
    query_final = ((TOK, 768), BF16)
    keyval_final = ((TOK, 1024), BF16)
    key_rope = ((TOK, SLOT), BF16)
    lse = ((TOK, 128), F32)
    query = ((8, SLOT, 768), BF16)
    w_keyval = ((KR, 1024), BF16)
    normed = ((TOK, D), BF16)
    latent_norm = ((TOK, KR), BF16)
    col = ((TOK, 128), F32)
    row = ((8, TOK), F32)
    cos = ((TOK, 128), F32)
    sin = ((TOK, 128), F32)
    gains = ((8, D), F32)
    latent_gain = ((8, KR), F32)
    latent_c = ((160, KR), F32)
    w_latent = ((D, KR + 128), BF16)
    mid = ((160, D), F32)
    mid_pair = ((8, 160, D), BF16)
    res = ((160, D), BF16)
    grad = ((160, D), BF16)
    valid = ((160, 128), F32)
    gates = ((8, TOK), F32)


class Landing:
    tokens = ((4, 160, D), BF16)
    pack = ((4, 8, 64, KR + 128), BF16)
    keyval = ((8, 64, 1024), BF16)
    part = ((4, 160, D), BF16)
    got_c = ((2, 160, D), BF16)
    give_x = ((1, 160, D), BF16)
    got_x = ((1, 160, D), BF16)
    gain_rows = ((KR, 128), BF16)
    masked = ((1, 160, D), BF16)
    own_pack = ((1, 64, KR + 128), BF16)
    own_query = ((1, SLOT, 768), BF16)


def fields(kind):
    return [name for name in vars(kind) if not name.startswith("_")]


def buffers(kind):
    return [getattr(kind, name) for name in fields(kind)]


def masks(col, row, cut):
    return (col[cut, 0:1] == row[0:1]) & (row[1:2] <= col[cut, 1:2])


def sort_columns(rows):
    column = lax.broadcasted_iota(jnp.int32, (768, 768), 1)
    row = lax.broadcasted_iota(jnp.int32, (768, 768), 0)
    wide = (column // 128) * 192 + lax.rem(column, 128)
    late = column - 512
    narrow = (lax.rem(late, 128) // 32) * 192 + 128 + (late // 128) * 32 + lax.rem(late, 32)
    return jnp.where(row == jnp.where(column < 512, wide, narrow), 1.0, 0.0).astype(BF16)


def front_kernel(
    width,
    count_ref,
    keyval_ref,
    output_ref,
    expert_in,
    expert_out,
    shared_in,
    shared_out,
    res_ref,
    grad_ref,
    query_ref,
    segment_row,
    table_ref,
    slot_gates,
    frequency_ref,
    latent_ref,
    attn_gain_ref,
    ffn_gain_ref,
    latent_gain_ref,
    grad_pair,
    gates_over,
    *rest,
):
    n_units = 3
    lows, highs = rest[:n_units], rest[n_units : 2 * n_units]
    rest = rest[2 * n_units :]
    kept, names = fields(Kept), fields(Kept) + fields(Landing)
    outs = types.SimpleNamespace(**dict(zip(kept, rest)))
    rest = rest[len(kept) :]
    at = types.SimpleNamespace(**dict(zip(names, rest)))
    send_sems, recv_sems, local_sems = rest[len(names) :]
    copies = Copies(send_sems, recv_sems, local_sems)
    places = Places()
    saved = []

    def save(pick):
        for source, target in zip(pick(at), pick(outs)):
            saved.append(copies.local(source, target))

    at.own_pack[0] = jnp.zeros((64, KR + 128), BF16)
    at.own_pack[0, :, : KR + RD] = latent_ref[...]
    lane = lax.broadcasted_iota(jnp.int32, (64, 128), 1)
    ends = at.own_pack[0, :, KR:].astype(F32)
    for k, gain_ref in ((64, attn_gain_ref), (65, ffn_gain_ref)):
        column = jnp.broadcast_to(gain_ref[...].astype(F32), (8, 64)).T[:, 0:1]
        ends = jnp.where(lane == k, column, ends)
    at.own_pack[0, :, KR:] = ends.astype(BF16)
    column = jnp.broadcast_to(latent_gain_ref[...].astype(F32), (8, 16)).T[:, 0:1]
    lane = lax.broadcasted_iota(jnp.int32, (16, 128), 1)
    at.own_pack[0, 0:16, KR:] = jnp.where(lane == 66, column, ends[0:16]).astype(BF16)
    pack = SlotGather(copies, at.own_pack, at.pack.at[0], FAR_FIRST)
    copies.greet((0, 1, 2))
    keyval = SlotGather(copies, keyval_ref, at.keyval, FAR_FIRST)
    part = query_ref.shape[0] // 4
    queries = [
        SlotGather(copies, at.own_query, at.query, FAR_FIRST, cut=(k * part, part)) for k in range(4)
    ]
    part = output_ref.shape[1] // 2
    outputs = [SlotGather(copies, output_ref, at.output, FAR_FIRST, cut=(k * part, part)) for k in range(2)]
    pack.start()
    keyval.start()
    for k in range(8):
        block = pl.ds(pl.multiple_of(places[k] * SLOT, SLOT), SLOT)
        at.res[:, lanes(k)] = res_ref[:, block]
        at.grad[:, lanes(k)] = grad_ref[:, block]
    at.tokens[0] = at.res[...]
    tokens = SlotGather(copies, None, at.tokens, TENSOR_BITS, TENSOR)
    tokens.start()
    at.own_query[0] = nn(query_ref[...], sort_columns(768)).astype(BF16)
    items = [pack, keyval, *queries, *outputs]
    units = [(p, part) for p in range(n_units) for part in range(CHUNKS)]
    flights = [None] * len(units)
    owns = [None] * len(units)
    state = [0, 0, 0]

    def unit_source(side, p, part):
        if p < 2:
            expert = pl.ds(side * 2 + p, 1)
            return expert_out.at[expert] if part == 2 else expert_in.at[expert, part]
        cut = pl.ds(pl.multiple_of(side * width, 16), width)
        return shared_out.at[pl.ds(0, 1), cut] if part == 2 else shared_in.at[pl.ds(part, 1), cut]

    def unit_first():
        i = state[0]
        if i >= len(units):
            return
        p, part = units[i]
        cut = pl.ds(part * width, width)
        side = places[12]
        owns[i] = copies.local(unit_source(side, p, part), lows[p].at[pl.ds(0, 1), cut])
        flights[i] = copies.start(
            unit_source(1 - side, p, part), lows[p].at[pl.ds(1, 1), cut], DP, FLIPS[0]
        )
        state[0] = i + 1

    def unit_second():
        i = state[1]
        if i >= min(state[0], SECONDS):
            return
        p, part = units[i]
        cut = pl.ds(part * width, width)
        flights[i].wait()
        owns[i].wait()
        flights[i] = copies.start(
            lows[p].at[pl.ds(0, 2), cut], lows[p].at[pl.ds(2, 2), cut], DP, FLIPS[1]
        )
        state[1] = i + 1

    def unit_third():
        i = state[2]
        if i >= min(state[1], THIRDS):
            return
        p, part = units[i]
        cut = pl.ds(part * width, width)
        flights[i].wait()
        flights[i] = copies.start(lows[p].at[pl.ds(0, 4), cut], highs[p].at[pl.ds(0, 4), cut], DP, FLIPS[2])
        state[2] = i + 1

    def pump():
        unit_third()
        unit_second()
        unit_first()

    def place_tokens():
        segments = segment_row[...].astype(F32)
        at.col[:, 0:8] = jnp.broadcast_to(segments, (8, TOK)).T
        for b in range(4):
            start = pl.multiple_of(places[8 + b] * 160, 8)
            at.cos[b * 160 : (b + 1) * 160] = jnp.broadcast_to(at.col[pl.ds(start, 160), 0:1], (160, 128))
        for b in range(4):
            start = pl.multiple_of(places[8 + b] * 160, 8)
            cut = slice(b * 160, (b + 1) * 160)
            segment = at.cos[cut, 0:1]
            token = start + lax.broadcasted_iota(jnp.int32, (160, 128), 0)
            lane = lax.broadcasted_iota(jnp.int32, (160, 128), 1)
            at.col[cut] = jnp.where(lane == 0, segment, token.astype(F32))
            before = jnp.sum((segments < segment).astype(F32), axis=1, keepdims=True)
            angle = (token.astype(F32) - before) * frequency_ref[...]
            at.cos[cut] = jnp.cos(angle)
            at.sin[cut] = jnp.sin(angle)
        at.row[...] = at.col[...].T[0:8]
        at.valid[...] = (at.col[0:160, 1:2] < count_ref[0].astype(F32)).astype(F32) + jnp.zeros((160, 128), F32)
        at.masked[0] = (at.grad[...].astype(F32) * at.valid[:, 0:1]).astype(BF16)

    def route_tokens():
        slots = jnp.concatenate([table_ref[...].astype(F32), slot_gates[...]], axis=0).T
        token_row = at.row[1:2]
        for e in range(4):
            hit = jnp.where(slots[:, e : e + 1] == token_row, slots[:, 4 + e : 5 + e], 0.0)
            at.gates[e : e + 1] = jnp.sum(hit, axis=0, keepdims=True)
        at.gates[4:8] = jnp.zeros((4, TOK), F32)
        save(lambda v: (v.col, v.row, v.cos, v.sin, v.valid, v.res, v.grad, v.gates))

    def make_keys():
        for s in range(4):
            for k in range(8):
                start = pl.multiple_of(k * SLOT + places[8 + s] * 64, 64)
                at.w_latent[pl.ds(start, 64)] = at.pack[s, k]
                start = pl.multiple_of(places[k] * 64 + places[8 + s] * 16, 16)
                at.gain_rows[pl.ds(start, 16)] = at.pack[s, k, 0:16, KR : KR + 128]
        for k in range(8):
            at.w_keyval[pl.ds(pl.multiple_of(places[k] * 64, 64), 64)] = at.keyval[k]
        tail = at.w_latent[:, KR : KR + 128]
        turned = tail.astype(F32).T
        attn_gain = turned[64:65]
        at.gains[...] = turned[64:72]
        latent_gain = at.gain_rows[...].astype(F32).T[66:67]
        at.latent_gain[...] = jnp.broadcast_to(latent_gain, (8, KR))
        row = lax.broadcasted_iota(jnp.int32, (128, SLOT), 0)
        lane = lax.broadcasted_iota(jnp.int32, (128, SLOT), 1)
        spread = jnp.where(row == lax.rem(lane, 32) + 32 * (lane // 128), 1.0, 0.0).astype(BF16)
        w_rope = nn(tail, spread).astype(BF16)
        for b in range(4):
            cut = slice(b * 160, (b + 1) * 160)
            x = at.tokens[b].astype(F32)
            factor = lax.rsqrt(jnp.mean(x * x, axis=1, keepdims=True) + NORM_EPS)
            at.normed[cut] = (x * factor * attn_gain).astype(BF16)
        for b in range(2):
            cut = slice(b * 320, (b + 1) * 320)
            normed = at.normed[cut]
            latent_c = nn(normed, at.w_latent[:, :KR])
            factor = lax.rsqrt(jnp.mean(latent_c * latent_c, axis=1, keepdims=True) + NORM_EPS)
            latent_norm = (latent_c * factor * latent_gain).astype(BF16)
            if b == 0:
                at.latent_c[...] = latent_c[:160]
            at.latent_norm[cut] = latent_norm
            rope = nn(normed, w_rope)
            key_a, key_b = turn(rope[:, :128], rope[:, 128:], at.cos[cut], at.sin[cut])
            at.key_rope[cut] = jnp.concatenate([key_a, key_b], axis=1).astype(BF16)
            at.keyval_final[cut] = nn(latent_norm, at.w_keyval[...]).astype(BF16)
        save(lambda v: (v.w_latent, v.w_keyval, v.gains, v.latent_gain, v.normed, v.latent_c, v.latent_norm, v.key_rope, v.keyval_final,))


    unit_first()
    for tau in range(len(items) + 1):
        if tau >= 1:
            items[tau - 1].wait()
        if tau < len(items):
            items[tau].wait()
        if tau + 2 < len(items):
            items[tau + 2].start()
        if tau == 0:
            place_tokens()
        elif tau == 1:
            tokens.wait()
            grad_own = copies.local(at.masked, grad_pair.at[pl.ds(0, 1)])
            grad_x = copies.start(at.masked, grad_pair.at[pl.ds(2, 1)], TENSOR, 1)
        elif tau == 3:
            pack.wait()
            pack_tensor = SlotGather(copies, None, at.pack, TENSOR_BITS, TENSOR)
            pack_tensor.start()
            unit_second()
        elif tau == 4:
            unit_first()
            route_tokens()
            gates_flight = copies.start(at.gates, gates_over, DP, 1)
        elif tau == 5:
            tokens.wait()
            unit_second()
        elif tau == 6:
            pack_tensor.wait()
            unit_first()
        elif tau == 7:
            keyval.wait()
            pack_tensor.wait()
            make_keys()
            unit_second()
    grad_x.wait()
    grad_z = copies.swapped(at.masked, grad_pair.at[pl.ds(1, 1)], 0, D)
    pump()
    for query in queries:
        query.wait()

    save(lambda v: (v.query,))
    gates_flight.wait()
    w_query = at.query[...].reshape(D, 768)
    scale = (HD + RD) ** (-0.5)
    for b in range(2):
        cut = slice(b * 320, (b + 1) * 320)
        found = nn(at.normed[cut], w_query)
        turned_a, turned_b = turn(found[:, 512:640], found[:, 640:768], at.cos[cut], at.sin[cut])
        at.query_final[cut] = jnp.concatenate([found[:, :512], turned_a, turned_b], axis=1).astype(BF16)
        allowed = masks(at.col, at.row, cut)
        lse_lane = lax.broadcasted_iota(jnp.int32, (320, 128), 1)
        lse_all = jnp.zeros((320, 128), F32)
        for h in range(4):
            rope = at.query_final[cut, 512:768]
            rope = jnp.where(head_lanes(320, h), rope, jnp.zeros_like(rope))
            keys = at.keyval_final[:, h * 256 : h * 256 + 128]
            scores = nt(at.query_final[cut, lanes(h, 128)], keys) + nt(rope, at.key_rope[...])
            scores = jnp.where(allowed, scores * scale, -1e30)
            top = jnp.max(scores, axis=1, keepdims=True)
            weight = jnp.exp(scores - top)
            total = jnp.sum(weight, axis=1, keepdims=True)
            probs = (weight / total).astype(BF16)
            lse_all = jnp.where(lse_lane == h, top + jnp.log(total), lse_all)
            mix = nn(probs, at.keyval_final[:, h * 256 + 128 : h * 256 + 256])
            at.mix[cut, lanes(h, 128)] = mix.astype(BF16)
        at.lse[cut] = lse_all
        if b == 0:
            pump()
            grad_z.wait()
            grad_zx = copies.start(
                grad_pair.at[pl.ds(1, 1)], grad_pair.at[pl.ds(3, 1)], TENSOR, 1
            )
    for output in outputs:
        output.wait()
    save(lambda v: (v.query_final, v.mix, v.lse, v.output,))
    for b in range(2):
        cut = slice((1 - b) * 320, (2 - b) * 320)
        for k in range(8):
            w_output = at.output[k]
            part = nn(at.mix[cut], w_output).astype(BF16)
            at.part[2 - 2 * b, :, lanes(k)] = part[:160]
            at.part[3 - 2 * b, :, lanes(k)] = part[160:]
        if b == 0:
            block = lambda ref, k: ref.at[pl.ds(k, 1)]
            c_far = copies.start(block(at.part, 3), block(at.got_c, 1), TENSOR, 0)
            c_near = copies.start(block(at.part, 2), block(at.got_c, 0), TENSOR, 0)
    c_far.wait()
    at.give_x[0] = (at.part[1].astype(F32) + at.got_c[1].astype(F32)).astype(BF16)
    x_far = copies.start(at.give_x, at.got_x, TENSOR, 1)
    pump()
    grad_zx.wait()
    grad_own.wait()
    grad_c = copies.start(grad_pair.at[pl.ds(0, 4)], grad_pair.at[pl.ds(4, 4)], TENSOR, 0)
    pump()
    c_near.wait()
    x_far.wait()
    attn_out = at.part[0].astype(F32) + at.got_c[0].astype(F32) + at.got_x[0].astype(F32)
    mid = at.res[...].astype(F32) + at.valid[:, 0:1] * attn_out
    at.mid[...] = mid
    save(lambda v: (v.mid,))
    factor = lax.rsqrt(jnp.mean(mid * mid, axis=1, keepdims=True) + NORM_EPS)
    at.mid_pair[0] = (mid * factor * at.gains[1:2]).astype(BF16)
    spread_block(copies, at.mid_pair, pump)
    save(lambda v: (v.mid_pair,))
    grad_c.wait()
    while state[0] < len(units) or state[1] < SECONDS or state[2] < THIRDS:
        pump()
    for i in range(SECONDS, len(units)):
        owns[i].wait()
    for flight in flights:
        if flight is not None:
            flight.wait()
    for copy in saved:
        copy.wait()


def front(counts, latent, gains, keyval, output, expert_in, expert_out, shared_in, shared_out, res, grad, query, segment, table, gates):
    n_units, width = 3, expert_out.shape[1]
    half = (4, 3 * width, SLOT)
    frequency = ROPE_BASE ** (-np.arange(RD // 2, dtype=np.float32) / np.float32(RD // 2))
    frequency = jnp.asarray(np.tile(frequency.astype(np.float32), 4)[None])
    operands = [
        counts,
        keyval[None],
        output[None],
        expert_in.transpose(0, 1, 3, 2),
        expert_out,
        shared_in.transpose(0, 2, 1),
        shared_out[None],
        res,
        grad,
        query,
        segment,
        table,
        gates,
        frequency,
        latent,
        *gains,
    ]
    shapes = [like((8, *res.shape)), like((8, TOK), F32)] + [like(half)] * (2 * n_units - 1) + [like((4, width, SLOT))]
    shapes += [like(*buffer) for buffer in buffers(Kept)]
    results = pl.pallas_call(
        functools.partial(front_kernel, width),
        out_shape=shapes,
        in_specs=[SMEM_SPEC] + [ANY_SPEC] * 6 + [VMEM_SPEC] * 11,
        out_specs=[ANY_SPEC] * len(shapes),
        scratch_shapes=[pltpu.VMEM(*buffer) for buffer in buffers(Kept) + buffers(Landing)]
        + [
            pltpu.SemaphoreType.DMA((80,)),
            pltpu.SemaphoreType.DMA((80,)),
            pltpu.SemaphoreType.DMA((48,)),
        ],
        compiler_params=pltpu.CompilerParams(
            collective_id=0, has_side_effects=True, vmem_limit_bytes=GIVEN_VMEM
        ),
        cost_estimate=cost(220),
        name="front",
    )(*operands)
    grad_pair, gates_over, results = results[0], results[1], results[2:]
    lows, results = results[:n_units], results[n_units:]
    highs, results = results[:n_units], results[n_units:]
    return grad_pair, gates_over, lows, highs, types.SimpleNamespace(**dict(zip(fields(Kept), results)))


TOKEN_BLOCK = 256


class Freight:
    def __init__(self, copies, bits, sources, targets):
        self.copies, self.bits, self.pairs = copies, bits, list(zip(sources, targets))
        self.flights = []

    def start(self):
        for bit, (source, target) in zip(self.bits, self.pairs):
            self.flights.append(self.copies.start(source, target, DP, bit))

    def wait(self):
        for flight in self.flights:
            flight.wait()


class Split:
    def __init__(self, copies, keep, got, kept, gone):
        self.copies, self.kept, self.gone = copies, kept, gone
        self.loads = [copies.local(keep, kept), copies.local(got, gone)]
        self.half = kept.shape[0] // 2
        self.flights = []

    def send(self, bit, target, stay=None):
        for load in self.loads:
            load.wait()
        for k in range(2 * self.half):
            target_ref = self.kept if k < self.half else self.gone
            target_ref[k] = (self.kept[k].astype(F32) + self.gone[k].astype(F32)).astype(BF16)
        self.flights.append(
            self.copies.start(self.gone.at[pl.ds(self.half, self.half)], target, DP, bit)
        )
        if stay is not None:
            self.flights.append(self.copies.local(self.kept.at[pl.ds(0, self.half)], stay))

    def wait(self):
        for flight in self.flights:
            flight.wait()


def split_scratch(splits):
    return [pltpu.VMEM(keep.shape, BF16) for keep, _, _ in splits for _ in range(2)] + [
        pltpu.SemaphoreType.DMA((4 * len(splits),))
    ]


def split_outputs(splits):
    return [like((keep.shape[0] // 2, *keep.shape[1:])) for keep, _, _ in splits for _ in range(2)]


def experts_kernel(width, has_sum, gated, bits, parts, *refs):
    refs = list(refs)
    take = lambda n: [refs.pop(0) for _ in range(n)]
    mid_ref, grad_ref = take(2)
    gate_ref = take(1)[0] if gated else None
    unit_refs = take(len(parts))
    if has_sum:
        back_in, out_in = take(2)
    sources = take(len(bits))
    back_ref, out_ref = take(2)
    keep_refs, give_refs = take(3), take(3)
    targets = take(len(bits))
    whole, total, send_sems, recv_sems, local_sems = take(5)
    step = pl.program_id(0)
    copies = Copies(send_sems, recv_sems, local_sems)

    def flights():
        return [
            pltpu.make_async_remote_copy(
                src_ref=cut.view(source),
                dst_ref=target,
                send_sem=send_sems.at[k],
                recv_sem=recv_sems.at[k],
                device_id=copies.across(DP, cut.bit),
                device_id_type=MESH,
            )
            for k, (cut, source, target) in enumerate(zip(bits, sources, targets))
        ]

    @pl.when(step == 0)
    def _():
        total[...] = jnp.zeros_like(total)
        copies.greet(sorted({cut.bit for cut in bits}), ())
        for flight in flights():
            flight.start()
        loads = []
        for ref, (slot, count, start, size, skip) in zip(unit_refs, parts):
            for j in range(count):
                k = COLUMNS.index(UNIT_SLOTS[slot + j])
                loads.append(
                    copies.local(
                        ref.at[j, pl.ds(skip, size)], whole.at[pl.ds(start, size), pl.ds(k * SLOT, SLOT)]
                    )
                )
        for load in loads:
            load.wait()

    mid, grad = mid_ref[...], grad_ref[...]
    gate_up = nt(whole[: 2 * width], mid)
    hidden_grad = nt(whole[2 * width :], grad)
    gate = gate_up[:width]
    up = gate_up[width:]
    sigma = 1.0 / (1.0 + jnp.exp(-gate))
    silu = gate * sigma
    slope = sigma * (1.0 + gate * (1.0 - sigma))
    hidden = silu * up
    if gated:
        hidden_grad = hidden_grad * gate_ref[...]
        hidden = hidden * gate_ref[...]
    hidden = hidden.astype(BF16)
    pre = jnp.concatenate(
        [(hidden_grad * up * slope).astype(BF16), (hidden_grad * silu).astype(BF16)], axis=0
    )
    back = tn(pre, whole[: 2 * width])
    out = tn(hidden, whole[2 * width :])
    if has_sum:
        back = back + back_in[...]
        out = out + out_in[...]
    back_ref[...] = back.astype(back_ref.dtype)
    out_ref[...] = out.astype(out_ref.dtype)
    total[: 2 * width] += nn(pre, mid)
    total[2 * width :] += nn(hidden, grad)

    @pl.when(step == pl.num_programs(0) - 1)
    def _():
        for g in range(3):
            cut = slice(g * width, (g + 1) * width)
            for k in range(4):
                keep_refs[g][k] = total[cut, lanes((0, 2, 1, 3)[k])].astype(BF16)
                give_refs[g][k] = total[cut, lanes(4 + (0, 2, 1, 3)[k])].astype(BF16)
        for flight in flights():
            flight.wait()


class Cut:
    def __init__(self, array, bit, slots=None, rows=None):
        self.array, self.bit = array, bit
        self.slots = slots or (0, array.shape[0])
        self.rows = rows or (0, array.shape[1])

    def shape(self):
        return (self.slots[1], self.rows[1], self.array.shape[2])

    def view(self, ref):
        return ref.at[pl.ds(*self.slots), pl.ds(*self.rows)]


def experts_step(mid_pair, grad_pair, unit, gate, sums, last, freight, ident):
    tokens, block = mid_pair.shape[0], TOKEN_BLOCK
    width = unit[0][0].shape[1] // 3
    rows = pl.BlockSpec((block, D), lambda i: (i, 0))
    fixed = lambda *shape: pl.BlockSpec(shape, lambda i: (0,) * len(shape))
    kind = BF16 if last else F32
    part = (4, width, SLOT)
    operands, specs = [mid_pair, grad_pair], [rows, rows]
    if gate is not None:
        operands, specs = operands + [gate[None]], specs + [pl.BlockSpec((1, block), lambda i: (0, i))]
    operands += [part[0] for part in unit]
    specs += [ANY_SPEC] * len(unit)
    if sums is not None:
        operands += list(sums)
        specs += [rows, rows]
    results = pl.pallas_call(
        functools.partial(
            experts_kernel, width, sums is not None, gate is not None, tuple(freight), tuple(p[1:] for p in unit)
        ),
        grid=(tokens // block,),
        out_shape=[like((tokens, D), kind)] * 2
        + [like(part)] * 6
        + [like(cut.shape()) for cut in freight],
        in_specs=specs + [ANY_SPEC] * len(freight),
        out_specs=[rows, rows] + [fixed(*part)] * 6 + [ANY_SPEC] * len(freight),
        scratch_shapes=[
            pltpu.VMEM((3 * width, D), BF16),
            pltpu.VMEM((3 * width, D), F32),
            pltpu.SemaphoreType.DMA((len(freight),)),
            pltpu.SemaphoreType.DMA((len(freight),)),
            pltpu.SemaphoreType.DMA((24,)),
        ],
        compiler_params=pltpu.CompilerParams(
            collective_id=ident, has_side_effects=True, vmem_limit_bytes=GIVEN_VMEM
        ),
        cost_estimate=cost(35),
        name="experts_step",
    )(*operands, *[cut.array for cut in freight])
    return list(results[:2]), list(results[2:5]), list(results[5:8]), list(results[8:])


def halve_kernel(count, *refs):
    keeps, gots, stays, gives = (refs[k * count : (k + 1) * count] for k in range(4))
    for keep, got, stay, give in zip(keeps, gots, stays, gives):
        half = stay.shape[0]
        for k in range(half):
            stay[k] = (keep[k].astype(F32) + got[k].astype(F32)).astype(BF16)
            give[k] = (keep[half + k].astype(F32) + got[half + k].astype(F32)).astype(BF16)


def halve(pairs):
    count = len(pairs)
    shapes = [like((keep.shape[0] // 2, *keep.shape[1:])) for keep, _ in pairs]
    results = pl.pallas_call(
        functools.partial(halve_kernel, count),
        out_shape=shapes * 2,
        in_specs=[VMEM_SPEC] * (2 * count),
        out_specs=[VMEM_SPEC] * (2 * count),
        cost_estimate=cost(3),
        name="halve",
    )(*[keep for keep, _ in pairs], *[got for _, got in pairs])
    return list(zip(results[:count], results[count:]))


class PairSum:
    def __init__(self, copies, blocks, got_c, give_a, give_b, got_a, got_b, end_a, end_b, last_a, last_b):
        self.copies, self.blocks, self.got_c = copies, blocks, got_c
        self.give_a, self.give_b, self.got_a, self.got_b = give_a, give_b, got_a, got_b
        self.end_a, self.end_b, self.last_a, self.last_b = end_a, end_b, last_a, last_b

    def both(self, k, first):
        cut = slice(first, first + 1024)
        return self.blocks[k, :, cut].astype(F32) + self.got_c[k, :, cut].astype(F32)

    def start(self):
        self.flights = {}
        for k in (3, 2, 1, 0):
            self.flights[k] = self.copies.start(
                self.blocks.at[pl.ds(4 + k, 1)], self.got_c.at[pl.ds(k, 1)], TENSOR, 0
            )

    def cross(self):
        self.flights[3].wait()
        self.give_a[1] = self.both(3, 0).astype(BF16)
        self.give_b[1] = self.both(3, 1024).astype(BF16)
        self.flights[2].wait()
        self.give_a[0] = self.both(2, 0).astype(BF16)
        self.across_a = self.copies.start(self.give_a, self.got_a, TENSOR, 1)
        self.flights[1].wait()
        self.give_b[0] = self.both(1, 1024).astype(BF16)
        self.across_b = self.copies.swapped(self.give_b, self.got_b, 0, 1024)
        self.flights[0].wait()

    def end(self):
        self.across_a.wait()
        self.end_a[0] = (self.both(1, 0) + self.got_a[1].astype(F32)).astype(BF16)
        self.ends_a = self.copies.swapped(self.end_a, self.last_a, 0, 1024)
        self.across_b.wait()
        self.end_b[0] = (self.both(2, 1024) + self.got_b[1].astype(F32)).astype(BF16)
        self.ends_b = self.copies.start(self.end_b, self.last_b, TENSOR, 1)

    def settle(self, total, end_a, end_b):
        self.across_a.wait()
        end_a[0] = (self.both(1, 0) + self.got_a[1].astype(F32)).astype(BF16)
        self.across_b.wait()
        end_b[0] = (self.both(2, 1024) + self.got_b[1].astype(F32)).astype(BF16)
        total[:, :1024] = self.both(0, 0) + self.got_a[0].astype(F32)
        total[:, 1024:] = self.both(0, 1024) + self.got_b[0].astype(F32)

    def total(self):
        self.ends_a.wait()
        self.ends_b.wait()
        return (
            self.both(0, 0) + self.got_a[0].astype(F32) + self.last_a[0].astype(F32),
            self.both(0, 1024) + self.got_b[0].astype(F32) + self.last_b[0].astype(F32),
        )


def sum_scratch():
    half = pltpu.VMEM((2, 160, 1024), BF16)
    end = pltpu.VMEM((1, 160, 1024), BF16)
    return [pltpu.VMEM((4, 160, D), BF16), half, half, half, half, end, end, end, end]


def back_kernel(bits, splits, *refs):
    refs = list(refs)
    take = lambda n: [refs.pop(0) for _ in range(n)]
    back_ref, grad_ref, mid_ref, gains_ref, valid_ref = take(5)
    sources = take(len(bits))
    pairs = take(2 * len(splits))
    mid_grad_ref, gain_part_ref, tokens_ref = take(3)
    targets = take(len(bits))
    ends = take(2 * len(splits))
    rooms = take(2 * len(splits))
    local_sems, *buffers, send_sems, recv_sems = refs
    copies = Copies(send_sems, recv_sems, local_sems)
    parts = [Split(copies, *pairs[2 * k : 2 * k + 2], *rooms[2 * k : 2 * k + 2]) for k in range(len(splits))]
    copies.greet((0, 1, 2))
    freight = Freight(copies, bits, sources, targets)
    freight.start()
    pair = PairSum(copies, back_ref, *buffers)
    pair.start()
    for k, bit in enumerate(splits):
        parts[k].send(bit, ends[2 * k + 1], ends[2 * k])
    pair.cross()
    pair.end()
    first, second = pair.total()
    mid_grad_ref[:, :1024] = first
    mid_grad_ref[:, 1024:] = second
    grad, mid = mid_grad_ref[...], mid_ref[...]
    factor = lax.rsqrt(jnp.mean(mid * mid, axis=1, keepdims=True) + NORM_EPS)
    scaled = grad * gains_ref[1:2]
    inner = jnp.mean(scaled * mid, axis=1, keepdims=True)
    gain_part_ref[...] = jnp.broadcast_to(jnp.sum(grad * mid * factor, axis=0, keepdims=True), (8, D))
    mid_grad = grad_ref[...].astype(F32) + factor * (scaled - mid * factor * factor * inner)
    mid_grad_ref[...] = mid_grad
    tokens_ref[0] = (valid_ref[:, 0:1] * mid_grad).astype(BF16)
    own = tokens_ref.at[pl.ds(0, 1)]
    x_own = copies.start(own, tokens_ref.at[pl.ds(1, 1)], TENSOR, 1)
    c_own = copies.start(own, tokens_ref.at[pl.ds(2, 1)], TENSOR, 0)
    x_own.wait()
    c_far = copies.start(tokens_ref.at[pl.ds(1, 1)], tokens_ref.at[pl.ds(3, 1)], TENSOR, 0)
    c_own.wait()
    c_far.wait()
    freight.wait()
    for part in parts:
        part.wait()


def back_tokens(back, grad_slots, mid, gains, valid, freight, splits):
    rows = (160, D)
    bits = tuple(bit for bit, _ in freight)
    goods = [array for _, array in freight]
    results = pl.pallas_call(
        functools.partial(back_kernel, bits, tuple(bit for _, _, bit in splits)),
        out_shape=[like(rows, F32), like((8, D), F32), like((4, *rows))]
        + [like(g.shape, g.dtype) for g in goods]
        + split_outputs(splits),
        in_specs=[VMEM_SPEC] * 5 + [ANY_SPEC] * (len(goods) + 2 * len(splits)),
        out_specs=[VMEM_SPEC] * 3 + [ANY_SPEC] * (len(goods) + 2 * len(splits)),
        scratch_shapes=split_scratch(splits)
        + sum_scratch() + [pltpu.SemaphoreType.DMA((24,)), pltpu.SemaphoreType.DMA((24,))],
        compiler_params=pltpu.CompilerParams(
            collective_id=2, has_side_effects=True, vmem_limit_bytes=GIVEN_VMEM
        ),
        cost_estimate=cost(55),
        name="back_tokens",
    )(back, grad_slots, mid, gains, valid, *goods, *[v for keep, got, _ in splits for v in (keep, got)])
    n = 3 + len(goods)
    return results[:3], list(results[3:n]), list(zip(results[n::2], results[n + 1 :: 2]))


def attention_backward_kernel(bits, splits, *refs):
    refs = list(refs)
    take = lambda n: [refs.pop(0) for _ in range(n)]
    (
        grad_ref,
        output_ref,
        mix_ref,
        query_ref,
        keyval_ref,
        key_rope_ref,
        lse_ref,
        w_query_ref,
        w_keyval_ref,
        normed_ref,
        latent_norm_ref,
        col_ref,
        row_ref,
        cos_ref,
        sin_ref,
        out_ref,
    ) = take(16)
    sources = take(len(bits))
    pairs = take(2 * len(splits))
    output_wgrad, query_wgrad, keyval_wgrad, part_ref, out_sum, out_end_a, out_end_b = take(7)
    targets = take(len(bits))
    output_got = take(1)[0]
    ends = take(2 * len(splits))
    rooms = take(2 * len(splits))
    local_sems = take(1)[0]
    mix_grad, query_grad, keyval_grad, key_grad, rope_grad, wide, send_sems, recv_sems = take(8)
    copies = Copies(send_sems, recv_sems, local_sems)
    parts = [Split(copies, *pairs[2 * k : 2 * k + 2], *rooms[2 * k : 2 * k + 2]) for k in range(len(splits))]
    copies.greet((0, 1, 2))
    pair = PairSum(copies, out_ref, *refs, None, None, None, None)
    pair.start()
    freight = Freight(copies, bits, sources, targets)
    freight.start()
    for k, bit in enumerate(splits):
        parts[k].send(bit, ends[2 * k + 1], ends[2 * k])
    places = Places()
    scale = (HD + RD) ** (-0.5)
    w_query = w_query_ref[...].reshape(D, w_query_ref.shape[2])
    for k in range(8):
        block = jnp.concatenate([grad_ref[b, :, lanes(k)] for b in range(4)], axis=0)
        s = k
        output_wgrad[s] = tn(mix_ref[...], block).astype(BF16)
        term = nt(block, output_ref[s])
        if k == 0:
            wide[:, :512] = term
        else:
            wide[:, :512] += term
    mix_grad[...] = wide[:, :512].astype(BF16)
    output_flight = copies.start(output_wgrad.at[pl.ds(4, 4)], output_got, DP, 0)
    pair.cross()
    for b in range(2):
        cut = slice(b * 320, (b + 1) * 320)
        allowed = masks(col_ref, row_ref, cut)
        lse_lane = lax.broadcasted_iota(jnp.int32, (320, 128), 1)
        rope_sum = jnp.zeros((320, SLOT), F32)
        for h in range(4):
            nope = query_ref[cut, lanes(h, 128)]
            rope = query_ref[cut, 512:768]
            mask = head_lanes(320, h)
            rope = jnp.where(mask, rope, jnp.zeros_like(rope))
            keys = keyval_ref[:, h * 256 : h * 256 + 128]
            values = keyval_ref[:, h * 256 + 128 : h * 256 + 256]
            scores = nt(nope, keys) + nt(rope, key_rope_ref[...])
            lse = jnp.sum(jnp.where(lse_lane == h, lse_ref[cut], 0.0), axis=1, keepdims=True)
            probs = jnp.where(allowed, jnp.exp(scores * scale - lse), 0.0)
            grad = mix_grad[cut, lanes(h, 128)]
            probs_grad = nt(grad, values)
            inner = jnp.sum(probs * probs_grad, axis=1, keepdims=True)
            scores_grad = (probs * (probs_grad - inner)).astype(BF16)
            value_grad = tn(probs.astype(BF16), grad)
            nope_grad = tn(scores_grad, nope) * scale
            rope_part = tn(scores_grad, rope)
            low, high = slice(h * 256, h * 256 + 128), slice(h * 256 + 128, h * 256 + 256)
            if b == 0:
                key_grad[:, low] = nope_grad
                key_grad[:, high] = value_grad
            else:
                key_grad[:, low] += nope_grad
                key_grad[:, high] += value_grad
            if b == 0 and h == 0:
                rope_grad[...] = rope_part
            else:
                rope_grad[...] += rope_part
            query_grad[cut, lanes(h, 128)] = (nn(scores_grad, keys) * scale).astype(BF16)
            rope_sum = rope_sum + jnp.where(mask, nn(scores_grad, key_rope_ref[...]), 0.0)
        rope_sum = rope_sum * scale
        back_a, back_b = turn(rope_sum[:, :128], rope_sum[:, 128:], cos_ref[cut], -sin_ref[cut])
        query_grad[cut, 512:640] = back_a.astype(BF16)
        query_grad[cut, 640:768] = back_b.astype(BF16)
    keyval_grad[...] = key_grad[...].astype(BF16)
    plain = nt(query_grad[...], sort_columns(768)).astype(BF16)
    for k in range(8):
        query_wgrad[k] = tn(normed_ref[:, lanes(k)], plain).astype(BF16)
    wide[:512, :] = tn(latent_norm_ref[...], keyval_grad[...])
    for k in range(8):
        start = pl.multiple_of(places[k] * 64, 64)
        keyval_wgrad[k] = wide[pl.ds(start, 64), :].astype(BF16)
    row = lax.broadcasted_iota(jnp.int32, (SLOT, 128), 0)
    lane = lax.broadcasted_iota(jnp.int32, (SLOT, 128), 1)
    fold = jnp.where(lane == lax.rem(row, 32) + 32 * (row // 128), scale, 0.0)
    for b in range(4):
        cut = slice(b * 160, (b + 1) * 160)
        for k in range(4):
            columns = lanes(k, 512)
            part_ref[b, :, columns] = nt(query_grad[cut], w_query[columns]).astype(BF16)
        part_ref[b, :, D : D + KR] = nt(keyval_grad[cut], w_keyval_ref[...]).astype(BF16)
        rope = lax.dot_general(
            rope_grad[cut],
            fold,
            (((1,), (0,)), ((), ())),
            precision=lax.Precision.HIGHEST,
            preferred_element_type=F32,
        )
        part_ref[b, :, D + KR :] = rope.astype(BF16)
    pair.settle(out_sum, out_end_a, out_end_b)
    output_flight.wait()
    freight.wait()
    for part in parts:
        part.wait()


def attention_backward(grad, saved, out, freight, splits):
    shapes = [like((8, 512, SLOT)), like((8, SLOT, 768)), like((8, 64, 1024)), like((4, 160, D + KR + 128))]
    shapes += [like((160, D), F32), like((1, 160, 1024)), like((1, 160, 1024))]
    bits = tuple(bit for bit, _ in freight)
    goods = [array for _, array in freight]
    kept = (saved.output, saved.mix, saved.query_final, saved.keyval_final, saved.key_rope, saved.lse, saved.query)
    kept += (saved.w_keyval, saved.normed, saved.latent_norm, saved.col, saved.row, saved.cos, saved.sin)
    results = pl.pallas_call(
        functools.partial(attention_backward_kernel, bits, tuple(bit for _, _, bit in splits)),
        out_shape=shapes + [like(g.shape) for g in goods] + [like((4, 512, SLOT))] + split_outputs(splits),
        in_specs=[VMEM_SPEC] * 16 + [ANY_SPEC] * (len(goods) + 2 * len(splits)),
        out_specs=[VMEM_SPEC] * len(shapes) + [ANY_SPEC] * (len(goods) + 1 + 2 * len(splits)),
        scratch_shapes=split_scratch(splits)
        + [
            pltpu.VMEM((TOK, 512), BF16),
            pltpu.VMEM((TOK, 768), BF16),
            pltpu.VMEM((TOK, 1024), BF16),
            pltpu.VMEM((TOK, 1024), F32),
            pltpu.VMEM((TOK, SLOT), F32),
            pltpu.VMEM((TOK, 1024), F32),
            pltpu.SemaphoreType.DMA((32,)),
            pltpu.SemaphoreType.DMA((32,)),
            *sum_scratch()[:5],
        ],
        compiler_params=pltpu.CompilerParams(
            collective_id=4, has_side_effects=True, vmem_limit_bytes=GIVEN_VMEM
        ),
        cost_estimate=cost(30),
        name="attention_backward",
    )(grad, *kept, out, *goods, *[v for keep, got, _ in splits for v in (keep, got)])
    n = 8 + len(goods)
    return results[:7], list(results[7:n]), list(zip(results[n::2], results[n + 1 :: 2]))


class SlotSum:
    def __init__(self, copies, values, bits, got, give, rows=None):
        self.copies, self.values, self.bits, self.got, self.give = copies, values, list(bits), got, give
        self.rows = rows or (0, values.shape[1])
        self.level = 0
        self.flying = None

    def view(self, ref, first, count):
        return ref.at[pl.ds(first, count), pl.ds(*self.rows)]

    def start(self):
        half = 4 >> self.level
        if self.level == 0:
            source = self.view(self.values, half, half)
        else:
            first, size = self.rows
            for k in range(half):
                self.give[self.level - 1][k, first : first + size] = self.total(half + k).astype(BF16)
            source = self.view(self.give[self.level - 1], 0, half)
        target = self.view(self.got[self.level], 0, half)
        self.flying = self.copies.start(source, target, DP, self.bits[self.level])
        self.level += 1

    def total(self, k):
        cut = slice(self.rows[0], self.rows[0] + self.rows[1])
        value = self.values[k, cut].astype(F32)
        for level in range(self.level):
            value = value + self.got[level][k, cut].astype(F32)
        return value

    def wait(self):
        self.flying.wait()
        if self.level < len(self.bits):
            self.start()


def slot_sum_scratch(shape):
    spaces = [pltpu.VMEM((n, *shape), BF16) for n in (4, 2, 1)]
    return spaces + [pltpu.VMEM((n, *shape), BF16) for n in (2, 1)]


def tail_kernel(
    n_rest,
    n_last,
    part_ref,
    output_wgrad,
    query_wgrad,
    keyval_wgrad,
    normed_ref,
    w_latent_ref,
    gains_ref,
    latent_gain_ref,
    latent_c_ref,
    res_ref,
    mid_grad_ref,
    ffn_gain_ref,
    output_came,
    mid_ref,
    valid_ref,
    out_sum,
    out_end_a,
    out_end_b,
    cos_ref,
    sin_ref,
    *refs,
):
    refs = list(refs)
    take = lambda n: [refs.pop(0) for _ in range(n)]
    rest_pairs, last_pairs = take(2 * n_rest), take(2 * n_last)
    output_owned, query_owned, keyval_owned, latent_owned, res_grad_ref, res_out_ref = take(6)
    rest_owned, end_cames = take(n_rest), take(n_rest)
    last_ends = take(2 * n_last)
    send_sems, recv_sems = take(2)
    sums = []
    copies = Copies(send_sems, recv_sems)
    for values, bits in (
        (query_wgrad, (0, 1, 2)),
        (keyval_wgrad, (0, 1, 2)),
        (output_wgrad, (0, 1, 2)),
    ):
        space = take(5)
        if values is query_wgrad:
            half = values.shape[1] // 2
            for k in range(2):
                sums.append(SlotSum(copies, values, bits, space[:3], space[3:], (k * half, half)))
        else:
            sums.append(SlotSum(copies, values, bits, space[:3], space[3:]))
    latent_values = take(1)[0]
    space = take(5)
    latent_sum = SlotSum(copies, latent_values, (0, 1, 2), space[:3], space[3:])
    got_c, give_x, got_x = take(3)
    latent_all, gain_rows, gain_c, gain_x, gain_columns, wide, rest_came, end_sum, _, local_sems = take(10)
    copies.local_sems = local_sems
    copies.greet((0, 1, 2))
    last_a, last_b = take(2)
    out_ends = [copies.swapped(out_end_a, last_a, 0, 1024), copies.start(out_end_b, last_b, TENSOR, 1)]
    rest_rooms, last_rooms = take(2 * n_rest), take(2 * n_last)
    rests = [Split(copies, *rest_pairs[2 * k : 2 * k + 2], *rest_rooms[2 * k : 2 * k + 2]) for k in range(n_rest)]
    lasts = [Split(copies, *last_pairs[2 * k : 2 * k + 2], *last_rooms[2 * k : 2 * k + 2]) for k in range(n_last)]
    query_first, query_second, keyval_sum, output_sum = sums
    output_sum.got[0] = output_came
    output_sum.level = 1
    query_first.start()
    output_sum.start()
    c_far = copies.start(part_ref.at[pl.ds(3, 1)], got_c.at[pl.ds(1, 1)], TENSOR, 0)
    c_near = copies.start(part_ref.at[pl.ds(2, 1)], got_c.at[pl.ds(0, 1)], TENSOR, 0)
    c_far.wait()
    give_x[0] = (part_ref[1].astype(F32) + got_c[1].astype(F32)).astype(BF16)
    x_far = copies.start(give_x, got_x, TENSOR, 1)
    for k in range(n_rest):
        rests[k].send(2, rest_came.at[pl.ds(2 * k, 2)])
    for k in range(n_last):
        lasts[k].send(1, last_ends[2 * k + 1], last_ends[2 * k])
    c_near.wait()
    query_first.wait()
    query_second.start()
    x_far.wait()

    def summed(columns):
        return (
            part_ref[0, :, columns].astype(F32)
            + got_c[0, :, columns].astype(F32)
            + got_x[0, :, columns].astype(F32)
        )

    latent_c = latent_c_ref[...]
    latent_gain = latent_gain_ref[0:1]
    factor = lax.rsqrt(jnp.mean(latent_c * latent_c, axis=1, keepdims=True) + NORM_EPS)
    grad = summed(slice(D, D + KR))
    scaled = grad * latent_gain
    inner = jnp.mean(scaled * latent_c, axis=1, keepdims=True)
    latent_back = factor * (scaled - latent_c * factor * factor * inner)
    latent_gain_part = jnp.sum(grad * latent_c * factor, axis=0, keepdims=True)
    rope = summed(slice(D + KR, D + KR + 128))
    cos, sin = cos_ref[...], sin_ref[...]
    lane = lax.broadcasted_iota(jnp.int32, rope.shape, 1)
    other = jnp.where(lane < 32, pltpu.roll(rope, 96, 1), pltpu.roll(rope, 32, 1))
    rope_back = jnp.where(lane < 32, rope * cos + other * sin, rope * cos - other * sin)
    rope_back = jnp.where(lane < RD, rope_back, 0.0)
    latent_all[0, :, :KR] = latent_back.astype(BF16)
    latent_all[0, :, KR:] = rope_back.astype(BF16)
    own = latent_all.at[pl.ds(0, 1)]
    l_x = copies.start(own, latent_all.at[pl.ds(1, 1)], TENSOR, 1)
    l_c = copies.start(own, latent_all.at[pl.ds(2, 1)], TENSOR, 0)
    res = res_ref[...].astype(F32)
    factor = lax.rsqrt(jnp.mean(res * res, axis=1, keepdims=True) + NORM_EPS)
    grad = summed(slice(0, D)) + nt(latent_all[0], w_latent_ref[...])
    scaled = grad * gains_ref[0:1]
    inner = jnp.mean(scaled * res, axis=1, keepdims=True)
    res_grad_ref[...] = mid_grad_ref[...] + factor * (scaled - res * factor * factor * inner)
    row = lax.broadcasted_iota(jnp.int32, (8, D), 0)
    attn_part = jnp.broadcast_to(jnp.sum(grad * res * factor, axis=0, keepdims=True), (8, D))
    gain_rows[0] = jnp.where(row == 0, attn_part, jnp.where(row == 1, ffn_gain_ref[...], 0.0))
    latent_row = jnp.broadcast_to(latent_gain_part, (8, KR))
    gain_rows[0, :, :KR] = jnp.where(
        lax.broadcasted_iota(jnp.int32, (8, KR), 0) == 2, latent_row, gain_rows[0, :, :KR]
    )
    g_c = copies.start(gain_rows, gain_c, TENSOR, 0)
    query_second.wait()
    keyval_sum.start()
    query_first.wait()
    l_x.wait()
    l_far = copies.start(latent_all.at[pl.ds(1, 1)], latent_all.at[pl.ds(3, 1)], TENSOR, 0)
    g_c.wait()
    gain_rows[0] = gain_rows[0] + gain_c[0]
    g_x = copies.start(gain_rows, gain_x, TENSOR, 1)
    l_c.wait()
    l_far.wait()
    g_x.wait()
    output_sum.wait()
    keyval_sum.wait()
    query_second.wait()
    gain_columns[:, 0:8] = (gain_rows[0] + gain_x[0]).T
    tensor = lax.axis_index(TENSOR)
    dp = lax.axis_index(DP)
    latent_rows = jnp.concatenate([latent_all[b] for b in range(4)], axis=0)
    for k in range(8):
        wide[...] = tn(normed_ref[:, lanes(k)], latent_rows)
        block = wide[pl.ds(pl.multiple_of(tensor * 64, 64), 64), :]
        start = pl.multiple_of(k * SLOT + tensor * 64, 64)
        columns = gain_columns[pl.ds(start, 64), 0:8]
        start = pl.multiple_of(crossed(dp, COLUMNS[k], 3) * 64 + tensor * 16, 16)
        latent_values[k] = block.astype(BF16)
        lane = lax.broadcasted_iota(jnp.int32, (64, 128), 1)
        ends = block[:, KR : KR + 128]
        ends = jnp.where(lane == 64, columns[:, 0:1], ends)
        ends = jnp.where(lane == 65, columns[:, 1:2], ends)
        latent_values[k, :, KR:] = ends.astype(BF16)
        corner = gain_columns[pl.ds(start, 16), 0:8][:, 2:3]
        lane = lax.broadcasted_iota(jnp.int32, (16, 128), 1)
        latent_values[k, 0:16, KR:] = jnp.where(lane == 66, corner, ends[0:16]).astype(BF16)
    latent_sum.start()
    ends = []
    for g in range(n_rest):
        rests[g].wait()
        own, over = rests[g].kept[0].astype(F32), rests[g].kept[1].astype(F32)
        rest_owned[g][0] = (own + rest_came[2 * g].astype(F32)).astype(BF16)
        end_sum[g] = (over + rest_came[2 * g + 1].astype(F32)).astype(BF16)
        ends.append(copies.start(end_sum.at[pl.ds(g, 1)], end_cames[g], DP, 1))
    keyval_sum.wait()
    output_sum.wait()
    output_owned[...] = output_sum.total(0)
    latent_sum.wait()
    for flight in out_ends:
        flight.wait()
    valid = valid_ref[:, 0:1]
    res_out_ref[:, :1024] = (mid_ref[:, :1024] + valid * (out_sum[:, :1024] + last_a[0].astype(F32))).astype(BF16)
    res_out_ref[:, 1024:] = (mid_ref[:, 1024:] + valid * (out_sum[:, 1024:] + last_b[0].astype(F32))).astype(BF16)
    latent_sum.wait()
    half = query_owned.shape[0] // 2
    query_first.wait()
    query_owned[:half] = query_first.total(0)
    keyval_sum.wait()
    keyval_owned[...] = keyval_sum.total(0)
    query_second.wait()
    query_owned[half:] = query_second.total(0)
    latent_sum.wait()
    latent_owned[...] = latent_sum.total(0)
    for copy in lasts + ends:
        copy.wait()


def tail(part, wgrads, output_came, out_parts, saved, mid_grad, ffn_gain, rests, lasts):
    output_wgrad, query_wgrad, keyval_wgrad = wgrads
    rows = (160, D)
    latent = (64, KR + 128)
    shapes = [
        like((512, SLOT), F32),
        like((SLOT, 768), F32),
        like((64, 1024), F32),
        like(latent, F32),
        like(rows, F32),
        like(rows),
    ]
    part_row = (160, D + KR + 128)
    unit = rests[0][0].shape[1:]
    rows_spec = pl.BlockSpec((160, 128), lambda i: (0, 0))
    results = pl.pallas_call(
        functools.partial(tail_kernel, len(rests), len(lasts)),
        out_shape=shapes + [like((1, *unit))] * (2 * len(rests) + 2 * len(lasts)),
        grid=(1,),
        in_specs=[VMEM_SPEC] * 18 + [rows_spec] * 2 + [ANY_SPEC] * (2 * len(rests) + 2 * len(lasts)),
        out_specs=[VMEM_SPEC] * (len(shapes) + len(rests)) + [ANY_SPEC] * (len(rests) + 2 * len(lasts)),
        scratch_shapes=[
            pltpu.SemaphoreType.DMA((40,)),
            pltpu.SemaphoreType.DMA((40,)),
            *slot_sum_scratch((SLOT, 768)),
            *slot_sum_scratch((64, 1024)),
            *slot_sum_scratch((512, SLOT)),
            pltpu.VMEM((8, *latent), BF16),
            *slot_sum_scratch(latent),
            pltpu.VMEM((2, *part_row), BF16),
            pltpu.VMEM((1, *part_row), BF16),
            pltpu.VMEM((1, *part_row), BF16),
            pltpu.VMEM((4, 160, KR + 128), BF16),
            pltpu.VMEM((1, 8, D), F32),
            pltpu.VMEM((1, 8, D), F32),
            pltpu.VMEM((1, 8, D), F32),
            pltpu.VMEM((D, 128), F32),
            pltpu.VMEM((SLOT, KR + 128), F32),
            pltpu.VMEM((2 * len(rests), *unit), BF16),
            pltpu.VMEM((len(rests), *unit), BF16),
            pltpu.SemaphoreType.DMA((1,)),
            pltpu.SemaphoreType.DMA((32,)),
            pltpu.VMEM((1, 160, 1024), BF16),
            pltpu.VMEM((1, 160, 1024), BF16),
            *split_scratch(rests)[:-1],
            *split_scratch(lasts)[:-1],
        ],
        compiler_params=pltpu.CompilerParams(
            collective_id=3, has_side_effects=True, vmem_limit_bytes=GIVEN_VMEM
        ),
        cost_estimate=cost(110),
        name="tail",
    )(
        part,
        output_wgrad,
        query_wgrad,
        keyval_wgrad,
        saved.normed,
        saved.w_latent,
        saved.gains,
        saved.latent_gain,
        saved.latent_c,
        saved.res,
        mid_grad,
        ffn_gain,
        output_came,
        saved.mid,
        saved.valid,
        *out_parts,
        saved.cos,
        saved.sin,
        *[v for keep, got, _ in rests + lasts for v in (keep, got)],
    )
    n = len(rests)
    return results[:6], results[6 : 6 + n], results[6 + n : 6 + 2 * n], list(zip(results[6 + 2 * n :: 2], results[7 + 2 * n :: 2]))


def finish_kernel(
    n_came,
    res_out_ref,
    res_grad_ref,
    latent_ref,
    *refs,
):
    refs = list(refs)
    take = lambda n: [refs.pop(0) for _ in range(n)]
    stays, cames, others = take(9), take(n_came), take(9)
    passed = take(3)
    res_out, res_grad, latent, attn_gain, ffn_gain, latent_gain, expert_in, expert_out, shared_in, shared_out, *out = refs
    for source, target in zip(passed, out):
        target[...] = source[...]
    places = Places()
    for k in range(8):
        block = pl.ds(pl.multiple_of(places[k] * SLOT, SLOT), SLOT)
        res_out[:, block] = res_out_ref[:, lanes(k)]
        res_grad[:, block] = res_grad_ref[:, lanes(k)]
    latent[...] = latent_ref[:, : KR + RD]
    turned = latent_ref[:, KR : KR + 128].T
    attn_gain[...] = turned[64:65]
    ffn_gain[...] = turned[65:66]
    latent_gain[...] = turned[66:67, : KR // 32]
    side = places[12]
    n_half = expert_in.shape[0] // 2
    width = expert_out.shape[1]
    for p in range(n_half + 1):
        for mine in (True, False):
            which = side if mine else 1 - side
            for g in range(3):
                value = (stays if mine else others)[3 * p + g][0].astype(F32)
                late = 3 * p + g - 9 + n_came
                if mine and late >= 0:
                    value = value + cames[late][0].astype(F32)
                if p < n_half and g < 2:
                    expert_in[which * n_half + p, g] = value
                elif p < n_half:
                    expert_out[which * n_half + p] = value
                else:
                    cut = pl.ds(pl.multiple_of(which * width, 8), width)
                    if g < 2:
                        shared_in[g, cut] = value
                    else:
                        shared_out[cut] = value


def finish(res_out, res_grad, latent, stays, cames, others, passed, width):
    shapes = [
        like(res_out.shape),
        like(res_grad.shape, F32),
        like((64, KR + RD), F32),
        like((1, 64), F32),
        like((1, 64), F32),
        like((1, KR // 32), F32),
        like((EXPERTS, 2, width, SLOT), F32),
        like((EXPERTS, width, SLOT), F32),
        like((2, 2 * width, SLOT), F32),
        like((2 * width, SLOT), F32),
    ] + [like(array.shape, F32) for array in passed]
    return pl.pallas_call(
        functools.partial(finish_kernel, len(cames)),
        out_shape=shapes,
        in_specs=[VMEM_SPEC] * (24 + len(cames)),
        out_specs=[VMEM_SPEC] * len(shapes),
        compiler_params=pltpu.CompilerParams(vmem_limit_bytes=GIVEN_VMEM),
        cost_estimate=cost(10),
        name="finish",
    )(res_out, res_grad, latent, *stays, *cames, *others, *passed)


def body(
    res_in,
    out_grad,
    seg_ids,
    tok_counts,
    slot_table,
    slot_gates,
    attn_gain,
    latent_gain,
    ffn_gain,
    w_latent,
    w_query,
    w_keyval,
    w_output,
    w_expert_in,
    w_expert_out,
    w_shared_in,
    w_shared_out,
):
    dp = lax.axis_index(DP)
    rows = res_in.shape[0]
    first = ((dp >> 1) & 1) == 0
    n_half = EXPERTS // 2
    width = w_expert_out.shape[1]
    grad_pair, over_gate, lows, highs, saved = front(
        tok_counts,
        w_latent,
        (attn_gain[None], ffn_gain[None], latent_gain[None]),
        w_keyval,
        w_output,
        w_expert_in,
        w_expert_out,
        w_shared_in,
        w_shared_out,
        res_in,
        out_grad,
        w_query,
        seg_ids,
        slot_table[0],
        slot_gates[0],
    )
    pair_gate = jnp.concatenate(
        [g[:, k * rows : (k + 1) * rows] for k in range(4) for g in (saved.gates, over_gate)], axis=1
    )
    pair_gate = jnp.where(first, pair_gate[:n_half], pair_gate[n_half : 2 * n_half])
    mid_pair = saved.mid_pair.reshape(-1, D)
    grad_pair = grad_pair.reshape(-1, D)
    whole = 3 * width
    low, high = lows[2], highs[2]
    sums, keep0, give0, (high_far,) = experts_step(
        mid_pair,
        grad_pair,
        [(lows[0], 0, 4, 0, whole, 0), (highs[0], 4, 4, 0, whole, 0)],
        pair_gate[0],
        None,
        False,
        [Cut(low, 0, (0, 4), (width, whole - width))],
        5,
    )
    sums, keep1, give1, (y0a, y0b) = experts_step(
        mid_pair,
        grad_pair,
        [(lows[1], 0, 4, 0, whole, 0), (highs[1], 4, 4, 0, whole, 0)],
        pair_gate[1],
        sums,
        False,
        [Cut(give0[0], 0), Cut(give0[1], 0)],
        6,
    )
    (k0a, h0a), (k0b, h0b) = halve([(keep0[0], y0a), (keep0[1], y0b)])
    (back, out), keep2, give2, (y0c, y1a, z0a, z0b) = experts_step(
        mid_pair,
        grad_pair,
        [
            (low, 0, 4, 0, whole, 0),
            (high, 4, 4, 0, width, 0),
            (high_far, 4, 4, width, whole - width, 0),
        ],
        None,
        sums,
        True,
        [Cut(give0[2], 0), Cut(give1[0], 0), Cut(h0a, 2), Cut(h0b, 2)],
        7,
    )
    back = back.reshape(8, rows, D)
    out = out.reshape(8, rows, D)
    (mid_grad, ffn_gain_part, attn_grad), (y1b, y1c, y2a, y2b), split = back_tokens(
        back,
        saved.grad,
        saved.mid,
        saved.gains,
        saved.valid,
        [(0, give1[1]), (0, give1[2]), (0, give2[0]), (0, give2[1])],
        [(keep0[2], y0c, 2), (keep1[0], y1a, 2), (k0a, z0a, 1), (k0b, z0b, 1)],
    )
    (k0c, z0c), (k1a, z1a), over0a, over0b = split
    (*wgrads, back_part, out_sum, out_a, out_b), (y2c, output_came), split = attention_backward(
        attn_grad,
        saved,
        out,
        [(0, give2[2])],
        [(keep1[1], y1b, 2), (keep1[2], y1c, 2), (keep2[0], y2a, 2), (k0c, z0c, 1), (k1a, z1a, 1)],
    )
    (k1b, z1b), (k1c, z1c), (k2a, z2a), over0c, over1a = split
    (output_owned, query_owned, keyval_owned, latent_owned, res_grad, res_out), own2, over2, late = tail(
        back_part,
        wgrads,
        output_came,
        (out_sum, out_a, out_b),
        saved,
        mid_grad,
        ffn_gain_part,
        [(keep2[1], y2b, 2), (keep2[2], y2c, 2)],
        [(k1b, z1b, 1), (k1c, z1c, 1), (k2a, z2a, 1)],
    )
    ready = [over0a, over0b, over0c, over1a, *late]
    (
        res_out,
        res_grad,
        latent_owned,
        attn_gain,
        ffn_gain,
        latent_gain,
        expert_in,
        expert_out,
        shared_in,
        shared_out,
        output_owned,
        query_owned,
        keyval_owned,
    ) = finish(
        res_out,
        res_grad,
        latent_owned,
        [mine for mine, _ in ready] + list(own2),
        [],
        [other for _, other in ready] + list(over2),
        [output_owned, query_owned, keyval_owned],
        width,
    )
    return (
        res_out,
        res_grad,
        attn_gain[0],
        latent_gain[0],
        ffn_gain[0],
        latent_owned,
        query_owned,
        keyval_owned,
        output_owned,
        expert_in.transpose(0, 1, 3, 2),
        expert_out,
        shared_in.transpose(0, 2, 1),
        shared_out,
    )


def solution(mesh):
    placed = (
        P((DP, TENSOR), None),
        P((DP, TENSOR), None),
        P(DP, None),
        P(DP),
        P(DP, None, None),
        P(DP, None, None),
        P((DP, TENSOR)),
        P((DP, TENSOR)),
        P((DP, TENSOR)),
        P((DP, TENSOR), None),
        P(DP, TENSOR),
        P(DP, TENSOR),
        P(TENSOR, DP),
        P(None, None, DP, TENSOR),
        P(None, TENSOR, DP),
        P(None, DP, TENSOR),
        P(TENSOR, DP),
    )
    fits = mesh.shape[DP] == 8 and mesh.shape[TENSOR] == 4
    return jax.shard_map(
        body if fits else general_body,
        mesh=mesh,
        in_specs=placed,
        out_specs=(
            P((DP, TENSOR), None),
            P((DP, TENSOR), None),
            P((DP, TENSOR)),
            P((DP, TENSOR)),
            P((DP, TENSOR)),
            P((DP, TENSOR), None),
            P(DP, TENSOR),
            P(DP, TENSOR),
            P(TENSOR, DP),
            P(None, None, DP, TENSOR),
            P(None, TENSOR, DP),
            P(None, DP, TENSOR),
            P(TENSOR, DP),
        ),
        check_vma=False,
    )
```

```python
import functools
import types

import jax
import jax.numpy as jnp
import numpy as np
from jax import lax
from jax.experimental import pallas as pl
from jax.experimental.pallas import tpu as pltpu
from jax.sharding import PartitionSpec as P

D = 2048
H = 16
HD = 128
RD = 64
VD = 128
KR = 512
TOK = 640
EXPERTS = 4


NORM_EPS = 1e-06
ROPE_BASE = 50000.0


def rms_factor(values):
    return lax.rsqrt(jnp.mean(values * values, axis=-1, keepdims=True) + NORM_EPS)


def norm_back(grad_out, values, factor, gain_vec):
    scaled = grad_out * gain_vec
    inner_sum = jnp.mean(scaled * values, axis=-1, keepdims=True)
    return (
        factor * (scaled - values * factor * factor * inner_sum),
        jnp.sum(grad_out * values * factor, axis=0),
    )


def rotary_tables(positions):
    half_width = RD // 2
    inv_freq = ROPE_BASE ** (-jnp.arange(half_width, dtype=jnp.float32) / half_width)
    angles = positions.astype(jnp.float32)[:, None] * inv_freq[None, :]
    return (jnp.cos(angles), jnp.sin(angles))


def rotate(values, cosine_table, sine_table):
    half_width = values.shape[-1] // 2
    first_half = values[..., :half_width]
    second_half = values[..., half_width:]
    return jnp.concatenate(
        [
            first_half * cosine_table - second_half * sine_table,
            second_half * cosine_table + first_half * sine_table,
        ],
        axis=-1,
    )


def silu_parts(gate_pre):
    sigma_gate = jax.nn.sigmoid(gate_pre)
    return (gate_pre * sigma_gate, sigma_gate * (1.0 + gate_pre * (1.0 - sigma_gate)))


def flip_pairs(count, bit):
    return [(i, i ^ (1 << bit)) for i in range(count)]


def swap_dp(values, bit):
    return lax.ppermute(values, DP, flip_pairs(lax.axis_size(DP), bit))


def swap_tensor(values, bit):
    return lax.ppermute(values, TENSOR, flip_pairs(lax.axis_size(TENSOR), bit))


def dp_bits():
    top = lax.axis_size(DP).bit_length() - 1
    return [1] + list(range(top - 1, 1, -1)) + [0]


def slot_order(bits):
    order = [0]
    for bit in bits:
        order = order + [j ^ (1 << bit) for j in order]
    return order


def select_blocks(blocks, index):
    step = 1
    while step < len(blocks):
        hit = (index & step) != 0
        blocks = [jnp.where(hit, blocks[i ^ step], blocks[i]) for i in range(len(blocks))]
        step *= 2
    return blocks


def to_slots(values, index, bits, axis):
    count = 1 << len(bits)
    blocks = select_blocks(jnp.split(values, count, axis=axis), index)
    return jnp.concatenate([blocks[j] for j in slot_order(bits)], axis=axis)


def from_slots(values, index, bits, axis):
    order = slot_order(bits)
    slots = jnp.split(values, len(order), axis=axis)
    blocks = [slots[order.index(i)] for i in range(len(order))]
    return jnp.concatenate(select_blocks(blocks, index), axis=axis)


def gather_dp(values, bits):
    for bit in bits:
        values = jnp.concatenate([values, swap_dp(values, bit)], axis=0)
    return values


def gather_tensor(values):
    for bit in (1, 0):
        values = jnp.concatenate([values, swap_tensor(values, bit)], axis=0)
    return values


def scatter_dp(values, bits, axis):
    values = values.astype(jnp.float32)
    for bit in reversed(bits):
        keep, give = jnp.split(values, 2, axis=axis)
        values = keep + swap_dp(give.astype(jnp.bfloat16), bit).astype(jnp.float32)
    return values


def scatter_tensor(values):
    for bit in (0, 1):
        keep, give = jnp.split(values, 2, axis=0)
        values = keep + swap_tensor(give.astype(jnp.bfloat16), bit).astype(jnp.float32)
    return values


def partner_columns(values):
    count = lax.axis_size(DP)
    slots = jnp.split(values, count, axis=-1)
    return jnp.concatenate([slots[k ^ 1] for k in range(count)], axis=-1)


def gather_pair(values, bit):
    over = swap_dp(partner_columns(values), bit)
    own = jnp.concatenate([values, over, swap_tensor(values, 1), swap_tensor(over, 1)], axis=0)
    return jnp.concatenate([own, swap_tensor(own, 0)], axis=0)


def scatter_pair(values, bit):
    values = scatter_tensor(values)
    keep, give = jnp.split(values, 2, axis=0)
    return keep + swap_dp(partner_columns(give).astype(jnp.bfloat16), bit).astype(jnp.float32)


def dot(a, b, contract):
    return lax.dot_general(a, b, (contract, ((), ())), preferred_element_type=jnp.float32)


def general_body(
    res_in,
    out_grad,
    seg_ids,
    tok_counts,
    slot_table,
    slot_gates,
    attn_gain,
    latent_gain,
    ffn_gain,
    w_latent,
    w_query,
    w_keyval,
    w_output,
    w_expert_in,
    w_expert_out,
    w_shared_in,
    w_shared_out,
):
    f32 = jnp.float32
    bf16 = jnp.bfloat16
    n_tensor = lax.axis_size(TENSOR)
    n_dp = lax.axis_size(DP)
    dp = lax.axis_index(DP)
    tensor = lax.axis_index(TENSOR)
    bits = dp_bits()
    merge = bits[0]
    half = (dp >> merge) & 1
    rows = res_in.shape[0]
    local_heads = H // n_tensor
    score_scale = (HD + RD) ** (-0.5)

    res_local = to_slots(res_in, dp, bits, 1)
    res_all = gather_tensor(res_local)
    tensor_slots = slot_order([1, 0])
    token_ids = jnp.concatenate(
        [(tensor ^ j) * rows + jnp.arange(rows, dtype=jnp.int32) for j in tensor_slots]
    )
    segment_canon = seg_ids[0]
    segment_row = jnp.concatenate(
        [lax.dynamic_slice_in_dim(segment_canon, (tensor ^ j) * rows, rows) for j in tensor_slots]
    )
    valid_all = (token_ids < tok_counts[0]).astype(f32)
    valid_rows = valid_all[:rows, None]
    group_gate = jnp.sum(
        jnp.where(slot_table[0][:, :, None] == token_ids[None, None, :], slot_gates[0][:, :, None], 0.0),
        axis=1,
    )
    grad_in = to_slots(out_grad, dp, bits, 1).astype(f32)
    ffn_grad = (valid_rows * grad_in).astype(bf16)

    pack_rows = w_latent.shape[0]
    gain_row = jnp.concatenate([attn_gain, ffn_gain, latent_gain])
    gain_row = jnp.pad(gain_row, (0, w_latent.shape[1] - gain_row.shape[0]))
    pack = jnp.concatenate([w_latent, jnp.broadcast_to(gain_row, (16, w_latent.shape[1]))], axis=0)
    pack = gather_dp(pack[None], bits)
    pack = gather_tensor(pack[None])
    pack_blocks = [pack[tensor_slots.index(j)] for j in range(n_tensor)]
    pack = jnp.stack(select_blocks(pack_blocks, tensor), axis=1)
    latent_full = pack[:, :, :pack_rows].reshape(D, KR + RD)
    gains = pack[:, :, pack_rows]
    gain_width, latent_width = D // (n_dp * n_tensor), KR // (n_dp * n_tensor)
    attn_gain_full = gains[..., :gain_width].reshape(D)
    ffn_gain_full = gains[..., gain_width : 2 * gain_width].reshape(D)
    latent_gain_full = from_slots(
        gains[..., 2 * gain_width : 2 * gain_width + latent_width].reshape(KR), dp, bits, 0
    )
    query_full = gather_dp(w_query, bits)
    keyval_full = from_slots(gather_dp(w_keyval, bits), dp, bits, 0)
    output_full = gather_dp(w_output[None], bits)
    output_full = jnp.concatenate([output_full[k] for k in range(n_dp)], axis=1)

    n_half = EXPERTS // 2
    expert_units = jnp.concatenate(
        [
            w_expert_in.transpose(0, 1, 3, 2).reshape(EXPERTS, -1, w_expert_in.shape[2]),
            w_expert_out,
        ],
        axis=1,
    )
    width = w_expert_out.shape[1]
    shared_t = w_shared_in.transpose(0, 2, 1)
    units = []
    for side in range(2):
        cut = slice(side * width, (side + 1) * width)
        shared_unit = jnp.concatenate([shared_t[0, cut], shared_t[1, cut], w_shared_out[cut]], axis=0)
        units.append(jnp.concatenate([expert_units[side * n_half : (side + 1) * n_half], shared_unit[None]], axis=0))
    first = half == 0
    own_units = jnp.where(first, units[0], units[1])
    other_units = jnp.where(first, units[1], units[0])
    pieces = []
    for p in range(n_half + 1):
        piece = jnp.stack([own_units[p], swap_dp(other_units[p], merge)], axis=0)
        piece = gather_dp(piece, bits[1:])
        pieces.append(jnp.concatenate([piece[k] for k in range(n_dp)], axis=1))

    positions = token_ids - jnp.sum(
        (segment_canon[None, :] < segment_row[:, None]).astype(jnp.int32), axis=1
    )
    cos_all, sin_all = rotary_tables(positions)
    allowed = (segment_row[:, None] == segment_row[None, :]) & (
        token_ids[None, :] <= token_ids[:, None]
    )
    resid_all = res_all.astype(f32)
    in_factor = rms_factor(resid_all)
    normed_all = (resid_all * in_factor * attn_gain_full).astype(bf16)
    latent_raw = jnp.dot(normed_all, latent_full, preferred_element_type=f32)
    latent_c = latent_raw[:, :KR]
    latent_factor = rms_factor(latent_c)
    latent_norm = (latent_c * latent_factor * latent_gain_full).astype(bf16)
    rope_all = rotate(latent_raw[:, KR:], cos_all, sin_all).astype(bf16)
    query_raw = jnp.dot(normed_all, query_full, preferred_element_type=f32).reshape(
        TOK, local_heads, HD + RD
    )
    query_final = jnp.concatenate(
        [
            query_raw[..., :HD],
            rotate(query_raw[..., HD:], cos_all[:, None, :], sin_all[:, None, :]),
        ],
        axis=-1,
    ).astype(bf16)
    keyval = (
        jnp.dot(latent_norm, keyval_full, preferred_element_type=f32)
        .astype(bf16)
        .reshape(TOK, local_heads, HD + VD)
    )
    key_nope = keyval[..., :HD]
    values_all = keyval[..., HD:]
    raw_scores = jnp.einsum(
        "qhd,khd->hqk", query_final[..., :HD], key_nope, preferred_element_type=f32
    )
    raw_scores = raw_scores + jnp.einsum(
        "qhr,kr->hqk", query_final[..., HD:], rope_all, preferred_element_type=f32
    )
    scores = jnp.where(allowed[None], raw_scores * score_scale, -1e30)
    top_score = jnp.max(scores, axis=-1, keepdims=True)
    exp_scores = jnp.exp(scores - top_score)
    probs_all = exp_scores / jnp.sum(exp_scores, axis=-1, keepdims=True)
    probs_low = probs_all.astype(bf16)
    attn_mix = (
        jnp.einsum("hqk,khd->qhd", probs_low, values_all, preferred_element_type=f32)
        .astype(bf16)
        .reshape(TOK, local_heads * VD)
    )
    attn_part = jnp.dot(attn_mix, output_full, preferred_element_type=f32)
    attn_out = scatter_tensor(attn_part)
    resid_in = res_local.astype(f32)
    mid_resid = resid_in + valid_rows * attn_out
    mid_factor = rms_factor(mid_resid)
    normed_mid = (mid_resid * mid_factor * ffn_gain_full).astype(bf16)

    mid_pair = gather_pair(normed_mid, merge)
    grad_pair = gather_pair(ffn_grad, merge)
    other_gate = swap_dp(group_gate, merge)
    pair_gate = jnp.concatenate(
        [
            gate[:, k * rows : (k + 1) * rows]
            for k in ((0, 0), (1, 0), (0, 1), (1, 1), (0, 2), (1, 2), (0, 3), (1, 3))
            for gate, k in (((group_gate, other_gate)[k[0]], k[1]),)
        ],
        axis=1,
    )
    pair_gate = jnp.where(first, pair_gate[:n_half], pair_gate[n_half:])
    mid_pair_grad = None
    hidden_parts, out_parts, unit_grads = [], [], []
    for p, piece in enumerate(pieces):
        gate_up = dot(piece[: 2 * width], mid_pair, ((1,), (1,)))
        gate_pre, up = gate_up[:width], gate_up[width:]
        silu, slope = silu_parts(gate_pre)
        hidden_grad = dot(piece[2 * width :], grad_pair, ((1,), (1,)))
        hidden = silu * up
        if p < n_half:
            hidden = hidden * pair_gate[p][None]
            hidden_grad = hidden_grad * pair_gate[p][None]
        hidden = hidden.astype(bf16)
        pre_grad = jnp.concatenate(
            [(hidden_grad * up * slope).astype(bf16), (hidden_grad * silu).astype(bf16)], axis=0
        )
        back = dot(pre_grad, piece[: 2 * width], ((0,), (0,)))
        mid_pair_grad = back if mid_pair_grad is None else mid_pair_grad + back
        hidden_parts.append(hidden)
        out_parts.append(piece[2 * width :])
        in_wgrad = dot(pre_grad, mid_pair, ((1,), (0,)))
        out_wgrad = dot(hidden, grad_pair, ((1,), (0,)))
        unit_grads.append(jnp.concatenate([in_wgrad, out_wgrad], axis=0).astype(bf16))
    ffn_part = dot(
        jnp.concatenate(hidden_parts, axis=0), jnp.concatenate(out_parts, axis=0), ((0,), (0,))
    )
    ffn_out = scatter_pair(ffn_part, merge)
    res_out = (mid_resid + valid_rows * ffn_out).astype(bf16)
    mid_grad_local = scatter_pair(mid_pair_grad, merge)

    mid_back, ffn_gain_part = norm_back(mid_grad_local, mid_resid, mid_factor, ffn_gain_full)
    mid_grad = grad_in + mid_back
    attn_grad = (valid_rows * mid_grad).astype(bf16)
    attn_grad_all = gather_tensor(attn_grad)
    output_wgrad = dot(attn_mix, attn_grad_all, ((0,), (0,)))
    mix_grad = (
        dot(attn_grad_all, output_full, ((1,), (1,))).astype(bf16).reshape(TOK, local_heads, VD)
    )
    probs_grad = jnp.einsum("qhd,khd->hqk", mix_grad, values_all, preferred_element_type=f32)
    value_grad = jnp.einsum("hqk,qhd->khd", probs_low, mix_grad, preferred_element_type=f32)
    scores_grad = (
        probs_all * (probs_grad - jnp.sum(probs_all * probs_grad, axis=-1, keepdims=True))
    ).astype(bf16)
    query_nope_grad = (
        jnp.einsum("hqk,khd->qhd", scores_grad, key_nope, preferred_element_type=f32) * score_scale
    )
    query_rope_grad = (
        jnp.einsum("hqk,kr->qhr", scores_grad, rope_all, preferred_element_type=f32) * score_scale
    )
    key_nope_grad = (
        jnp.einsum("hqk,qhd->khd", scores_grad, query_final[..., :HD], preferred_element_type=f32)
        * score_scale
    )
    rope_key_grad = (
        jnp.einsum("hqk,qhr->kr", scores_grad, query_final[..., HD:], preferred_element_type=f32)
        * score_scale
    )
    query_grad = (
        jnp.concatenate(
            [query_nope_grad, rotate(query_rope_grad, cos_all[:, None, :], -sin_all[:, None, :])],
            axis=-1,
        )
        .astype(bf16)
        .reshape(TOK, local_heads * (HD + RD))
    )
    keyval_grad = (
        jnp.concatenate([key_nope_grad, value_grad], axis=-1)
        .astype(bf16)
        .reshape(TOK, local_heads * (HD + VD))
    )
    latent_part = jnp.concatenate([dot(keyval_grad, keyval_full, ((1,), (1,))), rope_key_grad], axis=1)
    latent_grad_local = scatter_tensor(latent_part)
    normed_part = dot(query_grad, query_full, ((1,), (1,)))
    normed_grad_local = scatter_tensor(normed_part)
    query_wgrad = dot(normed_all, query_grad, ((0,), (0,)))
    keyval_wgrad = to_slots(dot(latent_norm, keyval_grad, ((0,), (0,))).astype(bf16), dp, bits, 0)
    latent_c_grad, latent_gain_part = norm_back(
        latent_grad_local[:, :KR], latent_c[:rows], latent_factor[:rows], latent_gain_full
    )
    rope_raw_grad = rotate(latent_grad_local[:, KR:], cos_all[:rows], -sin_all[:rows])
    latent_raw_grad = jnp.concatenate([latent_c_grad, rope_raw_grad], axis=1).astype(bf16)
    latent_raw_grad_all = gather_tensor(latent_raw_grad)
    latent_wgrad = dot(normed_all, latent_raw_grad_all, ((0,), (0,))).astype(bf16)
    latent_wgrad = lax.dynamic_index_in_dim(
        latent_wgrad.reshape(n_dp, n_tensor, pack_rows, KR + RD), tensor, 1, keepdims=False
    )
    normed_grad = normed_grad_local + dot(latent_raw_grad, latent_full, ((1,), (1,)))
    in_back, attn_gain_part = norm_back(normed_grad, resid_in, in_factor[:rows], attn_gain_full)
    res_grad = mid_grad + in_back

    output_owned = scatter_dp(output_wgrad, bits, 1)
    query_owned = scatter_dp(query_wgrad, bits, 0)
    keyval_owned = scatter_dp(keyval_wgrad, bits, 0)
    latent_owned = scatter_dp(latent_wgrad, bits, 0)[0]
    gain_parts = jnp.concatenate(
        [
            attn_gain_part.reshape(n_dp, n_tensor, gain_width),
            ffn_gain_part.reshape(n_dp, n_tensor, gain_width),
            to_slots(latent_gain_part, dp, bits, 0).reshape(n_dp, n_tensor, latent_width),
        ],
        axis=2,
    )
    gain_parts = jnp.stack(
        [
            select_blocks([gain_parts[:, i] for i in range(n_tensor)], tensor)[j]
            for j in tensor_slots
        ],
        axis=0,
    )
    for bit in (0, 1):
        keep, give = jnp.split(gain_parts, 2, axis=0)
        gain_parts = keep + swap_tensor(give, bit)
    gain_parts = gain_parts[0]
    for bit in reversed(bits):
        keep, give = jnp.split(gain_parts, 2, axis=0)
        gain_parts = keep + swap_dp(give, bit)
    gain_owned = gain_parts[0]
    own_grads, other_grads = [], []
    for grad in unit_grads:
        grad = grad.astype(f32)
        for bit in reversed(bits[1:]):
            keep, give = jnp.split(grad, 2, axis=1)
            grad = keep + swap_dp(give.astype(bf16), bit).astype(f32)
        keep, give = jnp.split(grad, 2, axis=1)
        own_grads.append(keep)
        other_grads.append(swap_dp(give.astype(bf16), merge).astype(f32))
    sides = []
    for side in (first, ~first):
        sides.append([jnp.where(side, a, b) for a, b in zip(own_grads, other_grads)])
    expert_units = jnp.stack([unit for side in sides for unit in side[:n_half]], axis=0)
    expert_in_owned = expert_units[:, : 2 * width].reshape(EXPERTS, 2, width, -1).transpose(0, 1, 3, 2)
    expert_out_owned = expert_units[:, 2 * width :]
    shared_in_owned = jnp.stack(
        [
            jnp.concatenate([side[n_half][k * width : (k + 1) * width] for side in sides], axis=0).T
            for k in range(2)
        ],
        axis=0,
    )
    shared_out_owned = jnp.concatenate([side[n_half][2 * width :] for side in sides], axis=0)
    return (
        from_slots(res_out, dp, bits, 1),
        from_slots(res_grad, dp, bits, 1),
        gain_owned[:gain_width],
        gain_owned[2 * gain_width :],
        gain_owned[gain_width : 2 * gain_width],
        latent_owned,
        query_owned,
        keyval_owned,
        output_owned,
        expert_in_owned,
        expert_out_owned,
        shared_in_owned,
        shared_out_owned,
    )


DP, TENSOR = "dp", "tensor"
MESH = pl.DeviceIdType.MESH
F32 = jnp.float32
BF16 = jnp.bfloat16
CHUNKS = 3
SECONDS = 9
THIRDS = 7
SLOT = 256
GIVEN_VMEM = 60 * 1024 * 1024
FAR_FIRST = (2, 1, 0)
FLIPS = (1, 2, 0)
TENSOR_BITS = (1, 0)


COLUMNS = slot_order(FAR_FIRST)
UNIT_SLOTS = slot_order(FLIPS)
ROWS = slot_order(TENSOR_BITS)


def nn(a, b):
    return lax.dot_general(a, b, (((1,), (0,)), ((), ())), preferred_element_type=F32)


def nt(a, b):
    return lax.dot_general(a, b, (((1,), (1,)), ((), ())), preferred_element_type=F32)


def tn(a, b):
    return lax.dot_general(a, b, (((0,), (0,)), ((), ())), preferred_element_type=F32)


def lanes(k, width=SLOT):
    return slice(k * width, (k + 1) * width)


def crossed(index, constant, bits):
    total = 0
    for bit in range(bits):
        own = lax.rem(index // (1 << bit), 2)
        total = total + ((1 - own) if (constant >> bit) & 1 else own) * (1 << bit)
    return total


class Copies:
    def __init__(self, send_sems, recv_sems, local_sems=None):
        self.send_sems, self.recv_sems, self.local_sems = send_sems, recv_sems, local_sems
        self.count = 0
        self.local_count = 0

    def across(self, axis, bit):
        index = lax.axis_index(axis)
        side = lax.rem(index // (1 << bit), 2)
        return {axis: index + (1 - 2 * side) * (1 << bit)}

    def start(self, source, target, axis, bit):
        copy = pltpu.make_async_remote_copy(
            src_ref=source,
            dst_ref=target,
            send_sem=self.send_sems.at[self.count],
            recv_sem=self.recv_sems.at[self.count],
            device_id=self.across(axis, bit),
            device_id_type=MESH,
        )
        self.count += 1
        copy.start()
        return copy

    def local(self, source, target):
        copy = pltpu.make_async_copy(source, target, self.local_sems.at[self.local_count])
        self.local_count += 1
        copy.start()
        return copy

    def greet(self, dp_bits, tensor_bits=TENSOR_BITS):
        barrier = pltpu.get_barrier_semaphore()
        for axis, bits in ((DP, dp_bits), (TENSOR, tensor_bits)):
            for bit in bits:
                pl.semaphore_signal(
                    barrier, inc=1, device_id=self.across(axis, bit), device_id_type=MESH
                )
        pl.semaphore_wait(barrier, len(dp_bits) + len(tensor_bits))

    def swapped(self, source, target, first, width):
        parts = []
        for a in range(first, first + width, 1024):
            for b, c in ((a, a + 512), (a + 512, a)):
                parts.append(
                    self.start(
                        source.at[(slice(None),) * (len(source.shape) - 1) + (pl.ds(b, 512),)],
                        target.at[(slice(None),) * (len(target.shape) - 1) + (pl.ds(c, 512),)],
                        DP,
                        1,
                    )
                )
        return Several(parts)


class Several:
    def __init__(self, parts):
        self.parts = parts

    def wait(self):
        for part in self.parts:
            part.wait()


class SlotGather:
    def __init__(self, copies, source, slots, bits, axis=DP, cut=None):
        self.copies, self.source, self.slots, self.bits, self.axis = copies, source, slots, list(bits), axis
        self.cut = (slice(None),) if cut is None else (pl.ds(*cut),)
        self.done, self.have, self.own, self.flying = 0, 1, None, None

    def view(self, first, count):
        return self.slots.at[(pl.ds(first, count), *self.cut)]

    def start(self):
        bit = self.bits[self.done]
        if self.done == 0 and self.source is not None:
            source = self.source.at[(pl.ds(0, 1), *self.cut)]
            self.own = self.copies.local(source, self.view(0, 1))
        else:
            if self.own is not None:
                self.own.wait()
                self.own = None
            source = self.view(0, self.have)
        self.flying = self.copies.start(source, self.view(self.have, self.have), self.axis, bit)
        self.done += 1
        self.have *= 2

    def wait(self):
        self.flying.wait()
        self.flying = None
        if self.done < len(self.bits):
            self.start()

    def finish(self):
        while self.flying is not None:
            self.wait()


ANY_SPEC = pl.BlockSpec(memory_space=pl.ANY)
VMEM_SPEC = pl.BlockSpec(memory_space=pltpu.VMEM)
SMEM_SPEC = pl.BlockSpec(memory_space=pltpu.SMEM)


def cost(micros):
    return pl.CostEstimate(flops=micros * 10**9, bytes_accessed=micros * 10**6, transcendentals=0)


def like(shape, dtype=BF16):
    return jax.ShapeDtypeStruct(shape, dtype)


def turn(a, b, cos, sin):
    return a * cos - b * sin, b * cos + a * sin


def head_lanes(rows, head):
    lane = lax.broadcasted_iota(jnp.int32, (rows, SLOT), 1)
    return lax.rem(lane // 32, 4) == head


def spread_block(copies, pair_ref, between):
    block = lambda k: pair_ref.at[pl.ds(k, 1)]
    x_own = copies.start(block(0), block(2), TENSOR, 1)
    z_own = copies.swapped(block(0), block(1), 0, D)
    waits = [copies.start(block(0), block(4), TENSOR, 0)]
    between()
    z_own.wait()
    over_both = copies.start(block(1), block(3), TENSOR, 1)
    waits.append(copies.start(block(1), block(5), TENSOR, 0))
    between()
    x_own.wait()
    waits.append(copies.start(block(2), block(6), TENSOR, 0))
    between()
    over_both.wait()
    waits.append(copies.start(block(3), block(7), TENSOR, 0))
    for copy in waits:
        copy.wait()


class Places:
    def __init__(self):
        self.dp, self.tensor = lax.axis_index(DP), lax.axis_index(TENSOR)

    def __getitem__(self, k):
        if k == 12:
            return lax.rem(self.dp // 2, 2)
        return crossed(self.dp, COLUMNS[k], 3) if k < 8 else crossed(self.tensor, ROWS[k - 8], 2)


class Kept:
    output = ((8, 512, SLOT), BF16)
    mix = ((TOK, 512), BF16)
    query_final = ((TOK, 768), BF16)
    keyval_final = ((TOK, 1024), BF16)
    key_rope = ((TOK, SLOT), BF16)
    lse = ((TOK, 128), F32)
    query = ((8, SLOT, 768), BF16)
    w_keyval = ((KR, 1024), BF16)
    normed = ((TOK, D), BF16)
    latent_norm = ((TOK, KR), BF16)
    col = ((TOK, 128), F32)
    row = ((8, TOK), F32)
    cos = ((TOK, 128), F32)
    sin = ((TOK, 128), F32)
    gains = ((8, D), F32)
    latent_gain = ((8, KR), F32)
    latent_c = ((160, KR), F32)
    w_latent = ((D, KR + 128), BF16)
    mid = ((160, D), F32)
    mid_pair = ((8, 160, D), BF16)
    res = ((160, D), BF16)
    grad = ((160, D), BF16)
    valid = ((160, 128), F32)
    gates = ((8, TOK), F32)


class Landing:
    tokens = ((4, 160, D), BF16)
    pack = ((4, 8, 64, KR + 128), BF16)
    keyval = ((8, 64, 1024), BF16)
    part = ((4, 160, D), BF16)
    got_c = ((2, 160, D), BF16)
    give_x = ((1, 160, D), BF16)
    got_x = ((1, 160, D), BF16)
    gain_rows = ((KR, 128), BF16)
    masked = ((1, 160, D), BF16)
    own_pack = ((1, 64, KR + 128), BF16)
    own_query = ((1, SLOT, 768), BF16)


def fields(kind):
    return [name for name in vars(kind) if not name.startswith("_")]


def buffers(kind):
    return [getattr(kind, name) for name in fields(kind)]


def masks(col, row, cut):
    return (col[cut, 0:1] == row[0:1]) & (row[1:2] <= col[cut, 1:2])


def sort_columns(rows):
    column = lax.broadcasted_iota(jnp.int32, (768, 768), 1)
    row = lax.broadcasted_iota(jnp.int32, (768, 768), 0)
    wide = (column // 128) * 192 + lax.rem(column, 128)
    late = column - 512
    narrow = (lax.rem(late, 128) // 32) * 192 + 128 + (late // 128) * 32 + lax.rem(late, 32)
    return jnp.where(row == jnp.where(column < 512, wide, narrow), 1.0, 0.0).astype(BF16)


def front_kernel(
    width,
    count_ref,
    keyval_ref,
    output_ref,
    expert_in,
    expert_out,
    shared_in,
    shared_out,
    res_ref,
    grad_ref,
    query_ref,
    segment_row,
    table_ref,
    slot_gates,
    frequency_ref,
    latent_ref,
    attn_gain_ref,
    ffn_gain_ref,
    latent_gain_ref,
    grad_pair,
    gates_over,
    *rest,
):
    n_units = 3
    lows, highs = rest[:n_units], rest[n_units : 2 * n_units]
    rest = rest[2 * n_units :]
    kept, names = fields(Kept), fields(Kept) + fields(Landing)
    outs = types.SimpleNamespace(**dict(zip(kept, rest)))
    rest = rest[len(kept) :]
    at = types.SimpleNamespace(**dict(zip(names, rest)))
    send_sems, recv_sems, local_sems = rest[len(names) :]
    copies = Copies(send_sems, recv_sems, local_sems)
    places = Places()
    saved = []

    def save(pick):
        for source, target in zip(pick(at), pick(outs)):
            saved.append(copies.local(source, target))

    at.own_pack[0] = jnp.zeros((64, KR + 128), BF16)
    at.own_pack[0, :, : KR + RD] = latent_ref[...]
    lane = lax.broadcasted_iota(jnp.int32, (64, 128), 1)
    ends = at.own_pack[0, :, KR:].astype(F32)
    for k, gain_ref in ((64, attn_gain_ref), (65, ffn_gain_ref)):
        column = jnp.broadcast_to(gain_ref[...].astype(F32), (8, 64)).T[:, 0:1]
        ends = jnp.where(lane == k, column, ends)
    at.own_pack[0, :, KR:] = ends.astype(BF16)
    column = jnp.broadcast_to(latent_gain_ref[...].astype(F32), (8, 16)).T[:, 0:1]
    lane = lax.broadcasted_iota(jnp.int32, (16, 128), 1)
    at.own_pack[0, 0:16, KR:] = jnp.where(lane == 66, column, ends[0:16]).astype(BF16)
    pack = SlotGather(copies, at.own_pack, at.pack.at[0], FAR_FIRST)
    copies.greet((0, 1, 2))
    keyval = SlotGather(copies, keyval_ref, at.keyval, FAR_FIRST)
    part = query_ref.shape[0] // 4
    queries = [
        SlotGather(copies, at.own_query, at.query, FAR_FIRST, cut=(k * part, part)) for k in range(4)
    ]
    part = output_ref.shape[1] // 2
    outputs = [SlotGather(copies, output_ref, at.output, FAR_FIRST, cut=(k * part, part)) for k in range(2)]
    pack.start()
    keyval.start()
    for k in range(8):
        block = pl.ds(pl.multiple_of(places[k] * SLOT, SLOT), SLOT)
        at.res[:, lanes(k)] = res_ref[:, block]
        at.grad[:, lanes(k)] = grad_ref[:, block]
    at.tokens[0] = at.res[...]
    tokens = SlotGather(copies, None, at.tokens, TENSOR_BITS, TENSOR)
    tokens.start()
    at.own_query[0] = nn(query_ref[...], sort_columns(768)).astype(BF16)
    items = [pack, keyval, *queries, *outputs]
    units = [(p, part) for p in range(n_units) for part in range(CHUNKS)]
    flights = [None] * len(units)
    owns = [None] * len(units)
    state = [0, 0, 0]

    def unit_source(side, p, part):
        if p < 2:
            expert = pl.ds(side * 2 + p, 1)
            return expert_out.at[expert] if part == 2 else expert_in.at[expert, part]
        cut = pl.ds(pl.multiple_of(side * width, 16), width)
        return shared_out.at[pl.ds(0, 1), cut] if part == 2 else shared_in.at[pl.ds(part, 1), cut]

    def unit_first():
        i = state[0]
        if i >= len(units):
            return
        p, part = units[i]
        cut = pl.ds(part * width, width)
        side = places[12]
        owns[i] = copies.local(unit_source(side, p, part), lows[p].at[pl.ds(0, 1), cut])
        flights[i] = copies.start(
            unit_source(1 - side, p, part), lows[p].at[pl.ds(1, 1), cut], DP, FLIPS[0]
        )
        state[0] = i + 1

    def unit_second():
        i = state[1]
        if i >= min(state[0], SECONDS):
            return
        p, part = units[i]
        cut = pl.ds(part * width, width)
        flights[i].wait()
        owns[i].wait()
        flights[i] = copies.start(
            lows[p].at[pl.ds(0, 2), cut], lows[p].at[pl.ds(2, 2), cut], DP, FLIPS[1]
        )
        state[1] = i + 1

    def unit_third():
        i = state[2]
        if i >= min(state[1], THIRDS):
            return
        p, part = units[i]
        cut = pl.ds(part * width, width)
        flights[i].wait()
        flights[i] = copies.start(lows[p].at[pl.ds(0, 4), cut], highs[p].at[pl.ds(0, 4), cut], DP, FLIPS[2])
        state[2] = i + 1

    def pump():
        unit_third()
        unit_second()
        unit_first()

    def place_tokens():
        segments = segment_row[...].astype(F32)
        at.col[:, 0:8] = jnp.broadcast_to(segments, (8, TOK)).T
        for b in range(4):
            start = pl.multiple_of(places[8 + b] * 160, 8)
            at.cos[b * 160 : (b + 1) * 160] = jnp.broadcast_to(at.col[pl.ds(start, 160), 0:1], (160, 128))
        for b in range(4):
            start = pl.multiple_of(places[8 + b] * 160, 8)
            cut = slice(b * 160, (b + 1) * 160)
            segment = at.cos[cut, 0:1]
            token = start + lax.broadcasted_iota(jnp.int32, (160, 128), 0)
            lane = lax.broadcasted_iota(jnp.int32, (160, 128), 1)
            at.col[cut] = jnp.where(lane == 0, segment, token.astype(F32))
            before = jnp.sum((segments < segment).astype(F32), axis=1, keepdims=True)
            angle = (token.astype(F32) - before) * frequency_ref[...]
            at.cos[cut] = jnp.cos(angle)
            at.sin[cut] = jnp.sin(angle)
        at.row[...] = at.col[...].T[0:8]
        at.valid[...] = (at.col[0:160, 1:2] < count_ref[0].astype(F32)).astype(F32) + jnp.zeros((160, 128), F32)
        at.masked[0] = (at.grad[...].astype(F32) * at.valid[:, 0:1]).astype(BF16)

    def route_tokens():
        slots = jnp.concatenate([table_ref[...].astype(F32), slot_gates[...]], axis=0).T
        token_row = at.row[1:2]
        for e in range(4):
            hit = jnp.where(slots[:, e : e + 1] == token_row, slots[:, 4 + e : 5 + e], 0.0)
            at.gates[e : e + 1] = jnp.sum(hit, axis=0, keepdims=True)
        at.gates[4:8] = jnp.zeros((4, TOK), F32)
        save(lambda v: (v.col, v.row, v.cos, v.sin, v.valid, v.res, v.grad, v.gates))

    def make_keys():
        for s in range(4):
            for k in range(8):
                start = pl.multiple_of(k * SLOT + places[8 + s] * 64, 64)
                at.w_latent[pl.ds(start, 64)] = at.pack[s, k]
                start = pl.multiple_of(places[k] * 64 + places[8 + s] * 16, 16)
                at.gain_rows[pl.ds(start, 16)] = at.pack[s, k, 0:16, KR : KR + 128]
        for k in range(8):
            at.w_keyval[pl.ds(pl.multiple_of(places[k] * 64, 64), 64)] = at.keyval[k]
        tail = at.w_latent[:, KR : KR + 128]
        turned = tail.astype(F32).T
        attn_gain = turned[64:65]
        at.gains[...] = turned[64:72]
        latent_gain = at.gain_rows[...].astype(F32).T[66:67]
        at.latent_gain[...] = jnp.broadcast_to(latent_gain, (8, KR))
        row = lax.broadcasted_iota(jnp.int32, (128, SLOT), 0)
        lane = lax.broadcasted_iota(jnp.int32, (128, SLOT), 1)
        spread = jnp.where(row == lax.rem(lane, 32) + 32 * (lane // 128), 1.0, 0.0).astype(BF16)
        w_rope = nn(tail, spread).astype(BF16)
        for b in range(4):
            cut = slice(b * 160, (b + 1) * 160)
            x = at.tokens[b].astype(F32)
            factor = lax.rsqrt(jnp.mean(x * x, axis=1, keepdims=True) + NORM_EPS)
            at.normed[cut] = (x * factor * attn_gain).astype(BF16)
        for b in range(2):
            cut = slice(b * 320, (b + 1) * 320)
            normed = at.normed[cut]
            latent_c = nn(normed, at.w_latent[:, :KR])
            factor = lax.rsqrt(jnp.mean(latent_c * latent_c, axis=1, keepdims=True) + NORM_EPS)
            latent_norm = (latent_c * factor * latent_gain).astype(BF16)
            if b == 0:
                at.latent_c[...] = latent_c[:160]
            at.latent_norm[cut] = latent_norm
            rope = nn(normed, w_rope)
            key_a, key_b = turn(rope[:, :128], rope[:, 128:], at.cos[cut], at.sin[cut])
            at.key_rope[cut] = jnp.concatenate([key_a, key_b], axis=1).astype(BF16)
            at.keyval_final[cut] = nn(latent_norm, at.w_keyval[...]).astype(BF16)
        save(lambda v: (v.w_latent, v.w_keyval, v.gains, v.latent_gain, v.normed, v.latent_c, v.latent_norm, v.key_rope, v.keyval_final,))


    unit_first()
    for tau in range(len(items) + 1):
        if tau >= 1:
            items[tau - 1].wait()
        if tau < len(items):
            items[tau].wait()
        if tau + 2 < len(items):
            items[tau + 2].start()
        if tau == 0:
            place_tokens()
        elif tau == 1:
            tokens.wait()
            grad_own = copies.local(at.masked, grad_pair.at[pl.ds(0, 1)])
            grad_x = copies.start(at.masked, grad_pair.at[pl.ds(2, 1)], TENSOR, 1)
        elif tau == 3:
            pack.wait()
            pack_tensor = SlotGather(copies, None, at.pack, TENSOR_BITS, TENSOR)
            pack_tensor.start()
            unit_second()
        elif tau == 4:
            unit_first()
            route_tokens()
            gates_flight = copies.start(at.gates, gates_over, DP, 1)
        elif tau == 5:
            tokens.wait()
            unit_second()
        elif tau == 6:
            pack_tensor.wait()
            unit_first()
        elif tau == 7:
            keyval.wait()
            pack_tensor.wait()
            make_keys()
            unit_second()
    grad_x.wait()
    grad_z = copies.swapped(at.masked, grad_pair.at[pl.ds(1, 1)], 0, D)
    pump()
    for query in queries:
        query.wait()

    save(lambda v: (v.query,))
    gates_flight.wait()
    w_query = at.query[...].reshape(D, 768)
    scale = (HD + RD) ** (-0.5)
    for b in range(2):
        cut = slice(b * 320, (b + 1) * 320)
        found = nn(at.normed[cut], w_query)
        turned_a, turned_b = turn(found[:, 512:640], found[:, 640:768], at.cos[cut], at.sin[cut])
        at.query_final[cut] = jnp.concatenate([found[:, :512], turned_a, turned_b], axis=1).astype(BF16)
        allowed = masks(at.col, at.row, cut)
        lse_lane = lax.broadcasted_iota(jnp.int32, (320, 128), 1)
        lse_all = jnp.zeros((320, 128), F32)
        for h in range(4):
            rope = at.query_final[cut, 512:768]
            rope = jnp.where(head_lanes(320, h), rope, jnp.zeros_like(rope))
            keys = at.keyval_final[:, h * 256 : h * 256 + 128]
            scores = nt(at.query_final[cut, lanes(h, 128)], keys) + nt(rope, at.key_rope[...])
            scores = jnp.where(allowed, scores * scale, -1e30)
            top = jnp.max(scores, axis=1, keepdims=True)
            weight = jnp.exp(scores - top)
            total = jnp.sum(weight, axis=1, keepdims=True)
            probs = (weight / total).astype(BF16)
            lse_all = jnp.where(lse_lane == h, top + jnp.log(total), lse_all)
            mix = nn(probs, at.keyval_final[:, h * 256 + 128 : h * 256 + 256])
            at.mix[cut, lanes(h, 128)] = mix.astype(BF16)
        at.lse[cut] = lse_all
        if b == 0:
            pump()
            grad_z.wait()
            grad_zx = copies.start(
                grad_pair.at[pl.ds(1, 1)], grad_pair.at[pl.ds(3, 1)], TENSOR, 1
            )
    for output in outputs:
        output.wait()
    save(lambda v: (v.query_final, v.mix, v.lse, v.output,))
    for b in range(2):
        cut = slice((1 - b) * 320, (2 - b) * 320)
        for k in range(8):
            w_output = at.output[k]
            part = nn(at.mix[cut], w_output).astype(BF16)
            at.part[2 - 2 * b, :, lanes(k)] = part[:160]
            at.part[3 - 2 * b, :, lanes(k)] = part[160:]
        if b == 0:
            block = lambda ref, k: ref.at[pl.ds(k, 1)]
            c_far = copies.start(block(at.part, 3), block(at.got_c, 1), TENSOR, 0)
            c_near = copies.start(block(at.part, 2), block(at.got_c, 0), TENSOR, 0)
    c_far.wait()
    at.give_x[0] = (at.part[1].astype(F32) + at.got_c[1].astype(F32)).astype(BF16)
    x_far = copies.start(at.give_x, at.got_x, TENSOR, 1)
    pump()
    grad_zx.wait()
    grad_own.wait()
    grad_c = copies.start(grad_pair.at[pl.ds(0, 4)], grad_pair.at[pl.ds(4, 4)], TENSOR, 0)
    pump()
    c_near.wait()
    x_far.wait()
    attn_out = at.part[0].astype(F32) + at.got_c[0].astype(F32) + at.got_x[0].astype(F32)
    mid = at.res[...].astype(F32) + at.valid[:, 0:1] * attn_out
    at.mid[...] = mid
    save(lambda v: (v.mid,))
    factor = lax.rsqrt(jnp.mean(mid * mid, axis=1, keepdims=True) + NORM_EPS)
    at.mid_pair[0] = (mid * factor * at.gains[1:2]).astype(BF16)
    spread_block(copies, at.mid_pair, pump)
    save(lambda v: (v.mid_pair,))
    grad_c.wait()
    while state[0] < len(units) or state[1] < SECONDS or state[2] < THIRDS:
        pump()
    for i in range(SECONDS, len(units)):
        owns[i].wait()
    for flight in flights:
        if flight is not None:
            flight.wait()
    for copy in saved:
        copy.wait()


def front(counts, latent, gains, keyval, output, expert_in, expert_out, shared_in, shared_out, res, grad, query, segment, table, gates):
    n_units, width = 3, expert_out.shape[1]
    half = (4, 3 * width, SLOT)
    frequency = ROPE_BASE ** (-np.arange(RD // 2, dtype=np.float32) / np.float32(RD // 2))
    frequency = jnp.asarray(np.tile(frequency.astype(np.float32), 4)[None])
    operands = [
        counts,
        keyval[None],
        output[None],
        expert_in.transpose(0, 1, 3, 2),
        expert_out,
        shared_in.transpose(0, 2, 1),
        shared_out[None],
        res,
        grad,
        query,
        segment,
        table,
        gates,
        frequency,
        latent,
        *gains,
    ]
    shapes = [like((8, *res.shape)), like((8, TOK), F32)] + [like(half)] * (2 * n_units - 1) + [like((4, width, SLOT))]
    shapes += [like(*buffer) for buffer in buffers(Kept)]
    results = pl.pallas_call(
        functools.partial(front_kernel, width),
        out_shape=shapes,
        in_specs=[SMEM_SPEC] + [ANY_SPEC] * 6 + [VMEM_SPEC] * 11,
        out_specs=[ANY_SPEC] * len(shapes),
        scratch_shapes=[pltpu.VMEM(*buffer) for buffer in buffers(Kept) + buffers(Landing)]
        + [
            pltpu.SemaphoreType.DMA((80,)),
            pltpu.SemaphoreType.DMA((80,)),
            pltpu.SemaphoreType.DMA((48,)),
        ],
        compiler_params=pltpu.CompilerParams(
            collective_id=0, has_side_effects=True, vmem_limit_bytes=GIVEN_VMEM
        ),
        cost_estimate=cost(220),
        name="front",
    )(*operands)
    grad_pair, gates_over, results = results[0], results[1], results[2:]
    lows, results = results[:n_units], results[n_units:]
    highs, results = results[:n_units], results[n_units:]
    return grad_pair, gates_over, lows, highs, types.SimpleNamespace(**dict(zip(fields(Kept), results)))


TOKEN_BLOCK = 256


class Freight:
    def __init__(self, copies, bits, sources, targets):
        self.copies, self.bits, self.pairs = copies, bits, list(zip(sources, targets))
        self.flights = []

    def start(self):
        for bit, (source, target) in zip(self.bits, self.pairs):
            self.flights.append(self.copies.start(source, target, DP, bit))

    def wait(self):
        for flight in self.flights:
            flight.wait()


class Split:
    def __init__(self, copies, keep, got, kept, gone):
        self.copies, self.kept, self.gone = copies, kept, gone
        self.loads = [copies.local(keep, kept), copies.local(got, gone)]
        self.half = kept.shape[0] // 2
        self.flights = []

    def send(self, bit, target, stay=None):
        for load in self.loads:
            load.wait()
        for k in range(2 * self.half):
            target_ref = self.kept if k < self.half else self.gone
            target_ref[k] = (self.kept[k].astype(F32) + self.gone[k].astype(F32)).astype(BF16)
        self.flights.append(
            self.copies.start(self.gone.at[pl.ds(self.half, self.half)], target, DP, bit)
        )
        if stay is not None:
            self.flights.append(self.copies.local(self.kept.at[pl.ds(0, self.half)], stay))

    def wait(self):
        for flight in self.flights:
            flight.wait()


def split_scratch(splits):
    return [pltpu.VMEM(keep.shape, BF16) for keep, _, _ in splits for _ in range(2)] + [
        pltpu.SemaphoreType.DMA((4 * len(splits),))
    ]


def split_outputs(splits):
    return [like((keep.shape[0] // 2, *keep.shape[1:])) for keep, _, _ in splits for _ in range(2)]


def experts_kernel(width, has_sum, gated, bits, parts, *refs):
    refs = list(refs)
    take = lambda n: [refs.pop(0) for _ in range(n)]
    mid_ref, grad_ref = take(2)
    gate_ref = take(1)[0] if gated else None
    unit_refs = take(len(parts))
    if has_sum:
        back_in, out_in = take(2)
    sources = take(len(bits))
    back_ref, out_ref = take(2)
    keep_refs, give_refs = take(3), take(3)
    targets = take(len(bits))
    whole, total, send_sems, recv_sems, local_sems = take(5)
    step = pl.program_id(0)
    copies = Copies(send_sems, recv_sems, local_sems)

    def flights():
        return [
            pltpu.make_async_remote_copy(
                src_ref=cut.view(source),
                dst_ref=target,
                send_sem=send_sems.at[k],
                recv_sem=recv_sems.at[k],
                device_id=copies.across(DP, cut.bit),
                device_id_type=MESH,
            )
            for k, (cut, source, target) in enumerate(zip(bits, sources, targets))
        ]

    @pl.when(step == 0)
    def _():
        copies.greet(sorted({cut.bit for cut in bits}), ())
        for flight in flights():
            flight.start()
        loads = []
        for ref, (slot, count, start, size, skip) in zip(unit_refs, parts):
            for j in range(count):
                k = COLUMNS.index(UNIT_SLOTS[slot + j])
                loads.append(
                    copies.local(
                        ref.at[j, pl.ds(skip, size)], whole.at[pl.ds(start, size), pl.ds(k * SLOT, SLOT)]
                    )
                )
        total[...] = jnp.zeros_like(total)
        for load in loads:
            load.wait()

    mid, grad = mid_ref[...], grad_ref[...]
    gate_up = nt(whole[: 2 * width], mid)
    hidden_grad = nt(whole[2 * width :], grad)
    gate = gate_up[:width]
    up = gate_up[width:]
    sigma = 1.0 / (1.0 + jnp.exp(-gate))
    silu = gate * sigma
    slope = sigma * (1.0 + gate * (1.0 - sigma))
    hidden = silu * up
    if gated:
        hidden_grad = hidden_grad * gate_ref[...]
        hidden = hidden * gate_ref[...]
    hidden = hidden.astype(BF16)
    pre = jnp.concatenate(
        [(hidden_grad * up * slope).astype(BF16), (hidden_grad * silu).astype(BF16)], axis=0
    )
    back = tn(pre, whole[: 2 * width])
    out = tn(hidden, whole[2 * width :])
    if has_sum:
        back = back + back_in[...]
        out = out + out_in[...]
    back_ref[...] = back.astype(back_ref.dtype)
    out_ref[...] = out.astype(out_ref.dtype)
    total[: 2 * width] += nn(pre, mid)
    total[2 * width :] += nn(hidden, grad)

    @pl.when(step == pl.num_programs(0) - 1)
    def _():
        for g in range(3):
            cut = slice(g * width, (g + 1) * width)
            for k in range(4):
                keep_refs[g][k] = total[cut, lanes((0, 2, 1, 3)[k])].astype(BF16)
                give_refs[g][k] = total[cut, lanes(4 + (0, 2, 1, 3)[k])].astype(BF16)
        for flight in flights():
            flight.wait()


class Cut:
    def __init__(self, array, bit, slots=None, rows=None):
        self.array, self.bit = array, bit
        self.slots = slots or (0, array.shape[0])
        self.rows = rows or (0, array.shape[1])

    def shape(self):
        return (self.slots[1], self.rows[1], self.array.shape[2])

    def view(self, ref):
        return ref.at[pl.ds(*self.slots), pl.ds(*self.rows)]


def experts_step(mid_pair, grad_pair, unit, gate, sums, last, freight, ident):
    tokens, block = mid_pair.shape[0], TOKEN_BLOCK
    width = unit[0][0].shape[1] // 3
    rows = pl.BlockSpec((block, D), lambda i: (i, 0))
    fixed = lambda *shape: pl.BlockSpec(shape, lambda i: (0,) * len(shape))
    kind = BF16 if last else F32
    part = (4, width, SLOT)
    operands, specs = [mid_pair, grad_pair], [rows, rows]
    if gate is not None:
        operands, specs = operands + [gate[None]], specs + [pl.BlockSpec((1, block), lambda i: (0, i))]
    operands += [part[0] for part in unit]
    specs += [ANY_SPEC] * len(unit)
    if sums is not None:
        operands += list(sums)
        specs += [rows, rows]
    results = pl.pallas_call(
        functools.partial(
            experts_kernel, width, sums is not None, gate is not None, tuple(freight), tuple(p[1:] for p in unit)
        ),
        grid=(tokens // block,),
        out_shape=[like((tokens, D), kind)] * 2
        + [like(part)] * 6
        + [like(cut.shape()) for cut in freight],
        in_specs=specs + [ANY_SPEC] * len(freight),
        out_specs=[rows, rows] + [fixed(*part)] * 6 + [ANY_SPEC] * len(freight),
        scratch_shapes=[
            pltpu.VMEM((3 * width, D), BF16),
            pltpu.VMEM((3 * width, D), F32),
            pltpu.SemaphoreType.DMA((len(freight),)),
            pltpu.SemaphoreType.DMA((len(freight),)),
            pltpu.SemaphoreType.DMA((24,)),
        ],
        compiler_params=pltpu.CompilerParams(
            collective_id=ident, has_side_effects=True, vmem_limit_bytes=GIVEN_VMEM
        ),
        cost_estimate=cost(35),
        name="experts_step",
    )(*operands, *[cut.array for cut in freight])
    return list(results[:2]), list(results[2:5]), list(results[5:8]), list(results[8:])


def halve_kernel(count, *refs):
    keeps, gots, stays, gives = (refs[k * count : (k + 1) * count] for k in range(4))
    for keep, got, stay, give in zip(keeps, gots, stays, gives):
        half = stay.shape[0]
        for k in range(half):
            stay[k] = (keep[k].astype(F32) + got[k].astype(F32)).astype(BF16)
            give[k] = (keep[half + k].astype(F32) + got[half + k].astype(F32)).astype(BF16)


def halve(pairs):
    count = len(pairs)
    shapes = [like((keep.shape[0] // 2, *keep.shape[1:])) for keep, _ in pairs]
    results = pl.pallas_call(
        functools.partial(halve_kernel, count),
        out_shape=shapes * 2,
        in_specs=[VMEM_SPEC] * (2 * count),
        out_specs=[VMEM_SPEC] * (2 * count),
        cost_estimate=cost(3),
        name="halve",
    )(*[keep for keep, _ in pairs], *[got for _, got in pairs])
    return list(zip(results[:count], results[count:]))


class PairSum:
    def __init__(self, copies, blocks, got_c, give_a, give_b, got_a, got_b, end_a, end_b, last_a, last_b):
        self.copies, self.blocks, self.got_c = copies, blocks, got_c
        self.give_a, self.give_b, self.got_a, self.got_b = give_a, give_b, got_a, got_b
        self.end_a, self.end_b, self.last_a, self.last_b = end_a, end_b, last_a, last_b

    def both(self, k, first):
        cut = slice(first, first + 1024)
        return self.blocks[k, :, cut].astype(F32) + self.got_c[k, :, cut].astype(F32)

    def start(self):
        self.flights = {}
        for k in (3, 2, 1, 0):
            self.flights[k] = self.copies.start(
                self.blocks.at[pl.ds(4 + k, 1)], self.got_c.at[pl.ds(k, 1)], TENSOR, 0
            )

    def cross(self):
        self.flights[3].wait()
        self.give_a[1] = self.both(3, 0).astype(BF16)
        self.give_b[1] = self.both(3, 1024).astype(BF16)
        self.flights[2].wait()
        self.give_a[0] = self.both(2, 0).astype(BF16)
        self.across_a = self.copies.start(self.give_a, self.got_a, TENSOR, 1)
        self.flights[1].wait()
        self.give_b[0] = self.both(1, 1024).astype(BF16)
        self.across_b = self.copies.swapped(self.give_b, self.got_b, 0, 1024)
        self.flights[0].wait()

    def end(self):
        self.across_a.wait()
        self.end_a[0] = (self.both(1, 0) + self.got_a[1].astype(F32)).astype(BF16)
        self.ends_a = self.copies.swapped(self.end_a, self.last_a, 0, 1024)
        self.across_b.wait()
        self.end_b[0] = (self.both(2, 1024) + self.got_b[1].astype(F32)).astype(BF16)
        self.ends_b = self.copies.start(self.end_b, self.last_b, TENSOR, 1)

    def settle(self, total, end_a, end_b):
        self.across_a.wait()
        end_a[0] = (self.both(1, 0) + self.got_a[1].astype(F32)).astype(BF16)
        self.across_b.wait()
        end_b[0] = (self.both(2, 1024) + self.got_b[1].astype(F32)).astype(BF16)
        total[:, :1024] = self.both(0, 0) + self.got_a[0].astype(F32)
        total[:, 1024:] = self.both(0, 1024) + self.got_b[0].astype(F32)

    def total(self):
        self.ends_a.wait()
        self.ends_b.wait()
        return (
            self.both(0, 0) + self.got_a[0].astype(F32) + self.last_a[0].astype(F32),
            self.both(0, 1024) + self.got_b[0].astype(F32) + self.last_b[0].astype(F32),
        )


def sum_scratch():
    half = pltpu.VMEM((2, 160, 1024), BF16)
    end = pltpu.VMEM((1, 160, 1024), BF16)
    return [pltpu.VMEM((4, 160, D), BF16), half, half, half, half, end, end, end, end]


def back_kernel(bits, splits, *refs):
    refs = list(refs)
    take = lambda n: [refs.pop(0) for _ in range(n)]
    back_ref, grad_ref, mid_ref, gains_ref, valid_ref = take(5)
    sources = take(len(bits))
    pairs = take(2 * len(splits))
    mid_grad_ref, gain_part_ref, tokens_ref = take(3)
    targets = take(len(bits))
    ends = take(2 * len(splits))
    rooms = take(2 * len(splits))
    local_sems, *buffers, send_sems, recv_sems = refs
    copies = Copies(send_sems, recv_sems, local_sems)
    parts = [Split(copies, *pairs[2 * k : 2 * k + 2], *rooms[2 * k : 2 * k + 2]) for k in range(len(splits))]
    copies.greet((0, 1, 2))
    freight = Freight(copies, bits, sources, targets)
    freight.start()
    pair = PairSum(copies, back_ref, *buffers)
    pair.start()
    for k, bit in enumerate(splits):
        parts[k].send(bit, ends[2 * k + 1], ends[2 * k])
    pair.cross()
    pair.end()
    first, second = pair.total()
    mid_grad_ref[:, :1024] = first
    mid_grad_ref[:, 1024:] = second
    grad, mid = mid_grad_ref[...], mid_ref[...]
    factor = lax.rsqrt(jnp.mean(mid * mid, axis=1, keepdims=True) + NORM_EPS)
    scaled = grad * gains_ref[1:2]
    inner = jnp.mean(scaled * mid, axis=1, keepdims=True)
    gain_part_ref[...] = jnp.broadcast_to(jnp.sum(grad * mid * factor, axis=0, keepdims=True), (8, D))
    mid_grad = grad_ref[...].astype(F32) + factor * (scaled - mid * factor * factor * inner)
    mid_grad_ref[...] = mid_grad
    tokens_ref[0] = (valid_ref[:, 0:1] * mid_grad).astype(BF16)
    own = tokens_ref.at[pl.ds(0, 1)]
    x_own = copies.start(own, tokens_ref.at[pl.ds(1, 1)], TENSOR, 1)
    c_own = copies.start(own, tokens_ref.at[pl.ds(2, 1)], TENSOR, 0)
    x_own.wait()
    c_far = copies.start(tokens_ref.at[pl.ds(1, 1)], tokens_ref.at[pl.ds(3, 1)], TENSOR, 0)
    c_own.wait()
    c_far.wait()
    freight.wait()
    for part in parts:
        part.wait()


def back_tokens(back, grad_slots, mid, gains, valid, freight, splits):
    rows = (160, D)
    bits = tuple(bit for bit, _ in freight)
    goods = [array for _, array in freight]
    results = pl.pallas_call(
        functools.partial(back_kernel, bits, tuple(bit for _, _, bit in splits)),
        out_shape=[like(rows, F32), like((8, D), F32), like((4, *rows))]
        + [like(g.shape, g.dtype) for g in goods]
        + split_outputs(splits),
        in_specs=[VMEM_SPEC] * 5 + [ANY_SPEC] * (len(goods) + 2 * len(splits)),
        out_specs=[VMEM_SPEC] * 3 + [ANY_SPEC] * (len(goods) + 2 * len(splits)),
        scratch_shapes=split_scratch(splits)
        + sum_scratch() + [pltpu.SemaphoreType.DMA((24,)), pltpu.SemaphoreType.DMA((24,))],
        compiler_params=pltpu.CompilerParams(
            collective_id=2, has_side_effects=True, vmem_limit_bytes=GIVEN_VMEM
        ),
        cost_estimate=cost(55),
        name="back_tokens",
    )(back, grad_slots, mid, gains, valid, *goods, *[v for keep, got, _ in splits for v in (keep, got)])
    n = 3 + len(goods)
    return results[:3], list(results[3:n]), list(zip(results[n::2], results[n + 1 :: 2]))


def attention_backward_kernel(bits, splits, *refs):
    refs = list(refs)
    take = lambda n: [refs.pop(0) for _ in range(n)]
    (
        grad_ref,
        output_ref,
        mix_ref,
        query_ref,
        keyval_ref,
        key_rope_ref,
        lse_ref,
        w_query_ref,
        w_keyval_ref,
        normed_ref,
        latent_norm_ref,
        col_ref,
        row_ref,
        cos_ref,
        sin_ref,
        out_ref,
    ) = take(16)
    sources = take(len(bits))
    pairs = take(2 * len(splits))
    output_wgrad, query_wgrad, keyval_wgrad, part_ref, out_sum, out_end_a, out_end_b = take(7)
    targets = take(len(bits))
    output_got = take(1)[0]
    ends = take(2 * len(splits))
    rooms = take(2 * len(splits))
    local_sems = take(1)[0]
    mix_grad, query_grad, keyval_grad, key_grad, rope_grad, wide, send_sems, recv_sems = take(8)
    copies = Copies(send_sems, recv_sems, local_sems)
    parts = [Split(copies, *pairs[2 * k : 2 * k + 2], *rooms[2 * k : 2 * k + 2]) for k in range(len(splits))]
    copies.greet((0, 1, 2))
    pair = PairSum(copies, out_ref, *refs, None, None, None, None)
    pair.start()
    freight = Freight(copies, bits, sources, targets)
    freight.start()
    for k, bit in enumerate(splits):
        parts[k].send(bit, ends[2 * k + 1], ends[2 * k])
    places = Places()
    scale = (HD + RD) ** (-0.5)
    w_query = w_query_ref[...].reshape(D, w_query_ref.shape[2])
    for k in range(8):
        block = jnp.concatenate([grad_ref[b, :, lanes(k)] for b in range(4)], axis=0)
        s = k
        output_wgrad[s] = tn(mix_ref[...], block).astype(BF16)
        term = nt(block, output_ref[s])
        if k == 0:
            wide[:, :512] = term
        else:
            wide[:, :512] += term
    mix_grad[...] = wide[:, :512].astype(BF16)
    output_flight = copies.start(output_wgrad.at[pl.ds(4, 4)], output_got, DP, 0)
    pair.cross()
    for b in range(2):
        cut = slice(b * 320, (b + 1) * 320)
        allowed = masks(col_ref, row_ref, cut)
        lse_lane = lax.broadcasted_iota(jnp.int32, (320, 128), 1)
        rope_sum = jnp.zeros((320, SLOT), F32)
        for h in range(4):
            nope = query_ref[cut, lanes(h, 128)]
            rope = query_ref[cut, 512:768]
            mask = head_lanes(320, h)
            rope = jnp.where(mask, rope, jnp.zeros_like(rope))
            keys = keyval_ref[:, h * 256 : h * 256 + 128]
            values = keyval_ref[:, h * 256 + 128 : h * 256 + 256]
            scores = nt(nope, keys) + nt(rope, key_rope_ref[...])
            lse = jnp.sum(jnp.where(lse_lane == h, lse_ref[cut], 0.0), axis=1, keepdims=True)
            probs = jnp.where(allowed, jnp.exp(scores * scale - lse), 0.0)
            grad = mix_grad[cut, lanes(h, 128)]
            probs_grad = nt(grad, values)
            inner = jnp.sum(probs * probs_grad, axis=1, keepdims=True)
            scores_grad = (probs * (probs_grad - inner)).astype(BF16)
            value_grad = tn(probs.astype(BF16), grad)
            nope_grad = tn(scores_grad, nope) * scale
            rope_part = tn(scores_grad, rope)
            low, high = slice(h * 256, h * 256 + 128), slice(h * 256 + 128, h * 256 + 256)
            if b == 0:
                key_grad[:, low] = nope_grad
                key_grad[:, high] = value_grad
            else:
                key_grad[:, low] += nope_grad
                key_grad[:, high] += value_grad
            if b == 0 and h == 0:
                rope_grad[...] = rope_part
            else:
                rope_grad[...] += rope_part
            query_grad[cut, lanes(h, 128)] = (nn(scores_grad, keys) * scale).astype(BF16)
            rope_sum = rope_sum + jnp.where(mask, nn(scores_grad, key_rope_ref[...]), 0.0)
        rope_sum = rope_sum * scale
        back_a, back_b = turn(rope_sum[:, :128], rope_sum[:, 128:], cos_ref[cut], -sin_ref[cut])
        query_grad[cut, 512:640] = back_a.astype(BF16)
        query_grad[cut, 640:768] = back_b.astype(BF16)
    keyval_grad[...] = key_grad[...].astype(BF16)
    plain = nt(query_grad[...], sort_columns(768)).astype(BF16)
    for k in range(8):
        query_wgrad[k] = tn(normed_ref[:, lanes(k)], plain).astype(BF16)
    wide[:512, :] = tn(latent_norm_ref[...], keyval_grad[...])
    for k in range(8):
        start = pl.multiple_of(places[k] * 64, 64)
        keyval_wgrad[k] = wide[pl.ds(start, 64), :].astype(BF16)
    row = lax.broadcasted_iota(jnp.int32, (SLOT, 128), 0)
    lane = lax.broadcasted_iota(jnp.int32, (SLOT, 128), 1)
    fold = jnp.where(lane == lax.rem(row, 32) + 32 * (row // 128), scale, 0.0)
    for b in range(4):
        cut = slice(b * 160, (b + 1) * 160)
        for k in range(4):
            columns = lanes(k, 512)
            part_ref[b, :, columns] = nt(query_grad[cut], w_query[columns]).astype(BF16)
        part_ref[b, :, D : D + KR] = nt(keyval_grad[cut], w_keyval_ref[...]).astype(BF16)
        rope = lax.dot_general(
            rope_grad[cut],
            fold,
            (((1,), (0,)), ((), ())),
            precision=lax.Precision.HIGHEST,
            preferred_element_type=F32,
        )
        part_ref[b, :, D + KR :] = rope.astype(BF16)
    pair.settle(out_sum, out_end_a, out_end_b)
    output_flight.wait()
    freight.wait()
    for part in parts:
        part.wait()


def attention_backward(grad, saved, out, freight, splits):
    shapes = [like((8, 512, SLOT)), like((8, SLOT, 768)), like((8, 64, 1024)), like((4, 160, D + KR + 128))]
    shapes += [like((160, D), F32), like((1, 160, 1024)), like((1, 160, 1024))]
    bits = tuple(bit for bit, _ in freight)
    goods = [array for _, array in freight]
    kept = (saved.output, saved.mix, saved.query_final, saved.keyval_final, saved.key_rope, saved.lse, saved.query)
    kept += (saved.w_keyval, saved.normed, saved.latent_norm, saved.col, saved.row, saved.cos, saved.sin)
    results = pl.pallas_call(
        functools.partial(attention_backward_kernel, bits, tuple(bit for _, _, bit in splits)),
        out_shape=shapes + [like(g.shape) for g in goods] + [like((4, 512, SLOT))] + split_outputs(splits),
        in_specs=[VMEM_SPEC] * 16 + [ANY_SPEC] * (len(goods) + 2 * len(splits)),
        out_specs=[VMEM_SPEC] * len(shapes) + [ANY_SPEC] * (len(goods) + 1 + 2 * len(splits)),
        scratch_shapes=split_scratch(splits)
        + [
            pltpu.VMEM((TOK, 512), BF16),
            pltpu.VMEM((TOK, 768), BF16),
            pltpu.VMEM((TOK, 1024), BF16),
            pltpu.VMEM((TOK, 1024), F32),
            pltpu.VMEM((TOK, SLOT), F32),
            pltpu.VMEM((TOK, 1024), F32),
            pltpu.SemaphoreType.DMA((32,)),
            pltpu.SemaphoreType.DMA((32,)),
            *sum_scratch()[:5],
        ],
        compiler_params=pltpu.CompilerParams(
            collective_id=4, has_side_effects=True, vmem_limit_bytes=GIVEN_VMEM
        ),
        cost_estimate=cost(30),
        name="attention_backward",
    )(grad, *kept, out, *goods, *[v for keep, got, _ in splits for v in (keep, got)])
    n = 8 + len(goods)
    return results[:7], list(results[7:n]), list(zip(results[n::2], results[n + 1 :: 2]))


class SlotSum:
    def __init__(self, copies, values, bits, got, give, rows=None):
        self.copies, self.values, self.bits, self.got, self.give = copies, values, list(bits), got, give
        self.rows = rows or (0, values.shape[1])
        self.level = 0
        self.flying = None

    def view(self, ref, first, count):
        return ref.at[pl.ds(first, count), pl.ds(*self.rows)]

    def start(self):
        half = 4 >> self.level
        if self.level == 0:
            source = self.view(self.values, half, half)
        else:
            first, size = self.rows
            for k in range(half):
                self.give[self.level - 1][k, first : first + size] = self.total(half + k).astype(BF16)
            source = self.view(self.give[self.level - 1], 0, half)
        target = self.view(self.got[self.level], 0, half)
        self.flying = self.copies.start(source, target, DP, self.bits[self.level])
        self.level += 1

    def total(self, k):
        cut = slice(self.rows[0], self.rows[0] + self.rows[1])
        value = self.values[k, cut].astype(F32)
        for level in range(self.level):
            value = value + self.got[level][k, cut].astype(F32)
        return value

    def wait(self):
        self.flying.wait()
        if self.level < len(self.bits):
            self.start()


def slot_sum_scratch(shape):
    spaces = [pltpu.VMEM((n, *shape), BF16) for n in (4, 2, 1)]
    return spaces + [pltpu.VMEM((n, *shape), BF16) for n in (2, 1)]


def tail_kernel(
    n_rest,
    n_last,
    part_ref,
    output_wgrad,
    query_wgrad,
    keyval_wgrad,
    normed_ref,
    w_latent_ref,
    gains_ref,
    latent_gain_ref,
    latent_c_ref,
    res_ref,
    mid_grad_ref,
    ffn_gain_ref,
    output_came,
    mid_ref,
    valid_ref,
    out_sum,
    out_end_a,
    out_end_b,
    cos_ref,
    sin_ref,
    *refs,
):
    refs = list(refs)
    take = lambda n: [refs.pop(0) for _ in range(n)]
    rest_pairs, last_pairs = take(2 * n_rest), take(2 * n_last)
    output_owned, query_owned, keyval_owned, latent_owned, res_grad_ref, res_out_ref = take(6)
    rest_owned, end_cames = take(n_rest), take(n_rest)
    last_ends = take(2 * n_last)
    send_sems, recv_sems = take(2)
    sums = []
    copies = Copies(send_sems, recv_sems)
    for values, bits in (
        (query_wgrad, (0, 1, 2)),
        (keyval_wgrad, (0, 1, 2)),
        (output_wgrad, (0, 1, 2)),
    ):
        space = take(5)
        if values is query_wgrad:
            half = values.shape[1] // 2
            for k in range(2):
                sums.append(SlotSum(copies, values, bits, space[:3], space[3:], (k * half, half)))
        else:
            sums.append(SlotSum(copies, values, bits, space[:3], space[3:]))
    latent_values = take(1)[0]
    space = take(5)
    latent_sum = SlotSum(copies, latent_values, (0, 1, 2), space[:3], space[3:])
    got_c, give_x, got_x = take(3)
    latent_all, gain_rows, gain_c, gain_x, gain_columns, wide, rest_came, end_sum, _, local_sems = take(10)
    copies.local_sems = local_sems
    copies.greet((0, 1, 2))
    last_a, last_b = take(2)
    out_ends = [copies.swapped(out_end_a, last_a, 0, 1024), copies.start(out_end_b, last_b, TENSOR, 1)]
    rest_rooms, last_rooms = take(2 * n_rest), take(2 * n_last)
    rests = [Split(copies, *rest_pairs[2 * k : 2 * k + 2], *rest_rooms[2 * k : 2 * k + 2]) for k in range(n_rest)]
    lasts = [Split(copies, *last_pairs[2 * k : 2 * k + 2], *last_rooms[2 * k : 2 * k + 2]) for k in range(n_last)]
    query_first, query_second, keyval_sum, output_sum = sums
    output_sum.got[0] = output_came
    output_sum.level = 1
    query_first.start()
    output_sum.start()
    c_far = copies.start(part_ref.at[pl.ds(3, 1)], got_c.at[pl.ds(1, 1)], TENSOR, 0)
    c_near = copies.start(part_ref.at[pl.ds(2, 1)], got_c.at[pl.ds(0, 1)], TENSOR, 0)
    c_far.wait()
    give_x[0] = (part_ref[1].astype(F32) + got_c[1].astype(F32)).astype(BF16)
    x_far = copies.start(give_x, got_x, TENSOR, 1)
    for k in range(n_rest):
        rests[k].send(2, rest_came.at[pl.ds(2 * k, 2)])
    for k in range(n_last):
        lasts[k].send(1, last_ends[2 * k + 1], last_ends[2 * k])
    c_near.wait()
    query_first.wait()
    query_second.start()
    x_far.wait()

    def summed(columns):
        return (
            part_ref[0, :, columns].astype(F32)
            + got_c[0, :, columns].astype(F32)
            + got_x[0, :, columns].astype(F32)
        )

    latent_c = latent_c_ref[...]
    latent_gain = latent_gain_ref[0:1]
    factor = lax.rsqrt(jnp.mean(latent_c * latent_c, axis=1, keepdims=True) + NORM_EPS)
    grad = summed(slice(D, D + KR))
    scaled = grad * latent_gain
    inner = jnp.mean(scaled * latent_c, axis=1, keepdims=True)
    latent_back = factor * (scaled - latent_c * factor * factor * inner)
    latent_gain_part = jnp.sum(grad * latent_c * factor, axis=0, keepdims=True)
    rope = summed(slice(D + KR, D + KR + 128))
    cos, sin = cos_ref[...], sin_ref[...]
    lane = lax.broadcasted_iota(jnp.int32, rope.shape, 1)
    other = jnp.where(lane < 32, pltpu.roll(rope, 96, 1), pltpu.roll(rope, 32, 1))
    rope_back = jnp.where(lane < 32, rope * cos + other * sin, rope * cos - other * sin)
    rope_back = jnp.where(lane < RD, rope_back, 0.0)
    latent_all[0, :, :KR] = latent_back.astype(BF16)
    latent_all[0, :, KR:] = rope_back.astype(BF16)
    own = latent_all.at[pl.ds(0, 1)]
    l_x = copies.start(own, latent_all.at[pl.ds(1, 1)], TENSOR, 1)
    l_c = copies.start(own, latent_all.at[pl.ds(2, 1)], TENSOR, 0)
    res = res_ref[...].astype(F32)
    factor = lax.rsqrt(jnp.mean(res * res, axis=1, keepdims=True) + NORM_EPS)
    grad = summed(slice(0, D)) + nt(latent_all[0], w_latent_ref[...])
    scaled = grad * gains_ref[0:1]
    inner = jnp.mean(scaled * res, axis=1, keepdims=True)
    res_grad_ref[...] = mid_grad_ref[...] + factor * (scaled - res * factor * factor * inner)
    row = lax.broadcasted_iota(jnp.int32, (8, D), 0)
    attn_part = jnp.broadcast_to(jnp.sum(grad * res * factor, axis=0, keepdims=True), (8, D))
    gain_rows[0] = jnp.where(row == 0, attn_part, jnp.where(row == 1, ffn_gain_ref[...], 0.0))
    latent_row = jnp.broadcast_to(latent_gain_part, (8, KR))
    gain_rows[0, :, :KR] = jnp.where(
        lax.broadcasted_iota(jnp.int32, (8, KR), 0) == 2, latent_row, gain_rows[0, :, :KR]
    )
    g_c = copies.start(gain_rows, gain_c, TENSOR, 0)
    query_second.wait()
    keyval_sum.start()
    query_first.wait()
    l_x.wait()
    l_far = copies.start(latent_all.at[pl.ds(1, 1)], latent_all.at[pl.ds(3, 1)], TENSOR, 0)
    g_c.wait()
    gain_rows[0] = gain_rows[0] + gain_c[0]
    g_x = copies.start(gain_rows, gain_x, TENSOR, 1)
    l_c.wait()
    l_far.wait()
    g_x.wait()
    output_sum.wait()
    keyval_sum.wait()
    query_second.wait()
    gain_columns[:, 0:8] = (gain_rows[0] + gain_x[0]).T
    tensor = lax.axis_index(TENSOR)
    dp = lax.axis_index(DP)
    latent_rows = jnp.concatenate([latent_all[b] for b in range(4)], axis=0)
    for k in range(8):
        wide[...] = tn(normed_ref[:, lanes(k)], latent_rows)
        block = wide[pl.ds(pl.multiple_of(tensor * 64, 64), 64), :]
        start = pl.multiple_of(k * SLOT + tensor * 64, 64)
        columns = gain_columns[pl.ds(start, 64), 0:8]
        start = pl.multiple_of(crossed(dp, COLUMNS[k], 3) * 64 + tensor * 16, 16)
        latent_values[k] = block.astype(BF16)
        lane = lax.broadcasted_iota(jnp.int32, (64, 128), 1)
        ends = block[:, KR : KR + 128]
        ends = jnp.where(lane == 64, columns[:, 0:1], ends)
        ends = jnp.where(lane == 65, columns[:, 1:2], ends)
        latent_values[k, :, KR:] = ends.astype(BF16)
        corner = gain_columns[pl.ds(start, 16), 0:8][:, 2:3]
        lane = lax.broadcasted_iota(jnp.int32, (16, 128), 1)
        latent_values[k, 0:16, KR:] = jnp.where(lane == 66, corner, ends[0:16]).astype(BF16)
    latent_sum.start()
    ends = []
    for g in range(n_rest):
        rests[g].wait()
        own, over = rests[g].kept[0].astype(F32), rests[g].kept[1].astype(F32)
        rest_owned[g][0] = (own + rest_came[2 * g].astype(F32)).astype(BF16)
        end_sum[g] = (over + rest_came[2 * g + 1].astype(F32)).astype(BF16)
        ends.append(copies.start(end_sum.at[pl.ds(g, 1)], end_cames[g], DP, 1))
    keyval_sum.wait()
    output_sum.wait()
    output_owned[...] = output_sum.total(0)
    latent_sum.wait()
    for flight in out_ends:
        flight.wait()
    valid = valid_ref[:, 0:1]
    res_out_ref[:, :1024] = (mid_ref[:, :1024] + valid * (out_sum[:, :1024] + last_a[0].astype(F32))).astype(BF16)
    res_out_ref[:, 1024:] = (mid_ref[:, 1024:] + valid * (out_sum[:, 1024:] + last_b[0].astype(F32))).astype(BF16)
    latent_sum.wait()
    half = query_owned.shape[0] // 2
    query_first.wait()
    query_owned[:half] = query_first.total(0)
    keyval_sum.wait()
    keyval_owned[...] = keyval_sum.total(0)
    query_second.wait()
    query_owned[half:] = query_second.total(0)
    latent_sum.wait()
    latent_owned[...] = latent_sum.total(0)
    for copy in lasts + ends:
        copy.wait()


def tail(part, wgrads, output_came, out_parts, saved, mid_grad, ffn_gain, rests, lasts):
    output_wgrad, query_wgrad, keyval_wgrad = wgrads
    rows = (160, D)
    latent = (64, KR + 128)
    shapes = [
        like((512, SLOT), F32),
        like((SLOT, 768), F32),
        like((64, 1024), F32),
        like(latent, F32),
        like(rows, F32),
        like(rows),
    ]
    part_row = (160, D + KR + 128)
    unit = rests[0][0].shape[1:]
    rows_spec = pl.BlockSpec((160, 128), lambda i: (0, 0))
    results = pl.pallas_call(
        functools.partial(tail_kernel, len(rests), len(lasts)),
        out_shape=shapes + [like((1, *unit))] * (2 * len(rests) + 2 * len(lasts)),
        grid=(1,),
        in_specs=[VMEM_SPEC] * 18 + [rows_spec] * 2 + [ANY_SPEC] * (2 * len(rests) + 2 * len(lasts)),
        out_specs=[VMEM_SPEC] * (len(shapes) + len(rests)) + [ANY_SPEC] * (len(rests) + 2 * len(lasts)),
        scratch_shapes=[
            pltpu.SemaphoreType.DMA((40,)),
            pltpu.SemaphoreType.DMA((40,)),
            *slot_sum_scratch((SLOT, 768)),
            *slot_sum_scratch((64, 1024)),
            *slot_sum_scratch((512, SLOT)),
            pltpu.VMEM((8, *latent), BF16),
            *slot_sum_scratch(latent),
            pltpu.VMEM((2, *part_row), BF16),
            pltpu.VMEM((1, *part_row), BF16),
            pltpu.VMEM((1, *part_row), BF16),
            pltpu.VMEM((4, 160, KR + 128), BF16),
            pltpu.VMEM((1, 8, D), F32),
            pltpu.VMEM((1, 8, D), F32),
            pltpu.VMEM((1, 8, D), F32),
            pltpu.VMEM((D, 128), F32),
            pltpu.VMEM((SLOT, KR + 128), F32),
            pltpu.VMEM((2 * len(rests), *unit), BF16),
            pltpu.VMEM((len(rests), *unit), BF16),
            pltpu.SemaphoreType.DMA((1,)),
            pltpu.SemaphoreType.DMA((32,)),
            pltpu.VMEM((1, 160, 1024), BF16),
            pltpu.VMEM((1, 160, 1024), BF16),
            *split_scratch(rests)[:-1],
            *split_scratch(lasts)[:-1],
        ],
        compiler_params=pltpu.CompilerParams(
            collective_id=3, has_side_effects=True, vmem_limit_bytes=GIVEN_VMEM
        ),
        cost_estimate=cost(110),
        name="tail",
    )(
        part,
        output_wgrad,
        query_wgrad,
        keyval_wgrad,
        saved.normed,
        saved.w_latent,
        saved.gains,
        saved.latent_gain,
        saved.latent_c,
        saved.res,
        mid_grad,
        ffn_gain,
        output_came,
        saved.mid,
        saved.valid,
        *out_parts,
        saved.cos,
        saved.sin,
        *[v for keep, got, _ in rests + lasts for v in (keep, got)],
    )
    n = len(rests)
    return results[:6], results[6 : 6 + n], results[6 + n : 6 + 2 * n], list(zip(results[6 + 2 * n :: 2], results[7 + 2 * n :: 2]))


def finish_kernel(
    n_came,
    res_out_ref,
    res_grad_ref,
    latent_ref,
    *refs,
):
    refs = list(refs)
    take = lambda n: [refs.pop(0) for _ in range(n)]
    stays, cames, others = take(9), take(n_came), take(9)
    passed = take(3)
    res_out, res_grad, latent, attn_gain, ffn_gain, latent_gain, expert_in, expert_out, shared_in, shared_out, *out = refs
    for source, target in zip(passed, out):
        target[...] = source[...]
    places = Places()
    for k in range(8):
        block = pl.ds(pl.multiple_of(places[k] * SLOT, SLOT), SLOT)
        res_out[:, block] = res_out_ref[:, lanes(k)]
        res_grad[:, block] = res_grad_ref[:, lanes(k)]
    latent[...] = latent_ref[:, : KR + RD]
    turned = latent_ref[:, KR : KR + 128].T
    attn_gain[...] = turned[64:65]
    ffn_gain[...] = turned[65:66]
    latent_gain[...] = turned[66:67, : KR // 32]
    side = places[12]
    n_half = expert_in.shape[0] // 2
    width = expert_out.shape[1]
    for p in range(n_half + 1):
        for mine in (True, False):
            which = side if mine else 1 - side
            for g in range(3):
                value = (stays if mine else others)[3 * p + g][0].astype(F32)
                late = 3 * p + g - 9 + n_came
                if mine and late >= 0:
                    value = value + cames[late][0].astype(F32)
                if p < n_half and g < 2:
                    expert_in[which * n_half + p, g] = value
                elif p < n_half:
                    expert_out[which * n_half + p] = value
                else:
                    cut = pl.ds(pl.multiple_of(which * width, 8), width)
                    if g < 2:
                        shared_in[g, cut] = value
                    else:
                        shared_out[cut] = value


def finish(res_out, res_grad, latent, stays, cames, others, passed, width):
    shapes = [
        like(res_out.shape),
        like(res_grad.shape, F32),
        like((64, KR + RD), F32),
        like((1, 64), F32),
        like((1, 64), F32),
        like((1, KR // 32), F32),
        like((EXPERTS, 2, width, SLOT), F32),
        like((EXPERTS, width, SLOT), F32),
        like((2, 2 * width, SLOT), F32),
        like((2 * width, SLOT), F32),
    ] + [like(array.shape, F32) for array in passed]
    return pl.pallas_call(
        functools.partial(finish_kernel, len(cames)),
        out_shape=shapes,
        in_specs=[VMEM_SPEC] * (24 + len(cames)),
        out_specs=[VMEM_SPEC] * len(shapes),
        compiler_params=pltpu.CompilerParams(vmem_limit_bytes=GIVEN_VMEM),
        cost_estimate=cost(10),
        name="finish",
    )(res_out, res_grad, latent, *stays, *cames, *others, *passed)


def body(
    res_in,
    out_grad,
    seg_ids,
    tok_counts,
    slot_table,
    slot_gates,
    attn_gain,
    latent_gain,
    ffn_gain,
    w_latent,
    w_query,
    w_keyval,
    w_output,
    w_expert_in,
    w_expert_out,
    w_shared_in,
    w_shared_out,
):
    dp = lax.axis_index(DP)
    rows = res_in.shape[0]
    first = ((dp >> 1) & 1) == 0
    n_half = EXPERTS // 2
    width = w_expert_out.shape[1]
    grad_pair, over_gate, lows, highs, saved = front(
        tok_counts,
        w_latent,
        (attn_gain[None], ffn_gain[None], latent_gain[None]),
        w_keyval,
        w_output,
        w_expert_in,
        w_expert_out,
        w_shared_in,
        w_shared_out,
        res_in,
        out_grad,
        w_query,
        seg_ids,
        slot_table[0],
        slot_gates[0],
    )
    pair_gate = jnp.concatenate(
        [g[:, k * rows : (k + 1) * rows] for k in range(4) for g in (saved.gates, over_gate)], axis=1
    )
    pair_gate = jnp.where(first, pair_gate[:n_half], pair_gate[n_half : 2 * n_half])
    mid_pair = saved.mid_pair.reshape(-1, D)
    grad_pair = grad_pair.reshape(-1, D)
    whole = 3 * width
    low, high = lows[2], highs[2]
    sums, keep0, give0, (high_far,) = experts_step(
        mid_pair,
        grad_pair,
        [(lows[0], 0, 4, 0, whole, 0), (highs[0], 4, 4, 0, whole, 0)],
        pair_gate[0],
        None,
        False,
        [Cut(low, 0, (0, 4), (width, whole - width))],
        5,
    )
    sums, keep1, give1, (y0a, y0b) = experts_step(
        mid_pair,
        grad_pair,
        [(lows[1], 0, 4, 0, whole, 0), (highs[1], 4, 4, 0, whole, 0)],
        pair_gate[1],
        sums,
        False,
        [Cut(give0[0], 0), Cut(give0[1], 0)],
        6,
    )
    (k0a, h0a), (k0b, h0b) = halve([(keep0[0], y0a), (keep0[1], y0b)])
    (back, out), keep2, give2, (y0c, y1a, z0a, z0b) = experts_step(
        mid_pair,
        grad_pair,
        [
            (low, 0, 4, 0, whole, 0),
            (high, 4, 4, 0, width, 0),
            (high_far, 4, 4, width, whole - width, 0),
        ],
        None,
        sums,
        True,
        [Cut(give0[2], 0), Cut(give1[0], 0), Cut(h0a, 2), Cut(h0b, 2)],
        7,
    )
    back = back.reshape(8, rows, D)
    out = out.reshape(8, rows, D)
    (mid_grad, ffn_gain_part, attn_grad), (y1b, y1c, y2a, y2b), split = back_tokens(
        back,
        saved.grad,
        saved.mid,
        saved.gains,
        saved.valid,
        [(0, give1[1]), (0, give1[2]), (0, give2[0]), (0, give2[1])],
        [(keep0[2], y0c, 2), (keep1[0], y1a, 2), (k0a, z0a, 1), (k0b, z0b, 1)],
    )
    (k0c, z0c), (k1a, z1a), over0a, over0b = split
    (*wgrads, back_part, out_sum, out_a, out_b), (y2c, output_came), split = attention_backward(
        attn_grad,
        saved,
        out,
        [(0, give2[2])],
        [(keep1[1], y1b, 2), (keep1[2], y1c, 2), (keep2[0], y2a, 2), (k0c, z0c, 1), (k1a, z1a, 1)],
    )
    (k1b, z1b), (k1c, z1c), (k2a, z2a), over0c, over1a = split
    (output_owned, query_owned, keyval_owned, latent_owned, res_grad, res_out), own2, over2, late = tail(
        back_part,
        wgrads,
        output_came,
        (out_sum, out_a, out_b),
        saved,
        mid_grad,
        ffn_gain_part,
        [(keep2[1], y2b, 2), (keep2[2], y2c, 2)],
        [(k1b, z1b, 1), (k1c, z1c, 1), (k2a, z2a, 1)],
    )
    ready = [over0a, over0b, over0c, over1a, *late]
    (
        res_out,
        res_grad,
        latent_owned,
        attn_gain,
        ffn_gain,
        latent_gain,
        expert_in,
        expert_out,
        shared_in,
        shared_out,
        output_owned,
        query_owned,
        keyval_owned,
    ) = finish(
        res_out,
        res_grad,
        latent_owned,
        [mine for mine, _ in ready] + list(own2),
        [],
        [other for _, other in ready] + list(over2),
        [output_owned, query_owned, keyval_owned],
        width,
    )
    return (
        res_out,
        res_grad,
        attn_gain[0],
        latent_gain[0],
        ffn_gain[0],
        latent_owned,
        query_owned,
        keyval_owned,
        output_owned,
        expert_in.transpose(0, 1, 3, 2),
        expert_out,
        shared_in.transpose(0, 2, 1),
        shared_out,
    )


def solution(mesh):
    placed = (
        P((DP, TENSOR), None),
        P((DP, TENSOR), None),
        P(DP, None),
        P(DP),
        P(DP, None, None),
        P(DP, None, None),
        P((DP, TENSOR)),
        P((DP, TENSOR)),
        P((DP, TENSOR)),
        P((DP, TENSOR), None),
        P(DP, TENSOR),
        P(DP, TENSOR),
        P(TENSOR, DP),
        P(None, None, DP, TENSOR),
        P(None, TENSOR, DP),
        P(None, DP, TENSOR),
        P(TENSOR, DP),
    )
    fits = mesh.shape[DP] == 8 and mesh.shape[TENSOR] == 4
    return jax.shard_map(
        body if fits else general_body,
        mesh=mesh,
        in_specs=placed,
        out_specs=(
            P((DP, TENSOR), None),
            P((DP, TENSOR), None),
            P((DP, TENSOR)),
            P((DP, TENSOR)),
            P((DP, TENSOR)),
            P((DP, TENSOR), None),
            P(DP, TENSOR),
            P(DP, TENSOR),
            P(TENSOR, DP),
            P(None, None, DP, TENSOR),
            P(None, TENSOR, DP),
            P(None, DP, TENSOR),
            P(TENSOR, DP),
        ),
        check_vma=False,
    )
```
